32 devices in a mesh: dp: 8 (over y, x, core), tensor: 4 (over z).
Axes of the slice: x: 2, y: 2, z: 4, core: 2. Of those that a mesh axis runs over, the one named last changes fastest.
Arguments:
- target: bfloat16 [8192, 768], P('dp'), may hold values from -6 to 6
- memory: bfloat16 [8192, 768], P('dp'), may hold values from -6 to 6
- target_segments: int32 [8, 1024], P('dp'), may hold values from 0 to 4, as said below
- memory_segments: int32 [8, 1024], P('dp'), may hold values from 0 to 4, as said below
- self_query: bfloat16 [768, 768], P(None, 'tensor'), may hold values from -0.21875 to 0.21875
- self_query_bias: float32 [768], P('tensor'), may hold values from -3 to 3
- self_key: bfloat16 [768, 768], P(None, 'tensor'), may hold values from -0.21875 to 0.21875
- self_value: bfloat16 [768, 768], P(None, 'tensor'), may hold values from -0.21875 to 0.21875
- self_value_bias: float32 [768], P('tensor'), may hold values from -3 to 3
- self_output: bfloat16 [768, 768], P('tensor'), may hold values from -1.25 to 1.25
- self_output_bias: float32 [768], replicated, may hold values from -2 to 2
- first_gain: float32 [768], replicated, may hold values from 0.25 to 1.75
- first_shift: float32 [768], replicated, may hold values from -2 to 2
- cross_query: bfloat16 [768, 768], P(None, 'tensor'), may hold values from -0.21875 to 0.21875
- cross_query_bias: float32 [768], P('tensor'), may hold values from -3 to 3
- cross_key: bfloat16 [768, 768], P(None, 'tensor'), may hold values from -0.21875 to 0.21875
- cross_value: bfloat16 [768, 768], P(None, 'tensor'), may hold values from -0.21875 to 0.21875
- cross_value_bias: float32 [768], P('tensor'), may hold values from -3 to 3
- cross_output: bfloat16 [768, 768], P('tensor'), may hold values from -1.75 to 1.75
- cross_output_bias: float32 [768], replicated, may hold values from -2 to 2
- second_gain: float32 [768], replicated, may hold values from 0.25 to 1.75
- second_shift: float32 [768], replicated, may hold values from -2 to 2
- expand_weight: bfloat16 [768, 3072], P(None, 'tensor'), may hold values from -0.21875 to 0.21875
- expand_bias: float32 [3072], P('tensor'), may hold values from -3 to 3
- contract_weight: bfloat16 [3072, 768], P('tensor'), may hold values from -0.21875 to 0.21875
- contract_bias: float32 [768], replicated, may hold values from -2 to 2
- third_gain: float32 [768], replicated, may hold values from 0.25 to 1.75
- third_shift: float32 [768], replicated, may hold values from -2 to 2
- output_grad: bfloat16 [8192, 768], P('dp'), may hold values from -6 to 6
Outputs:
- layer_output: bfloat16 [8192, 768], P('dp')
- target_grad: bfloat16 [8192, 768], P('dp', 'tensor')
- memory_grad: bfloat16 [8192, 768], P('dp', 'tensor')
- grad_self_query: float32 [768, 768], P('dp', 'tensor')
- grad_self_query_bias: float32 [768], P('tensor')
- grad_self_key: float32 [768, 768], P('dp', 'tensor')
- grad_self_value: float32 [768, 768], P('dp', 'tensor')
- grad_self_value_bias: float32 [768], P('tensor')
- grad_self_output: float32 [768, 768], P('tensor', 'dp')
- grad_self_output_bias: float32 [768], replicated
- grad_first_gain: float32 [768], replicated
- grad_first_shift: float32 [768], replicated
- grad_cross_query: float32 [768, 768], P('dp', 'tensor')
- grad_cross_query_bias: float32 [768], P('tensor')
- grad_cross_key: float32 [768, 768], P('dp', 'tensor')
- grad_cross_value: float32 [768, 768], P('dp', 'tensor')
- grad_cross_value_bias: float32 [768], P('tensor')
- grad_cross_output: float32 [768, 768], P('tensor', 'dp')
- grad_cross_output_bias: float32 [768], replicated
- grad_second_gain: float32 [768], replicated
- grad_second_shift: float32 [768], replicated
- grad_expand_weight: float32 [768, 3072], P('dp', 'tensor')
- grad_expand_bias: float32 [3072], P('tensor')
- grad_contract_weight: float32 [3072, 768], P('tensor', 'dp')
- grad_contract_bias: float32 [768], replicated
- grad_third_gain: float32 [768], replicated
- grad_third_shift: float32 [768], replicated
The draws below stay inside these ranges and needn't reach their ends.
Inputs may be any that keep to these rules, and one draw needn't show every extreme that they name: `target_segments`: along each row the ids never fall. Ids 0 to 3 are documents, every one present in every row with one or more positions; id 4 marks the padding at the row's end, 1 to 128 positions, and appears in every row. `memory_segments`: same law as target_segments, drawn independently: document d of a memory row belongs to document d of the same target row, and padding of target rows reads padding of memory rows.
All inputs are finite; a program needn't handle non-finite values.
Results may differ from the reference program's by a relative error of at most 0.025.
The reference program's roundings to bfloat16 on the way count: a program that leaves them out, or rounds other values in their place, can miss the bound.
Values sent between devices are 32-bit elements; how exact they have to be, the bound alone decides.
A program may use at most 128 MiB of HBM per device.

```python
from functools import partial
import jax
import jax.numpy as jnp
from jax import lax

D = 768
HEADS = 12
FF = 3072
HEAD_DIM = 64
SEQ = 1024
DOCS = 4
ROWS = 8
TOKENS = 8192


def segment_rows(base_key):

    def one_row(row_key):
        first_key, second_key = jax.random.split(row_key)
        live_count = SEQ - jax.random.randint(first_key, (), 1, SEQ // 8 + 1, dtype=jnp.int32)
        choices_all = jax.random.permutation(second_key, jnp.arange(1, SEQ - SEQ // 8, dtype=jnp.int32))
        cut_points = choices_all[:DOCS - 1]
        positions = jnp.arange(SEQ, dtype=jnp.int32)
        doc_ids = jnp.sum((cut_points[None, :] <= positions[:, None]).astype(jnp.int32), axis=1)
        return jnp.where(positions < live_count, doc_ids, DOCS).astype(jnp.int32)
    return jax.vmap(one_row)(jax.random.split(base_key, ROWS))


def draw_target_segments(key, part):
    return segment_rows(jax.random.fold_in(key, 11))


def draw_memory_segments(key, part):
    return segment_rows(jax.random.fold_in(key, 23))


def with_spikes(values, rng, source, target, shards_of, factor):
    owner, partner = [(jnp.arange(values.shape[dim]) // (values.shape[dim] // shards_of)).reshape([-1 if axis == dim else 1 for axis in range(values.ndim)]) for dim in (source, target)]
    chosen = jax.random.permutation(rng, shards_of)[partner]
    strong = (owner == chosen) | (owner == (partner + shards_of // 2) % shards_of)
    return jnp.where(strong, factor * values, values)


def steps_of(own_key, shape, cuts, smallest, top_value):
    def one(axis_at, parts):
        steps = jax.random.uniform(jax.random.fold_in(jax.random.fold_in(own_key, 6), axis_at), (parts,), jnp.float32, smallest / len(cuts), top_value / len(cuts))
        return jnp.repeat(jnp.exp(steps), shape[axis_at] // parts).reshape((-1,) + (1,) * (len(shape) - axis_at - 1))

    level = one(*cuts[0])
    for cut in cuts[1:]:
        level = level * one(*cut)
    return level


def centred(own_key, shape, scale, reach, cuts=(), kind=jnp.bfloat16):
    values = scale * jax.random.normal(own_key, shape, jnp.float32)
    if cuts:
        values = values * steps_of(own_key, shape, cuts, -0.22, 0.18)
    return jnp.clip(values, -reach, reach).astype(kind)


def gaussian_with(key, shape, scale, bound, pieces, heavy, kind=jnp.bfloat16):
    array = scale * jax.random.normal(key, shape, jnp.float32)
    if pieces:
        array = array * steps_of(key, shape, pieces, -0.22, 0.18)
    return jnp.clip(with_spikes(array, jax.random.fold_in(key, 3), *heavy), -bound, bound).astype(kind)


def setup_inputs(seed: int = 0) -> dict:
    keys = jax.random.split(jax.random.key(seed), 30)
    target = centred(keys[0], (TOKENS, D), 1.0, 6.0, ((0, 8),))
    memory = centred(keys[1], (TOKENS, D), 1.0, 6.0, ((0, 8),))
    target_segments = draw_target_segments(jax.random.fold_in(keys[29], 71), 0)
    memory_segments = draw_memory_segments(jax.random.fold_in(keys[29], 71), 0)
    self_query = centred(keys[4], (D, D), D ** -0.5, 0.21875, ((1, 4),))
    self_query_bias = centred(keys[5], (D,), 0.5, 3.0, ((0, 4),), jnp.float32)
    self_key = centred(keys[6], (D, D), D ** -0.5, 0.21875, ((1, 4),))
    self_value = centred(keys[7], (D, D), D ** -0.5, 0.21875, ((1, 4),))
    self_value_bias = centred(keys[8], (D,), 0.5, 3.0, ((0, 4),), jnp.float32)
    self_output = centred(keys[9], (D, D), (D // 32) ** -0.5, 1.25, ((0, 4),))
    self_output_bias = centred(keys[10], (D,), 0.3, 2.0, (), jnp.float32)
    first_gain = jnp.clip(1.0 + 0.15 * jax.random.normal(keys[11], (D,), jnp.float32), 0.25, 1.75)
    first_shift = centred(keys[12], (D,), 0.3, 2.0, (), jnp.float32)
    cross_query = centred(keys[13], (D, D), D ** -0.5, 0.21875, ((1, 4),))
    cross_query_bias = centred(keys[14], (D,), 0.5, 3.0, ((0, 4),), jnp.float32)
    cross_key = centred(keys[15], (D, D), D ** -0.5, 0.21875, ((1, 4),))
    cross_value = centred(keys[16], (D, D), D ** -0.5, 0.21875, ((1, 4),))
    cross_value_bias = centred(keys[17], (D,), 0.5, 3.0, ((0, 4),), jnp.float32)
    cross_output = centred(keys[18], (D, D), (D // 64) ** -0.5, 1.75, ((0, 4),))
    cross_output_bias = centred(keys[19], (D,), 0.3, 2.0, (), jnp.float32)
    second_gain = jnp.clip(1.0 + 0.15 * jax.random.normal(keys[20], (D,), jnp.float32), 0.25, 1.75)
    second_shift = centred(keys[21], (D,), 0.3, 2.0, (), jnp.float32)
    expand_weight = centred(keys[22], (D, FF), D ** -0.5, 0.21875, ((1, 4),))
    expand_bias = centred(keys[23], (FF,), 0.5, 3.0, ((0, 4),), jnp.float32)
    contract_weight = centred(keys[24], (FF, D), (FF // 4) ** -0.5, 0.21875, ((0, 4),))
    contract_bias = centred(keys[25], (D,), 0.3, 2.0, (), jnp.float32)
    third_gain = jnp.clip(1.0 + 0.15 * jax.random.normal(keys[26], (D,), jnp.float32), 0.25, 1.75)
    third_shift = centred(keys[27], (D,), 0.3, 2.0, (), jnp.float32)
    output_grad = gaussian_with(keys[28], (TOKENS, D), 1.0, 6.0, ((0, 8),), (0, 1, 8, 2.0))
    return {"target": target, "memory": memory, "target_segments": target_segments, "memory_segments": memory_segments, "self_query": self_query, "self_query_bias": self_query_bias, "self_key": self_key, "self_value": self_value, "self_value_bias": self_value_bias, "self_output": self_output, "self_output_bias": self_output_bias, "first_gain": first_gain, "first_shift": first_shift, "cross_query": cross_query, "cross_query_bias": cross_query_bias, "cross_key": cross_key, "cross_value": cross_value, "cross_value_bias": cross_value_bias, "cross_output": cross_output, "cross_output_bias": cross_output_bias, "second_gain": second_gain, "second_shift": second_shift, "expand_weight": expand_weight, "expand_bias": expand_bias, "contract_weight": contract_weight, "contract_bias": contract_bias, "third_gain": third_gain, "third_shift": third_shift, "output_grad": output_grad}


EPSILON = 1e-05
NEGATIVE = -1e+30

@jax.custom_vjp
def low(v):
    return lax.optimization_barrier(v.astype(jnp.bfloat16)).astype(jnp.float32)

@jax.custom_vjp
def low_back(v):
    return v

def low_keep(v):
    return (low(v), None)

def low_pass(kept, grad):
    return (grad,)

def back_keep(v):
    return (v, None)

def back_low(kept, grad):
    return (low(grad),)
low.defvjp(low_keep, low_pass)
low_back.defvjp(back_keep, back_low)

def both_round(value):
    return low(low_back(value))

def matmul(left_side, right_side):
    return jnp.dot(left_side, right_side, preferred_element_type=jnp.float32, precision=lax.Precision.HIGHEST)

def normalize(summed, norm_gain, norm_shift):
    center = lax.optimization_barrier(jnp.mean(summed, axis=-1, keepdims=True))
    centered = summed - center
    spread = lax.optimization_barrier(jnp.mean(centered * centered, axis=-1, keepdims=True))
    return centered * lax.rsqrt(spread + EPSILON) * norm_gain + norm_shift

def attention(causal, query_rows, key_rows, value_rows, query_ids, key_ids):
    length = query_rows.shape[0]
    block_rows = min(512, length)
    score_scale = HEAD_DIM ** (-0.5)

    def one_block(block_index, queries, key_part, value_part, all_query_ids, all_key_ids):
        first_row = block_index * block_rows
        chosen = lax.dynamic_slice_in_dim(queries, first_row, block_rows, 0)
        chosen_ids = lax.dynamic_slice_in_dim(all_query_ids, first_row, block_rows, 0)
        allowed = chosen_ids[:, None] == all_key_ids[None, :]
        if causal:
            query_pos = first_row + jnp.arange(block_rows, dtype=jnp.int32)
            key_pos = jnp.arange(length, dtype=jnp.int32)
            allowed = allowed & (query_pos[:, None] >= key_pos[None, :])
        scores = jnp.einsum('qhd,khd->hqk', chosen, key_part, precision=lax.Precision.HIGHEST) * score_scale
        scores = jnp.where(allowed[None], low_back(scores), NEGATIVE)
        weights_soft = low(jax.nn.softmax(scores, axis=-1))
        return jnp.einsum('hqk,khd->qhd', weights_soft, value_part, precision=lax.Precision.HIGHEST)
    checked = jax.checkpoint(one_block)

    def run_block(block_index):
        return checked(block_index, query_rows, key_rows, value_rows, query_ids, key_ids)
    mixture = lax.map(run_block, jnp.arange(length // block_rows, dtype=jnp.int32))
    return mixture.reshape(length, -1)

def layer(params, target_rows, memory_rows, target_ids, memory_ids):
    self_query, self_query_bias, self_key, self_value, self_value_bias, self_output, self_output_bias, first_gain, first_shift, cross_query, cross_query_bias, cross_key, cross_value, cross_value_bias, cross_output, cross_output_bias, second_gain, second_shift, expand_weight, expand_bias, contract_weight, contract_bias, third_gain, third_shift = params
    row_count = target_ids.shape[0]

    def to_heads(matrix):
        return matrix.reshape(row_count, SEQ, HEADS, HEAD_DIM)
    self_queries = both_round(matmul(target_rows, self_query) + self_query_bias)
    self_keys = both_round(matmul(target_rows, self_key))
    self_values = both_round(matmul(target_rows, self_value) + self_value_bias)
    self_mixed = jax.vmap(partial(attention, True))(to_heads(self_queries), to_heads(self_keys), to_heads(self_values), target_ids, target_ids)
    self_mixed = both_round(self_mixed.reshape(-1, D))
    self_branch = low_back(matmul(self_mixed, self_output) + self_output_bias)
    first = normalize(target_rows + self_branch, first_gain, first_shift)
    first_low = low(first)
    cross_queries = both_round(matmul(first_low, cross_query) + cross_query_bias)
    cross_keys = both_round(matmul(memory_rows, cross_key))
    cross_values = both_round(matmul(memory_rows, cross_value) + cross_value_bias)
    cross_mixed = jax.vmap(partial(attention, False))(to_heads(cross_queries), to_heads(cross_keys), to_heads(cross_values), target_ids, memory_ids)
    cross_mixed = both_round(cross_mixed.reshape(-1, D))
    cross_branch = low_back(matmul(cross_mixed, cross_output) + cross_output_bias)
    second = normalize(first + cross_branch, second_gain, second_shift)
    second_low = low(second)
    hidden = low_back(matmul(second_low, expand_weight) + expand_bias)
    activated = low(jax.nn.gelu(hidden, approximate=False))
    ffn_branch = low_back(matmul(activated, contract_weight) + contract_bias)
    return normalize(second + ffn_branch, third_gain, third_shift)

def reference(target, memory, target_segments, memory_segments, self_query, self_query_bias, self_key, self_value, self_value_bias, self_output, self_output_bias, first_gain, first_shift, cross_query, cross_query_bias, cross_key, cross_value, cross_value_bias, cross_output, cross_output_bias, second_gain, second_shift, expand_weight, expand_bias, contract_weight, contract_bias, third_gain, third_shift, output_grad):
    weights = (self_query, self_query_bias, self_key, self_value, self_value_bias, self_output, self_output_bias, first_gain, first_shift, cross_query, cross_query_bias, cross_key, cross_value, cross_value_bias, cross_output, cross_output_bias, second_gain, second_shift, expand_weight, expand_bias, contract_weight, contract_bias, third_gain, third_shift)
    weights = tuple((member.astype(jnp.float32) for member in weights))
    group_rows = 4 if ROWS % 4 == 0 else 1
    group_count = ROWS // group_rows
    target_ids = target_segments.reshape(group_count, group_rows, SEQ)
    memory_ids = memory_segments.reshape(group_count, group_rows, SEQ)
    checked_layer = jax.checkpoint(layer)

    def forward(params, target_float, memory_float):
        grouped_target = target_float.reshape(group_count, group_rows * SEQ, D)
        grouped_memory = memory_float.reshape(group_count, group_rows * SEQ, D)

        def one_group(items):
            return checked_layer(params, items[0], items[1], items[2], items[3])
        result = lax.map(one_group, (grouped_target, grouped_memory, target_ids, memory_ids))
        return result.reshape(ROWS * SEQ, D)
    final, pullback = jax.vjp(forward, weights, target.astype(jnp.float32), memory.astype(jnp.float32))
    grad_params, grad_target, grad_memory = pullback(output_grad.astype(jnp.float32))
    return (final.astype(jnp.bfloat16), grad_target.astype(jnp.bfloat16), grad_memory.astype(jnp.bfloat16), grad_params[0], grad_params[1], grad_params[2], grad_params[3], grad_params[4], grad_params[5], grad_params[6], grad_params[7], grad_params[8], grad_params[9], grad_params[10], grad_params[11], grad_params[12], grad_params[13], grad_params[14], grad_params[15], grad_params[16], grad_params[17], grad_params[18], grad_params[19], grad_params[20], grad_params[21], grad_params[22], grad_params[23])
```

```python
from functools import partial

import jax
import jax.numpy as jnp
from jax import lax
from jax.experimental import pallas as pl
from jax.experimental.pallas import tpu as pltpu
from jax.sharding import PartitionSpec as P

HEAD_DIM = 64
EPSILON = 1e-05
NEGATIVE = -1e30
BF = jnp.bfloat16
F32 = jnp.float32
MESH = pl.DeviceIdType.MESH
MIB = 2**20


def dot_nn(a, b):
    return lax.dot_general(a, b, (((1,), (0,)), ((), ())), preferred_element_type=F32)


def dot_nt(a, b):
    return lax.dot_general(a, b, (((1,), (1,)), ((), ())), preferred_element_type=F32)


def dot_tn(a, b):
    return lax.dot_general(a, b, (((0,), (0,)), ((), ())), preferred_element_type=F32)


def normalize(summed, norm_gain, norm_shift):
    center = jnp.mean(summed, axis=-1, keepdims=True)
    centered = summed - center
    spread = jnp.mean(centered * centered, axis=-1, keepdims=True)
    return centered * lax.rsqrt(spread + EPSILON) * norm_gain + norm_shift


def exact_gelu(values):
    return jax.nn.gelu(values, approximate=False)


def column_sums(values):
    return jnp.sum(values.astype(F32), axis=0)


def row_groups(width, hidden):
    half = 2 * width
    sizes = [half, half, half, half, hidden, hidden]
    starts = [sum(sizes[:i]) for i in range(len(sizes))]
    return list(zip(starts, sizes, strict=True))


def gather_kernel(
    groups, n_dp, n_tensor, chunk_ref, bias_ref, own_ref, found_ref, full_ref, bias_out_ref, stage, low, send_sem, recv_sem,
    bias_send, bias_recv, local_sem
):
    d = lax.axis_index("dp")
    z = lax.axis_index("tensor")
    bit_c = d % 2
    bit_x = (d // 2) % 2
    bit_y = d // 4
    dc = d + 1 - 2 * bit_c
    dx = d + 2 - 4 * bit_x
    dy = d + 4 - 8 * bit_y
    dxy = dx + 4 - 8 * bit_y
    barrier = pltpu.get_barrier_semaphore()
    for k in range(1, n_tensor):
        pl.semaphore_signal(barrier, inc=1, device_id={"tensor": (z + k) % n_tensor}, device_id_type=MESH)
    for other in (dc, dx, dy):
        pl.semaphore_signal(barrier, inc=1, device_id={"dp": other}, device_id_type=MESH)
    pl.semaphore_wait(barrier, n_tensor + 2)

    spans = []
    at = 0
    for _, size in groups:
        spans.append((at, size // n_dp))
        at += size // n_dp

    def to_z(g, k):
        start, rows = spans[g]
        return pltpu.make_async_remote_copy(
            src_ref=chunk_ref.at[pl.ds(start, rows)],
            dst_ref=found_ref.at[d, k, pl.ds(start, rows)],
            send_sem=send_sem.at[g, k],
            recv_sem=recv_sem.at[g, k],
            device_id={"tensor": (z + k + 1) % n_tensor},
            device_id_type=MESH,
        )

    def in_plane(g, slot, chunk, first, rows, other):
        piece = found_ref.at[chunk, :, pl.ds(first, rows)]
        return pltpu.make_async_remote_copy(
            src_ref=piece,
            dst_ref=piece,
            send_sem=send_sem.at[g, slot],
            recv_sem=recv_sem.at[g, slot],
            device_id={"dp": other},
            device_id_type=MESH,
        )

    def bias_copy(k):
        return pltpu.make_async_remote_copy(
            src_ref=bias_ref,
            dst_ref=bias_out_ref.at[z],
            send_sem=bias_send.at[k],
            recv_sem=bias_recv.at[k],
            device_id={"tensor": (z + k + 1) % n_tensor},
            device_id_type=MESH,
        )

    def own_x(g):
        return in_plane(g, 3, d, *spans[g], dx)

    def own_y(g):
        return in_plane(g, 4, d, *spans[g], dy)

    def own_c(g):
        return in_plane(g, 5, d, *spans[g], dc)

    def pass_y(g):
        start, rows = spans[g]
        return in_plane(g, 6, dx, start, rows // 2, dy)

    def pass_x(g):
        start, rows = spans[g]
        return in_plane(g, 7, dy, start + rows // 2, rows // 2, dx)

    def pass_c(g, i):
        return in_plane(g, 8 + i, (dx, dy, dxy)[i], *spans[g], dc)

    def arrive(g, slot, chunk, first, rows):
        in_plane(g, slot, chunk, first, rows, dc).wait_recv()

    count = len(groups)
    for k in range(n_tensor - 1):
        bias_copy(k).start()
    own_bias = pltpu.make_async_copy(bias_ref, bias_out_ref.at[z], local_sem.at[4])
    own_bias.start()
    for g in range(count):
        for k in range(n_tensor - 1):
            to_z(g, k).start()

    def stage_in(g):
        for k in range(n_tensor - 1):
            to_z(g, k).wait_recv()
        own_x(g).start()
        own_y(g).start()
        own_c(g).start()

    def stage_pass(g):
        start, rows = spans[g]
        arrive(g, 3, dx, start, rows)
        pass_y(g).start()
        pass_c(g, 0).start()
        arrive(g, 4, dy, start, rows)
        pass_x(g).start()
        pass_c(g, 1).start()

    def stage_last(g):
        start, rows = spans[g]
        arrive(g, 6, dxy, start, rows // 2)
        arrive(g, 7, dxy, start + rows // 2, rows // 2)
        pass_c(g, 2).start()

    def stage_out(g):
        start, rows = spans[g]
        arrive(g, 5, dc, start, rows)
        for i in range(3):
            arrive(g, 8 + i, dc, start, rows)
        first, size = groups[g]
        for k in range(n_tensor):
            slot = k % 2
            s = (z + n_tensor - 1 - k) % n_tensor
            low_piece = low.at[slot, pl.ds(0, size)]
            if k < n_tensor - 1:
                piece = stage.at[:, pl.ds(0, rows)]
                load = pltpu.make_async_copy(found_ref.at[:, k, pl.ds(start, rows)], piece, local_sem.at[slot])
                load.start()
                load.wait()
                low[slot, pl.ds(0, size)] = stage[:, pl.ds(0, rows)].reshape(size, stage.shape[2]).astype(BF)
            else:
                load = pltpu.make_async_copy(own_ref.at[pl.ds(first, size)], low_piece, local_sem.at[slot])
                load.start()
                load.wait()
            store = pltpu.make_async_copy(low_piece, full_ref.at[s, pl.ds(first, size)], local_sem.at[2 + slot])
            store.start()
            store.wait()

    for g in range(count + 3):
        if g < count:
            stage_in(g)
        if 0 <= g - 1 < count:
            stage_pass(g - 1)
        if 0 <= g - 2 < count:
            stage_last(g - 2)
        if 0 <= g - 3 < count:
            stage_out(g - 3)
    own_bias.wait()
    for k in range(n_tensor - 1):
        bias_copy(k).wait_recv()
        bias_copy(k).wait_send()
    for g in range(count):
        for k in range(n_tensor - 1):
            to_z(g, k).wait_send()
        own_x(g).wait_send()
        own_y(g).wait_send()
        own_c(g).wait_send()
        pass_y(g).wait_send()
        pass_x(g).wait_send()
        for i in range(3):
            pass_c(g, i).wait_send()


def round_kernel(wide_ref, low_ref):
    low_ref[...] = wide_ref[...].astype(BF)


def rounded(array):
    slices, rows, width = array.shape
    block = pl.BlockSpec((1, rows // 4, width), lambda i, j: (i, j, 0))
    return pl.pallas_call(
        round_kernel,
        grid=(slices, 4),
        in_specs=[block],
        out_specs=block,
        out_shape=jax.ShapeDtypeStruct(array.shape, BF),
    )(array)


def gather_weights(own, biases, groups, n_dp, n_tensor):
    rows, width = own.shape
    if n_dp != 8 or n_tensor != 4:
        full = lax.all_gather(own.astype(F32), "tensor", axis=0)
        return rounded(full), lax.all_gather(biases, "tensor", axis=0)
    d = lax.axis_index("dp")
    pieces = [
        lax.dynamic_slice_in_dim(own, start + d * (size // n_dp), size // n_dp, 0) for start, size in groups
    ]
    chunk = jnp.concatenate(pieces, axis=0).astype(F32)
    most = max(size for _, size in groups)
    anywhere = pl.BlockSpec(memory_space=pl.ANY)
    _, full, all_biases = pl.pallas_call(
        partial(gather_kernel, groups, n_dp, n_tensor),
        out_shape=(
            jax.ShapeDtypeStruct((n_dp, n_tensor - 1, rows // n_dp, width), F32),
            jax.ShapeDtypeStruct((n_tensor, rows, width), BF),
            jax.ShapeDtypeStruct((n_tensor,) + biases.shape, F32),
        ),
        in_specs=[anywhere] * 3,
        out_specs=[anywhere] * 3,
        scratch_shapes=[
            pltpu.VMEM((n_dp, most // n_dp, width), F32),
            pltpu.VMEM((2, most, width), BF),
            pltpu.SemaphoreType.DMA((len(groups), 11)),
            pltpu.SemaphoreType.DMA((len(groups), 11)),
            pltpu.SemaphoreType.DMA((n_tensor - 1,)),
            pltpu.SemaphoreType.DMA((n_tensor - 1,)),
            pltpu.SemaphoreType.DMA((5,)),
        ],
        compiler_params=pltpu.CompilerParams(collective_id=0, has_side_effects=True, vmem_limit_bytes=32 * MIB),
    )(chunk, biases, own)
    return full, all_biases


def attend_kernel(block, causal, q_ref, k_ref, v_ref, q_ids_ref, k_ids_ref, mixed_ref, sums_ref):
    length = q_ref.shape[0]
    lane = lax.broadcasted_iota(jnp.int32, (1, 2 * HEAD_DIM), 1)
    k_ids = k_ids_ref[...]
    for start in range(0, length, block):
        reach = start + block if causal else length
        queries = q_ref[start : start + block, :] * jnp.asarray(HEAD_DIM**-0.5, BF)
        allowed = q_ids_ref[start : start + block, :] == k_ids[:, :reach]
        if causal:
            allowed = allowed & (
                lax.broadcasted_iota(jnp.int32, (block, reach), 0) + start
                >= lax.broadcasted_iota(jnp.int32, (block, reach), 1)
            )
        outs, logs = [], []
        for head in range(2):
            mine = (lane < HEAD_DIM) if head == 0 else (lane >= HEAD_DIM)
            scores = dot_nt(jnp.where(mine, queries, jnp.zeros_like(queries)), k_ref[:reach, :])
            scores = jnp.where(allowed, scores, NEGATIVE)
            top = jnp.max(scores, axis=1, keepdims=True)
            weights = jnp.exp(scores - top)
            total = jnp.sum(weights, axis=1, keepdims=True)
            outs.append(dot_nn(weights.astype(BF), v_ref[:reach, :]) * (1.0 / total))
            logs.append(top + jnp.log(total))
        mixed_ref[start : start + block, :] = jnp.where(lane < HEAD_DIM, outs[0], outs[1]).astype(BF)
        sums_ref[start : start + block, :] = jnp.where(lane < HEAD_DIM, logs[0], logs[1])


def attend(causal, queries, keys, values, query_ids, key_ids):
    length, width = queries.shape
    pair = 2 * HEAD_DIM
    wide = pl.BlockSpec((length, pair), lambda i: (0, i))
    return pl.pallas_call(
        partial(attend_kernel, 512, causal),
        grid=(width // pair,),
        in_specs=[wide] * 3 + [pl.BlockSpec((length, 1), lambda i: (0, 0)), pl.BlockSpec((1, length), lambda i: (0, 0))],
        out_specs=[wide] * 2,
        out_shape=[jax.ShapeDtypeStruct((length, width), BF), jax.ShapeDtypeStruct((length, width), F32)],
        compiler_params=pltpu.CompilerParams(vmem_limit_bytes=60 * MIB),
    )(queries, keys, values, query_ids.reshape(length, 1), key_ids.reshape(1, length))


def attend_back_kernel(
    block, causal, q_ref, k_ref, v_ref, gm_ref, mixed_ref, sums_ref, q_ids_ref, k_ids_ref, gq_ref, gk_ref, gv_ref, gq_sum,
    logs, dots
):
    length = q_ref.shape[0]
    lane = lax.broadcasted_iota(jnp.int32, (1, 2 * HEAD_DIM), 1)
    scale = HEAD_DIM**-0.5
    gq_sum[...] = jnp.zeros_like(gq_sum)
    logs[...] = jnp.transpose(sums_ref[...])
    products = jnp.transpose(gm_ref[...].astype(F32) * mixed_ref[...].astype(F32))
    dots[0:1, :] = jnp.sum(products[:HEAD_DIM], axis=0, keepdims=True)
    dots[1:2, :] = jnp.sum(products[HEAD_DIM:], axis=0, keepdims=True)
    for start in range(0, length, block):
        first = start if causal else 0
        reach = length - first
        keys = k_ref[start : start + block, :]
        values = v_ref[start : start + block, :]
        allowed = k_ids_ref[start : start + block, :] == q_ids_ref[:, first:]
        if causal:
            allowed = allowed & (
                lax.broadcasted_iota(jnp.int32, (block, reach), 0) + start
                <= lax.broadcasted_iota(jnp.int32, (block, reach), 1) + first
            )
        gk = jnp.zeros((block, 2 * HEAD_DIM), F32)
        gv = jnp.zeros((block, 2 * HEAD_DIM), F32)
        queries = q_ref[first:, :]
        gm = gm_ref[first:, :]
        for head in range(2):
            mine = (lane < HEAD_DIM) if head == 0 else (lane >= HEAD_DIM)
            keys_h = jnp.where(mine, keys, jnp.zeros_like(keys))
            values_h = jnp.where(mine, values, jnp.zeros_like(values))
            scores = dot_nt(keys_h * jnp.asarray(scale, BF), queries)
            probs = jnp.where(allowed, jnp.exp(scores - logs[HEAD_DIM * head : HEAD_DIM * head + 1, first:]), 0.0)
            grad_probs = dot_nt(values_h, gm)
            grad_scores = (probs * (grad_probs - dots[head : head + 1, first:])).astype(BF)
            gv = gv + dot_nn(probs.astype(BF), jnp.where(mine, gm, jnp.zeros_like(gm)))
            gk = gk + dot_nn(grad_scores, jnp.where(mine, queries, jnp.zeros_like(queries)))
            gq_sum[first:, :] += dot_tn(grad_scores, keys_h)
        gk_ref[start : start + block, :] = (gk * scale).astype(BF)
        gv_ref[start : start + block, :] = gv.astype(BF)
    gq_ref[...] = (gq_sum[...] * scale).astype(BF)


def attend_back(causal, queries, keys, values, grad_mixed, mixed, sums, query_ids, key_ids):
    length, width = queries.shape
    pair = 2 * HEAD_DIM
    wide = pl.BlockSpec((length, pair), lambda i: (0, i))
    low = jax.ShapeDtypeStruct((length, width), BF)
    return pl.pallas_call(
        partial(attend_back_kernel, 256, causal),
        grid=(width // pair,),
        in_specs=[wide] * 6 + [pl.BlockSpec((1, length), lambda i: (0, 0)), pl.BlockSpec((length, 1), lambda i: (0, 0))],
        out_specs=[wide] * 3,
        out_shape=[low] * 3,
        scratch_shapes=[
            pltpu.VMEM((length, pair), F32),
            pltpu.VMEM((pair, length), F32),
            pltpu.VMEM((8, length), F32),
        ],
        compiler_params=pltpu.CompilerParams(vmem_limit_bytes=60 * MIB),
    )(queries, keys, values, grad_mixed, mixed, sums, query_ids.reshape(1, length), key_ids.reshape(length, 1))


def per_device(
    n_dp,
    n_tensor,
    target,
    memory,
    target_segments,
    memory_segments,
    self_query,
    self_query_bias,
    self_key,
    self_value,
    self_value_bias,
    self_output,
    self_output_bias,
    first_gain,
    first_shift,
    cross_query,
    cross_query_bias,
    cross_key,
    cross_value,
    cross_value_bias,
    cross_output,
    cross_output_bias,
    second_gain,
    second_shift,
    expand_weight,
    expand_bias,
    contract_weight,
    contract_bias,
    third_gain,
    third_shift,
    output_grad,
):
    model, width = self_query.shape
    hidden_own = expand_weight.shape[1]
    z = lax.axis_index("tensor")
    heads_all = width * n_tensor

    own = jnp.concatenate(
        (
            self_query.T,
            self_key.T,
            self_value.T,
            self_output,
            cross_key.T,
            cross_value.T,
            cross_query.T,
            cross_output,
            expand_weight.T,
            contract_weight,
        ),
        axis=0,
    )
    biases = jnp.concatenate((self_query_bias, self_value_bias, cross_query_bias, cross_value_bias, expand_bias))
    bias_count = biases.shape[0]
    bias_rows = -(-bias_count // 1024) * 8
    biases = jnp.pad(biases, (0, bias_rows * 128 - bias_count)).reshape(bias_rows, 128)
    groups = row_groups(width, hidden_own)
    full, all_biases = gather_weights(own, biases, groups, n_dp, n_tensor)

    def matrix(index):
        return full[:, index * width : (index + 1) * width].reshape(heads_all, model)

    w_sq, w_sk, w_sv, w_so, w_ck, w_cv, w_cq, w_co = (matrix(i) for i in range(8))
    w_ex = full[:, 8 * width : 8 * width + hidden_own].reshape(hidden_own * n_tensor, model)
    w_ct = full[:, 8 * width + hidden_own :].reshape(hidden_own * n_tensor, model)
    all_biases = all_biases.reshape(n_tensor, -1)
    b_sq, b_sv, b_cq, b_cv = (all_biases[:, i * width : (i + 1) * width].reshape(-1) for i in range(4))
    b_ex = all_biases[:, 4 * width : 4 * width + hidden_own].reshape(-1)

    target_ids = target_segments
    memory_ids = memory_segments

    self_queries = (dot_nt(target, w_sq) + b_sq).astype(BF)
    self_keys = dot_nt(target, w_sk).astype(BF)
    self_values = (dot_nt(target, w_sv) + b_sv).astype(BF)
    self_mixed, self_sums = attend(True, self_queries, self_keys, self_values, target_ids, target_ids)
    self_branch = dot_nn(self_mixed, w_so) + self_output_bias
    first_norm, first_back = jax.vjp(normalize, target.astype(F32) + self_branch, first_gain, first_shift)
    first_low = first_norm.astype(BF)
    cross_queries = (dot_nt(first_low, w_cq) + b_cq).astype(BF)
    cross_keys = dot_nt(memory, w_ck).astype(BF)
    cross_values = (dot_nt(memory, w_cv) + b_cv).astype(BF)
    cross_mixed, cross_sums = attend(False, cross_queries, cross_keys, cross_values, target_ids, memory_ids)
    cross_branch = dot_nn(cross_mixed, w_co) + cross_output_bias
    second_norm, second_back = jax.vjp(normalize, first_norm + cross_branch, second_gain, second_shift)
    second_low = second_norm.astype(BF)
    hidden = dot_nt(second_low, w_ex) + b_ex
    activated_float, gelu_back = jax.vjp(exact_gelu, hidden)
    activated = activated_float.astype(BF)
    ffn_branch = dot_nn(activated, w_ct) + contract_bias
    final_norm, third_back = jax.vjp(normalize, second_norm + ffn_branch, third_gain, third_shift)
    layer_output = final_norm.astype(BF)
    grad_third_sum, grad_third_gain, grad_third_shift = third_back(output_grad.astype(F32))
    grad_ffn = grad_third_sum.astype(BF)
    grad_hidden = gelu_back(dot_nt(grad_ffn, w_ct))[0].astype(BF)

    def own_hidden(array):
        return lax.dynamic_slice_in_dim(array, z * hidden_own, hidden_own, 1)

    def own_heads(array):
        return lax.dynamic_slice_in_dim(array, z * width, width, 1)

    grad_contract = dot_tn(grad_ffn, own_hidden(activated))
    grad_contract_bias = column_sums(grad_ffn)
    grad_hidden_own = own_hidden(grad_hidden)
    grad_expand = dot_tn(second_low, grad_hidden_own)
    grad_expand_bias = column_sums(grad_hidden_own)
    grad_second = grad_third_sum + dot_nn(grad_hidden, w_ex)
    grad_second_sum, grad_second_gain, grad_second_shift = second_back(grad_second)
    grad_cross = grad_second_sum.astype(BF)
    grad_cross_output = dot_tn(grad_cross, own_heads(cross_mixed))
    grad_cross_output_bias = column_sums(grad_cross)
    grad_cross_mixed = dot_nt(grad_cross, w_co).astype(BF)
    gcq, gck, gcv = attend_back(
        False, cross_queries, cross_keys, cross_values, grad_cross_mixed, cross_mixed, cross_sums, target_ids, memory_ids
    )
    gcq_own, gck_own, gcv_own = own_heads(gcq), own_heads(gck), own_heads(gcv)
    grad_cross_query = dot_tn(first_low, gcq_own)
    grad_cross_query_bias = column_sums(gcq_own)
    grad_cross_key = dot_tn(memory, gck_own)
    grad_cross_value = dot_tn(memory, gcv_own)
    grad_cross_value_bias = column_sums(gcv_own)
    share = model // n_tensor

    def columns(weight):
        return lax.dynamic_slice_in_dim(weight, z * share, share, 1)

    memory_grad = (dot_nn(gck, columns(w_ck)) + dot_nn(gcv, columns(w_cv))).astype(BF)
    grad_first = grad_second_sum + dot_nn(gcq, w_cq)
    grad_first_sum, grad_first_gain, grad_first_shift = first_back(grad_first)
    grad_self = grad_first_sum.astype(BF)
    grad_self_output = dot_tn(grad_self, own_heads(self_mixed))
    grad_self_output_bias = column_sums(grad_self)
    grad_self_mixed = dot_nt(grad_self, w_so).astype(BF)
    gsq, gsk, gsv = attend_back(
        True, self_queries, self_keys, self_values, grad_self_mixed, self_mixed, self_sums, target_ids, target_ids
    )
    gsq_own, gsk_own, gsv_own = own_heads(gsq), own_heads(gsk), own_heads(gsv)
    grad_self_query = dot_tn(target, gsq_own)
    grad_self_query_bias = column_sums(gsq_own)
    grad_self_key = dot_tn(target, gsk_own)
    grad_self_value = dot_tn(target, gsv_own)
    grad_self_value_bias = column_sums(gsv_own)
    target_grad = (
        lax.dynamic_slice_in_dim(grad_first_sum, z * share, share, 1)
        + dot_nn(gsq, columns(w_sq))
        + dot_nn(gsk, columns(w_sk))
        + dot_nn(gsv, columns(w_sv))
    ).astype(BF)

    partial_grads = jnp.concatenate(
        (
            grad_self_query,
            grad_self_key,
            grad_self_value,
            grad_self_output,
            grad_cross_query,
            grad_cross_key,
            grad_cross_value,
            grad_cross_output,
            grad_expand,
            grad_contract,
        ),
        axis=1,
    )
    total = lax.psum_scatter(partial_grads, "dp", scatter_dimension=0, tiled=True)
    parts = [total[:, i * width : (i + 1) * width] for i in range(8)]
    expand_total = total[:, 8 * width : 8 * width + hidden_own]
    contract_total = total[:, 8 * width + hidden_own :]
    vectors = (
        grad_self_query_bias,
        grad_self_value_bias,
        grad_self_output_bias,
        grad_first_gain,
        grad_first_shift,
        grad_cross_query_bias,
        grad_cross_value_bias,
        grad_cross_output_bias,
        grad_second_gain,
        grad_second_shift,
        grad_expand_bias,
        grad_contract_bias,
        grad_third_gain,
        grad_third_shift,
    )
    packed = lax.psum(jnp.concatenate(vectors), "dp")
    sums = []
    at = 0
    for vector in vectors:
        sums.append(packed[at : at + vector.shape[0]])
        at += vector.shape[0]
    return (
        layer_output,
        target_grad,
        memory_grad,
        parts[0],
        sums[0],
        parts[1],
        parts[2],
        sums[1],
        parts[3].T,
        sums[2],
        sums[3],
        sums[4],
        parts[4],
        sums[5],
        parts[5],
        parts[6],
        sums[6],
        parts[7].T,
        sums[7],
        sums[8],
        sums[9],
        expand_total,
        sums[10],
        contract_total.T,
        sums[11],
        sums[12],
        sums[13],
    )


def solution(mesh):
    rows = P("dp", None)
    split = P(None, "tensor")
    both = P("dp", "tensor")
    turned = P("tensor", "dp")
    own = P("tensor")
    in_specs = (
        rows, rows, rows, rows,
        split, own, split, split, own, P("tensor", None), P(), P(), P(),
        split, own, split, split, own, P("tensor", None), P(), P(), P(),
        split, own, P("tensor", None), P(), P(), P(),
        rows,
    )
    out_specs = (
        rows, both, both,
        both, own, both, both, own, turned, P(), P(), P(),
        both, own, both, both, own, turned, P(), P(), P(),
        both, own, turned, P(), P(), P(),
    )
    return jax.shard_map(
        partial(per_device, mesh.shape["dp"], mesh.shape["tensor"]),
        mesh=mesh,
        in_specs=in_specs,
        out_specs=out_specs,
        check_vma=False,
    )
```

```python
from functools import partial

import jax
import jax.numpy as jnp
from jax import lax
from jax.experimental import pallas as pl
from jax.experimental.pallas import tpu as pltpu
from jax.sharding import PartitionSpec as P

HEAD_DIM = 64
EPSILON = 1e-05
NEGATIVE = -1e30
BF = jnp.bfloat16
F32 = jnp.float32
MESH = pl.DeviceIdType.MESH
MIB = 2**20


def dot_nn(a, b):
    return lax.dot_general(a, b, (((1,), (0,)), ((), ())), preferred_element_type=F32)


def dot_nt(a, b):
    return lax.dot_general(a, b, (((1,), (1,)), ((), ())), preferred_element_type=F32)


def dot_tn(a, b):
    return lax.dot_general(a, b, (((0,), (0,)), ((), ())), preferred_element_type=F32)


def normalize(summed, norm_gain, norm_shift):
    center = jnp.mean(summed, axis=-1, keepdims=True)
    centered = summed - center
    spread = jnp.mean(centered * centered, axis=-1, keepdims=True)
    return centered * lax.rsqrt(spread + EPSILON) * norm_gain + norm_shift


def exact_gelu(values):
    return jax.nn.gelu(values, approximate=False)


def column_sums(values):
    return jnp.sum(values.astype(F32), axis=0)


WIDE = 256


def erf_pair(hidden):
    phi = 0.5 * (1.0 + lax.erf(hidden * 0.7071067811865476))
    slope = phi + hidden * (jnp.exp(-0.5 * hidden * hidden) * 0.3989422804014327)
    return hidden * phi, slope


def forward_kernel(
    n_dp, n_tensor, count, rows, head_rows, hidden_rows,
    chunk_ref, own_ref, bias_ref, target_ref, memory_ref, t_col_ref, t_row_ref, m_row_ref, vectors_ref,
    found_ref, full_ref, sq_ref, sk_ref, sv_ref, sm_ref, cq_ref, ck_ref, cv_ref, cm_ref, logs_ref, hat1_ref, hat2_ref,
    r_ref, low1_ref, low2_ref, act_ref, slope_ref,
    stage, full, low, bias, q_all, k_all, v_all, mixed, logs, hat1, hat2, spread, low1, low2, act, slope,
    send_sem, recv_sem, bias_send, bias_recv, load_sem, store_sem, out_sem,
):
    d = lax.axis_index("dp")
    z = lax.axis_index("tensor")
    others = n_tensor - 1
    length, model = target_ref.shape
    size = n_dp * rows
    dc = d + 1 - 2 * (d % 2)
    dx = d + 2 - 4 * ((d // 2) % 2)
    dy = d + 4 - 8 * (d // 4)
    dxy = dx + 4 - 8 * (d // 4)

    def slice_of(k):
        return (z + others - k) % n_tensor

    def to_z(g, k):
        return pltpu.make_async_remote_copy(
            src_ref=chunk_ref.at[pl.ds(g * rows, rows)],
            dst_ref=found_ref.at[d, k, pl.ds(g * rows, rows)],
            send_sem=send_sem.at[g, k],
            recv_sem=recv_sem.at[g, k],
            device_id={"tensor": (z + k + 1) % n_tensor},
            device_id_type=MESH,
        )

    def in_plane(g, slot, chunk, half, other):
        span = pl.ds(g * rows, rows) if half is None else pl.ds(g * rows + half * (rows // 2), rows // 2)
        piece = found_ref.at[chunk, :, span]
        return pltpu.make_async_remote_copy(
            src_ref=piece,
            dst_ref=piece,
            send_sem=send_sem.at[g, slot],
            recv_sem=recv_sem.at[g, slot],
            device_id={"dp": other},
            device_id_type=MESH,
        )

    def bias_copy(k):
        return pltpu.make_async_remote_copy(
            src_ref=bias_ref,
            dst_ref=bias.at[z],
            send_sem=bias_send.at[k],
            recv_sem=bias_recv.at[k],
            device_id={"tensor": (z + k + 1) % n_tensor},
            device_id_type=MESH,
        )

    routes = {3: (d, None, dx), 4: (d, None, dy), 5: (d, None, dc), 6: (dx, 0, dy), 7: (dy, 1, dx)}
    routes.update({8 + i: (chunk, None, dc) for i, chunk in enumerate((dx, dy, dxy))})

    def send(g, slot):
        return in_plane(g, slot, *routes[slot])

    def arrive(g, slot, half=None):
        in_plane(g, slot, d, half, dc).wait_recv()

    def first_hop(g):
        for k in range(others):
            to_z(g, k).wait_recv()
        for slot in (3, 4, 5):
            send(g, slot).start()

    def pass_on(g):
        arrive(g, 3)
        send(g, 6).start()
        send(g, 8).start()
        arrive(g, 4)
        send(g, 7).start()
        send(g, 9).start()

    def load_of(g, k):
        return pltpu.make_async_copy(found_ref.at[:, k, pl.ds(g * rows, rows)], stage.at[k], load_sem.at[k])

    def last_hop(g):
        arrive(g, 6, 0)
        arrive(g, 7, 1)
        send(g, 10).start()

    def landed(g):
        arrive(g, 5)
        for slot in (8, 9, 10):
            arrive(g, slot)
        for k in range(others):
            load_of(g, k).start()

    def home(g):
        kept = hidden_rows // size + head_rows // size
        return (full, pl.ds(g * size, size)) if g < kept else (low, pl.ds((g % 2) * size, size))

    def store_of(g, s):
        place, span = home(g)
        return pltpu.make_async_copy(place.at[s, span], full_ref.at[s, pl.ds(g * size, size)], store_sem.at[g, s])

    def rounded(g):
        place, span = home(g)
        for k in range(others):
            load_of(g, k).wait()
            place[slice_of(k), span] = stage[k].reshape(size, model).astype(BF)
        for s in range(n_tensor):
            store_of(g, s).start()

    def project(x_ref, s, first, bias_row, out_ref):
        @pl.loop(0, 2)
        def _(i):
            span = pl.ds(pl.multiple_of(i * (length // 2), length // 2), length // 2)
            value = dot_nt(x_ref[span, :], full[s, pl.ds(first, WIDE), :])
            if bias_row is not None:
                value = value + bias[s, bias_row : bias_row + 1, :WIDE]
            filled = lax.broadcasted_iota(jnp.int32, (1, WIDE), 1) < head_rows // 8
            out_ref[s, span, :] = jnp.where(filled, value, 0.0).astype(BF)

    def attend(s, causal, k_ids_ref, base):
        half = length // 2
        lane = lax.broadcasted_iota(jnp.int32, (1, 128), 1)

        @pl.loop(0, 3)
        def _(h):
            columns = pl.ds(pl.multiple_of((h // 2) * 128, 128), 128)
            mine = (lane // HEAD_DIM) == (h % 2)
            log_lane = lane == base + 3 * s + h
            for b in range(2):
                reach = (b + 1) * half if causal else length
                span = slice(b * half, (b + 1) * half)
                queries = q_all[s, span, columns] * jnp.asarray(HEAD_DIM**-0.5, BF)
                scores = dot_nt(jnp.where(mine, queries, jnp.zeros_like(queries)), k_all[s, :reach, columns])
                allowed = t_col_ref[span, :] == k_ids_ref[:, :reach]
                if causal:
                    allowed = allowed & (
                        lax.broadcasted_iota(jnp.int32, (half, reach), 0) + b * half
                        >= lax.broadcasted_iota(jnp.int32, (half, reach), 1)
                    )
                scores = jnp.where(allowed, scores, NEGATIVE)
                top = jnp.max(scores, axis=1, keepdims=True)
                weights = jnp.exp(scores - top)
                total = jnp.sum(weights, axis=1, keepdims=True)
                out = (dot_nn(weights.astype(BF), v_all[s, :reach, columns]) * (1.0 / total)).astype(BF)
                before = mixed[s, span, columns]
                before = jnp.where(h % 2 == 1, before, jnp.zeros_like(before))
                mixed[s, span, columns] = jnp.where(mine, out, before)
                logs[span, :] = jnp.where(log_lane, top + jnp.log(total), logs[span, :])

    def close(first, bias_row, residual, hat, low_out, column):
        block = length // 4

        @pl.loop(0, 4)
        def _(i):
            span = pl.ds(pl.multiple_of(i * block, block), block)
            value = residual(span) + vectors_ref[bias_row : bias_row + 1, :]
            for s in range(n_tensor):
                value = value + dot_nn(mixed[s, span, :], full[s, pl.ds(first, WIDE), :])
            centered = value - jnp.mean(value, axis=1, keepdims=True)
            scale = lax.rsqrt(jnp.mean(centered * centered, axis=1, keepdims=True) + EPSILON)
            normed = centered * scale
            hat[span, :] = normed
            here = lax.broadcasted_iota(jnp.int32, (1, 128), 1) == column
            spread[span, :] = jnp.where(here, scale, spread[span, :])
            low_out[span, :] = (
                normed * vectors_ref[bias_row + 1 : bias_row + 2, :] + vectors_ref[bias_row + 2 : bias_row + 3, :]
            ).astype(BF)

    def expand(s, slot):
        @pl.loop(0, 4)
        def _(i):
            span = pl.ds(pl.multiple_of(i * (length // 4), length // 4), length // 4)
            hidden = dot_nt(low2[span, :], full[s, pl.ds(head_rows, hidden_rows), :]) + bias[s, 4:5, :]
            value, change = erf_pair(hidden)
            act[slot, span, :] = value.astype(BF)
            slope[slot, span, :] = change.astype(BF)

    def out_copy(i, source, target):
        return pltpu.make_async_copy(source, target, out_sem.at[i])

    def expand_out(s, slot):
        return (
            out_copy(13 + 2 * slot, act.at[slot], act_ref.at[s]),
            out_copy(14 + 2 * slot, slope.at[slot], slope_ref.at[s]),
        )

    barrier = pltpu.get_barrier_semaphore()
    for k in range(1, n_tensor):
        pl.semaphore_signal(barrier, inc=1, device_id={"tensor": (z + k) % n_tensor}, device_id_type=MESH)
    for other in (dc, dx, dy):
        pl.semaphore_signal(barrier, inc=1, device_id={"dp": other}, device_id_type=MESH)
    own_loads = []
    kept_rows = head_rows + hidden_rows
    for i, (first, last) in enumerate(((0, 2 * size), (2 * size, kept_rows))):
        own_loads.append(
            pltpu.make_async_copy(
                own_ref.at[pl.ds(first, last - first)], full.at[z, pl.ds(first, last - first)], load_sem.at[3 + i]
            )
        )
    own_loads.append(pltpu.make_async_copy(own_ref.at[pl.ds(kept_rows, hidden_rows)], low.at[z], load_sem.at[5]))
    for load in own_loads:
        load.start()
    bias[z] = bias_ref[...]
    pl.semaphore_wait(barrier, others + 3)
    for k in range(others):
        bias_copy(k).start()
    for g in range(count):
        for k in range(others):
            to_z(g, k).start()

    logs[...] = jnp.zeros_like(logs)
    spread[...] = jnp.zeros_like(spread)
    own_loads[0].wait()
    q0, k0, v0, o0, ck0, cv0, cq0, co0 = (i * (head_rows // 8) for i in range(8))
    project(target_ref, z, q0, 0, q_all)
    project(target_ref, z, k0, None, k_all)
    project(target_ref, z, v0, 1, v_all)
    attend(z, True, t_row_ref, 0)
    own_loads[1].wait()
    own_loads[2].wait()
    for k in range(others):
        bias_copy(k).wait_recv()
    first_hop(0)
    pass_on(0)
    first_hop(1)
    last_hop(0)
    landed(0)
    rounded(0)
    for k in range(others):
        project(target_ref, slice_of(k), q0, 0, q_all)
        project(target_ref, slice_of(k), k0, None, k_all)
    pass_on(1)
    first_hop(2)
    last_hop(1)
    first_hop(3)
    landed(1)
    rounded(1)
    for k in range(others):
        project(target_ref, slice_of(k), v0, 1, v_all)
    pass_on(2)
    attend(slice_of(0), True, t_row_ref, 0)
    attend(slice_of(1), True, t_row_ref, 0)
    first_hop(4)
    last_hop(2)
    landed(2)
    attend(slice_of(2), True, t_row_ref, 0)
    pass_on(3)
    rounded(2)
    self_out = [
        out_copy(0, q_all, sq_ref), out_copy(1, k_all, sk_ref), out_copy(2, v_all, sv_ref), out_copy(3, mixed, sm_ref)
    ]
    for copy in self_out:
        copy.start()
    close(o0, 0, lambda span: target_ref[span, :].astype(F32), hat1, low1, 0)
    first_hop(5)
    out_copy(4, hat1, hat1_ref).start()
    out_copy(5, low1, low1_ref).start()
    for copy in self_out:
        copy.wait()

    @pl.loop(0, n_tensor)
    def _(s):
        project(memory_ref, s, ck0, None, k_all)
        project(memory_ref, s, cv0, 3, v_all)

    project(low1, z, cq0, 2, q_all)
    pass_on(4)
    last_hop(3)
    attend(z, False, m_row_ref, 3 * n_tensor)
    landed(3)
    first_hop(6)
    rounded(3)
    for k in range(others):
        project(low1, slice_of(k), cq0, 2, q_all)
    attend(slice_of(0), False, m_row_ref, 3 * n_tensor)
    pass_on(5)
    last_hop(4)
    attend(slice_of(1), False, m_row_ref, 3 * n_tensor)
    landed(4)
    first_hop(7)
    attend(slice_of(2), False, m_row_ref, 3 * n_tensor)
    rounded(4)
    cross_out = [
        out_copy(0, q_all, cq_ref), out_copy(1, k_all, ck_ref), out_copy(2, v_all, cv_ref), out_copy(3, mixed, cm_ref),
        out_copy(6, logs, logs_ref),
    ]
    for copy in cross_out:
        copy.start()
    close(co0, 3, lambda span: hat1[span, :] * vectors_ref[1:2, :] + vectors_ref[2:3, :], hat2, low2, 1)
    out_copy(7, hat2, hat2_ref).start()
    out_copy(8, low2, low2_ref).start()
    out_copy(9, spread, r_ref).start()
    pass_on(6)
    last_hop(5)
    expand(z, 0)
    for copy in expand_out(z, 0):
        copy.start()
    landed(5)
    rounded(5)
    expand(slice_of(0), 1)
    for copy in expand_out(slice_of(0), 1):
        copy.start()
    pass_on(7)
    last_hop(6)
    for copy in expand_out(z, 0):
        copy.wait()
    landed(6)
    expand(slice_of(1), 0)
    for copy in expand_out(slice_of(1), 0):
        copy.start()
    last_hop(7)
    rounded(6)
    landed(7)
    for copy in expand_out(slice_of(0), 1):
        copy.wait()
    expand(slice_of(2), 1)
    for copy in expand_out(slice_of(2), 1):
        copy.start()
    rounded(7)

    for copy in expand_out(slice_of(1), 0) + expand_out(slice_of(2), 1) + tuple(cross_out):
        copy.wait()
    for i, source, target in ((4, hat1, hat1_ref), (5, low1, low1_ref), (7, hat2, hat2_ref), (8, low2, low2_ref)):
        out_copy(i, source, target).wait()
    out_copy(9, spread, r_ref).wait()
    for g in range(count):
        for s in range(n_tensor):
            store_of(g, s).wait()
    for k in range(others):
        bias_copy(k).wait_send()
    for g in range(count):
        for k in range(others):
            to_z(g, k).wait_send()
        for slot in routes:
            send(g, slot).wait_send()


def forward(own, biases, target, memory, target_ids, memory_ids, vectors, n_dp, n_tensor, head_rows, hidden_rows):
    length, model = target.shape
    d = lax.axis_index("dp")
    count = 8
    total = head_rows + 2 * hidden_rows
    size = total // count
    rows = size // n_dp
    chunk = lax.dynamic_index_in_dim(own.reshape(count, n_dp, rows, model), d, 1, keepdims=False)
    chunk = chunk.astype(F32).reshape(count * rows, model)
    anywhere = pl.BlockSpec(memory_space=pl.ANY)
    inside = pl.BlockSpec(memory_space=pltpu.VMEM)
    heads = jax.ShapeDtypeStruct((n_tensor, length, WIDE), BF)
    tokens = jax.ShapeDtypeStruct((length, model), F32)
    tokens_low = jax.ShapeDtypeStruct((length, model), BF)
    lanes = jax.ShapeDtypeStruct((length, 128), F32)
    units = jax.ShapeDtypeStruct((n_tensor, length, hidden_rows), BF)
    out_shape = (
        jax.ShapeDtypeStruct((n_dp, n_tensor - 1, count * rows, model), F32),
        jax.ShapeDtypeStruct((n_tensor, total, model), BF),
        heads, heads, heads, heads, heads, heads, heads, heads,
        lanes, tokens, tokens, lanes, tokens_low, tokens_low, units, units,
    )
    flops = 2 * length * model * (2 * n_tensor * head_rows) + 4 * length * model * n_tensor * hidden_rows
    return pl.pallas_call(
        partial(forward_kernel, n_dp, n_tensor, count, rows, head_rows, hidden_rows),
        out_shape=out_shape,
        in_specs=[anywhere, anywhere] + [inside] * 7,
        out_specs=[anywhere] * len(out_shape),
        scratch_shapes=[
            pltpu.VMEM((n_tensor - 1, n_dp, rows, model), F32),
            pltpu.VMEM((n_tensor, head_rows + hidden_rows, model), BF),
            pltpu.VMEM((n_tensor, hidden_rows, model), BF),
            pltpu.VMEM((n_tensor, 8, model), F32),
            pltpu.VMEM(heads.shape, BF),
            pltpu.VMEM(heads.shape, BF),
            pltpu.VMEM(heads.shape, BF),
            pltpu.VMEM(heads.shape, BF),
            pltpu.VMEM(lanes.shape, F32),
            pltpu.VMEM(tokens.shape, F32),
            pltpu.VMEM(tokens.shape, F32),
            pltpu.VMEM(lanes.shape, F32),
            pltpu.VMEM(tokens.shape, BF),
            pltpu.VMEM(tokens.shape, BF),
            pltpu.VMEM((2, length, hidden_rows), BF),
            pltpu.VMEM((2, length, hidden_rows), BF),
            pltpu.SemaphoreType.DMA((count, 11)),
            pltpu.SemaphoreType.DMA((count, 11)),
            pltpu.SemaphoreType.DMA((n_tensor - 1,)),
            pltpu.SemaphoreType.DMA((n_tensor - 1,)),
            pltpu.SemaphoreType.DMA((6,)),
            pltpu.SemaphoreType.DMA((count, n_tensor)),
            pltpu.SemaphoreType.DMA((17,)),
        ],
        cost_estimate=pl.CostEstimate(flops=flops, bytes_accessed=60 * MIB, transcendentals=0),
        compiler_params=pltpu.CompilerParams(collective_id=0, has_side_effects=True, vmem_limit_bytes=63 * MIB),
    )(
        chunk, own, biases, target, memory, target_ids.reshape(length, 1), target_ids.reshape(1, length),
        memory_ids.reshape(1, length), vectors,
    )[1:]

def round_kernel(wide_ref, low_ref):
    low_ref[...] = wide_ref[...].astype(BF)


def rounded_copy(array):
    slices, rows, width = array.shape
    block = pl.BlockSpec((1, rows // 4, width), lambda i, j: (i, j, 0))
    return pl.pallas_call(
        round_kernel,
        grid=(slices, 4),
        in_specs=[block],
        out_specs=block,
        out_shape=jax.ShapeDtypeStruct(array.shape, BF),
    )(array)


def forward_plain(own, biases, target, memory, target_ids, memory_ids, vectors, n_dp, n_tensor, head_rows, hidden_rows):
    length, model = target.shape
    width = head_rows // 8
    full = rounded_copy(lax.all_gather(own.astype(F32), "tensor", axis=0))
    bias = lax.all_gather(biases, "tensor", axis=0)

    def weight(i):
        return full[:, i * width : (i + 1) * width]

    def padded(x):
        return jnp.pad(x, ((0, 0), (0, 0), (0, WIDE - width)))

    def project(x, i, row=None):
        value = jnp.einsum("td,swd->stw", x, weight(i), preferred_element_type=F32)
        if row is not None:
            value = value + bias[:, row, None, :width]
        return value.astype(BF)

    def attend(queries, keys, values, key_ids, causal):
        def split(x):
            return x.reshape(n_tensor, length, -1, HEAD_DIM)

        def one(items):
            q, k, v = items
            scores = jnp.einsum("qhd,khd->hqk", q, k, preferred_element_type=F32) * HEAD_DIM**-0.5
            allowed = target_ids[:, None] == key_ids[None, :]
            if causal:
                at = jnp.arange(length, dtype=jnp.int32)
                allowed = allowed & (at[:, None] >= at[None, :])
            scores = jnp.where(allowed[None], scores, NEGATIVE)
            probs = jax.nn.softmax(scores, axis=-1).astype(BF)
            out = jnp.einsum("hqk,khd->qhd", probs, v, preferred_element_type=F32)
            return out.astype(BF), jax.nn.logsumexp(scores, axis=-1)

        mixed, logs = lax.map(one, (split(queries), split(keys), split(values)))
        return mixed.reshape(n_tensor, length, width), logs.reshape(-1, length)

    def close(mixed, i, residual, row):
        value = residual + vectors[row] + jnp.einsum("stw,swd->td", mixed, weight(i), preferred_element_type=F32)
        centered = value - jnp.mean(value, axis=1, keepdims=True)
        scale = lax.rsqrt(jnp.mean(centered * centered, axis=1, keepdims=True) + EPSILON)
        hat = centered * scale
        normed = hat * vectors[row + 1] + vectors[row + 2]
        return hat, scale, normed, normed.astype(BF)

    sq, sk, sv = project(target, 0, 0), project(target, 1), project(target, 2, 1)
    sm, self_logs = attend(sq, sk, sv, target_ids, True)
    hat1, r1, first, low1 = close(sm, 3, target.astype(F32), 0)
    ck, cv, cq = project(memory, 4), project(memory, 5, 3), project(low1, 6, 2)
    cm, cross_logs = attend(cq, ck, cv, memory_ids, False)
    hat2, r2, _, low2 = close(cm, 7, first, 3)
    hidden = jnp.einsum("td,shd->sth", low2, full[:, head_rows : head_rows + hidden_rows], preferred_element_type=F32)
    act, slope = erf_pair(hidden + bias[:, 4, None, :])
    logs = jnp.concatenate((self_logs, cross_logs), axis=0).T
    logs = jnp.pad(logs, ((0, 0), (0, 128 - logs.shape[1])))
    spread = jnp.pad(jnp.concatenate((r1, r2), axis=1), ((0, 0), (0, 126)))
    heads = [padded(x) for x in (sq, sk, sv, sm, cq, ck, cv, cm)]
    return full, *heads, logs, hat1, hat2, spread, low1, low2, act.astype(BF), slope.astype(BF)


def attend_back_kernel(
    heads, base, block, causal, q_ref, k_ref, v_ref, gm_ref, logs_ref, dots_ref, q_ids_ref, k_ids_ref, gq_ref, gk_ref,
    gv_ref, gq_sum, logs, dots
):
    length = q_ref.shape[1]
    lane = lax.broadcasted_iota(jnp.int32, (1, 128), 1)
    scale = HEAD_DIM**-0.5
    s = pl.program_id(0)

    @pl.when(s == 0)
    def _():
        logs[...] = jnp.transpose(logs_ref[...])
        dots[...] = jnp.transpose(dots_ref[...])

    gq_sum[...] = jnp.zeros_like(gq_sum)

    def one_block(at, first):
        k_span = pl.ds(at, block)
        reach = length - first
        allowed = k_ids_ref[k_span, :] == q_ids_ref[:, first:]
        if causal:
            allowed = allowed & (
                lax.broadcasted_iota(jnp.int32, (block, reach), 0) <= lax.broadcasted_iota(jnp.int32, (block, reach), 1)
            )
        grads = []
        for h in range(heads):
            mine = (lane // HEAD_DIM) == (h % 2)
            columns = slice(128 * (h // 2), 128 * (h // 2) + 128)
            keys = k_ref[0, k_span, columns]
            keys = jnp.where(mine, keys, jnp.zeros_like(keys))
            values = v_ref[0, k_span, columns]
            values = jnp.where(mine, values, jnp.zeros_like(values))
            queries = q_ref[0, first:, columns]
            gm = gm_ref[0, first:, columns]
            scores = dot_nt(keys * jnp.asarray(scale, BF), queries)
            probs = jnp.where(allowed, jnp.exp(scores - logs[pl.ds(base + heads * s + h, 1), first:]), 0.0)
            grad_scores = (probs * (dot_nt(values, gm) - dots[pl.ds(heads * s + h, 1), first:])).astype(BF)
            grads.append((dot_nn(grad_scores, queries) * scale, dot_nn(probs.astype(BF), gm)))
            gq_sum[first:, columns] += dot_tn(grad_scores, keys)
        left = lane < HEAD_DIM
        for i, out_ref in enumerate((gk_ref, gv_ref)):
            out_ref[0, k_span, 0:128] = jnp.where(left, grads[0][i], grads[1][i]).astype(BF)
            out_ref[0, k_span, 128:256] = jnp.where(left, grads[2][i], 0.0).astype(BF)

    if causal:
        for b in range(length // block):
            one_block(b * block, b * block)
    else:

        @pl.loop(0, length // block)
        def _(b):
            one_block(pl.multiple_of(b * block, block), 0)

    gq_ref[0] = (gq_sum[...] * scale).astype(BF)


def attend_back(causal, base, queries, keys, values, grad_mixed, logs, dots, query_ids, key_ids):
    slices, length, wide = queries.shape
    part = pl.BlockSpec((1, length, wide), lambda i: (i, 0, 0))
    out = jax.ShapeDtypeStruct((slices, length, wide), BF)
    lanes = pl.BlockSpec((length, 128), lambda i: (0, 0))
    return pl.pallas_call(
        partial(attend_back_kernel, 3, base, 256, causal),
        grid=(slices,),
        in_specs=[part] * 4
        + [lanes, lanes, pl.BlockSpec((1, length), lambda i: (0, 0)), pl.BlockSpec((length, 1), lambda i: (0, 0))],
        out_specs=[part] * 3,
        out_shape=[out] * 3,
        scratch_shapes=[pltpu.VMEM((length, wide), F32), pltpu.VMEM((128, length), F32), pltpu.VMEM((128, length), F32)],
        compiler_params=pltpu.CompilerParams(vmem_limit_bytes=60 * MIB),
    )(queries, keys, values, grad_mixed, logs, dots, query_ids.reshape(1, length), key_ids.reshape(length, 1))


def norm_back(grad, hat, scale, gain):
    scaled = grad * gain
    return scale * (
        scaled - jnp.mean(scaled, axis=1, keepdims=True) - hat * jnp.mean(scaled * hat, axis=1, keepdims=True)
    )


def add_sums(sums_ref, rows):
    @pl.when(pl.program_id(0) == 0)
    def _():
        sums_ref[...] = jnp.zeros_like(sums_ref)

    for row, value in rows:
        sums_ref[row : row + 1, :] += jnp.sum(value, axis=0, keepdims=True)


def head_products(grad_mixed, mixed, s, heads, dots):
    product = grad_mixed * mixed.astype(F32)
    lane = lax.broadcasted_iota(jnp.int32, (1, WIDE), 1)
    out_lane = lax.broadcasted_iota(jnp.int32, (1, 128), 1)
    for h in range(heads):
        total = jnp.sum(jnp.where(lane // HEAD_DIM == h, product, 0.0), axis=1, keepdims=True)
        dots = jnp.where(out_lane == heads * s + h, total, dots)
    return dots


def mixed_back(grad_low, out_weight, mixed_ref, gm_ref, dots_ref):
    slices = mixed_ref.shape[0]
    width = out_weight.shape[1]
    dots = jnp.zeros(dots_ref.shape, F32)
    for s in range(slices):
        grad_mixed = dot_nt(grad_low, out_weight[s]).astype(BF)
        grad_mixed = jnp.concatenate((grad_mixed, jnp.zeros((grad_mixed.shape[0], WIDE - width), BF)), axis=1)
        gm_ref[s] = grad_mixed
        dots = head_products(grad_mixed.astype(F32), mixed_ref[s], s, 3, dots)
    dots_ref[...] = dots


def feed_back_kernel(
    act_ref, slope_ref, hat2_ref, r_ref, grad_ref, mixed_ref, expand_ref, contract_ref, out_weight_ref, vectors_ref,
    out_ref, grad_ffn_ref, grad_hidden_ref, grad_sum_ref, grad_cross_ref, gm_ref, dots_ref, sums_ref
):
    slices = act_ref.shape[0]
    vector = [vectors_ref[i : i + 1, :] for i in range(5)]
    hat2 = hat2_ref[...]
    value = hat2 * vector[0] + vector[1] + vector[2]
    for s in range(slices):
        value = value + dot_nn(act_ref[s], contract_ref[s])
    centered = value - jnp.mean(value, axis=1, keepdims=True)
    scale = lax.rsqrt(jnp.mean(centered * centered, axis=1, keepdims=True) + EPSILON)
    hat3 = centered * scale
    out_ref[...] = (hat3 * vector[3] + vector[4]).astype(BF)
    grad = grad_ref[...].astype(F32)
    grad_third = norm_back(grad, hat3, scale, vector[3])
    grad_ffn = grad_third.astype(BF)
    grad_ffn_ref[...] = grad_ffn
    grad_second = grad_third
    rows = [(0, grad * hat3), (1, grad), (2, grad_ffn.astype(F32))]
    for s in range(slices):
        grad_hidden = (dot_nt(grad_ffn, contract_ref[s]) * slope_ref[s].astype(F32)).astype(BF)
        grad_hidden_ref[s] = grad_hidden
        rows.append((8 + s, grad_hidden.astype(F32)))
        grad_second = grad_second + dot_nn(grad_hidden, expand_ref[s])
    grad_sum = norm_back(grad_second, hat2, r_ref[:, 1:2], vector[0])
    grad_sum_ref[...] = grad_sum
    grad_cross = grad_sum.astype(BF)
    grad_cross_ref[...] = grad_cross
    rows += [(3, grad_second * hat2), (4, grad_second), (5, grad_cross.astype(F32))]
    add_sums(sums_ref, rows)
    mixed_back(grad_cross, out_weight_ref, mixed_ref, gm_ref, dots_ref)


def feed_back(act, slope, hat2, spread, output_grad, mixed, full, vectors, head_rows):
    slices, length, units = act.shape
    model = hat2.shape[1]
    block = 256
    width = head_rows // 8
    tokens = pl.BlockSpec((block, model), lambda i: (i, 0))
    lanes = pl.BlockSpec((block, 128), lambda i: (i, 0))
    wide = pl.BlockSpec((slices, block, units), lambda i: (0, i, 0))
    heads = pl.BlockSpec((slices, block, WIDE), lambda i: (0, i, 0))
    rows = pl.BlockSpec((16, model), lambda i: (0, 0))

    def weight(first, size):
        return pl.BlockSpec((slices, size, model), lambda i: (0, first // size, 0))

    low = jax.ShapeDtypeStruct((length, model), BF)
    return pl.pallas_call(
        feed_back_kernel,
        grid=(length // block,),
        in_specs=[wide, wide, tokens, lanes, tokens, heads]
        + [weight(head_rows, units), weight(head_rows + units, units), weight(7 * width, width)]
        + [pl.BlockSpec((8, model), lambda i: (0, 0))],
        out_specs=[tokens, tokens, wide, tokens, tokens, heads, lanes, rows],
        out_shape=[
            low,
            low,
            jax.ShapeDtypeStruct(act.shape, BF),
            jax.ShapeDtypeStruct((length, model), F32),
            low,
            jax.ShapeDtypeStruct((slices, length, WIDE), BF),
            jax.ShapeDtypeStruct((length, 128), F32),
            jax.ShapeDtypeStruct((16, model), F32),
        ],
        compiler_params=pltpu.CompilerParams(vmem_limit_bytes=62 * MIB),
    )(act, slope, hat2, spread, output_grad, mixed, full, full, full, vectors)


def first_back_kernel(
    gq_ref, grad_sum_ref, hat1_ref, r_ref, mixed_ref, query_ref, out_weight_ref, vectors_ref,
    grad_first_ref, grad_self_ref, gm_ref, dots_ref, sums_ref
):
    slices = gq_ref.shape[0]
    width = query_ref.shape[1]
    grad = grad_sum_ref[...]
    for s in range(slices):
        grad = grad + dot_nn(gq_ref[s][:, :width], query_ref[s])
    hat = hat1_ref[...]
    grad_first = norm_back(grad, hat, r_ref[:, 0:1], vectors_ref[0:1, :])
    grad_first_ref[...] = grad_first
    grad_self = grad_first.astype(BF)
    grad_self_ref[...] = grad_self
    add_sums(sums_ref, [(0, grad * hat), (1, grad), (2, grad_self.astype(F32))])
    mixed_back(grad_self, out_weight_ref, mixed_ref, gm_ref, dots_ref)


def first_back(gq, grad_sum, hat1, spread, mixed, full, vectors, head_rows):
    slices, length, _ = gq.shape
    model = hat1.shape[1]
    block = 256
    width = head_rows // 8
    tokens = pl.BlockSpec((block, model), lambda i: (i, 0))
    lanes = pl.BlockSpec((block, 128), lambda i: (i, 0))
    heads = pl.BlockSpec((slices, block, WIDE), lambda i: (0, i, 0))
    rows = pl.BlockSpec((8, model), lambda i: (0, 0))
    low = jax.ShapeDtypeStruct((length, model), BF)
    return pl.pallas_call(
        first_back_kernel,
        grid=(length // block,),
        in_specs=[heads, tokens, tokens, lanes, heads]
        + [pl.BlockSpec((slices, width, model), lambda i, j=j: (0, j, 0)) for j in (6, 3)]
        + [rows],
        out_specs=[tokens, tokens, heads, lanes, rows],
        out_shape=[
            jax.ShapeDtypeStruct((length, model), F32),
            low,
            jax.ShapeDtypeStruct((slices, length, WIDE), BF),
            jax.ShapeDtypeStruct((length, 128), F32),
            jax.ShapeDtypeStruct((8, model), F32),
        ],
        compiler_params=pltpu.CompilerParams(vmem_limit_bytes=62 * MIB),
    )(gq, grad_sum, hat1, spread, mixed, full, full, vectors)


def input_grad_kernel(count, *refs):
    out_ref = refs[-1]
    weight_ref = refs[count]
    slices = refs[0].shape[0]
    width = weight_ref.shape[1] // count
    total = refs[count + 1][...] if len(refs) == count + 3 else jnp.zeros(out_ref.shape, F32)
    for i in range(count):
        for s in range(slices):
            total = total + dot_nn(refs[i][s][:, :width], weight_ref[s, i * width : (i + 1) * width, :])
    out_ref[...] = total.astype(BF)


def input_grad(grads, weights, rest=None):
    slices, length, wide = grads[0].shape
    share = weights.shape[2]
    block = length // 2
    tokens = pl.BlockSpec((block, share), lambda i: (i, 0))
    specs = [pl.BlockSpec((slices, block, wide), lambda i: (0, i, 0))] * len(grads)
    specs.append(pl.BlockSpec(weights.shape, lambda i: (0, 0, 0)))
    operands = (*grads, weights)
    if rest is not None:
        operands += (rest,)
        specs.append(tokens)
    return pl.pallas_call(
        partial(input_grad_kernel, len(grads)),
        grid=(2,),
        in_specs=specs,
        out_specs=tokens,
        out_shape=jax.ShapeDtypeStruct((length, share), BF),
        compiler_params=pltpu.CompilerParams(vmem_limit_bytes=60 * MIB),
    )(*operands)


def weight_grad_kernel(plan, width, z_ref, *refs):
    del z_ref
    out_ref, sums_ref = refs[-2:]
    sums_ref[...] = jnp.zeros_like(sums_ref)
    products = []
    index = 0
    row = 0
    for count in plan:
        left = refs[index][...]
        rights = [refs[index + 1 + i][0][:, :width] for i in range(count)]
        index += 1 + count
        for right in rights:
            sums_ref[row : row + 1, 0:width] = jnp.sum(right.astype(F32), axis=0, keepdims=True)
            row += 1
        products.append(dot_tn(left, rights[0] if count == 1 else jnp.concatenate(rights, axis=1)))
    out_ref[...] = jnp.concatenate(products, axis=1)


def weight_grad(z, width, *pairs):
    operands, specs = [], []
    for left, rights in pairs:
        operands.append(left)
        specs.append(pl.BlockSpec(left.shape, lambda i, z_ref: (0, 0)))
        for right in rights:
            operands.append(right)
            specs.append(pl.BlockSpec((1,) + right.shape[1:], lambda i, z_ref: (z_ref[0], 0, 0)))
    model = pairs[0][0].shape[1]
    plan = [len(rights) for _, rights in pairs]
    return pl.pallas_call(
        partial(weight_grad_kernel, plan, width),
        grid_spec=pltpu.PrefetchScalarGridSpec(
            num_scalar_prefetch=1,
            grid=(1,),
            in_specs=specs,
            out_specs=[
                pl.BlockSpec((model, sum(plan) * width), lambda i, z_ref: (0, 0)),
                pl.BlockSpec((8, model), lambda i, z_ref: (0, 0)),
            ],
        ),
        out_shape=[jax.ShapeDtypeStruct((model, sum(plan) * width), F32), jax.ShapeDtypeStruct((8, model), F32)],
        compiler_params=pltpu.CompilerParams(vmem_limit_bytes=60 * MIB),
    )(z.reshape(1), *operands)


def row_sums(values):
    if lax.axis_size("dp") != 8:
        return lax.psum(values, "dp")
    for bit in (1, 2, 4):
        values = values + lax.ppermute(values, "dp", [(i, i ^ bit) for i in range(8)])
    return values


def scattered(products):
    return lax.psum_scatter(products, "dp", scatter_dimension=0, tiled=True)


def per_device(
    n_dp, n_tensor, target, memory, target_segments, memory_segments, self_query, self_query_bias, self_key, self_value,
    self_value_bias, self_output, self_output_bias, first_gain, first_shift, cross_query, cross_query_bias, cross_key,
    cross_value, cross_value_bias, cross_output, cross_output_bias, second_gain, second_shift, expand_weight, expand_bias,
    contract_weight, contract_bias, third_gain, third_shift, output_grad,
):
    model, width = self_query.shape
    units = expand_weight.shape[1]
    head_rows = 8 * width
    z = lax.axis_index("tensor")
    target_ids = target_segments.reshape(-1)
    memory_ids = memory_segments.reshape(-1)

    across = jnp.concatenate((self_query, self_key, self_value), axis=1).T
    cross_across = jnp.concatenate((cross_key, cross_value, cross_query), axis=1).T
    own = jnp.concatenate((across, self_output, cross_across, cross_output, expand_weight.T, contract_weight), axis=0)

    def rows_of(count, vectors):
        return jnp.stack([jnp.pad(v, (0, model - v.shape[0])) for v in vectors] + [jnp.zeros(model, F32)] * (count - len(vectors)))

    biases = rows_of(8, (self_query_bias, self_value_bias, cross_query_bias, cross_value_bias, expand_bias))
    vectors = rows_of(8, (self_output_bias, first_gain, first_shift, cross_output_bias, second_gain, second_shift))
    run = forward if (n_dp, n_tensor) == (8, 4) else forward_plain
    full, sq, sk, sv, sm, cq, ck, cv, cm, logs, hat1, hat2, spread, low1, low2, act, slope = run(
        own, biases, target, memory, target_ids, memory_ids, vectors, n_dp, n_tensor, head_rows, units
    )
    layer_output, grad_ffn, grad_hidden, grad_second_sum, grad_cross, gcm, cross_dots, sums = feed_back(
        act, slope, hat2, spread, output_grad, cm, full,
        rows_of(8, (second_gain, second_shift, contract_bias, third_gain, third_shift)), head_rows,
    )
    ffn_total = scattered(weight_grad(z, units, (low2, [grad_hidden]), (grad_ffn, [act]))[0])
    gcq, gck, gcv = attend_back(False, 3 * n_tensor, cq, ck, cv, gcm, logs, cross_dots, target_ids, memory_ids)
    cross_products, cross_sums = weight_grad(z, width, (low1, [gcq]), (memory, [gck, gcv]), (grad_cross, [cm]))
    cross_total = scattered(cross_products)
    grad_first_sum, grad_self, gsm, self_dots, first_sums = first_back(
        gcq, grad_second_sum, hat1, spread, sm, full, rows_of(8, (first_gain,)), head_rows
    )
    gsq, gsk, gsv = attend_back(True, 0, sq, sk, sv, gsm, logs, self_dots, target_ids, target_ids)
    self_products, self_sums = weight_grad(z, width, (target, [gsq, gsk, gsv]), (grad_self, [sm]))
    self_total = scattered(self_products)
    share = model // n_tensor

    def columns(weight):
        return lax.dynamic_slice_in_dim(weight, z * share, share, weight.ndim - 1)

    memory_grad = input_grad((gck, gcv), columns(full[:, 4 * width : 6 * width]))
    target_grad = input_grad((gsq, gsk, gsv), columns(full[:, : 3 * width]), columns(grad_first_sum))

    vectors = (
        self_sums[0, :width],
        self_sums[2, :width],
        first_sums[2],
        first_sums[0],
        first_sums[1],
        cross_sums[0, :width],
        cross_sums[2, :width],
        sums[5],
        sums[3],
        sums[4],
        lax.dynamic_index_in_dim(sums, 8 + z, 0, keepdims=False),
        sums[2],
        sums[0],
        sums[1],
    )
    packed = row_sums(jnp.concatenate(vectors))
    totals = []
    at = 0
    for vector in vectors:
        totals.append(packed[at : at + vector.shape[0]])
        at += vector.shape[0]
    self_parts = [self_total[:, i * width : (i + 1) * width] for i in range(4)]
    cross_parts = [cross_total[:, i * width : (i + 1) * width] for i in range(4)]
    return (
        layer_output,
        target_grad,
        memory_grad,
        self_parts[0],
        totals[0],
        self_parts[1],
        self_parts[2],
        totals[1],
        self_parts[3].T,
        totals[2],
        totals[3],
        totals[4],
        cross_parts[0],
        totals[5],
        cross_parts[1],
        cross_parts[2],
        totals[6],
        cross_parts[3].T,
        totals[7],
        totals[8],
        totals[9],
        ffn_total[:, :units],
        totals[10],
        ffn_total[:, units:].T,
        totals[11],
        totals[12],
        totals[13],
    )


def solution(mesh):
    rows = P("dp", None)
    split = P(None, "tensor")
    both = P("dp", "tensor")
    turned = P("tensor", "dp")
    own = P("tensor")
    in_specs = (
        rows, rows, rows, rows,
        split, own, split, split, own, P("tensor", None), P(), P(), P(),
        split, own, split, split, own, P("tensor", None), P(), P(), P(),
        split, own, P("tensor", None), P(), P(), P(),
        rows,
    )
    out_specs = (
        rows, both, both,
        both, own, both, both, own, turned, P(), P(), P(),
        both, own, both, both, own, turned, P(), P(), P(),
        both, own, turned, P(), P(), P(),
    )
    return jax.shard_map(
        partial(per_device, mesh.shape["dp"], mesh.shape["tensor"]),
        mesh=mesh,
        in_specs=in_specs,
        out_specs=out_specs,
        check_vma=False,
    )
```

```python
from functools import partial

import jax
import jax.numpy as jnp
from jax import lax
from jax.experimental import pallas as pl
from jax.experimental.pallas import tpu as pltpu
from jax.sharding import PartitionSpec as P

HEAD_DIM = 64
EPSILON = 1e-05
NEGATIVE = -1e30
BF = jnp.bfloat16
F32 = jnp.float32
MESH = pl.DeviceIdType.MESH
MIB = 2**20


def dot_nn(a, b):
    return lax.dot_general(a, b, (((1,), (0,)), ((), ())), preferred_element_type=F32)


def dot_nt(a, b):
    return lax.dot_general(a, b, (((1,), (1,)), ((), ())), preferred_element_type=F32)


def dot_tn(a, b):
    return lax.dot_general(a, b, (((0,), (0,)), ((), ())), preferred_element_type=F32)


WIDE = 256
TOKEN_BLOCK = 256


def as_column(row):
    return jnp.transpose(jnp.broadcast_to(row, (128, row.shape[1])))[:, 0:1]


def fill_rows(rows_ref, lines):
    rows_ref[...] = jnp.zeros_like(rows_ref)
    for i, line in enumerate(lines):
        rows_ref[i, 0 : line.shape[0]] = line[...]


def erf_pair(hidden):
    phi = 0.5 * (1.0 + lax.erf(hidden * 0.7071067811865476))
    slope = phi + hidden * (jnp.exp(-0.5 * hidden * hidden) * 0.3989422804014327)
    return hidden * phi, slope


def forward_kernel(
    n_dp, n_tensor, count, rows, head_rows, hidden_rows,
    sqw_ref, skw_ref, svw_ref, sow_ref, ckw_ref, cvw_ref, cqw_ref, cow_ref, exw_ref, ctw_ref, target_ref, memory_ref, t_ids_ref, m_ids_ref,
    b0_ref, b1_ref, b2_ref, b3_ref, b4_ref, v0_ref, v1_ref, v2_ref, v3_ref, v4_ref, v5_ref,
    chunk_ref, columns_ref, found_ref, full_ref, sq_ref, sk_ref, sv_ref, sm_ref, cq_ref, ck_ref, cv_ref, cm_ref, logs_ref, hat1_ref, hat2_ref,
    r_ref, low1_ref, low2_ref, act_ref, slope_ref,
    columns, vectors_ref, bias_ref, t_row_ref, m_row_ref, t_col_ref, stage, full, low, bias, q_all, k_all, v_all, mixed, logs, hat1, hat2, spread, low1, low2, act, slope,
    send_sem, recv_sem, bias_send, bias_recv, load_sem, store_sem, out_sem,
):
    d = lax.axis_index("dp")
    z = lax.axis_index("tensor")
    others = n_tensor - 1
    length, model = target_ref.shape
    size = n_dp * rows
    dc = d + 1 - 2 * (d % 2)
    dx = d + 2 - 4 * ((d // 2) % 2)
    dy = d + 4 - 8 * (d // 4)
    dxy = dx + 4 - 8 * (d // 4)

    def slice_of(k):
        return (z + others - k) % n_tensor

    def to_z(g, k):
        return pltpu.make_async_remote_copy(
            src_ref=chunk_ref.at[pl.ds(g * rows, rows)],
            dst_ref=found_ref.at[d, k, pl.ds(g * rows, rows)],
            send_sem=send_sem.at[g, k],
            recv_sem=recv_sem.at[g, k],
            device_id={"tensor": (z + k + 1) % n_tensor},
            device_id_type=MESH,
        )

    def in_plane(g, slot, chunk, half, other):
        span = pl.ds(g * rows, rows) if half is None else pl.ds(g * rows + half * (rows // 2), rows // 2)
        piece = found_ref.at[chunk, :, span]
        return pltpu.make_async_remote_copy(
            src_ref=piece,
            dst_ref=piece,
            send_sem=send_sem.at[g, slot],
            recv_sem=recv_sem.at[g, slot],
            device_id={"dp": other},
            device_id_type=MESH,
        )

    def bias_copy(k):
        return pltpu.make_async_remote_copy(
            src_ref=bias_ref,
            dst_ref=bias.at[z],
            send_sem=bias_send.at[k],
            recv_sem=bias_recv.at[k],
            device_id={"tensor": (z + k + 1) % n_tensor},
            device_id_type=MESH,
        )

    routes = {3: (d, None, dx), 4: (d, None, dy), 5: (d, None, dc), 6: (dx, 0, dy), 7: (dy, 1, dx)}
    routes.update({8 + i: (chunk, None, dc) for i, chunk in enumerate((dx, dy, dxy))})

    def send(g, slot):
        return in_plane(g, slot, *routes[slot])

    def arrive(g, slot, half=None):
        in_plane(g, slot, d, half, dc).wait_recv()

    def first_hop(g):
        for k in range(others):
            to_z(g, k).wait_recv()
        for slot in (3, 4, 5):
            send(g, slot).start()

    def pass_on(g):
        arrive(g, 3)
        send(g, 6).start()
        send(g, 8).start()
        arrive(g, 4)
        send(g, 7).start()
        send(g, 9).start()

    def load_of(g, k):
        return pltpu.make_async_copy(found_ref.at[:, k, pl.ds(g * rows, rows)], stage.at[k], load_sem.at[k])

    def last_hop(g):
        arrive(g, 6, 0)
        arrive(g, 7, 1)
        send(g, 10).start()

    def landed(g):
        arrive(g, 5)
        for slot in (8, 9, 10):
            arrive(g, slot)
        for k in range(others):
            load_of(g, k).start()

    def home(g):
        kept = hidden_rows // size + head_rows // size
        return (full, pl.ds(g * size, size)) if g < kept else (low, pl.ds((g % 2) * size, size))

    def store_of(g, s):
        place, span = home(g)
        return pltpu.make_async_copy(place.at[s, span], full_ref.at[s, pl.ds(g * size, size)], store_sem.at[g, s])

    def rounded(g):
        place, span = home(g)
        for k in range(others):
            load_of(g, k).wait()
            place[slice_of(k), span] = stage[k].reshape(size, model).astype(BF)
        for s in range(n_tensor):
            store_of(g, s).start()

    def project(x_ref, s, first, bias_row, out_ref):
        @pl.loop(0, 2)
        def _(i):
            span = pl.ds(pl.multiple_of(i * (length // 2), length // 2), length // 2)
            value = dot_nt(x_ref[span, :], full[s, pl.ds(first, WIDE), :])
            if bias_row is not None:
                value = value + bias[s, bias_row : bias_row + 1, :WIDE]
            filled = lax.broadcasted_iota(jnp.int32, (1, WIDE), 1) < head_rows // 8
            out_ref[s, span, :] = jnp.where(filled, value, 0.0).astype(BF)

    def attend(s, causal, k_ids_ref, base):
        half = length // 2
        lane = lax.broadcasted_iota(jnp.int32, (1, 128), 1)

        @pl.loop(0, 3)
        def _(h):
            columns = pl.ds(pl.multiple_of((h // 2) * 128, 128), 128)
            mine = (lane // HEAD_DIM) == (h % 2)
            log_lane = lane == base + 3 * s + h
            for b in range(2):
                reach = (b + 1) * half if causal else length
                span = slice(b * half, (b + 1) * half)
                queries = q_all[s, span, columns] * jnp.asarray(HEAD_DIM**-0.5, BF)
                scores = dot_nt(jnp.where(mine, queries, jnp.zeros_like(queries)), k_all[s, :reach, columns])
                allowed = t_col_ref[span, :] == k_ids_ref[:, :reach]
                if causal:
                    allowed = allowed & (
                        lax.broadcasted_iota(jnp.int32, (half, reach), 0) + b * half
                        >= lax.broadcasted_iota(jnp.int32, (half, reach), 1)
                    )
                scores = jnp.where(allowed, scores, NEGATIVE)
                top = jnp.max(scores, axis=1, keepdims=True)
                weights = jnp.exp(scores - top)
                total = jnp.sum(weights, axis=1, keepdims=True)
                out = (dot_nn(weights.astype(BF), v_all[s, :reach, columns]) * (1.0 / total)).astype(BF)
                before = mixed[s, span, columns]
                before = jnp.where(h % 2 == 1, before, jnp.zeros_like(before))
                mixed[s, span, columns] = jnp.where(mine, out, before)
                logs[span, :] = jnp.where(log_lane, top + jnp.log(total), logs[span, :])

    def close(first, bias_row, residual, hat, low_out, column):
        block = length // 4

        @pl.loop(0, 4)
        def _(i):
            span = pl.ds(pl.multiple_of(i * block, block), block)
            value = residual(span) + vectors_ref[bias_row : bias_row + 1, :]
            for s in range(n_tensor):
                value = value + dot_nn(mixed[s, span, :], full[s, pl.ds(first, WIDE), :])
            centered = value - jnp.mean(value, axis=1, keepdims=True)
            scale = lax.rsqrt(jnp.mean(centered * centered, axis=1, keepdims=True) + EPSILON)
            normed = centered * scale
            hat[span, :] = normed
            here = lax.broadcasted_iota(jnp.int32, (1, 128), 1) == column
            spread[span, :] = jnp.where(here, scale, spread[span, :])
            low_out[span, :] = (
                normed * vectors_ref[bias_row + 1 : bias_row + 2, :] + vectors_ref[bias_row + 2 : bias_row + 3, :]
            ).astype(BF)

    def expand(s, slot):
        @pl.loop(0, 4)
        def _(i):
            span = pl.ds(pl.multiple_of(i * (length // 4), length // 4), length // 4)
            hidden = dot_nt(low2[span, :], full[s, pl.ds(head_rows, hidden_rows), :]) + bias[s, 4:5, :]
            value, change = erf_pair(hidden)
            act[slot, span, :] = value.astype(BF)
            slope[slot, span, :] = change.astype(BF)

    def own_columns(s):
        for i, first in enumerate((q0, k0, v0, ck0, cv0)):
            value = full[s, pl.ds(first, step), :].astype(F32)
            columns[s, pl.ds(i * step, step), :] = pltpu.roll(value, model - z * step, 1)[:, :WIDE].astype(BF)

    def out_copy(i, source, target):
        return pltpu.make_async_copy(source, target, out_sem.at[i])

    def expand_out(s, slot):
        return (
            out_copy(13 + 2 * slot, act.at[slot], act_ref.at[s]),
            out_copy(14 + 2 * slot, slope.at[slot], slope_ref.at[s]),
        )

    barrier = pltpu.get_barrier_semaphore()
    for k in range(1, n_tensor):
        pl.semaphore_signal(barrier, inc=1, device_id={"tensor": (z + k) % n_tensor}, device_id_type=MESH)
    for other in (dc, dx, dy):
        pl.semaphore_signal(barrier, inc=1, device_id={"dp": other}, device_id_type=MESH)
    step = head_rows // 8
    q0, k0, v0, o0, ck0, cv0, cq0, co0 = (i * step for i in range(8))
    own_loads = [
        pltpu.make_async_copy(source, place, load_sem.at[3 + i])
        for i, (source, place) in enumerate(
            (
                (sqw_ref, full.at[z, pl.ds(q0, step)]),
                (skw_ref, full.at[z, pl.ds(k0, step)]),
                (svw_ref, full.at[z, pl.ds(v0, step)]),
                (ckw_ref, full.at[z, pl.ds(ck0, step)]),
                (cvw_ref, full.at[z, pl.ds(cv0, step)]),
                (cqw_ref, full.at[z, pl.ds(cq0, step)]),
                (sow_ref, full.at[z, pl.ds(o0, step)]),
                (cow_ref, full.at[z, pl.ds(co0, step)]),
                (exw_ref, act.at[0, pl.ds(0, model)]),
                (ctw_ref, low.at[z]),
            )
        )
    ]
    for load in own_loads:
        load.start()
    t_row_ref[...] = t_ids_ref[...].astype(F32)
    m_row_ref[...] = m_ids_ref[...].astype(F32)
    t_col_ref[...] = as_column(t_row_ref[...])
    fill_rows(bias_ref, (b0_ref, b1_ref, b2_ref, b3_ref, b4_ref))
    fill_rows(vectors_ref, (v0_ref, v1_ref, v2_ref, v3_ref, v4_ref, v5_ref))
    bias[z] = bias_ref[...]
    pl.semaphore_wait(barrier, others + 3)
    for k in range(others):
        bias_copy(k).start()
    def chunk_copy(g):
        return pltpu.make_async_copy(stage.at[0, g], chunk_ref.at[pl.ds(g * rows, rows)], load_sem.at[g % 3])

    def offer(g):
        place, span = home(g)
        first = span.start + d * rows
        stage[0, g] = place[z, pl.ds(pl.multiple_of(first, 16), rows), :].astype(F32)
        chunk_copy(g).start()

    def give(g):
        chunk_copy(g).wait()
        for k in range(others):
            to_z(g, k).start()

    own_loads[0].wait()
    own_loads[1].wait()
    offer(0)
    own_loads[2].wait()
    own_loads[6].wait()
    give(0)
    offer(1)
    own_loads[3].wait()
    own_loads[4].wait()
    give(1)
    offer(2)
    own_loads[5].wait()
    own_loads[7].wait()
    give(2)
    offer(3)
    own_loads[8].wait()
    full[z, pl.ds(head_rows, hidden_rows), :] = jnp.transpose(act[0, :model, :].astype(F32)).astype(BF)
    offer(4)
    give(3)
    offer(5)
    own_loads[9].wait()
    give(4)
    offer(6)
    give(5)
    offer(7)
    give(6)
    give(7)

    logs[...] = jnp.zeros_like(logs)
    spread[...] = jnp.zeros_like(spread)
    project(target_ref, z, q0, 0, q_all)
    project(target_ref, z, k0, None, k_all)
    project(target_ref, z, v0, 1, v_all)
    attend(z, True, t_row_ref, 0)
    for k in range(others):
        bias_copy(k).wait_recv()
    first_hop(0)
    pass_on(0)
    first_hop(1)
    last_hop(0)
    landed(0)
    rounded(0)
    for k in range(others):
        project(target_ref, slice_of(k), q0, 0, q_all)
        project(target_ref, slice_of(k), k0, None, k_all)
    pass_on(1)
    first_hop(2)
    last_hop(1)
    first_hop(3)
    landed(1)
    rounded(1)
    for k in range(others):
        project(target_ref, slice_of(k), v0, 1, v_all)
    pass_on(2)
    attend(slice_of(0), True, t_row_ref, 0)
    attend(slice_of(1), True, t_row_ref, 0)
    first_hop(4)
    last_hop(2)
    landed(2)
    attend(slice_of(2), True, t_row_ref, 0)
    pass_on(3)
    rounded(2)
    self_out = [
        out_copy(0, q_all, sq_ref), out_copy(1, k_all, sk_ref), out_copy(2, v_all, sv_ref), out_copy(3, mixed, sm_ref)
    ]
    for copy in self_out:
        copy.start()
    close(o0, 0, lambda span: target_ref[span, :].astype(F32), hat1, low1, 0)
    first_hop(5)
    out_copy(4, hat1, hat1_ref).start()
    out_copy(5, low1, low1_ref).start()
    for copy in self_out:
        copy.wait()

    @pl.loop(0, n_tensor)
    def _(s):
        project(memory_ref, s, ck0, None, k_all)
        project(memory_ref, s, cv0, 3, v_all)

    for s in range(n_tensor):
        own_columns(s)
    out_copy(10, columns, columns_ref).start()
    project(low1, z, cq0, 2, q_all)
    pass_on(4)
    last_hop(3)
    attend(z, False, m_row_ref, 3 * n_tensor)
    landed(3)
    first_hop(6)
    rounded(3)
    for k in range(others):
        project(low1, slice_of(k), cq0, 2, q_all)
    attend(slice_of(0), False, m_row_ref, 3 * n_tensor)
    pass_on(5)
    last_hop(4)
    attend(slice_of(1), False, m_row_ref, 3 * n_tensor)
    landed(4)
    first_hop(7)
    attend(slice_of(2), False, m_row_ref, 3 * n_tensor)
    rounded(4)
    cross_out = [
        out_copy(0, q_all, cq_ref), out_copy(1, k_all, ck_ref), out_copy(2, v_all, cv_ref), out_copy(3, mixed, cm_ref),
        out_copy(6, logs, logs_ref),
    ]
    for copy in cross_out:
        copy.start()
    close(co0, 3, lambda span: hat1[span, :] * vectors_ref[1:2, :] + vectors_ref[2:3, :], hat2, low2, 1)
    out_copy(7, hat2, hat2_ref).start()
    out_copy(8, low2, low2_ref).start()
    out_copy(9, spread, r_ref).start()
    pass_on(6)
    last_hop(5)
    expand(z, 0)
    for copy in expand_out(z, 0):
        copy.start()
    landed(5)
    rounded(5)
    expand(slice_of(0), 1)
    for copy in expand_out(slice_of(0), 1):
        copy.start()
    pass_on(7)
    last_hop(6)
    for copy in expand_out(z, 0):
        copy.wait()
    landed(6)
    expand(slice_of(1), 0)
    for copy in expand_out(slice_of(1), 0):
        copy.start()
    last_hop(7)
    rounded(6)
    landed(7)
    for copy in expand_out(slice_of(0), 1):
        copy.wait()
    expand(slice_of(2), 1)
    for copy in expand_out(slice_of(2), 1):
        copy.start()
    rounded(7)

    for copy in expand_out(slice_of(1), 0) + expand_out(slice_of(2), 1) + tuple(cross_out):
        copy.wait()
    for i, source, target in ((4, hat1, hat1_ref), (5, low1, low1_ref), (7, hat2, hat2_ref), (8, low2, low2_ref)):
        out_copy(i, source, target).wait()
    out_copy(9, spread, r_ref).wait()
    out_copy(10, columns, columns_ref).wait()
    for g in range(count):
        for s in range(n_tensor):
            store_of(g, s).wait()
    for k in range(others):
        bias_copy(k).wait_send()
    for g in range(count):
        for k in range(others):
            to_z(g, k).wait_send()
        for slot in routes:
            send(g, slot).wait_send()


def forward(own, biases, target, memory, target_ids, memory_ids, vectors, n_dp, n_tensor, head_rows, hidden_rows):
    length, model = target.shape
    count = 8
    total = head_rows + 2 * hidden_rows
    size = total // count
    rows = size // n_dp
    step = head_rows // 8
    anywhere = pl.BlockSpec(memory_space=pl.ANY)
    inside = pl.BlockSpec(memory_space=pltpu.VMEM)
    heads = jax.ShapeDtypeStruct((n_tensor, length, WIDE), BF)
    tokens = jax.ShapeDtypeStruct((length, model), F32)
    tokens_low = jax.ShapeDtypeStruct((length, model), BF)
    lanes = jax.ShapeDtypeStruct((length, 128), F32)
    units = jax.ShapeDtypeStruct((n_tensor, length, hidden_rows), BF)
    out_shape = (
        jax.ShapeDtypeStruct((count * rows, model), F32),
        jax.ShapeDtypeStruct((n_tensor, 5 * step, WIDE), BF),
        jax.ShapeDtypeStruct((n_dp, n_tensor - 1, count * rows, model), F32),
        jax.ShapeDtypeStruct((n_tensor, total, model), BF),
        heads, heads, heads, heads, heads, heads, heads, heads,
        lanes, tokens, tokens, lanes, tokens_low, tokens_low, units, units,
    )
    flops = 2 * length * model * (2 * n_tensor * head_rows) + 4 * length * model * n_tensor * hidden_rows
    outs = pl.pallas_call(
        partial(forward_kernel, n_dp, n_tensor, count, rows, head_rows, hidden_rows),
        out_shape=out_shape,
        in_specs=[anywhere] * 10 + [inside] * 15,
        out_specs=[anywhere] * len(out_shape),
        scratch_shapes=[
            pltpu.VMEM((n_tensor, 5 * step, WIDE), BF),
            pltpu.VMEM((8, model), F32),
            pltpu.VMEM((8, model), F32),
            pltpu.VMEM((1, length), F32),
            pltpu.VMEM((1, length), F32),
            pltpu.VMEM((length, 1), F32),
            pltpu.VMEM((n_tensor - 1, n_dp, rows, model), F32),
            pltpu.VMEM((n_tensor, head_rows + hidden_rows, model), BF),
            pltpu.VMEM((n_tensor, hidden_rows, model), BF),
            pltpu.VMEM((n_tensor, 8, model), F32),
            pltpu.VMEM(heads.shape, BF),
            pltpu.VMEM(heads.shape, BF),
            pltpu.VMEM(heads.shape, BF),
            pltpu.VMEM(heads.shape, BF),
            pltpu.VMEM(lanes.shape, F32),
            pltpu.VMEM(tokens.shape, F32),
            pltpu.VMEM(tokens.shape, F32),
            pltpu.VMEM(lanes.shape, F32),
            pltpu.VMEM(tokens.shape, BF),
            pltpu.VMEM(tokens.shape, BF),
            pltpu.VMEM((2, length, hidden_rows), BF),
            pltpu.VMEM((2, length, hidden_rows), BF),
            pltpu.SemaphoreType.DMA((count, 11)),
            pltpu.SemaphoreType.DMA((count, 11)),
            pltpu.SemaphoreType.DMA((n_tensor - 1,)),
            pltpu.SemaphoreType.DMA((n_tensor - 1,)),
            pltpu.SemaphoreType.DMA((13,)),
            pltpu.SemaphoreType.DMA((count, n_tensor)),
            pltpu.SemaphoreType.DMA((17,)),
        ],
        cost_estimate=pl.CostEstimate(flops=flops, bytes_accessed=60 * MIB, transcendentals=0),
        compiler_params=pltpu.CompilerParams(collective_id=0, has_side_effects=True, vmem_limit_bytes=63 * MIB),
    )(
        *(x.T if x.shape[0] > x.shape[1] else x for x in own), target, memory, target_ids, memory_ids, *biases, *vectors
    )
    return outs[1], *outs[3:]


def round_kernel(wide_ref, low_ref):
    low_ref[...] = wide_ref[...].astype(BF)


def rounded_copy(array):
    slices, rows, width = array.shape
    block = pl.BlockSpec((1, rows // 4, width), lambda i, j: (i, j, 0))
    return pl.pallas_call(
        round_kernel,
        grid=(slices, 4),
        in_specs=[block],
        out_specs=block,
        out_shape=jax.ShapeDtypeStruct(array.shape, BF),
    )(array)


def forward_plain(own, biases, target, memory, target_ids, memory_ids, vectors, n_dp, n_tensor, head_rows, hidden_rows):
    length, model = target.shape
    width = head_rows // 8
    sq, sk, sv, so, ck, cv, cq, co, expand, contract = own
    own = jnp.concatenate((sq.T, sk.T, sv.T, so, ck.T, cv.T, cq.T, co, expand.T, contract), axis=0)
    full = rounded_copy(lax.all_gather(own.astype(F32), "tensor", axis=0))
    bias = lax.all_gather(jnp.stack([jnp.pad(b, (0, model - b.shape[0])) for b in biases]), "tensor", axis=0)
    target_ids, memory_ids = target_ids.reshape(-1), memory_ids.reshape(-1)

    def weight(i):
        return full[:, i * width : (i + 1) * width]

    def padded(x):
        return jnp.pad(x, ((0, 0), (0, 0), (0, WIDE - width)))

    def project(x, i, row=None):
        value = jnp.einsum("td,swd->stw", x, weight(i), preferred_element_type=F32)
        if row is not None:
            value = value + bias[:, row, None, :width]
        return value.astype(BF)

    def attend(queries, keys, values, key_ids, causal):
        def split(x):
            return x.reshape(n_tensor, length, -1, HEAD_DIM)

        def one(items):
            q, k, v = items
            scores = jnp.einsum("qhd,khd->hqk", q, k, preferred_element_type=F32) * HEAD_DIM**-0.5
            allowed = target_ids[:, None] == key_ids[None, :]
            if causal:
                at = jnp.arange(length, dtype=jnp.int32)
                allowed = allowed & (at[:, None] >= at[None, :])
            scores = jnp.where(allowed[None], scores, NEGATIVE)
            probs = jax.nn.softmax(scores, axis=-1).astype(BF)
            out = jnp.einsum("hqk,khd->qhd", probs, v, preferred_element_type=F32)
            return out.astype(BF), jax.nn.logsumexp(scores, axis=-1)

        mixed, logs = lax.map(one, (split(queries), split(keys), split(values)))
        return mixed.reshape(n_tensor, length, width), logs.reshape(-1, length)

    def close(mixed, i, residual, row):
        value = residual + vectors[row] + jnp.einsum("stw,swd->td", mixed, weight(i), preferred_element_type=F32)
        centered = value - jnp.mean(value, axis=1, keepdims=True)
        scale = lax.rsqrt(jnp.mean(centered * centered, axis=1, keepdims=True) + EPSILON)
        hat = centered * scale
        normed = hat * vectors[row + 1] + vectors[row + 2]
        return hat, scale, normed, normed.astype(BF)

    sq, sk, sv = project(target, 0, 0), project(target, 1), project(target, 2, 1)
    sm, self_logs = attend(sq, sk, sv, target_ids, True)
    hat1, r1, first, low1 = close(sm, 3, target.astype(F32), 0)
    ck, cv, cq = project(memory, 4), project(memory, 5, 3), project(low1, 6, 2)
    cm, cross_logs = attend(cq, ck, cv, memory_ids, False)
    hat2, r2, _, low2 = close(cm, 7, first, 3)
    hidden = jnp.einsum("td,shd->sth", low2, full[:, head_rows : head_rows + hidden_rows], preferred_element_type=F32)
    act, slope = erf_pair(hidden + bias[:, 4, None, :])
    logs = jnp.concatenate((self_logs, cross_logs), axis=0).T
    logs = jnp.pad(logs, ((0, 0), (0, 128 - logs.shape[1])))
    spread = jnp.pad(jnp.concatenate((r1, r2), axis=1), ((0, 0), (0, 126)))
    heads = [padded(x) for x in (sq, sk, sv, sm, cq, ck, cv, cm)]
    kept = jnp.concatenate((full[:, : 3 * width], full[:, 4 * width : 6 * width]), axis=1)
    columns = padded(lax.dynamic_slice_in_dim(kept, lax.axis_index("tensor") * width, width, 2))
    return columns, full, *heads, logs, hat1, hat2, spread, low1, low2, act.astype(BF), slope.astype(BF)


def attend_back_kernel(
    heads, base, block, causal, q_ref, k_ref, v_ref, gm_ref, logs_ref, dots_ref, q_row_ref, k_row_ref, gq_ref, gk_ref,
    gv_ref, gq_sum, logs, dots, k_ids_ref, q_ids_ref
):
    length = q_ref.shape[1]
    lane = lax.broadcasted_iota(jnp.int32, (1, 128), 1)
    scale = HEAD_DIM**-0.5
    s = pl.program_id(0)

    @pl.when(s == 0)
    def _():
        logs[...] = jnp.transpose(logs_ref[...])
        dots[...] = jnp.transpose(dots_ref[...])
        k_ids_ref[...] = as_column(k_row_ref[...].astype(F32))
        q_ids_ref[...] = q_row_ref[...].astype(F32)

    gq_sum[...] = jnp.zeros_like(gq_sum)

    def one_block(at, first):
        k_span = pl.ds(at, block)
        reach = length - first
        allowed = k_ids_ref[k_span, :] == q_ids_ref[:, first:]
        if causal:
            allowed = allowed & (
                lax.broadcasted_iota(jnp.int32, (block, reach), 0) <= lax.broadcasted_iota(jnp.int32, (block, reach), 1)
            )
        grads = []
        for h in range(heads):
            mine = (lane // HEAD_DIM) == (h % 2)
            columns = slice(128 * (h // 2), 128 * (h // 2) + 128)
            keys = k_ref[0, k_span, columns]
            keys = jnp.where(mine, keys, jnp.zeros_like(keys))
            values = v_ref[0, k_span, columns]
            values = jnp.where(mine, values, jnp.zeros_like(values))
            queries = q_ref[0, first:, columns]
            gm = gm_ref[0, first:, columns]
            scores = dot_nt(keys * jnp.asarray(scale, BF), queries)
            probs = jnp.where(allowed, jnp.exp(scores - logs[pl.ds(base + heads * s + h, 1), first:]), 0.0)
            grad_scores = (probs * (dot_nt(values, gm) - dots[pl.ds(heads * s + h, 1), first:])).astype(BF)
            grads.append((dot_nn(grad_scores, queries) * scale, dot_nn(probs.astype(BF), gm)))
            gq_sum[first:, columns] += dot_tn(grad_scores, keys)
        left = lane < HEAD_DIM
        for i, out_ref in enumerate((gk_ref, gv_ref)):
            out_ref[0, k_span, 0:128] = jnp.where(left, grads[0][i], grads[1][i]).astype(BF)
            out_ref[0, k_span, 128:256] = jnp.where(left, grads[2][i], 0.0).astype(BF)

    if causal:
        for b in range(length // block):
            one_block(b * block, b * block)
    else:

        @pl.loop(0, length // block)
        def _(b):
            one_block(pl.multiple_of(b * block, block), 0)

    gq_ref[0] = (gq_sum[...] * scale).astype(BF)


def attend_back(causal, base, queries, keys, values, grad_mixed, logs, dots, query_ids, key_ids):
    slices, length, wide = queries.shape
    part = pl.BlockSpec((1, length, wide), lambda i: (i, 0, 0))
    out = jax.ShapeDtypeStruct((slices, length, wide), BF)
    lanes = pl.BlockSpec((length, 128), lambda i: (0, 0))
    return pl.pallas_call(
        partial(attend_back_kernel, 3, base, 256, causal),
        grid=(slices,),
        in_specs=[part] * 4
        + [lanes, lanes, pl.BlockSpec((1, length), lambda i: (0, 0)), pl.BlockSpec((1, length), lambda i: (0, 0))],
        out_specs=[part] * 3,
        out_shape=[out] * 3,
        scratch_shapes=[
            pltpu.VMEM((length, wide), F32),
            pltpu.VMEM((128, length), F32),
            pltpu.VMEM((128, length), F32),
            pltpu.VMEM((length, 1), F32),
            pltpu.VMEM((1, length), F32),
        ],
        compiler_params=pltpu.CompilerParams(vmem_limit_bytes=60 * MIB),
    )(queries, keys, values, grad_mixed, logs, dots, query_ids, key_ids)


def norm_back(grad, hat, scale, gain):
    scaled = grad * gain
    return scale * (
        scaled - jnp.mean(scaled, axis=1, keepdims=True) - hat * jnp.mean(scaled * hat, axis=1, keepdims=True)
    )


def add_sums(sums_ref, rows):
    @pl.when(pl.program_id(0) == 0)
    def _():
        sums_ref[...] = jnp.zeros_like(sums_ref)

    for row, value in rows:
        sums_ref[row : row + 1, :] += jnp.sum(value, axis=0, keepdims=True)


def head_products(grad_mixed, mixed, s, heads, dots):
    product = grad_mixed * mixed.astype(F32)
    lane = lax.broadcasted_iota(jnp.int32, (1, WIDE), 1)
    out_lane = lax.broadcasted_iota(jnp.int32, (1, 128), 1)
    for h in range(heads):
        total = jnp.sum(jnp.where(lane // HEAD_DIM == h, product, 0.0), axis=1, keepdims=True)
        dots = jnp.where(out_lane == heads * s + h, total, dots)
    return dots


def mixed_back(grad_low, out_weight, mixed_ref, gm_ref, dots_ref):
    slices = mixed_ref.shape[0]
    width = out_weight.shape[1]
    dots = jnp.zeros(dots_ref.shape, F32)
    for s in range(slices):
        grad_mixed = dot_nt(grad_low, out_weight[s]).astype(BF)
        grad_mixed = jnp.concatenate((grad_mixed, jnp.zeros((grad_mixed.shape[0], WIDE - width), BF)), axis=1)
        gm_ref[s] = grad_mixed
        dots = head_products(grad_mixed.astype(F32), mixed_ref[s], s, 3, dots)
    dots_ref[...] = dots


def feed_back_kernel(
    act_ref, slope_ref, hat2_ref, r_ref, grad_ref, mixed_ref, expand_ref, contract_ref, out_weight_ref,
    v0_ref, v1_ref, v2_ref, v3_ref, v4_ref, out_ref, grad_ffn_ref, grad_hidden_ref, grad_sum_ref, grad_cross_ref, gm_ref, dots_ref, sums_ref,
    vectors_ref
):
    slices = act_ref.shape[0]
    fill_rows(vectors_ref, (v0_ref, v1_ref, v2_ref, v3_ref, v4_ref))
    vector = [vectors_ref[i : i + 1, :] for i in range(5)]
    hat2 = hat2_ref[...]
    value = hat2 * vector[0] + vector[1] + vector[2]
    for s in range(slices):
        value = value + dot_nn(act_ref[s], contract_ref[s])
    centered = value - jnp.mean(value, axis=1, keepdims=True)
    scale = lax.rsqrt(jnp.mean(centered * centered, axis=1, keepdims=True) + EPSILON)
    hat3 = centered * scale
    out_ref[...] = (hat3 * vector[3] + vector[4]).astype(BF)
    grad = grad_ref[...].astype(F32)
    grad_third = norm_back(grad, hat3, scale, vector[3])
    grad_ffn = grad_third.astype(BF)
    grad_ffn_ref[...] = grad_ffn
    grad_second = grad_third
    rows = [(0, grad * hat3), (1, grad), (2, grad_ffn.astype(F32))]
    for s in range(slices):
        grad_hidden = (dot_nt(grad_ffn, contract_ref[s]) * slope_ref[s].astype(F32)).astype(BF)
        grad_hidden_ref[s] = grad_hidden
        rows.append((8 + s, grad_hidden.astype(F32)))
        grad_second = grad_second + dot_nn(grad_hidden, expand_ref[s])
    grad_sum = norm_back(grad_second, hat2, r_ref[:, 1:2], vector[0])
    grad_sum_ref[...] = grad_sum
    grad_cross = grad_sum.astype(BF)
    grad_cross_ref[...] = grad_cross
    rows += [(3, grad_second * hat2), (4, grad_second), (5, grad_cross.astype(F32))]
    add_sums(sums_ref, rows)
    mixed_back(grad_cross, out_weight_ref, mixed_ref, gm_ref, dots_ref)


def feed_back(act, slope, hat2, spread, output_grad, mixed, full, vectors, head_rows):
    slices, length, units = act.shape
    model = hat2.shape[1]
    block = TOKEN_BLOCK
    width = head_rows // 8
    tokens = pl.BlockSpec((block, model), lambda i: (i, 0))
    lanes = pl.BlockSpec((block, 128), lambda i: (i, 0))
    wide = pl.BlockSpec((slices, block, units), lambda i: (0, i, 0))
    heads = pl.BlockSpec((slices, block, WIDE), lambda i: (0, i, 0))
    rows = pl.BlockSpec((16, model), lambda i: (0, 0))

    def weight(first, size):
        return pl.BlockSpec((slices, size, model), lambda i: (0, first // size, 0))

    low = jax.ShapeDtypeStruct((length, model), BF)
    return pl.pallas_call(
        feed_back_kernel,
        grid=(length // block,),
        in_specs=[wide, wide, tokens, lanes, tokens, heads]
        + [weight(head_rows, units), weight(head_rows + units, units), weight(7 * width, width)]
        + [pl.BlockSpec((model,), lambda i: (0,))] * 5,
        scratch_shapes=[pltpu.VMEM((8, model), F32)],
        out_specs=[tokens, tokens, wide, tokens, tokens, heads, lanes, rows],
        out_shape=[
            low,
            low,
            jax.ShapeDtypeStruct(act.shape, BF),
            jax.ShapeDtypeStruct((length, model), F32),
            low,
            jax.ShapeDtypeStruct((slices, length, WIDE), BF),
            jax.ShapeDtypeStruct((length, 128), F32),
            jax.ShapeDtypeStruct((16, model), F32),
        ],
        compiler_params=pltpu.CompilerParams(vmem_limit_bytes=62 * MIB),
    )(act, slope, hat2, spread, output_grad, mixed, full, full, full, *vectors)


def first_back_kernel(
    z_ref, gq_ref, grad_sum_ref, hat1_ref, r_ref, mixed_ref, query_ref, out_weight_ref, gain_ref,
    rest_ref, grad_self_ref, gm_ref, dots_ref, sums_ref, vectors_ref
):
    fill_rows(vectors_ref, (gain_ref,))
    slices = gq_ref.shape[0]
    width = query_ref.shape[1]
    grad = grad_sum_ref[...]
    for s in range(slices):
        grad = grad + dot_nn(gq_ref[s][:, :width], query_ref[s])
    hat = hat1_ref[...]
    grad_first = norm_back(grad, hat, r_ref[:, 0:1], vectors_ref[0:1, :])
    rest_ref[...] = pltpu.roll(grad_first, grad_first.shape[1] - z_ref[0] * width, 1)[:, :width]
    grad_self = grad_first.astype(BF)
    grad_self_ref[...] = grad_self
    add_sums(sums_ref, [(0, grad * hat), (1, grad), (2, grad_self.astype(F32))])
    mixed_back(grad_self, out_weight_ref, mixed_ref, gm_ref, dots_ref)


def first_back(z, gq, grad_sum, hat1, spread, mixed, full, vectors, head_rows):
    slices, length, _ = gq.shape
    model = hat1.shape[1]
    block = TOKEN_BLOCK
    width = head_rows // 8
    tokens = pl.BlockSpec((block, model), lambda i, _: (i, 0))
    lanes = pl.BlockSpec((block, 128), lambda i, _: (i, 0))
    share = pl.BlockSpec((block, width), lambda i, _: (i, 0))
    heads = pl.BlockSpec((slices, block, WIDE), lambda i, _: (0, i, 0))
    rows = pl.BlockSpec((8, model), lambda i, _: (0, 0))
    return pl.pallas_call(
        first_back_kernel,
        grid_spec=pltpu.PrefetchScalarGridSpec(
            num_scalar_prefetch=1,
            grid=(length // block,),
            in_specs=[heads, tokens, tokens, lanes, heads]
            + [pl.BlockSpec((slices, width, model), lambda i, _, j=j: (0, j, 0)) for j in (6, 3)]
            + [pl.BlockSpec((model,), lambda i, _: (0,))],
            scratch_shapes=[pltpu.VMEM((8, model), F32)],
            out_specs=[share, tokens, heads, lanes, rows],
        ),
        out_shape=[
            jax.ShapeDtypeStruct((length, width), F32),
            jax.ShapeDtypeStruct((length, model), BF),
            jax.ShapeDtypeStruct((slices, length, WIDE), BF),
            jax.ShapeDtypeStruct((length, 128), F32),
            jax.ShapeDtypeStruct((8, model), F32),
        ],
        compiler_params=pltpu.CompilerParams(vmem_limit_bytes=62 * MIB),
    )(z.reshape(1), gq, grad_sum, hat1, spread, mixed, full, full, vectors)


def input_grad_kernel(count, *refs):
    out_ref = refs[-1]
    weight_ref = refs[count]
    slices = refs[0].shape[0]
    width = weight_ref.shape[1] // count
    total = refs[count + 1][...] if len(refs) == count + 3 else jnp.zeros(out_ref.shape, F32)
    for i in range(count):
        for s in range(slices):
            total = total + dot_nn(refs[i][s][:, :width], weight_ref[s, i * width : (i + 1) * width, :])
    out_ref[...] = total.astype(BF)


def input_grad(grads, weights, rest=None):
    slices, length, wide = grads[0].shape
    share = weights.shape[2]
    block = length // 2
    tokens = pl.BlockSpec((block, share), lambda i: (i, 0))
    specs = [pl.BlockSpec((slices, block, wide), lambda i: (0, i, 0))] * len(grads)
    specs.append(pl.BlockSpec(weights.shape, lambda i: (0, 0, 0)))
    operands = (*grads, weights)
    if rest is not None:
        operands += (rest,)
        specs.append(tokens)
    return pl.pallas_call(
        partial(input_grad_kernel, len(grads)),
        grid=(2,),
        in_specs=specs,
        out_specs=tokens,
        out_shape=jax.ShapeDtypeStruct((length, share), BF),
        compiler_params=pltpu.CompilerParams(vmem_limit_bytes=60 * MIB),
    )(*operands)


def weight_grad_kernel(plan, width, z_ref, *refs):
    del z_ref
    out_ref, sums_ref = refs[-2:]
    sums_ref[...] = jnp.zeros_like(sums_ref)
    products = []
    index = 0
    row = 0
    for count in plan:
        left = refs[index][...]
        rights = [refs[index + 1 + i][0][:, :width] for i in range(count)]
        index += 1 + count
        for right in rights:
            sums_ref[row : row + 1, 0:width] = jnp.sum(right.astype(F32), axis=0, keepdims=True)
            row += 1
        products.append(dot_tn(left, rights[0] if count == 1 else jnp.concatenate(rights, axis=1)))
    out_ref[...] = jnp.concatenate(products, axis=1)


def weight_grad(z, width, *pairs):
    operands, specs = [], []
    for left, rights in pairs:
        operands.append(left)
        specs.append(pl.BlockSpec(left.shape, lambda i, z_ref: (0, 0)))
        for right in rights:
            operands.append(right)
            specs.append(pl.BlockSpec((1,) + right.shape[1:], lambda i, z_ref: (z_ref[0], 0, 0)))
    model = pairs[0][0].shape[1]
    plan = [len(rights) for _, rights in pairs]
    return pl.pallas_call(
        partial(weight_grad_kernel, plan, width),
        grid_spec=pltpu.PrefetchScalarGridSpec(
            num_scalar_prefetch=1,
            grid=(1,),
            in_specs=specs,
            out_specs=[
                pl.BlockSpec((model, sum(plan) * width), lambda i, z_ref: (0, 0)),
                pl.BlockSpec((8, model), lambda i, z_ref: (0, 0)),
            ],
        ),
        out_shape=[jax.ShapeDtypeStruct((model, sum(plan) * width), F32), jax.ShapeDtypeStruct((8, model), F32)],
        compiler_params=pltpu.CompilerParams(vmem_limit_bytes=60 * MIB),
    )(z.reshape(1), *operands)


def scattered(products):
    return lax.psum_scatter(products, "dp", scatter_dimension=0, tiled=True)


def finish_kernel(
    width, prod_f_ref, prod_c_ref, q_ref, k_ref, v_ref, gm_ref, sm_ref, gck_ref, gcv_ref, target_ref, grad_self_ref,
    logs_ref, dots_ref, t_ids_ref, columns_ref, rest_ref, sums_ref, cross_sums_ref, first_sums_ref,
    total_f_ref, total_c_ref, total_s_ref, vector_total_ref, target_grad_ref, memory_grad_ref,
    q_all, k_all, v_all, gm_all, sm_own, gck_all, gcv_all, target, grad_self, gq_all, gk_all, gv_all, gq_sum, logs, dots,
    mine_f, mine_c, prod_s, land_f, land_c, land_s, one_f, one_c, one_s, two_f, two_c, two_s, vec, vec_land, t_col_ref, t_row_ref,
    send_sem, recv_sem, load_sem,
):
    d = lax.axis_index("dp")
    z = lax.axis_index("tensor")
    c = d % 2
    x = (d // 2) % 2
    y = d // 4
    dc = d + 1 - 2 * c
    dx = d + 2 - 4 * x
    dy = d + 4 - 8 * y
    slices, length, _ = q_all.shape
    heads = 3

    def to(slot, source, place, other):
        return pltpu.make_async_remote_copy(
            src_ref=source,
            dst_ref=place,
            send_sem=send_sem.at[slot],
            recv_sem=recv_sem.at[slot],
            device_id={"dp": other},
            device_id_type=MESH,
        )

    families = (
        (prod_f_ref, mine_f, land_f, one_f, two_f, total_f_ref),
        (prod_c_ref, mine_c, land_c, one_c, two_c, total_c_ref),
        (prod_s, None, land_s, one_s, two_s, total_s_ref),
    )

    def over_core(i):
        return to(5 * i, families[i][0].at[:, :, 1 - c], families[i][2], dc)

    def halves(i):
        half = families[i][2].shape[3] // 2
        return pl.ds(0, half), pl.ds(half, half)

    def first_a(i):
        return to(5 * i + 1, families[i][2].at[:, 1 - x, :, halves(i)[0]], families[i][3].at[0], dx)

    def first_b(i):
        return to(5 * i + 2, families[i][2].at[1 - y, :, :, halves(i)[1]], families[i][3].at[1], dy)

    def second_a(i):
        return to(5 * i + 3, families[i][3].at[0, 1 - y], families[i][4].at[0], dy)

    def second_b(i):
        return to(5 * i + 4, families[i][3].at[1, 1 - x], families[i][4].at[1], dx)

    def after_core(i):
        _, mine, land, _, _, _ = families[i]
        over_core(i).wait_recv()

        @pl.loop(0, 4)
        def _(j):
            part = prod_s[j // 2, j % 2, c] if mine is None else mine[j // 2, j % 2]
            land[j // 2, j % 2] = land[j // 2, j % 2] + part

        first_a(i).start()
        first_b(i).start()

    def after_first(i):
        _, _, land, one, _, _ = families[i]
        first_a(i).wait_recv()
        first_b(i).wait_recv()
        left, right = halves(i)
        for j in range(2):
            one[0, j] = one[0, j] + land[j, x, :, left]
            one[1, j] = one[1, j] + land[y, j, :, right]
        second_a(i).start()
        second_b(i).start()

    def after_second(i):
        _, _, _, one, two, total_ref = families[i]
        second_a(i).wait_recv()
        second_b(i).wait_recv()
        left, right = halves(i)
        total_ref[:, left] = one[0, y] + two[0]
        total_ref[:, right] = one[1, x] + two[1]

    def vector_copy(i):
        return to(15 + i, vec.at[i], vec_land.at[i], (dc, dx, dy)[i])

    def vector_step(i):
        vector_copy(i).wait_recv()
        vec[i + 1] = vec[i] + vec_land[i]
        if i < 2:
            vector_copy(i + 1).start()

    barrier = pltpu.get_barrier_semaphore()
    for other in (dc, dx, dy):
        pl.semaphore_signal(barrier, inc=1, device_id={"dp": other}, device_id_type=MESH)

    def slice_loads(s):
        pairs = ((q_ref, q_all), (k_ref, k_all), (v_ref, v_all), (gm_ref, gm_all))
        return [
            pltpu.make_async_copy(source.at[s], place.at[s], load_sem.at[4 * s + i])
            for i, (source, place) in enumerate(pairs)
        ]

    late = 4 * slices
    late_loads = [
        pltpu.make_async_copy(sm_ref.at[z], sm_own, load_sem.at[late]),
        pltpu.make_async_copy(target_ref, target, load_sem.at[late + 1]),
        pltpu.make_async_copy(grad_self_ref, grad_self, load_sem.at[late + 2]),
        pltpu.make_async_copy(gck_ref, gck_all, load_sem.at[late + 3]),
        pltpu.make_async_copy(gcv_ref, gcv_all, load_sem.at[late + 4]),
    ]
    mine_loads = [
        pltpu.make_async_copy(prod_f_ref.at[:, :, c], mine_f, load_sem.at[late + 5]),
        pltpu.make_async_copy(prod_c_ref.at[:, :, c], mine_c, load_sem.at[late + 6]),
    ]
    for s in range(slices):
        for load in slice_loads(s):
            load.start()
    for load in mine_loads + late_loads:
        load.start()
    t_row_ref[...] = t_ids_ref[...].astype(F32)
    t_col_ref[...] = as_column(t_row_ref[...])
    logs[...] = jnp.transpose(logs_ref[...])
    dots[...] = jnp.transpose(dots_ref[...])
    pl.semaphore_wait(barrier, 3)
    over_core(0).start()
    over_core(1).start()

    vec[0] = jnp.zeros(vec.shape[1:], F32)
    for row, source, at in (
        (2, first_sums_ref, 2), (3, first_sums_ref, 0), (4, first_sums_ref, 1), (5, cross_sums_ref, 0),
        (6, cross_sums_ref, 2), (7, sums_ref, 5), (8, sums_ref, 3), (9, sums_ref, 4), (11, sums_ref, 2),
        (12, sums_ref, 0), (13, sums_ref, 1),
    ):
        vec[0, row : row + 1, :] = source[at : at + 1, :]
    vec[0, 10:11, :] = sums_ref[pl.ds(8 + z, 1), :]

    lane = lax.broadcasted_iota(jnp.int32, (1, 128), 1)
    scale = HEAD_DIM**-0.5
    block = 256

    def one_block(s, at):
        reach = length - at
        span = slice(at, at + block)
        allowed = (t_col_ref[span, :] == t_row_ref[:, at:]) & (
            lax.broadcasted_iota(jnp.int32, (block, reach), 0) <= lax.broadcasted_iota(jnp.int32, (block, reach), 1)
        )
        grads = []
        for h in range(heads):
            mine = (lane // HEAD_DIM) == (h % 2)
            columns = slice(128 * (h // 2), 128 * (h // 2) + 128)
            keys = k_all[s, span, columns]
            keys = jnp.where(mine, keys, jnp.zeros_like(keys))
            values = v_all[s, span, columns]
            values = jnp.where(mine, values, jnp.zeros_like(values))
            queries = q_all[s, at:, columns]
            gm = gm_all[s, at:, columns]
            scores = dot_nt(keys * jnp.asarray(scale, BF), queries)
            row = pl.ds(heads * s + h, 1)
            probs = jnp.where(allowed, jnp.exp(scores - logs[row, at:]), 0.0)
            grad_scores = (probs * (dot_nt(values, gm) - dots[row, at:])).astype(BF)
            grads.append((dot_nn(grad_scores, queries) * scale, dot_nn(probs.astype(BF), gm)))
            gq_sum[at:, columns] += dot_tn(grad_scores, keys)
        left = lane < HEAD_DIM
        for i, out in enumerate((gk_all, gv_all)):
            out[s, span, 0:128] = jnp.where(left, grads[0][i], grads[1][i]).astype(BF)
            out[s, span, 128:256] = jnp.where(left, grads[2][i], 0.0).astype(BF)

    for s in range(slices):
        for load in slice_loads(s):
            load.wait()

    @pl.loop(0, slices)
    def _(s):
        gq_sum[...] = jnp.zeros_like(gq_sum)
        for at in range(0, length, block):
            one_block(s, at)
        gq_all[s] = (gq_sum[...] * scale).astype(BF)

        @pl.when(s == 0)
        def _():
            for load in mine_loads:
                load.wait()
            after_core(0)
            after_core(1)

        @pl.when(s == slices - 1)
        def _():
            after_first(0)
            after_first(1)

    for load in late_loads:
        load.wait()
    right = jnp.concatenate((gq_all[z][:, :width], gk_all[z][:, :width], gv_all[z][:, :width]), axis=1)
    products = jnp.concatenate((dot_tn(target[...], right), dot_tn(grad_self[...], sm_own[:, :width])), axis=1)
    prod_s[...] = products.reshape(prod_s.shape)
    vec[0, 0:1, 0:width] = jnp.sum(gq_all[z][:, :width].astype(F32), axis=0, keepdims=True)
    vec[0, 1:2, 0:width] = jnp.sum(gv_all[z][:, :width].astype(F32), axis=0, keepdims=True)
    over_core(2).start()
    vector_copy(0).start()

    def input_grad(grads, first, rest, out_ref):
        @pl.loop(0, 4)
        def _(i):
            span = pl.ds(pl.multiple_of(i * (length // 4), length // 4), length // 4)
            total = 0.0
            for j, grad in enumerate(grads):
                for s in range(slices):
                    weight = columns_ref[s, (first + j) * width : (first + j + 1) * width, :]
                    total = total + dot_nn(grad[s, span, :width], weight)
            total = total[:, :width]
            if rest is not None:
                total = total + rest[span, :]
            out_ref[span, :] = total.astype(BF)

    after_core(2)
    vector_step(0)
    input_grad((gq_all, gk_all, gv_all), 0, rest_ref, target_grad_ref)
    after_first(2)
    vector_step(1)
    input_grad((gck_all, gcv_all), 3, None, memory_grad_ref)
    after_second(0)
    after_second(1)
    after_second(2)
    vector_step(2)
    vector_total_ref[...] = vec[3]
    for i in range(3):
        over_core(i).wait_send()
        for copy in (first_a(i), first_b(i), second_a(i), second_b(i)):
            copy.wait_send()
        vector_copy(i).wait_send()


def finish(prod_f, prod_c, heads, cross_grads, target, grad_self, logs, dots, ids, columns, rest, sums, cross_sums, first_sums):
    slices, length, wide = heads[0].shape
    model = target.shape[1]
    width = model // slices
    n = model // 8
    anywhere = pl.BlockSpec(memory_space=pl.ANY)
    inside = pl.BlockSpec(memory_space=pltpu.VMEM)
    columns_f, columns_c = prod_f.shape[1], prod_c.shape[1]

    def half(size):
        return pltpu.VMEM((2, 2, n, size), F32)

    sizes = (columns_f, columns_c, model)
    group = pltpu.VMEM((slices, length, wide), BF)
    tokens = pltpu.VMEM((length, model), BF)
    share = jax.ShapeDtypeStruct((length, model // slices), BF)
    return pl.pallas_call(
        partial(finish_kernel, width),
        out_shape=[jax.ShapeDtypeStruct((n, size), F32) for size in sizes]
        + [jax.ShapeDtypeStruct((16, model), F32), share, share],
        in_specs=[anywhere] * 11 + [inside] * 8,
        out_specs=[inside] * 6,
        scratch_shapes=[group] * 4
        + [pltpu.VMEM((length, wide), BF), group, group, tokens, tokens, group, group, group]
        + [pltpu.VMEM((length, wide), F32), pltpu.VMEM((128, length), F32), pltpu.VMEM((128, length), F32)]
        + [half(columns_f), half(columns_c), pltpu.VMEM((2, 2, 2, n, model), F32)]
        + [half(size) for size in sizes]
        + [pltpu.VMEM((2, 2, n, size // 2), F32) for size in sizes]
        + [pltpu.VMEM((2, n, size // 2), F32) for size in sizes]
        + [pltpu.VMEM((4, 16, model), F32), pltpu.VMEM((3, 16, model), F32), pltpu.VMEM((length, 1), F32), pltpu.VMEM((1, length), F32)]
        + [pltpu.SemaphoreType.DMA((18,)), pltpu.SemaphoreType.DMA((18,)), pltpu.SemaphoreType.DMA((4 * slices + 7,))],
        compiler_params=pltpu.CompilerParams(collective_id=1, has_side_effects=True, vmem_limit_bytes=63 * MIB),
    )(
        prod_f.reshape(2, 2, 2, n, columns_f), prod_c.reshape(2, 2, 2, n, columns_c), *heads, *cross_grads, target,
        grad_self, logs, dots, ids, columns, rest, sums, cross_sums, first_sums,
    )


def part_kernel(width, units, total_f_ref, total_c_ref, total_s_ref, vectors_ref, *outs):
    matrices, lines = outs[:10], outs[10:]
    for i, ref in enumerate((total_s_ref, total_c_ref)):
        for j in range(4):
            part = ref[:, j * width : (j + 1) * width]
            matrices[4 * i + j][...] = part.T if j == 3 else part
    matrices[8][...] = total_f_ref[:, :units]
    matrices[9][...] = total_f_ref[:, units:].T
    for i, out in enumerate(lines):
        out[...] = vectors_ref[i, : out.shape[0]]


def parts_of(total_f, total_c, total_s, vectors, width, units):
    n, model = total_s.shape
    matrices = [(n, width), (n, width), (n, width), (width, n)] * 2 + [(n, units), (units, n)]
    lines = [width, width, model, model, model, width, width] + [model] * 3 + [units] + [model] * 3
    out = pl.pallas_call(
        partial(part_kernel, width, units),
        out_shape=[jax.ShapeDtypeStruct(shape, F32) for shape in matrices]
        + [jax.ShapeDtypeStruct((size,), F32) for size in lines],
    )(total_f, total_c, total_s, vectors)
    return out[:10], out[10:]


def per_device(
    n_dp, n_tensor, target, memory, target_segments, memory_segments, self_query, self_query_bias, self_key, self_value,
    self_value_bias, self_output, self_output_bias, first_gain, first_shift, cross_query, cross_query_bias, cross_key,
    cross_value, cross_value_bias, cross_output, cross_output_bias, second_gain, second_shift, expand_weight, expand_bias,
    contract_weight, contract_bias, third_gain, third_shift, output_grad,
):
    model, width = self_query.shape
    units = expand_weight.shape[1]
    head_rows = 8 * width
    z = lax.axis_index("tensor")
    target_ids = target_segments.reshape(1, -1)
    memory_ids = memory_segments.reshape(1, -1)

    own = (
        self_query, self_key, self_value, self_output, cross_key, cross_value, cross_query, cross_output, expand_weight,
        contract_weight,
    )

    def rows_of(count, vectors):
        return jnp.stack([jnp.pad(v, (0, model - v.shape[0])) for v in vectors] + [jnp.zeros(model, F32)] * (count - len(vectors)))

    biases = (self_query_bias, self_value_bias, cross_query_bias, cross_value_bias, expand_bias)
    vectors = (self_output_bias, first_gain, first_shift, cross_output_bias, second_gain, second_shift)
    run = forward if (n_dp, n_tensor) == (8, 4) else forward_plain
    columns, full, sq, sk, sv, sm, cq, ck, cv, cm, logs, hat1, hat2, spread, low1, low2, act, slope = run(
        own, biases, target, memory, target_ids, memory_ids, vectors, n_dp, n_tensor, head_rows, units
    )
    layer_output, grad_ffn, grad_hidden, grad_second_sum, grad_cross, gcm, cross_dots, sums = feed_back(
        act, slope, hat2, spread, output_grad, cm, full,
        (second_gain, second_shift, contract_bias, third_gain, third_shift), head_rows,
    )
    ffn_products = weight_grad(z, units, (low2, [grad_hidden]), (grad_ffn, [act]))[0]
    gcq, gck, gcv = attend_back(False, 3 * n_tensor, cq, ck, cv, gcm, logs, cross_dots, target_ids, memory_ids)
    cross_products, cross_sums = weight_grad(z, width, (low1, [gcq]), (memory, [gck, gcv]), (grad_cross, [cm]))
    rest, grad_self, gsm, self_dots, first_sums = first_back(
        z, gcq, grad_second_sum, hat1, spread, sm, full, first_gain, head_rows
    )
    if (n_dp, n_tensor) == (8, 4):
        total_f, total_c, total_s, vectors, target_grad, memory_grad = finish(
            ffn_products, cross_products, (sq, sk, sv, gsm, sm), (gck, gcv), target, grad_self, logs, self_dots, target_ids,
            columns, rest, sums, cross_sums, first_sums,
        )
    else:
        gsq, gsk, gsv = attend_back(True, 0, sq, sk, sv, gsm, logs, self_dots, target_ids, target_ids)
        self_products, self_sums = weight_grad(z, width, (target, [gsq, gsk, gsv]), (grad_self, [sm]))
        total_f, total_c, total_s = scattered(ffn_products), scattered(cross_products), scattered(self_products)
        memory_grad = input_grad((gck, gcv), columns[:, 3 * width :, :width])
        target_grad = input_grad((gsq, gsk, gsv), columns[:, : 3 * width, :width], rest)
        vectors = (
            self_sums[0], self_sums[2], first_sums[2], first_sums[0], first_sums[1], cross_sums[0], cross_sums[2], sums[5],
            sums[3], sums[4], lax.dynamic_index_in_dim(sums, 8 + z, 0, keepdims=False), sums[2], sums[0], sums[1],
        )
        vectors = lax.psum(rows_of(16, vectors), "dp")
    parts, totals = parts_of(total_f, total_c, total_s, vectors, width, units)
    return (
        layer_output, target_grad, memory_grad, parts[0], totals[0], parts[1], parts[2], totals[1], parts[3], totals[2],
        totals[3], totals[4], parts[4], totals[5], parts[5], parts[6], totals[6], parts[7], totals[7], totals[8], totals[9],
        parts[8], totals[10], parts[9], totals[11], totals[12], totals[13],
    )


def solution(mesh):
    rows = P("dp", None)
    split = P(None, "tensor")
    both = P("dp", "tensor")
    turned = P("tensor", "dp")
    own = P("tensor")
    in_specs = (
        rows, rows, rows, rows,
        split, own, split, split, own, P("tensor", None), P(), P(), P(),
        split, own, split, split, own, P("tensor", None), P(), P(), P(),
        split, own, P("tensor", None), P(), P(), P(),
        rows,
    )
    out_specs = (
        rows, both, both,
        both, own, both, both, own, turned, P(), P(), P(),
        both, own, both, both, own, turned, P(), P(), P(),
        both, own, turned, P(), P(), P(),
    )
    return jax.shard_map(
        partial(per_device, mesh.shape["dp"], mesh.shape["tensor"]),
        mesh=mesh,
        in_specs=in_specs,
        out_specs=out_specs,
        check_vma=False,
    )
```

```python
from functools import partial

import jax
import jax.numpy as jnp
from jax import lax
from jax.experimental import pallas as pl
from jax.experimental.pallas import tpu as pltpu
from jax.sharding import PartitionSpec as P

HEAD_DIM = 64
EPSILON = 1e-05
NEGATIVE = -1e30
BF = jnp.bfloat16
F32 = jnp.float32
MESH = pl.DeviceIdType.MESH
MIB = 2**20


def dot_nn(a, b):
    return lax.dot_general(a, b, (((1,), (0,)), ((), ())), preferred_element_type=F32)


def dot_nt(a, b):
    return lax.dot_general(a, b, (((1,), (1,)), ((), ())), preferred_element_type=F32)


def dot_tn(a, b):
    return lax.dot_general(a, b, (((0,), (0,)), ((), ())), preferred_element_type=F32)


WIDE = 256
TOKEN_BLOCK = 256


def as_column(row):
    return jnp.transpose(jnp.broadcast_to(row, (128, row.shape[1])))[:, 0:1]


def fill_rows(rows_ref, lines):
    rows_ref[...] = jnp.zeros_like(rows_ref)
    for i, line in enumerate(lines):
        rows_ref[i, 0 : line.shape[0]] = line[...]


def erf_pair(hidden):
    phi = 0.5 * (1.0 + lax.erf(hidden * 0.7071067811865476))
    slope = phi + hidden * (jnp.exp(-0.5 * hidden * hidden) * 0.3989422804014327)
    return hidden * phi, slope


def forward_kernel(
    n_dp, n_tensor, count, rows, head_rows, hidden_rows,
    sqw_ref, skw_ref, svw_ref, sow_ref, ckw_ref, cvw_ref, cqw_ref, cow_ref, exw_ref, ctw_ref, target_ref, memory_ref, t_ids_ref, m_ids_ref,
    b0_ref, b1_ref, b2_ref, b3_ref, b4_ref, v0_ref, v1_ref, v2_ref, v3_ref, v4_ref, v5_ref,
    chunk_ref, columns_ref, found_ref, full_ref, sq_ref, sk_ref, sv_ref, sm_ref, cq_ref, ck_ref, cv_ref, cm_ref, logs_ref, hat1_ref, hat2_ref,
    r_ref, low1_ref, low2_ref, act_ref, slope_ref,
    columns, vectors_ref, bias_ref, t_row_ref, m_row_ref, t_col_ref, stage, full, low, bias, q_all, k_all, v_all, mixed, logs, hat1, hat2, spread, low1, low2, act, slope,
    send_sem, recv_sem, bias_send, bias_recv, load_sem, store_sem, out_sem,
):
    d = lax.axis_index("dp")
    z = lax.axis_index("tensor")
    others = n_tensor - 1
    length, model = target_ref.shape
    size = n_dp * rows
    dc = d + 1 - 2 * (d % 2)
    dx = d + 2 - 4 * ((d // 2) % 2)
    dy = d + 4 - 8 * (d // 4)
    dxy = dx + 4 - 8 * (d // 4)

    def slice_of(k):
        return (z + others - k) % n_tensor

    def along_z(g, source, k, step, slot):
        return pltpu.make_async_remote_copy(
            src_ref=source,
            dst_ref=found_ref.at[d, k, pl.ds(g * rows, rows)],
            send_sem=send_sem.at[g, slot],
            recv_sem=recv_sem.at[g, k],
            device_id={"tensor": z + step},
            device_id_type=MESH,
        )

    near = ((1, 0, 0), (2, 1, 1), (-1, 2, 2), (-2, 1, 11))

    def own_along(g, step, k, slot):
        return along_z(g, chunk_ref.at[pl.ds(g * rows, rows)], k, step, slot)

    def reaches(step):
        return z + step <= others if step > 0 else z + step >= 0

    inner = jnp.logical_and(z > 0, z < others)

    def relay(g):
        step = 2 * z - 3
        return along_z(g, found_ref.at[d, 1, pl.ds(g * rows, rows)], 1 + step, step, 12)

    def from_z(g, k):
        own_along(g, 0, k, 0).wait_recv()

    lead = 2

    def own_z(g):
        for step_z, k, slot in near:

            @pl.when(reaches(step_z))
            def _(step_z=step_z, k=k, slot=slot):
                own_along(g, step_z, k, slot).start()

    def pass_z(g):
        @pl.when(inner)
        def _():
            from_z(g, 1)
            relay(g).start()

        if g + lead < count:
            own_z(g + lead)

    def in_plane(g, slot, chunk, half, other):
        span = pl.ds(g * rows, rows) if half is None else pl.ds(g * rows + half * (rows // 2), rows // 2)
        piece = found_ref.at[chunk, :, span]
        return pltpu.make_async_remote_copy(
            src_ref=piece,
            dst_ref=piece,
            send_sem=send_sem.at[g, slot],
            recv_sem=recv_sem.at[g, slot],
            device_id={"dp": other},
            device_id_type=MESH,
        )

    def bias_copy(k):
        return pltpu.make_async_remote_copy(
            src_ref=bias_ref,
            dst_ref=bias.at[z],
            send_sem=bias_send.at[k],
            recv_sem=bias_recv.at[k],
            device_id={"tensor": (z + k + 1) % n_tensor},
            device_id_type=MESH,
        )

    routes = {3: (d, None, dx), 4: (d, None, dy), 5: (d, None, dc), 6: (dx, 0, dy), 7: (dy, 1, dx)}
    routes.update({8 + i: (chunk, None, dc) for i, chunk in enumerate((dx, dy, dxy))})

    def send(g, slot):
        return in_plane(g, slot, *routes[slot])

    def arrive(g, slot, half=None):
        in_plane(g, slot, d, half, dc).wait_recv()

    def first_hop(g):
        from_z(g, 0)
        from_z(g, 2)

        @pl.when(jnp.logical_not(inner))
        def _():
            from_z(g, 1)

        for slot in (3, 4, 5):
            send(g, slot).start()

    def pass_on(g):
        arrive(g, 3)
        send(g, 6).start()
        send(g, 8).start()
        arrive(g, 4)
        send(g, 7).start()
        send(g, 9).start()

    def load_of(g, k):
        return pltpu.make_async_copy(found_ref.at[:, k, pl.ds(g * rows, rows)], stage.at[k], load_sem.at[k])

    def last_hop(g):
        arrive(g, 6, 0)
        arrive(g, 7, 1)
        send(g, 10).start()

    def landed(g):
        arrive(g, 5)
        for slot in (8, 9, 10):
            arrive(g, slot)
        for k in range(others):
            load_of(g, k).start()

    def home(g):
        kept = hidden_rows // size + head_rows // size
        return (full, pl.ds(g * size, size)) if g < kept else (low, pl.ds((g % 2) * size, size))

    def store_of(g, s):
        place, span = home(g)
        return pltpu.make_async_copy(place.at[s, span], full_ref.at[s, pl.ds(g * size, size)], store_sem.at[g, s])

    def rounded(g):
        place, span = home(g)
        for k in range(others):
            load_of(g, k).wait()
            place[slice_of(k), span] = stage[k].reshape(size, model).astype(BF)
        for s in range(n_tensor):
            store_of(g, s).start()

    def pause(step, between):
        for at, *moves in between:

            @pl.when(step == at)
            def _(moves=moves):
                for move, g in moves:
                    move(g)

    def project(x_ref, s, first, bias_row, out_ref):
        @pl.loop(0, 2)
        def _(i):
            span = pl.ds(pl.multiple_of(i * (length // 2), length // 2), length // 2)
            value = dot_nt(x_ref[span, :], full[s, pl.ds(first, WIDE), :])
            if bias_row is not None:
                value = value + bias[s, bias_row : bias_row + 1, :WIDE]
            filled = lax.broadcasted_iota(jnp.int32, (1, WIDE), 1) < head_rows // 8
            out_ref[s, span, :] = jnp.where(filled, value, 0.0).astype(BF)

    def attend(s, causal, k_ids_ref, base, *between):
        half = length // 2
        lane = lax.broadcasted_iota(jnp.int32, (1, 128), 1)

        @pl.loop(0, 3)
        def _(h):
            columns = pl.ds(pl.multiple_of((h // 2) * 128, 128), 128)
            mine = (lane // HEAD_DIM) == (h % 2)
            log_lane = lane == base + 3 * s + h
            for b in range(2):
                reach = (b + 1) * half if causal else length
                span = slice(b * half, (b + 1) * half)
                queries = q_all[s, span, columns] * jnp.asarray(HEAD_DIM**-0.5, BF)
                scores = dot_nt(jnp.where(mine, queries, jnp.zeros_like(queries)), k_all[s, :reach, columns])
                allowed = t_col_ref[span, :] == k_ids_ref[:, :reach]
                if causal:
                    allowed = allowed & (
                        lax.broadcasted_iota(jnp.int32, (half, reach), 0) + b * half
                        >= lax.broadcasted_iota(jnp.int32, (half, reach), 1)
                    )
                scores = jnp.where(allowed, scores, NEGATIVE)
                top = jnp.max(scores, axis=1, keepdims=True)
                weights = jnp.exp(scores - top)
                total = jnp.sum(weights, axis=1, keepdims=True)
                out = (dot_nn(weights.astype(BF), v_all[s, :reach, columns]) * (1.0 / total)).astype(BF)
                before = mixed[s, span, columns]
                before = jnp.where(h % 2 == 1, before, jnp.zeros_like(before))
                mixed[s, span, columns] = jnp.where(mine, out, before)
                logs[span, :] = jnp.where(log_lane, top + jnp.log(total), logs[span, :])
            pause(h, between)

    def close(first, bias_row, residual, hat, low_out, column):
        block = length // 4

        @pl.loop(0, 4)
        def _(i):
            span = pl.ds(pl.multiple_of(i * block, block), block)
            value = residual(span) + vectors_ref[bias_row : bias_row + 1, :]
            for s in range(n_tensor):
                value = value + dot_nn(mixed[s, span, :], full[s, pl.ds(first, WIDE), :])
            centered = value - jnp.mean(value, axis=1, keepdims=True)
            scale = lax.rsqrt(jnp.mean(centered * centered, axis=1, keepdims=True) + EPSILON)
            normed = centered * scale
            hat[span, :] = normed
            here = lax.broadcasted_iota(jnp.int32, (1, 128), 1) == column
            spread[span, :] = jnp.where(here, scale, spread[span, :])
            low_out[span, :] = (
                normed * vectors_ref[bias_row + 1 : bias_row + 2, :] + vectors_ref[bias_row + 2 : bias_row + 3, :]
            ).astype(BF)

    def expand(s, slot):
        @pl.loop(0, 4)
        def _(i):
            span = pl.ds(pl.multiple_of(i * (length // 4), length // 4), length // 4)
            hidden = dot_nt(low2[span, :], full[s, pl.ds(head_rows, hidden_rows), :]) + bias[s, 4:5, :]
            value, change = erf_pair(hidden)
            act[slot, span, :] = value.astype(BF)
            slope[slot, span, :] = change.astype(BF)

    def own_columns(s):
        for i, first in enumerate((q0, k0, v0, ck0, cv0)):
            value = full[s, pl.ds(first, step), :].astype(F32)
            columns[s, pl.ds(i * step, step), :] = pltpu.roll(value, model - z * step, 1)[:, :WIDE].astype(BF)

    def out_copy(i, source, target):
        return pltpu.make_async_copy(source, target, out_sem.at[i])

    def expand_out(s, slot):
        return (
            out_copy(13 + 2 * slot, act.at[slot], act_ref.at[s]),
            out_copy(14 + 2 * slot, slope.at[slot], slope_ref.at[s]),
        )

    barrier = pltpu.get_barrier_semaphore()
    for k in range(1, n_tensor):
        pl.semaphore_signal(barrier, inc=1, device_id={"tensor": (z + k) % n_tensor}, device_id_type=MESH)
    for other in (dc, dx, dy):
        pl.semaphore_signal(barrier, inc=1, device_id={"dp": other}, device_id_type=MESH)
    step = head_rows // 8
    q0, k0, v0, o0, ck0, cv0, cq0, co0 = (i * step for i in range(8))
    own_loads = [
        pltpu.make_async_copy(source, place, load_sem.at[3 + i])
        for i, (source, place) in enumerate(
            (
                (sqw_ref, full.at[z, pl.ds(q0, step)]),
                (skw_ref, full.at[z, pl.ds(k0, step)]),
                (svw_ref, full.at[z, pl.ds(v0, step)]),
                (ckw_ref, full.at[z, pl.ds(ck0, step)]),
                (cvw_ref, full.at[z, pl.ds(cv0, step)]),
                (cqw_ref, full.at[z, pl.ds(cq0, step)]),
                (sow_ref, full.at[z, pl.ds(o0, step)]),
                (cow_ref, full.at[z, pl.ds(co0, step)]),
                (exw_ref, act.at[0, pl.ds(0, model)]),
                (ctw_ref, low.at[z]),
            )
        )
    ]
    for load in own_loads:
        load.start()
    t_row_ref[...] = t_ids_ref[...].astype(F32)
    m_row_ref[...] = m_ids_ref[...].astype(F32)
    t_col_ref[...] = as_column(t_row_ref[...])
    fill_rows(bias_ref, (b0_ref, b1_ref, b2_ref, b3_ref, b4_ref))
    fill_rows(vectors_ref, (v0_ref, v1_ref, v2_ref, v3_ref, v4_ref, v5_ref))
    bias[z] = bias_ref[...]
    pl.semaphore_wait(barrier, others + 3)
    for k in range(others):
        bias_copy(k).start()
    def chunk_copy(g):
        return pltpu.make_async_copy(stage.at[0, g], chunk_ref.at[pl.ds(g * rows, rows)], load_sem.at[g % 3])

    def offer(g):
        place, span = home(g)
        first = span.start + d * rows
        stage[0, g] = place[z, pl.ds(pl.multiple_of(first, 16), rows), :].astype(F32)
        chunk_copy(g).start()

    def give(g):
        chunk_copy(g).wait()
        if g < lead:
            own_z(g)

    own_loads[0].wait()
    own_loads[1].wait()
    offer(0)
    own_loads[2].wait()
    own_loads[6].wait()
    give(0)
    offer(1)
    own_loads[3].wait()
    own_loads[4].wait()
    give(1)
    offer(2)
    own_loads[5].wait()
    own_loads[7].wait()
    give(2)
    offer(3)
    own_loads[8].wait()
    full[z, pl.ds(head_rows, hidden_rows), :] = jnp.transpose(act[0, :model, :].astype(F32)).astype(BF)
    offer(4)
    give(3)
    offer(5)
    own_loads[9].wait()
    give(4)
    offer(6)
    give(5)
    offer(7)
    give(6)
    give(7)

    logs[...] = jnp.zeros_like(logs)
    spread[...] = jnp.zeros_like(spread)
    project(target_ref, z, q0, 0, q_all)
    project(target_ref, z, k0, None, k_all)
    project(target_ref, z, v0, 1, v_all)
    attend(z, True, t_row_ref, 0)
    for k in range(others):
        bias_copy(k).wait_recv()
    pass_z(0)
    first_hop(0)
    pass_z(1)
    first_hop(1)
    pass_on(0)
    pass_z(2)
    first_hop(2)
    pass_on(1)
    pass_z(3)
    last_hop(0)
    landed(0)
    first_hop(3)
    rounded(0)
    for k in range(others):
        project(target_ref, slice_of(k), q0, 0, q_all)
        project(target_ref, slice_of(k), k0, None, k_all)
    pass_z(4)
    pass_on(2)
    last_hop(1)
    first_hop(4)
    landed(1)
    pass_z(5)
    rounded(1)
    for k in range(others):
        project(target_ref, slice_of(k), v0, 1, v_all)
    attend(slice_of(0), True, t_row_ref, 0, (0, (last_hop, 2)), (1, (pass_on, 3), (first_hop, 5)))
    attend(slice_of(1), True, t_row_ref, 0, (0, (landed, 2)), (1, (pass_z, 6)))
    rounded(2)
    attend(slice_of(2), True, t_row_ref, 0, (0, (last_hop, 3), (pass_on, 4)), (1, (first_hop, 6)))
    pass_z(7)
    self_out = [
        out_copy(0, q_all, sq_ref), out_copy(1, k_all, sk_ref), out_copy(2, v_all, sv_ref), out_copy(3, mixed, sm_ref)
    ]
    for copy in self_out:
        copy.start()
    close(o0, 0, lambda span: target_ref[span, :].astype(F32), hat1, low1, 0)
    landed(3)
    out_copy(4, hat1, hat1_ref).start()
    out_copy(5, low1, low1_ref).start()
    for copy in self_out:
        copy.wait()

    @pl.loop(0, n_tensor)
    def _(s):
        project(memory_ref, s, ck0, None, k_all)
        project(memory_ref, s, cv0, 3, v_all)

    pass_on(5)
    first_hop(7)
    project(low1, z, cq0, 2, q_all)
    attend(z, False, m_row_ref, 3 * n_tensor, (1, (last_hop, 4)))
    rounded(3)
    for k in range(others):
        project(low1, slice_of(k), cq0, 2, q_all)
    landed(4)
    attend(slice_of(0), False, m_row_ref, 3 * n_tensor, (0, (pass_on, 6)), (1, (last_hop, 5)))
    rounded(4)
    attend(slice_of(1), False, m_row_ref, 3 * n_tensor, (0, (landed, 5)), (1, (pass_on, 7)))
    for s in range(n_tensor):
        own_columns(s)
    out_copy(10, columns, columns_ref).start()
    rounded(5)
    attend(slice_of(2), False, m_row_ref, 3 * n_tensor, (0, (last_hop, 6)), (2, (last_hop, 7)))
    cross_out = [
        out_copy(0, q_all, cq_ref), out_copy(1, k_all, ck_ref), out_copy(2, v_all, cv_ref), out_copy(3, mixed, cm_ref),
        out_copy(6, logs, logs_ref),
    ]
    for copy in cross_out:
        copy.start()
    close(co0, 3, lambda span: hat1[span, :] * vectors_ref[1:2, :] + vectors_ref[2:3, :], hat2, low2, 1)
    out_copy(7, hat2, hat2_ref).start()
    out_copy(8, low2, low2_ref).start()
    out_copy(9, spread, r_ref).start()
    landed(6)
    expand(z, 0)
    for copy in expand_out(z, 0):
        copy.start()
    rounded(6)
    landed(7)
    expand(slice_of(0), 1)
    for copy in expand_out(slice_of(0), 1):
        copy.start()
    rounded(7)
    for copy in expand_out(z, 0):
        copy.wait()
    expand(slice_of(1), 0)
    for copy in expand_out(slice_of(1), 0):
        copy.start()
    for copy in expand_out(slice_of(0), 1):
        copy.wait()
    expand(slice_of(2), 1)
    for copy in expand_out(slice_of(2), 1):
        copy.start()

    for copy in expand_out(slice_of(1), 0) + expand_out(slice_of(2), 1) + tuple(cross_out):
        copy.wait()
    for i, source, target in ((4, hat1, hat1_ref), (5, low1, low1_ref), (7, hat2, hat2_ref), (8, low2, low2_ref)):
        out_copy(i, source, target).wait()
    out_copy(9, spread, r_ref).wait()
    out_copy(10, columns, columns_ref).wait()
    for g in range(count):
        for s in range(n_tensor):
            store_of(g, s).wait()
    for k in range(others):
        bias_copy(k).wait_send()
    for g in range(count):
        for step_z, k, slot in near:

            @pl.when(reaches(step_z))
            def _(g=g, step_z=step_z, k=k, slot=slot):
                own_along(g, step_z, k, slot).wait_send()

        @pl.when(inner)
        def _(g=g):
            relay(g).wait_send()

        for slot in routes:
            send(g, slot).wait_send()


def forward(own, biases, target, memory, target_ids, memory_ids, vectors, n_dp, n_tensor, head_rows, hidden_rows):
    length, model = target.shape
    count = 8
    total = head_rows + 2 * hidden_rows
    size = total // count
    rows = size // n_dp
    step = head_rows // 8
    anywhere = pl.BlockSpec(memory_space=pl.ANY)
    inside = pl.BlockSpec(memory_space=pltpu.VMEM)
    heads = jax.ShapeDtypeStruct((n_tensor, length, WIDE), BF)
    tokens = jax.ShapeDtypeStruct((length, model), F32)
    tokens_low = jax.ShapeDtypeStruct((length, model), BF)
    lanes = jax.ShapeDtypeStruct((length, 128), F32)
    units = jax.ShapeDtypeStruct((n_tensor, length, hidden_rows), BF)
    out_shape = (
        jax.ShapeDtypeStruct((count * rows, model), F32),
        jax.ShapeDtypeStruct((n_tensor, 5 * step, WIDE), BF),
        jax.ShapeDtypeStruct((n_dp, n_tensor - 1, count * rows, model), F32),
        jax.ShapeDtypeStruct((n_tensor, total, model), BF),
        heads, heads, heads, heads, heads, heads, heads, heads,
        lanes, tokens, tokens, lanes, tokens_low, tokens_low, units, units,
    )
    flops = 2 * length * model * (2 * n_tensor * head_rows) + 4 * length * model * n_tensor * hidden_rows
    outs = pl.pallas_call(
        partial(forward_kernel, n_dp, n_tensor, count, rows, head_rows, hidden_rows),
        out_shape=out_shape,
        in_specs=[anywhere] * 10 + [inside] * 15,
        out_specs=[anywhere] * len(out_shape),
        scratch_shapes=[
            pltpu.VMEM((n_tensor, 5 * step, WIDE), BF),
            pltpu.VMEM((8, model), F32),
            pltpu.VMEM((8, model), F32),
            pltpu.VMEM((1, length), F32),
            pltpu.VMEM((1, length), F32),
            pltpu.VMEM((length, 1), F32),
            pltpu.VMEM((n_tensor - 1, n_dp, rows, model), F32),
            pltpu.VMEM((n_tensor, head_rows + hidden_rows, model), BF),
            pltpu.VMEM((n_tensor, hidden_rows, model), BF),
            pltpu.VMEM((n_tensor, 8, model), F32),
            pltpu.VMEM(heads.shape, BF),
            pltpu.VMEM(heads.shape, BF),
            pltpu.VMEM(heads.shape, BF),
            pltpu.VMEM(heads.shape, BF),
            pltpu.VMEM(lanes.shape, F32),
            pltpu.VMEM(tokens.shape, F32),
            pltpu.VMEM(tokens.shape, F32),
            pltpu.VMEM(lanes.shape, F32),
            pltpu.VMEM(tokens.shape, BF),
            pltpu.VMEM(tokens.shape, BF),
            pltpu.VMEM((2, length, hidden_rows), BF),
            pltpu.VMEM((2, length, hidden_rows), BF),
            pltpu.SemaphoreType.DMA((count, 13)),
            pltpu.SemaphoreType.DMA((count, 11)),
            pltpu.SemaphoreType.DMA((n_tensor - 1,)),
            pltpu.SemaphoreType.DMA((n_tensor - 1,)),
            pltpu.SemaphoreType.DMA((13,)),
            pltpu.SemaphoreType.DMA((count, n_tensor)),
            pltpu.SemaphoreType.DMA((17,)),
        ],
        cost_estimate=pl.CostEstimate(flops=flops, bytes_accessed=60 * MIB, transcendentals=0),
        compiler_params=pltpu.CompilerParams(collective_id=0, has_side_effects=True, vmem_limit_bytes=63 * MIB),
    )(
        *(x.T if x.shape[0] > x.shape[1] else x for x in own), target, memory, target_ids, memory_ids, *biases, *vectors
    )
    return outs[1], *outs[3:]


def round_kernel(wide_ref, low_ref):
    low_ref[...] = wide_ref[...].astype(BF)


def rounded_copy(array):
    slices, rows, width = array.shape
    block = pl.BlockSpec((1, rows // 4, width), lambda i, j: (i, j, 0))
    return pl.pallas_call(
        round_kernel,
        grid=(slices, 4),
        in_specs=[block],
        out_specs=block,
        out_shape=jax.ShapeDtypeStruct(array.shape, BF),
    )(array)


def forward_plain(own, biases, target, memory, target_ids, memory_ids, vectors, n_dp, n_tensor, head_rows, hidden_rows):
    length, model = target.shape
    width = head_rows // 8
    sq, sk, sv, so, ck, cv, cq, co, expand, contract = own
    own = jnp.concatenate((sq.T, sk.T, sv.T, so, ck.T, cv.T, cq.T, co, expand.T, contract), axis=0)
    full = rounded_copy(lax.all_gather(own.astype(F32), "tensor", axis=0))
    bias = lax.all_gather(jnp.stack([jnp.pad(b, (0, model - b.shape[0])) for b in biases]), "tensor", axis=0)
    target_ids, memory_ids = target_ids.reshape(-1), memory_ids.reshape(-1)

    def weight(i):
        return full[:, i * width : (i + 1) * width]

    def padded(x):
        return jnp.pad(x, ((0, 0), (0, 0), (0, WIDE - width)))

    def project(x, i, row=None):
        value = jnp.einsum("td,swd->stw", x, weight(i), preferred_element_type=F32)
        if row is not None:
            value = value + bias[:, row, None, :width]
        return value.astype(BF)

    def attend(queries, keys, values, key_ids, causal):
        def split(x):
            return x.reshape(n_tensor, length, -1, HEAD_DIM)

        def one(items):
            q, k, v = items
            scores = jnp.einsum("qhd,khd->hqk", q, k, preferred_element_type=F32) * HEAD_DIM**-0.5
            allowed = target_ids[:, None] == key_ids[None, :]
            if causal:
                at = jnp.arange(length, dtype=jnp.int32)
                allowed = allowed & (at[:, None] >= at[None, :])
            scores = jnp.where(allowed[None], scores, NEGATIVE)
            probs = jax.nn.softmax(scores, axis=-1).astype(BF)
            out = jnp.einsum("hqk,khd->qhd", probs, v, preferred_element_type=F32)
            return out.astype(BF), jax.nn.logsumexp(scores, axis=-1)

        mixed, logs = lax.map(one, (split(queries), split(keys), split(values)))
        return mixed.reshape(n_tensor, length, width), logs.reshape(-1, length)

    def close(mixed, i, residual, row):
        value = residual + vectors[row] + jnp.einsum("stw,swd->td", mixed, weight(i), preferred_element_type=F32)
        centered = value - jnp.mean(value, axis=1, keepdims=True)
        scale = lax.rsqrt(jnp.mean(centered * centered, axis=1, keepdims=True) + EPSILON)
        hat = centered * scale
        normed = hat * vectors[row + 1] + vectors[row + 2]
        return hat, scale, normed, normed.astype(BF)

    sq, sk, sv = project(target, 0, 0), project(target, 1), project(target, 2, 1)
    sm, self_logs = attend(sq, sk, sv, target_ids, True)
    hat1, r1, first, low1 = close(sm, 3, target.astype(F32), 0)
    ck, cv, cq = project(memory, 4), project(memory, 5, 3), project(low1, 6, 2)
    cm, cross_logs = attend(cq, ck, cv, memory_ids, False)
    hat2, r2, _, low2 = close(cm, 7, first, 3)
    hidden = jnp.einsum("td,shd->sth", low2, full[:, head_rows : head_rows + hidden_rows], preferred_element_type=F32)
    act, slope = erf_pair(hidden + bias[:, 4, None, :])
    logs = jnp.concatenate((self_logs, cross_logs), axis=0).T
    logs = jnp.pad(logs, ((0, 0), (0, 128 - logs.shape[1])))
    spread = jnp.pad(jnp.concatenate((r1, r2), axis=1), ((0, 0), (0, 126)))
    heads = [padded(x) for x in (sq, sk, sv, sm, cq, ck, cv, cm)]
    kept = jnp.concatenate((full[:, : 3 * width], full[:, 4 * width : 6 * width]), axis=1)
    columns = padded(lax.dynamic_slice_in_dim(kept, lax.axis_index("tensor") * width, width, 2))
    return columns, full, *heads, logs, hat1, hat2, spread, low1, low2, act.astype(BF), slope.astype(BF)


def attend_back_kernel(
    heads, base, block, causal, q_ref, k_ref, v_ref, gm_ref, logs_ref, dots_ref, q_row_ref, k_row_ref, gq_ref, gk_ref,
    gv_ref, gq_sum, logs, dots, k_ids_ref, q_ids_ref
):
    length = q_ref.shape[1]
    lane = lax.broadcasted_iota(jnp.int32, (1, 128), 1)
    scale = HEAD_DIM**-0.5
    s = pl.program_id(0)

    @pl.when(s == 0)
    def _():
        logs[...] = jnp.transpose(logs_ref[...])
        dots[...] = jnp.transpose(dots_ref[...])
        k_ids_ref[...] = as_column(k_row_ref[...].astype(F32))
        q_ids_ref[...] = q_row_ref[...].astype(F32)

    gq_sum[...] = jnp.zeros_like(gq_sum)

    def one_block(at, first):
        k_span = pl.ds(at, block)
        reach = length - first
        allowed = k_ids_ref[k_span, :] == q_ids_ref[:, first:]
        if causal:
            allowed = allowed & (
                lax.broadcasted_iota(jnp.int32, (block, reach), 0) <= lax.broadcasted_iota(jnp.int32, (block, reach), 1)
            )
        grads = []
        for h in range(heads):
            mine = (lane // HEAD_DIM) == (h % 2)
            columns = slice(128 * (h // 2), 128 * (h // 2) + 128)
            keys = k_ref[0, k_span, columns]
            keys = jnp.where(mine, keys, jnp.zeros_like(keys))
            values = v_ref[0, k_span, columns]
            values = jnp.where(mine, values, jnp.zeros_like(values))
            queries = q_ref[0, first:, columns]
            gm = gm_ref[0, first:, columns]
            scores = dot_nt(keys * jnp.asarray(scale, BF), queries)
            probs = jnp.where(allowed, jnp.exp(scores - logs[pl.ds(base + heads * s + h, 1), first:]), 0.0)
            grad_scores = (probs * (dot_nt(values, gm) - dots[pl.ds(heads * s + h, 1), first:])).astype(BF)
            grads.append((dot_nn(grad_scores, queries) * scale, dot_nn(probs.astype(BF), gm)))
            gq_sum[first:, columns] += dot_tn(grad_scores, keys)
        left = lane < HEAD_DIM
        for i, out_ref in enumerate((gk_ref, gv_ref)):
            out_ref[0, k_span, 0:128] = jnp.where(left, grads[0][i], grads[1][i]).astype(BF)
            out_ref[0, k_span, 128:256] = jnp.where(left, grads[2][i], 0.0).astype(BF)

    if causal:
        for b in range(length // block):
            one_block(b * block, b * block)
    else:

        @pl.loop(0, length // block)
        def _(b):
            one_block(pl.multiple_of(b * block, block), 0)

    gq_ref[0] = (gq_sum[...] * scale).astype(BF)


def attend_back(causal, base, queries, keys, values, grad_mixed, logs, dots, query_ids, key_ids):
    slices, length, wide = queries.shape
    part = pl.BlockSpec((1, length, wide), lambda i: (i, 0, 0))
    out = jax.ShapeDtypeStruct((slices, length, wide), BF)
    lanes = pl.BlockSpec((length, 128), lambda i: (0, 0))
    return pl.pallas_call(
        partial(attend_back_kernel, 3, base, 256, causal),
        grid=(slices,),
        in_specs=[part] * 4
        + [lanes, lanes, pl.BlockSpec((1, length), lambda i: (0, 0)), pl.BlockSpec((1, length), lambda i: (0, 0))],
        out_specs=[part] * 3,
        out_shape=[out] * 3,
        scratch_shapes=[
            pltpu.VMEM((length, wide), F32),
            pltpu.VMEM((128, length), F32),
            pltpu.VMEM((128, length), F32),
            pltpu.VMEM((length, 1), F32),
            pltpu.VMEM((1, length), F32),
        ],
        compiler_params=pltpu.CompilerParams(vmem_limit_bytes=60 * MIB),
    )(queries, keys, values, grad_mixed, logs, dots, query_ids, key_ids)


def norm_back(grad, hat, scale, gain):
    scaled = grad * gain
    return scale * (
        scaled - jnp.mean(scaled, axis=1, keepdims=True) - hat * jnp.mean(scaled * hat, axis=1, keepdims=True)
    )


def add_sums(sums_ref, rows):
    @pl.when(pl.program_id(0) == 0)
    def _():
        sums_ref[...] = jnp.zeros_like(sums_ref)

    for row, value in rows:
        sums_ref[row : row + 1, :] += jnp.sum(value, axis=0, keepdims=True)


def head_products(grad_mixed, mixed, s, heads, dots):
    product = grad_mixed * mixed.astype(F32)
    lane = lax.broadcasted_iota(jnp.int32, (1, WIDE), 1)
    out_lane = lax.broadcasted_iota(jnp.int32, (1, 128), 1)
    for h in range(heads):
        total = jnp.sum(jnp.where(lane // HEAD_DIM == h, product, 0.0), axis=1, keepdims=True)
        dots = jnp.where(out_lane == heads * s + h, total, dots)
    return dots


def mixed_back(grad_low, out_weight, mixed_ref, gm_ref, dots_ref):
    slices = mixed_ref.shape[0]
    width = out_weight.shape[1]
    dots = jnp.zeros(dots_ref.shape, F32)
    for s in range(slices):
        grad_mixed = dot_nt(grad_low, out_weight[s]).astype(BF)
        grad_mixed = jnp.concatenate((grad_mixed, jnp.zeros((grad_mixed.shape[0], WIDE - width), BF)), axis=1)
        gm_ref[s] = grad_mixed
        dots = head_products(grad_mixed.astype(F32), mixed_ref[s], s, 3, dots)
    dots_ref[...] = dots


def feed_back_kernel(
    act_ref, slope_ref, hat2_ref, r_ref, grad_ref, mixed_ref, expand_ref, contract_ref, out_weight_ref,
    v0_ref, v1_ref, v2_ref, v3_ref, v4_ref, out_ref, grad_ffn_ref, grad_hidden_ref, grad_sum_ref, grad_cross_ref, gm_ref, dots_ref, sums_ref,
    vectors_ref
):
    slices = act_ref.shape[0]
    fill_rows(vectors_ref, (v0_ref, v1_ref, v2_ref, v3_ref, v4_ref))
    vector = [vectors_ref[i : i + 1, :] for i in range(5)]
    hat2 = hat2_ref[...]
    value = hat2 * vector[0] + vector[1] + vector[2]
    for s in range(slices):
        value = value + dot_nn(act_ref[s], contract_ref[s])
    centered = value - jnp.mean(value, axis=1, keepdims=True)
    scale = lax.rsqrt(jnp.mean(centered * centered, axis=1, keepdims=True) + EPSILON)
    hat3 = centered * scale
    out_ref[...] = (hat3 * vector[3] + vector[4]).astype(BF)
    grad = grad_ref[...].astype(F32)
    grad_third = norm_back(grad, hat3, scale, vector[3])
    grad_ffn = grad_third.astype(BF)
    grad_ffn_ref[...] = grad_ffn
    grad_second = grad_third
    rows = [(0, grad * hat3), (1, grad), (2, grad_ffn.astype(F32))]
    for s in range(slices):
        grad_hidden = (dot_nt(grad_ffn, contract_ref[s]) * slope_ref[s].astype(F32)).astype(BF)
        grad_hidden_ref[s] = grad_hidden
        rows.append((8 + s, grad_hidden.astype(F32)))
        grad_second = grad_second + dot_nn(grad_hidden, expand_ref[s])
    grad_sum = norm_back(grad_second, hat2, r_ref[:, 1:2], vector[0])
    grad_sum_ref[...] = grad_sum
    grad_cross = grad_sum.astype(BF)
    grad_cross_ref[...] = grad_cross
    rows += [(3, grad_second * hat2), (4, grad_second), (5, grad_cross.astype(F32))]
    add_sums(sums_ref, rows)
    mixed_back(grad_cross, out_weight_ref, mixed_ref, gm_ref, dots_ref)


def feed_back(act, slope, hat2, spread, output_grad, mixed, full, vectors, head_rows):
    slices, length, units = act.shape
    model = hat2.shape[1]
    block = TOKEN_BLOCK
    width = head_rows // 8
    tokens = pl.BlockSpec((block, model), lambda i: (i, 0))
    lanes = pl.BlockSpec((block, 128), lambda i: (i, 0))
    wide = pl.BlockSpec((slices, block, units), lambda i: (0, i, 0))
    heads = pl.BlockSpec((slices, block, WIDE), lambda i: (0, i, 0))
    rows = pl.BlockSpec((16, model), lambda i: (0, 0))

    def weight(first, size):
        return pl.BlockSpec((slices, size, model), lambda i: (0, first // size, 0))

    low = jax.ShapeDtypeStruct((length, model), BF)
    return pl.pallas_call(
        feed_back_kernel,
        grid=(length // block,),
        in_specs=[wide, wide, tokens, lanes, tokens, heads]
        + [weight(head_rows, units), weight(head_rows + units, units), weight(7 * width, width)]
        + [pl.BlockSpec((model,), lambda i: (0,))] * 5,
        scratch_shapes=[pltpu.VMEM((8, model), F32)],
        out_specs=[tokens, tokens, wide, tokens, tokens, heads, lanes, rows],
        out_shape=[
            low,
            low,
            jax.ShapeDtypeStruct(act.shape, BF),
            jax.ShapeDtypeStruct((length, model), F32),
            low,
            jax.ShapeDtypeStruct((slices, length, WIDE), BF),
            jax.ShapeDtypeStruct((length, 128), F32),
            jax.ShapeDtypeStruct((16, model), F32),
        ],
        compiler_params=pltpu.CompilerParams(vmem_limit_bytes=62 * MIB),
    )(act, slope, hat2, spread, output_grad, mixed, full, full, full, *vectors)


def first_back_kernel(
    z_ref, gq_ref, grad_sum_ref, hat1_ref, r_ref, mixed_ref, query_ref, out_weight_ref, gain_ref,
    rest_ref, grad_self_ref, gm_ref, dots_ref, sums_ref, vectors_ref
):
    fill_rows(vectors_ref, (gain_ref,))
    slices = gq_ref.shape[0]
    width = query_ref.shape[1]
    grad = grad_sum_ref[...]
    for s in range(slices):
        grad = grad + dot_nn(gq_ref[s][:, :width], query_ref[s])
    hat = hat1_ref[...]
    grad_first = norm_back(grad, hat, r_ref[:, 0:1], vectors_ref[0:1, :])
    rest_ref[...] = pltpu.roll(grad_first, grad_first.shape[1] - z_ref[0] * width, 1)[:, :width]
    grad_self = grad_first.astype(BF)
    grad_self_ref[...] = grad_self
    add_sums(sums_ref, [(0, grad * hat), (1, grad), (2, grad_self.astype(F32))])
    mixed_back(grad_self, out_weight_ref, mixed_ref, gm_ref, dots_ref)


def first_back(z, gq, grad_sum, hat1, spread, mixed, full, vectors, head_rows):
    slices, length, _ = gq.shape
    model = hat1.shape[1]
    block = TOKEN_BLOCK
    width = head_rows // 8
    tokens = pl.BlockSpec((block, model), lambda i, _: (i, 0))
    lanes = pl.BlockSpec((block, 128), lambda i, _: (i, 0))
    share = pl.BlockSpec((block, width), lambda i, _: (i, 0))
    heads = pl.BlockSpec((slices, block, WIDE), lambda i, _: (0, i, 0))
    rows = pl.BlockSpec((8, model), lambda i, _: (0, 0))
    return pl.pallas_call(
        first_back_kernel,
        grid_spec=pltpu.PrefetchScalarGridSpec(
            num_scalar_prefetch=1,
            grid=(length // block,),
            in_specs=[heads, tokens, tokens, lanes, heads]
            + [pl.BlockSpec((slices, width, model), lambda i, _, j=j: (0, j, 0)) for j in (6, 3)]
            + [pl.BlockSpec((model,), lambda i, _: (0,))],
            scratch_shapes=[pltpu.VMEM((8, model), F32)],
            out_specs=[share, tokens, heads, lanes, rows],
        ),
        out_shape=[
            jax.ShapeDtypeStruct((length, width), F32),
            jax.ShapeDtypeStruct((length, model), BF),
            jax.ShapeDtypeStruct((slices, length, WIDE), BF),
            jax.ShapeDtypeStruct((length, 128), F32),
            jax.ShapeDtypeStruct((8, model), F32),
        ],
        compiler_params=pltpu.CompilerParams(vmem_limit_bytes=62 * MIB),
    )(z.reshape(1), gq, grad_sum, hat1, spread, mixed, full, full, vectors)


def input_grad_kernel(count, *refs):
    out_ref = refs[-1]
    weight_ref = refs[count]
    slices = refs[0].shape[0]
    width = weight_ref.shape[1] // count
    total = refs[count + 1][...] if len(refs) == count + 3 else jnp.zeros(out_ref.shape, F32)
    for i in range(count):
        for s in range(slices):
            total = total + dot_nn(refs[i][s][:, :width], weight_ref[s, i * width : (i + 1) * width, :])
    out_ref[...] = total.astype(BF)


def input_grad(grads, weights, rest=None):
    slices, length, wide = grads[0].shape
    share = weights.shape[2]
    block = length // 2
    tokens = pl.BlockSpec((block, share), lambda i: (i, 0))
    specs = [pl.BlockSpec((slices, block, wide), lambda i: (0, i, 0))] * len(grads)
    specs.append(pl.BlockSpec(weights.shape, lambda i: (0, 0, 0)))
    operands = (*grads, weights)
    if rest is not None:
        operands += (rest,)
        specs.append(tokens)
    return pl.pallas_call(
        partial(input_grad_kernel, len(grads)),
        grid=(2,),
        in_specs=specs,
        out_specs=tokens,
        out_shape=jax.ShapeDtypeStruct((length, share), BF),
        compiler_params=pltpu.CompilerParams(vmem_limit_bytes=60 * MIB),
    )(*operands)


def weight_grad_kernel(plan, width, z_ref, *refs):
    del z_ref
    out_ref, sums_ref = refs[-2:]
    sums_ref[...] = jnp.zeros_like(sums_ref)
    products = []
    index = 0
    row = 0
    for count in plan:
        left = refs[index][...]
        rights = [refs[index + 1 + i][0][:, :width] for i in range(count)]
        index += 1 + count
        for right in rights:
            sums_ref[row : row + 1, 0:width] = jnp.sum(right.astype(F32), axis=0, keepdims=True)
            row += 1
        products.append(dot_tn(left, rights[0] if count == 1 else jnp.concatenate(rights, axis=1)))
    out_ref[...] = jnp.concatenate(products, axis=1)


def weight_grad(z, width, *pairs):
    operands, specs = [], []
    for left, rights in pairs:
        operands.append(left)
        specs.append(pl.BlockSpec(left.shape, lambda i, z_ref: (0, 0)))
        for right in rights:
            operands.append(right)
            specs.append(pl.BlockSpec((1,) + right.shape[1:], lambda i, z_ref: (z_ref[0], 0, 0)))
    model = pairs[0][0].shape[1]
    plan = [len(rights) for _, rights in pairs]
    return pl.pallas_call(
        partial(weight_grad_kernel, plan, width),
        grid_spec=pltpu.PrefetchScalarGridSpec(
            num_scalar_prefetch=1,
            grid=(1,),
            in_specs=specs,
            out_specs=[
                pl.BlockSpec((model, sum(plan) * width), lambda i, z_ref: (0, 0)),
                pl.BlockSpec((8, model), lambda i, z_ref: (0, 0)),
            ],
        ),
        out_shape=[jax.ShapeDtypeStruct((model, sum(plan) * width), F32), jax.ShapeDtypeStruct((8, model), F32)],
        compiler_params=pltpu.CompilerParams(vmem_limit_bytes=60 * MIB),
    )(z.reshape(1), *operands)


def scattered(products):
    return lax.psum_scatter(products, "dp", scatter_dimension=0, tiled=True)


def finish_kernel(
    width, prod_f_ref, prod_c_ref, q_ref, k_ref, v_ref, gm_ref, sm_ref, gck_ref, gcv_ref, target_ref, grad_self_ref,
    logs_ref, dots_ref, t_ids_ref, columns_ref, rest_ref, sums_ref, cross_sums_ref, first_sums_ref,
    total_f_ref, total_c_ref, total_s_ref, vector_total_ref, target_grad_ref, memory_grad_ref,
    q_all, k_all, v_all, gm_all, sm_own, gck_all, gcv_all, target, grad_self, gq_all, gk_all, gv_all, gq_sum, logs, dots,
    mine_f, mine_c, prod_s, land_f, land_c, land_s, one_f, one_c, one_s, two_f, two_c, two_s, vec, vec_land, t_col_ref, t_row_ref,
    send_sem, recv_sem, load_sem,
):
    d = lax.axis_index("dp")
    z = lax.axis_index("tensor")
    c = d % 2
    x = (d // 2) % 2
    y = d // 4
    dc = d + 1 - 2 * c
    dx = d + 2 - 4 * x
    dy = d + 4 - 8 * y
    slices, length, _ = q_all.shape
    heads = 3

    def to(slot, source, place, other):
        return pltpu.make_async_remote_copy(
            src_ref=source,
            dst_ref=place,
            send_sem=send_sem.at[slot],
            recv_sem=recv_sem.at[slot],
            device_id={"dp": other},
            device_id_type=MESH,
        )

    families = (
        (prod_f_ref, mine_f, land_f, one_f, two_f, total_f_ref),
        (prod_c_ref, mine_c, land_c, one_c, two_c, total_c_ref),
        (prod_s, None, land_s, one_s, two_s, total_s_ref),
    )

    def over_core(i):
        return to(5 * i, families[i][0].at[:, :, 1 - c], families[i][2], dc)

    def halves(i):
        half = families[i][2].shape[3] // 2
        return pl.ds(0, half), pl.ds(half, half)

    def first_a(i):
        return to(5 * i + 1, families[i][2].at[:, 1 - x, :, halves(i)[0]], families[i][3].at[0], dx)

    def first_b(i):
        return to(5 * i + 2, families[i][2].at[1 - y, :, :, halves(i)[1]], families[i][3].at[1], dy)

    def second_a(i):
        return to(5 * i + 3, families[i][3].at[0, 1 - y], families[i][4].at[0], dy)

    def second_b(i):
        return to(5 * i + 4, families[i][3].at[1, 1 - x], families[i][4].at[1], dx)

    def after_core(i):
        _, mine, land, _, _, _ = families[i]
        over_core(i).wait_recv()

        @pl.loop(0, 4)
        def _(j):
            part = prod_s[j // 2, j % 2, c] if mine is None else mine[j // 2, j % 2]
            land[j // 2, j % 2] = land[j // 2, j % 2] + part

        first_a(i).start()
        first_b(i).start()

    def after_first(i):
        _, _, land, one, _, _ = families[i]
        first_a(i).wait_recv()
        first_b(i).wait_recv()
        left, right = halves(i)
        for j in range(2):
            one[0, j] = one[0, j] + land[j, x, :, left]
            one[1, j] = one[1, j] + land[y, j, :, right]
        second_a(i).start()
        second_b(i).start()

    def after_second(i):
        _, _, _, one, two, total_ref = families[i]
        second_a(i).wait_recv()
        second_b(i).wait_recv()
        left, right = halves(i)
        total_ref[:, left] = one[0, y] + two[0]
        total_ref[:, right] = one[1, x] + two[1]

    def vector_copy(i):
        return to(15 + i, vec.at[i], vec_land.at[i], (dc, dx, dy)[i])

    def vector_step(i):
        vector_copy(i).wait_recv()
        vec[i + 1] = vec[i] + vec_land[i]
        if i < 2:
            vector_copy(i + 1).start()

    barrier = pltpu.get_barrier_semaphore()
    for other in (dc, dx, dy):
        pl.semaphore_signal(barrier, inc=1, device_id={"dp": other}, device_id_type=MESH)

    def slice_loads(s):
        pairs = ((q_ref, q_all), (k_ref, k_all), (v_ref, v_all), (gm_ref, gm_all))
        return [
            pltpu.make_async_copy(source.at[s], place.at[s], load_sem.at[4 * s + i])
            for i, (source, place) in enumerate(pairs)
        ]

    late = 4 * slices
    late_loads = [
        pltpu.make_async_copy(sm_ref.at[z], sm_own, load_sem.at[late]),
        pltpu.make_async_copy(target_ref, target, load_sem.at[late + 1]),
        pltpu.make_async_copy(grad_self_ref, grad_self, load_sem.at[late + 2]),
        pltpu.make_async_copy(gck_ref, gck_all, load_sem.at[late + 3]),
        pltpu.make_async_copy(gcv_ref, gcv_all, load_sem.at[late + 4]),
    ]
    mine_loads = [
        pltpu.make_async_copy(prod_f_ref.at[:, :, c], mine_f, load_sem.at[late + 5]),
        pltpu.make_async_copy(prod_c_ref.at[:, :, c], mine_c, load_sem.at[late + 6]),
    ]
    for s in range(slices):
        for load in slice_loads(s):
            load.start()
    for load in mine_loads + late_loads:
        load.start()
    t_row_ref[...] = t_ids_ref[...].astype(F32)
    t_col_ref[...] = as_column(t_row_ref[...])
    logs[...] = jnp.transpose(logs_ref[...])
    dots[...] = jnp.transpose(dots_ref[...])
    pl.semaphore_wait(barrier, 3)
    over_core(0).start()
    over_core(1).start()

    vec[0] = jnp.zeros(vec.shape[1:], F32)
    for row, source, at in (
        (2, first_sums_ref, 2), (3, first_sums_ref, 0), (4, first_sums_ref, 1), (5, cross_sums_ref, 0),
        (6, cross_sums_ref, 2), (7, sums_ref, 5), (8, sums_ref, 3), (9, sums_ref, 4), (11, sums_ref, 2),
        (12, sums_ref, 0), (13, sums_ref, 1),
    ):
        vec[0, row : row + 1, :] = source[at : at + 1, :]
    vec[0, 10:11, :] = sums_ref[pl.ds(8 + z, 1), :]

    lane = lax.broadcasted_iota(jnp.int32, (1, 128), 1)
    scale = HEAD_DIM**-0.5
    block = 256

    def one_block(s, at):
        reach = length - at
        span = slice(at, at + block)
        allowed = (t_col_ref[span, :] == t_row_ref[:, at:]) & (
            lax.broadcasted_iota(jnp.int32, (block, reach), 0) <= lax.broadcasted_iota(jnp.int32, (block, reach), 1)
        )
        grads = []
        for h in range(heads):
            mine = (lane // HEAD_DIM) == (h % 2)
            columns = slice(128 * (h // 2), 128 * (h // 2) + 128)
            keys = k_all[s, span, columns]
            keys = jnp.where(mine, keys, jnp.zeros_like(keys))
            values = v_all[s, span, columns]
            values = jnp.where(mine, values, jnp.zeros_like(values))
            queries = q_all[s, at:, columns]
            gm = gm_all[s, at:, columns]
            scores = dot_nt(keys * jnp.asarray(scale, BF), queries)
            row = pl.ds(heads * s + h, 1)
            probs = jnp.where(allowed, jnp.exp(scores - logs[row, at:]), 0.0)
            grad_scores = (probs * (dot_nt(values, gm) - dots[row, at:])).astype(BF)
            grads.append((dot_nn(grad_scores, queries) * scale, dot_nn(probs.astype(BF), gm)))
            gq_sum[at:, columns] += dot_tn(grad_scores, keys)
        left = lane < HEAD_DIM
        for i, out in enumerate((gk_all, gv_all)):
            out[s, span, 0:128] = jnp.where(left, grads[0][i], grads[1][i]).astype(BF)
            out[s, span, 128:256] = jnp.where(left, grads[2][i], 0.0).astype(BF)

    for s in range(slices):
        for load in slice_loads(s):
            load.wait()

    @pl.loop(0, slices)
    def _(s):
        gq_sum[...] = jnp.zeros_like(gq_sum)
        for at in range(0, length, block):
            one_block(s, at)
        gq_all[s] = (gq_sum[...] * scale).astype(BF)

        @pl.when(s == 0)
        def _():
            for load in mine_loads:
                load.wait()
            after_core(0)
            after_core(1)

        @pl.when(s == slices - 1)
        def _():
            after_first(0)
            after_first(1)

    for load in late_loads:
        load.wait()
    right = jnp.concatenate((gq_all[z][:, :width], gk_all[z][:, :width], gv_all[z][:, :width]), axis=1)
    products = jnp.concatenate((dot_tn(target[...], right), dot_tn(grad_self[...], sm_own[:, :width])), axis=1)
    prod_s[...] = products.reshape(prod_s.shape)
    vec[0, 0:1, 0:width] = jnp.sum(gq_all[z][:, :width].astype(F32), axis=0, keepdims=True)
    vec[0, 1:2, 0:width] = jnp.sum(gv_all[z][:, :width].astype(F32), axis=0, keepdims=True)
    over_core(2).start()
    vector_copy(0).start()

    def input_grad(grads, first, rest, out_ref):
        @pl.loop(0, 4)
        def _(i):
            span = pl.ds(pl.multiple_of(i * (length // 4), length // 4), length // 4)
            total = 0.0
            for j, grad in enumerate(grads):
                for s in range(slices):
                    weight = columns_ref[s, (first + j) * width : (first + j + 1) * width, :]
                    total = total + dot_nn(grad[s, span, :width], weight)
            total = total[:, :width]
            if rest is not None:
                total = total + rest[span, :]
            out_ref[span, :] = total.astype(BF)

    after_core(2)
    vector_step(0)
    input_grad((gq_all, gk_all, gv_all), 0, rest_ref, target_grad_ref)
    after_first(2)
    vector_step(1)
    input_grad((gck_all, gcv_all), 3, None, memory_grad_ref)
    after_second(0)
    after_second(1)
    after_second(2)
    vector_step(2)
    vector_total_ref[...] = vec[3]
    for i in range(3):
        over_core(i).wait_send()
        for copy in (first_a(i), first_b(i), second_a(i), second_b(i)):
            copy.wait_send()
        vector_copy(i).wait_send()


def finish(prod_f, prod_c, heads, cross_grads, target, grad_self, logs, dots, ids, columns, rest, sums, cross_sums, first_sums):
    slices, length, wide = heads[0].shape
    model = target.shape[1]
    width = model // slices
    n = model // 8
    anywhere = pl.BlockSpec(memory_space=pl.ANY)
    inside = pl.BlockSpec(memory_space=pltpu.VMEM)
    columns_f, columns_c = prod_f.shape[1], prod_c.shape[1]

    def half(size):
        return pltpu.VMEM((2, 2, n, size), F32)

    sizes = (columns_f, columns_c, model)
    group = pltpu.VMEM((slices, length, wide), BF)
    tokens = pltpu.VMEM((length, model), BF)
    share = jax.ShapeDtypeStruct((length, model // slices), BF)
    return pl.pallas_call(
        partial(finish_kernel, width),
        out_shape=[jax.ShapeDtypeStruct((n, size), F32) for size in sizes]
        + [jax.ShapeDtypeStruct((16, model), F32), share, share],
        in_specs=[anywhere] * 11 + [inside] * 8,
        out_specs=[inside] * 6,
        scratch_shapes=[group] * 4
        + [pltpu.VMEM((length, wide), BF), group, group, tokens, tokens, group, group, group]
        + [pltpu.VMEM((length, wide), F32), pltpu.VMEM((128, length), F32), pltpu.VMEM((128, length), F32)]
        + [half(columns_f), half(columns_c), pltpu.VMEM((2, 2, 2, n, model), F32)]
        + [half(size) for size in sizes]
        + [pltpu.VMEM((2, 2, n, size // 2), F32) for size in sizes]
        + [pltpu.VMEM((2, n, size // 2), F32) for size in sizes]
        + [pltpu.VMEM((4, 16, model), F32), pltpu.VMEM((3, 16, model), F32), pltpu.VMEM((length, 1), F32), pltpu.VMEM((1, length), F32)]
        + [pltpu.SemaphoreType.DMA((18,)), pltpu.SemaphoreType.DMA((18,)), pltpu.SemaphoreType.DMA((4 * slices + 7,))],
        compiler_params=pltpu.CompilerParams(collective_id=1, has_side_effects=True, vmem_limit_bytes=63 * MIB),
    )(
        prod_f.reshape(2, 2, 2, n, columns_f), prod_c.reshape(2, 2, 2, n, columns_c), *heads, *cross_grads, target,
        grad_self, logs, dots, ids, columns, rest, sums, cross_sums, first_sums,
    )


def part_kernel(width, units, total_f_ref, total_c_ref, total_s_ref, vectors_ref, *outs):
    matrices, lines = outs[:10], outs[10:]
    for i, ref in enumerate((total_s_ref, total_c_ref)):
        for j in range(4):
            part = ref[:, j * width : (j + 1) * width]
            matrices[4 * i + j][...] = part
    matrices[8][...] = total_f_ref[:, :units]
    matrices[9][...] = total_f_ref[:, units:]
    for i, out in enumerate(lines):
        out[...] = vectors_ref[i, : out.shape[0]]


def parts_of(total_f, total_c, total_s, vectors, width, units):
    n, model = total_s.shape
    matrices = [(n, width)] * 8 + [(n, units)] * 2
    lines = [width, width, model, model, model, width, width] + [model] * 3 + [units] + [model] * 3
    out = pl.pallas_call(
        partial(part_kernel, width, units),
        out_shape=[jax.ShapeDtypeStruct(shape, F32) for shape in matrices]
        + [jax.ShapeDtypeStruct((size,), F32) for size in lines],
    )(total_f, total_c, total_s, vectors)
    return [x.T if i in (3, 7, 9) else x for i, x in enumerate(out[:10])], out[10:]


def per_device(
    n_dp, n_tensor, target, memory, target_segments, memory_segments, self_query, self_query_bias, self_key, self_value,
    self_value_bias, self_output, self_output_bias, first_gain, first_shift, cross_query, cross_query_bias, cross_key,
    cross_value, cross_value_bias, cross_output, cross_output_bias, second_gain, second_shift, expand_weight, expand_bias,
    contract_weight, contract_bias, third_gain, third_shift, output_grad,
):
    model, width = self_query.shape
    units = expand_weight.shape[1]
    head_rows = 8 * width
    z = lax.axis_index("tensor")
    target_ids = target_segments.reshape(1, -1)
    memory_ids = memory_segments.reshape(1, -1)

    own = (
        self_query, self_key, self_value, self_output, cross_key, cross_value, cross_query, cross_output, expand_weight,
        contract_weight,
    )

    def rows_of(count, vectors):
        return jnp.stack([jnp.pad(v, (0, model - v.shape[0])) for v in vectors] + [jnp.zeros(model, F32)] * (count - len(vectors)))

    biases = (self_query_bias, self_value_bias, cross_query_bias, cross_value_bias, expand_bias)
    vectors = (self_output_bias, first_gain, first_shift, cross_output_bias, second_gain, second_shift)
    run = forward if (n_dp, n_tensor) == (8, 4) else forward_plain
    columns, full, sq, sk, sv, sm, cq, ck, cv, cm, logs, hat1, hat2, spread, low1, low2, act, slope = run(
        own, biases, target, memory, target_ids, memory_ids, vectors, n_dp, n_tensor, head_rows, units
    )
    layer_output, grad_ffn, grad_hidden, grad_second_sum, grad_cross, gcm, cross_dots, sums = feed_back(
        act, slope, hat2, spread, output_grad, cm, full,
        (second_gain, second_shift, contract_bias, third_gain, third_shift), head_rows,
    )
    ffn_products = weight_grad(z, units, (low2, [grad_hidden]), (grad_ffn, [act]))[0]
    gcq, gck, gcv = attend_back(False, 3 * n_tensor, cq, ck, cv, gcm, logs, cross_dots, target_ids, memory_ids)
    cross_products, cross_sums = weight_grad(z, width, (low1, [gcq]), (memory, [gck, gcv]), (grad_cross, [cm]))
    rest, grad_self, gsm, self_dots, first_sums = first_back(
        z, gcq, grad_second_sum, hat1, spread, sm, full, first_gain, head_rows
    )
    if (n_dp, n_tensor) == (8, 4):
        total_f, total_c, total_s, vectors, target_grad, memory_grad = finish(
            ffn_products, cross_products, (sq, sk, sv, gsm, sm), (gck, gcv), target, grad_self, logs, self_dots, target_ids,
            columns, rest, sums, cross_sums, first_sums,
        )
    else:
        gsq, gsk, gsv = attend_back(True, 0, sq, sk, sv, gsm, logs, self_dots, target_ids, target_ids)
        self_products, self_sums = weight_grad(z, width, (target, [gsq, gsk, gsv]), (grad_self, [sm]))
        total_f, total_c, total_s = scattered(ffn_products), scattered(cross_products), scattered(self_products)
        memory_grad = input_grad((gck, gcv), columns[:, 3 * width :, :width])
        target_grad = input_grad((gsq, gsk, gsv), columns[:, : 3 * width, :width], rest)
        vectors = (
            self_sums[0], self_sums[2], first_sums[2], first_sums[0], first_sums[1], cross_sums[0], cross_sums[2], sums[5],
            sums[3], sums[4], lax.dynamic_index_in_dim(sums, 8 + z, 0, keepdims=False), sums[2], sums[0], sums[1],
        )
        vectors = lax.psum(rows_of(16, vectors), "dp")
    parts, totals = parts_of(total_f, total_c, total_s, vectors, width, units)
    return (
        layer_output, target_grad, memory_grad, parts[0], totals[0], parts[1], parts[2], totals[1], parts[3], totals[2],
        totals[3], totals[4], parts[4], totals[5], parts[5], parts[6], totals[6], parts[7], totals[7], totals[8], totals[9],
        parts[8], totals[10], parts[9], totals[11], totals[12], totals[13],
    )


def solution(mesh):
    rows = P("dp", None)
    split = P(None, "tensor")
    both = P("dp", "tensor")
    turned = P("tensor", "dp")
    own = P("tensor")
    in_specs = (
        rows, rows, rows, rows,
        split, own, split, split, own, P("tensor", None), P(), P(), P(),
        split, own, split, split, own, P("tensor", None), P(), P(), P(),
        split, own, P("tensor", None), P(), P(), P(),
        rows,
    )
    out_specs = (
        rows, both, both,
        both, own, both, both, own, turned, P(), P(), P(),
        both, own, both, both, own, turned, P(), P(), P(),
        both, own, turned, P(), P(), P(),
    )
    return jax.shard_map(
        partial(per_device, mesh.shape["dp"], mesh.shape["tensor"]),
        mesh=mesh,
        in_specs=in_specs,
        out_specs=out_specs,
        check_vma=False,
    )
```

```python
from functools import partial

import jax
import jax.numpy as jnp
from jax import lax
from jax.experimental import pallas as pl
from jax.experimental.pallas import tpu as pltpu
from jax.sharding import PartitionSpec as P

HEAD_DIM = 64
EPSILON = 1e-05
NEGATIVE = -1e30
BF = jnp.bfloat16
F32 = jnp.float32
MESH = pl.DeviceIdType.MESH
MIB = 2**20


def dot_nn(a, b):
    return lax.dot_general(a, b, (((1,), (0,)), ((), ())), preferred_element_type=F32)


def dot_nt(a, b):
    return lax.dot_general(a, b, (((1,), (1,)), ((), ())), preferred_element_type=F32)


def dot_tn(a, b):
    return lax.dot_general(a, b, (((0,), (0,)), ((), ())), preferred_element_type=F32)


WIDE = 256
TOKEN_BLOCK = 256


def as_column(row):
    return jnp.transpose(jnp.broadcast_to(row, (128, row.shape[1])))[:, 0:1]


def fill_rows(rows_ref, lines):
    rows_ref[...] = jnp.zeros_like(rows_ref)
    for i, line in enumerate(lines):
        rows_ref[i, 0 : line.shape[0]] = line[...]


def erf_pair(hidden):
    phi = 0.5 * (1.0 + lax.erf(hidden * 0.7071067811865476))
    slope = phi + hidden * (jnp.exp(-0.5 * hidden * hidden) * 0.3989422804014327)
    return hidden * phi, slope


def forward_kernel(
    n_dp, n_tensor, count, rows, head_rows, hidden_rows,
    sqw_ref, skw_ref, svw_ref, sow_ref, ckw_ref, cvw_ref, cqw_ref, cow_ref, exw_ref, ctw_ref, target_ref, memory_ref, t_ids_ref, m_ids_ref,
    b0_ref, b1_ref, b2_ref, b3_ref, b4_ref, v0_ref, v1_ref, v2_ref, v3_ref, v4_ref, v5_ref,
    chunk_ref, columns_ref, found_ref, full_ref, sq_ref, sk_ref, sv_ref, sm_ref, cq_ref, ck_ref, cv_ref, cm_ref, logs_ref, hat1_ref, hat2_ref,
    r_ref, low1_ref, low2_ref, act_ref, slope_ref,
    columns, vectors_ref, bias_ref, t_row_ref, m_row_ref, t_col_ref, stage, full, low, bias, q_all, k_all, v_all, mixed, logs, hat1, hat2, spread, low1, low2, act, slope,
    send_sem, recv_sem, bias_send, bias_recv, load_sem, store_sem, out_sem,
):
    d = lax.axis_index("dp")
    z = lax.axis_index("tensor")
    others = n_tensor - 1
    length, model = target_ref.shape
    size = n_dp * rows
    dc = d + 1 - 2 * (d % 2)
    dx = d + 2 - 4 * ((d // 2) % 2)
    dy = d + 4 - 8 * (d // 4)
    dxy = dx + 4 - 8 * (d // 4)

    def slice_of(k):
        return (z + others - k) % n_tensor

    def slice_at(j):
        return (z + n_tensor - j) % n_tensor

    def along_z(g, source, k, step, slot):
        return pltpu.make_async_remote_copy(
            src_ref=source,
            dst_ref=found_ref.at[d, k, pl.ds(g * rows, rows)],
            send_sem=send_sem.at[g, slot],
            recv_sem=recv_sem.at[g, k],
            device_id={"tensor": z + step},
            device_id_type=MESH,
        )

    near = ((1, 0, 0), (2, 1, 1), (-1, 2, 2), (-2, 1, 11))

    def own_along(g, step, k, slot):
        return along_z(g, chunk_ref.at[pl.ds(g * rows, rows)], k, step, slot)

    def reaches(step):
        return z + step <= others if step > 0 else z + step >= 0

    inner = jnp.logical_and(z > 0, z < others)

    def relay(g):
        step = 2 * z - 3
        return along_z(g, found_ref.at[d, 1, pl.ds(g * rows, rows)], 1 + step, step, 12)

    def from_z(g, k):
        own_along(g, 0, k, 0).wait_recv()

    lead = 2

    def own_z(g):
        for step_z, k, slot in near:

            @pl.when(reaches(step_z))
            def _(step_z=step_z, k=k, slot=slot):
                own_along(g, step_z, k, slot).start()

    def pass_z(g):
        @pl.when(inner)
        def _():
            from_z(g, 1)
            relay(g).start()

        if g + lead < count:
            own_z(g + lead)

    def in_plane(g, slot, chunk, half, other):
        span = pl.ds(g * rows, rows) if half is None else pl.ds(g * rows + half * (rows // 2), rows // 2)
        piece = found_ref.at[chunk, :, span]
        return pltpu.make_async_remote_copy(
            src_ref=piece,
            dst_ref=piece,
            send_sem=send_sem.at[g, slot],
            recv_sem=recv_sem.at[g, slot],
            device_id={"dp": other},
            device_id_type=MESH,
        )

    def bias_copy(k):
        return pltpu.make_async_remote_copy(
            src_ref=bias_ref,
            dst_ref=bias.at[z],
            send_sem=bias_send.at[k],
            recv_sem=bias_recv.at[k],
            device_id={"tensor": (z + k + 1) % n_tensor},
            device_id_type=MESH,
        )

    routes = {3: (d, None, dx), 4: (d, None, dy), 5: (d, None, dc), 6: (dx, 0, dy), 7: (dy, 1, dx)}
    routes.update({8 + i: (chunk, None, dc) for i, chunk in enumerate((dx, dy, dxy))})

    def send(g, slot):
        return in_plane(g, slot, *routes[slot])

    def arrive(g, slot, half=None):
        in_plane(g, slot, d, half, dc).wait_recv()

    def first_hop(g):
        from_z(g, 0)
        from_z(g, 2)

        @pl.when(jnp.logical_not(inner))
        def _():
            from_z(g, 1)

        for slot in (3, 4, 5):
            send(g, slot).start()

    def pass_on(g):
        arrive(g, 3)
        send(g, 6).start()
        send(g, 8).start()
        arrive(g, 4)
        send(g, 7).start()
        send(g, 9).start()

    def load_of(g, k):
        return pltpu.make_async_copy(found_ref.at[:, k, pl.ds(g * rows, rows)], stage.at[k], load_sem.at[k])

    def last_hop(g):
        arrive(g, 6, 0)
        arrive(g, 7, 1)
        send(g, 10).start()

    def landed(g):
        arrive(g, 5)
        for slot in (8, 9, 10):
            arrive(g, slot)
        for k in range(others):
            load_of(g, k).start()

    def home(g):
        kept = hidden_rows // size + head_rows // size
        return (full, pl.ds(g * size, size)) if g < kept else (low, pl.ds((g % 2) * size, size))

    def store_of(g, s):
        place, span = home(g)
        return pltpu.make_async_copy(place.at[s, span], full_ref.at[s, pl.ds(g * size, size)], store_sem.at[g, s])

    def rounded(g):
        place, span = home(g)
        @pl.loop(0, others)
        def _(k):
            load_of(g, k).wait()
            place[slice_of(k), span] = stage[k].reshape(size, model).astype(BF)

        for s in range(n_tensor):
            store_of(g, s).start()

    def pause(step, between):
        for at, *moves in between:

            @pl.when(step == at)
            def _(moves=moves):
                for move, g in moves:
                    move(g)

    def project(x_ref, s, first, bias_row, out_ref):
        @pl.loop(0, 2)
        def _(i):
            span = pl.ds(pl.multiple_of(i * (length // 2), length // 2), length // 2)
            value = dot_nt(x_ref[span, :], full[s, pl.ds(first, WIDE), :])
            if bias_row is not None:
                value = value + bias[s, bias_row : bias_row + 1, :WIDE]
            filled = lax.broadcasted_iota(jnp.int32, (1, WIDE), 1) < head_rows // 8
            out_ref[s, span, :] = jnp.where(filled, value, 0.0).astype(BF)

    def attend(first, number, causal, k_ids_ref, base, *between):
        half = length // 2
        lane = lax.broadcasted_iota(jnp.int32, (1, 128), 1)

        @pl.loop(3 * first, 3 * (first + number))
        def _(step):
            s = (z + n_tensor - step // 3) % n_tensor
            h = step % 3
            columns = pl.ds(pl.multiple_of((h // 2) * 128, 128), 128)
            mine = (lane // HEAD_DIM) == (h % 2)
            log_lane = lane == base + 3 * s + h
            for b in range(2):
                reach = (b + 1) * half if causal else length
                span = slice(b * half, (b + 1) * half)
                queries = q_all[s, span, columns] * jnp.asarray(HEAD_DIM**-0.5, BF)
                scores = dot_nt(jnp.where(mine, queries, jnp.zeros_like(queries)), k_all[s, :reach, columns])
                allowed = t_col_ref[span, :] == k_ids_ref[:, :reach]
                if causal:
                    allowed = allowed & (
                        lax.broadcasted_iota(jnp.int32, (half, reach), 0) + b * half
                        >= lax.broadcasted_iota(jnp.int32, (half, reach), 1)
                    )
                scores = jnp.where(allowed, scores, NEGATIVE)
                top = jnp.max(scores, axis=1, keepdims=True)
                weights = jnp.exp(scores - top)
                total = jnp.sum(weights, axis=1, keepdims=True)
                out = (dot_nn(weights.astype(BF), v_all[s, :reach, columns]) * (1.0 / total)).astype(BF)
                before = mixed[s, span, columns]
                before = jnp.where(h % 2 == 1, before, jnp.zeros_like(before))
                mixed[s, span, columns] = jnp.where(mine, out, before)
                logs[span, :] = jnp.where(log_lane, top + jnp.log(total), logs[span, :])
            pause(step, between)

    def close(first, bias_row, residual, hat, low_out, column):
        block = length // 4

        @pl.loop(0, 4)
        def _(i):
            span = pl.ds(pl.multiple_of(i * block, block), block)
            value = residual(span) + vectors_ref[bias_row : bias_row + 1, :]
            for s in range(n_tensor):
                value = value + dot_nn(mixed[s, span, :], full[s, pl.ds(first, WIDE), :])
            centered = value - jnp.mean(value, axis=1, keepdims=True)
            scale = lax.rsqrt(jnp.mean(centered * centered, axis=1, keepdims=True) + EPSILON)
            normed = centered * scale
            hat[span, :] = normed
            here = lax.broadcasted_iota(jnp.int32, (1, 128), 1) == column
            spread[span, :] = jnp.where(here, scale, spread[span, :])
            low_out[span, :] = (
                normed * vectors_ref[bias_row + 1 : bias_row + 2, :] + vectors_ref[bias_row + 2 : bias_row + 3, :]
            ).astype(BF)

    def expand(s, slot):
        @pl.loop(0, 4)
        def _(i):
            span = pl.ds(pl.multiple_of(i * (length // 4), length // 4), length // 4)
            hidden = dot_nt(low2[span, :], full[s, pl.ds(head_rows, hidden_rows), :]) + bias[s, 4:5, :]
            value, change = erf_pair(hidden)
            act[slot, span, :] = value.astype(BF)
            slope[slot, span, :] = change.astype(BF)

    def own_columns(s):
        for i, first in enumerate((q0, k0, v0, ck0, cv0)):
            value = full[s, pl.ds(first, step), :].astype(F32)
            columns[s, pl.ds(i * step, step), :] = pltpu.roll(value, model - z * step, 1)[:, :WIDE].astype(BF)

    def out_copy(i, source, target):
        return pltpu.make_async_copy(source, target, out_sem.at[i])

    def expand_out(s, slot):
        return (
            out_copy(13 + 2 * slot, act.at[slot], act_ref.at[s]),
            out_copy(14 + 2 * slot, slope.at[slot], slope_ref.at[s]),
        )

    barrier = pltpu.get_barrier_semaphore()
    for k in range(1, n_tensor):
        pl.semaphore_signal(barrier, inc=1, device_id={"tensor": (z + k) % n_tensor}, device_id_type=MESH)
    for other in (dc, dx, dy):
        pl.semaphore_signal(barrier, inc=1, device_id={"dp": other}, device_id_type=MESH)
    step = head_rows // 8
    q0, k0, v0, o0, ck0, cv0, cq0, co0 = (i * step for i in range(8))
    own_loads = [
        pltpu.make_async_copy(source, place, load_sem.at[3 + i])
        for i, (source, place) in enumerate(
            (
                (sqw_ref, full.at[z, pl.ds(q0, step)]),
                (skw_ref, full.at[z, pl.ds(k0, step)]),
                (svw_ref, full.at[z, pl.ds(v0, step)]),
                (ckw_ref, full.at[z, pl.ds(ck0, step)]),
                (cvw_ref, full.at[z, pl.ds(cv0, step)]),
                (cqw_ref, full.at[z, pl.ds(cq0, step)]),
                (sow_ref, full.at[z, pl.ds(o0, step)]),
                (cow_ref, full.at[z, pl.ds(co0, step)]),
                (exw_ref, act.at[0, pl.ds(0, model)]),
                (ctw_ref, low.at[z]),
            )
        )
    ]
    for load in own_loads:
        load.start()
    t_row_ref[...] = t_ids_ref[...].astype(F32)
    m_row_ref[...] = m_ids_ref[...].astype(F32)
    t_col_ref[...] = as_column(t_row_ref[...])
    fill_rows(bias_ref, (b0_ref, b1_ref, b2_ref, b3_ref, b4_ref))
    fill_rows(vectors_ref, (v0_ref, v1_ref, v2_ref, v3_ref, v4_ref, v5_ref))
    bias[z] = bias_ref[...]
    pl.semaphore_wait(barrier, others + 3)
    for k in range(others):
        bias_copy(k).start()
    def chunk_copy(g):
        return pltpu.make_async_copy(stage.at[0, g], chunk_ref.at[pl.ds(g * rows, rows)], load_sem.at[g % 3])

    def offer(g):
        place, span = home(g)
        first = span.start + d * rows
        stage[0, g] = place[z, pl.ds(pl.multiple_of(first, 16), rows), :].astype(F32)
        chunk_copy(g).start()

    def give(g):
        chunk_copy(g).wait()
        if g < lead:
            own_z(g)

    own_loads[0].wait()
    own_loads[1].wait()
    offer(0)
    own_loads[2].wait()
    own_loads[6].wait()
    give(0)
    offer(1)
    own_loads[3].wait()
    own_loads[4].wait()
    give(1)
    offer(2)
    own_loads[5].wait()
    own_loads[7].wait()
    give(2)
    offer(3)
    own_loads[8].wait()
    full[z, pl.ds(head_rows, hidden_rows), :] = jnp.transpose(act[0, :model, :].astype(F32)).astype(BF)
    offer(4)
    give(3)
    offer(5)
    own_loads[9].wait()
    give(4)
    offer(6)
    give(5)
    offer(7)
    give(6)
    give(7)

    logs[...] = jnp.zeros_like(logs)
    spread[...] = jnp.zeros_like(spread)
    project(target_ref, z, q0, 0, q_all)
    project(target_ref, z, k0, None, k_all)
    project(target_ref, z, v0, 1, v_all)
    attend(0, 1, True, t_row_ref, 0)
    for k in range(others):
        bias_copy(k).wait_recv()
    pass_z(0)
    first_hop(0)
    pass_z(1)
    first_hop(1)
    pass_on(0)
    pass_z(2)
    first_hop(2)
    pass_on(1)
    pass_z(3)
    last_hop(0)
    landed(0)
    first_hop(3)
    rounded(0)
    @pl.loop(0, others)
    def _(k):
        project(target_ref, slice_of(k), q0, 0, q_all)
        project(target_ref, slice_of(k), k0, None, k_all)

    pass_z(4)
    pass_on(2)
    last_hop(1)
    first_hop(4)
    landed(1)
    pass_z(5)
    rounded(1)
    @pl.loop(0, others)
    def _(k):
        project(target_ref, slice_of(k), v0, 1, v_all)

    attend(
        1, 3, True, t_row_ref, 0, (3, (last_hop, 2)), (4, (pass_on, 3), (first_hop, 5)), (6, (landed, 2)), (7, (pass_z, 6)),
        (8, (rounded, 2)), (9, (last_hop, 3), (pass_on, 4)), (10, (first_hop, 6)),
    )
    pass_z(7)
    self_out = [
        out_copy(0, q_all, sq_ref), out_copy(1, k_all, sk_ref), out_copy(2, v_all, sv_ref), out_copy(3, mixed, sm_ref)
    ]
    for copy in self_out:
        copy.start()
    close(o0, 0, lambda span: target_ref[span, :].astype(F32), hat1, low1, 0)
    landed(3)
    out_copy(4, hat1, hat1_ref).start()
    out_copy(5, low1, low1_ref).start()
    for copy in self_out:
        copy.wait()

    @pl.loop(0, n_tensor)
    def _(s):
        project(memory_ref, s, ck0, None, k_all)
        project(memory_ref, s, cv0, 3, v_all)

    pass_on(5)
    first_hop(7)
    project(low1, z, cq0, 2, q_all)

    def rest_of_queries(g):
        rounded(g)

        @pl.loop(0, others)
        def _(k):
            project(low1, slice_of(k), cq0, 2, q_all)

    def shares(g):
        @pl.loop(0, n_tensor)
        def _(s):
            own_columns(s)

        out_copy(10, columns, columns_ref).start()
        rounded(g)

    attend(
        0, 4, False, m_row_ref, 3 * n_tensor, (1, (last_hop, 4)), (2, (rest_of_queries, 3), (landed, 4)), (3, (pass_on, 6)),
        (4, (last_hop, 5)), (5, (rounded, 4)), (6, (landed, 5)), (7, (pass_on, 7)), (8, (shares, 5)), (9, (last_hop, 6)),
        (11, (last_hop, 7)),
    )
    cross_out = [
        out_copy(0, q_all, cq_ref), out_copy(1, k_all, ck_ref), out_copy(2, v_all, cv_ref), out_copy(3, mixed, cm_ref),
        out_copy(6, logs, logs_ref),
    ]
    for copy in cross_out:
        copy.start()
    close(co0, 3, lambda span: hat1[span, :] * vectors_ref[1:2, :] + vectors_ref[2:3, :], hat2, low2, 1)
    out_copy(7, hat2, hat2_ref).start()
    out_copy(8, low2, low2_ref).start()
    out_copy(9, spread, r_ref).start()
    landed(6)

    @pl.loop(0, n_tensor)
    def _(j):
        @pl.when(j >= 2)
        def _():
            for copy in expand_out(slice_at(j - 2), j % 2):
                copy.wait()

        @pl.when(j == 1)
        def _():
            rounded(6)
            landed(7)

        @pl.when(j == 2)
        def _():
            rounded(7)

        expand(slice_at(j), j % 2)
        for copy in expand_out(slice_at(j), j % 2):
            copy.start()

    for copy in expand_out(slice_at(2), 0) + expand_out(slice_at(3), 1) + tuple(cross_out):
        copy.wait()
    for i, source, target in ((4, hat1, hat1_ref), (5, low1, low1_ref), (7, hat2, hat2_ref), (8, low2, low2_ref)):
        out_copy(i, source, target).wait()
    out_copy(9, spread, r_ref).wait()
    out_copy(10, columns, columns_ref).wait()
    for g in range(count):
        for s in range(n_tensor):
            store_of(g, s).wait()
    for k in range(others):
        bias_copy(k).wait_send()
    for g in range(count):
        for step_z, k, slot in near:

            @pl.when(reaches(step_z))
            def _(g=g, step_z=step_z, k=k, slot=slot):
                own_along(g, step_z, k, slot).wait_send()

        @pl.when(inner)
        def _(g=g):
            relay(g).wait_send()

        for slot in routes:
            send(g, slot).wait_send()


def forward(own, biases, target, memory, target_ids, memory_ids, vectors, n_dp, n_tensor, head_rows, hidden_rows):
    length, model = target.shape
    count = 8
    total = head_rows + 2 * hidden_rows
    size = total // count
    rows = size // n_dp
    step = head_rows // 8
    anywhere = pl.BlockSpec(memory_space=pl.ANY)
    inside = pl.BlockSpec(memory_space=pltpu.VMEM)
    heads = jax.ShapeDtypeStruct((n_tensor, length, WIDE), BF)
    tokens = jax.ShapeDtypeStruct((length, model), F32)
    tokens_low = jax.ShapeDtypeStruct((length, model), BF)
    lanes = jax.ShapeDtypeStruct((length, 128), F32)
    units = jax.ShapeDtypeStruct((n_tensor, length, hidden_rows), BF)
    out_shape = (
        jax.ShapeDtypeStruct((count * rows, model), F32),
        jax.ShapeDtypeStruct((n_tensor, 5 * step, WIDE), BF),
        jax.ShapeDtypeStruct((n_dp, n_tensor - 1, count * rows, model), F32),
        jax.ShapeDtypeStruct((n_tensor, total, model), BF),
        heads, heads, heads, heads, heads, heads, heads, heads,
        lanes, tokens, tokens, lanes, tokens_low, tokens_low, units, units,
    )
    flops = 2 * length * model * (2 * n_tensor * head_rows) + 4 * length * model * n_tensor * hidden_rows
    outs = pl.pallas_call(
        partial(forward_kernel, n_dp, n_tensor, count, rows, head_rows, hidden_rows),
        out_shape=out_shape,
        in_specs=[anywhere] * 10 + [inside] * 15,
        out_specs=[anywhere] * len(out_shape),
        scratch_shapes=[
            pltpu.VMEM((n_tensor, 5 * step, WIDE), BF),
            pltpu.VMEM((8, model), F32),
            pltpu.VMEM((8, model), F32),
            pltpu.VMEM((1, length), F32),
            pltpu.VMEM((1, length), F32),
            pltpu.VMEM((length, 1), F32),
            pltpu.VMEM((n_tensor - 1, n_dp, rows, model), F32),
            pltpu.VMEM((n_tensor, head_rows + hidden_rows, model), BF),
            pltpu.VMEM((n_tensor, hidden_rows, model), BF),
            pltpu.VMEM((n_tensor, 8, model), F32),
            pltpu.VMEM(heads.shape, BF),
            pltpu.VMEM(heads.shape, BF),
            pltpu.VMEM(heads.shape, BF),
            pltpu.VMEM(heads.shape, BF),
            pltpu.VMEM(lanes.shape, F32),
            pltpu.VMEM(tokens.shape, F32),
            pltpu.VMEM(tokens.shape, F32),
            pltpu.VMEM(lanes.shape, F32),
            pltpu.VMEM(tokens.shape, BF),
            pltpu.VMEM(tokens.shape, BF),
            pltpu.VMEM((2, length, hidden_rows), BF),
            pltpu.VMEM((2, length, hidden_rows), BF),
            pltpu.SemaphoreType.DMA((count, 13)),
            pltpu.SemaphoreType.DMA((count, 11)),
            pltpu.SemaphoreType.DMA((n_tensor - 1,)),
            pltpu.SemaphoreType.DMA((n_tensor - 1,)),
            pltpu.SemaphoreType.DMA((13,)),
            pltpu.SemaphoreType.DMA((count, n_tensor)),
            pltpu.SemaphoreType.DMA((17,)),
        ],
        cost_estimate=pl.CostEstimate(flops=flops, bytes_accessed=60 * MIB, transcendentals=0),
        compiler_params=pltpu.CompilerParams(collective_id=0, has_side_effects=True, vmem_limit_bytes=63 * MIB),
    )(
        *(x.T if x.shape[0] > x.shape[1] else x for x in own), target, memory, target_ids, memory_ids, *biases, *vectors
    )
    return outs[1], *outs[3:]


def round_kernel(wide_ref, low_ref):
    low_ref[...] = wide_ref[...].astype(BF)


def rounded_copy(array):
    slices, rows, width = array.shape
    block = pl.BlockSpec((1, rows // 4, width), lambda i, j: (i, j, 0))
    return pl.pallas_call(
        round_kernel,
        grid=(slices, 4),
        in_specs=[block],
        out_specs=block,
        out_shape=jax.ShapeDtypeStruct(array.shape, BF),
    )(array)


def forward_plain(own, biases, target, memory, target_ids, memory_ids, vectors, n_dp, n_tensor, head_rows, hidden_rows):
    length, model = target.shape
    width = head_rows // 8
    sq, sk, sv, so, ck, cv, cq, co, expand, contract = own
    own = jnp.concatenate((sq.T, sk.T, sv.T, so, ck.T, cv.T, cq.T, co, expand.T, contract), axis=0)
    full = rounded_copy(lax.all_gather(own.astype(F32), "tensor", axis=0))
    bias = lax.all_gather(jnp.stack([jnp.pad(b, (0, model - b.shape[0])) for b in biases]), "tensor", axis=0)
    target_ids, memory_ids = target_ids.reshape(-1), memory_ids.reshape(-1)

    def weight(i):
        return full[:, i * width : (i + 1) * width]

    def padded(x):
        return jnp.pad(x, ((0, 0), (0, 0), (0, WIDE - width)))

    def project(x, i, row=None):
        value = jnp.einsum("td,swd->stw", x, weight(i), preferred_element_type=F32)
        if row is not None:
            value = value + bias[:, row, None, :width]
        return value.astype(BF)

    def attend(queries, keys, values, key_ids, causal):
        def split(x):
            return x.reshape(n_tensor, length, -1, HEAD_DIM)

        def one(items):
            q, k, v = items
            scores = jnp.einsum("qhd,khd->hqk", q, k, preferred_element_type=F32) * HEAD_DIM**-0.5
            allowed = target_ids[:, None] == key_ids[None, :]
            if causal:
                at = jnp.arange(length, dtype=jnp.int32)
                allowed = allowed & (at[:, None] >= at[None, :])
            scores = jnp.where(allowed[None], scores, NEGATIVE)
            probs = jax.nn.softmax(scores, axis=-1).astype(BF)
            out = jnp.einsum("hqk,khd->qhd", probs, v, preferred_element_type=F32)
            return out.astype(BF), jax.nn.logsumexp(scores, axis=-1)

        mixed, logs = lax.map(one, (split(queries), split(keys), split(values)))
        return mixed.reshape(n_tensor, length, width), logs.reshape(-1, length)

    def close(mixed, i, residual, row):
        value = residual + vectors[row] + jnp.einsum("stw,swd->td", mixed, weight(i), preferred_element_type=F32)
        centered = value - jnp.mean(value, axis=1, keepdims=True)
        scale = lax.rsqrt(jnp.mean(centered * centered, axis=1, keepdims=True) + EPSILON)
        hat = centered * scale
        normed = hat * vectors[row + 1] + vectors[row + 2]
        return hat, scale, normed, normed.astype(BF)

    sq, sk, sv = project(target, 0, 0), project(target, 1), project(target, 2, 1)
    sm, self_logs = attend(sq, sk, sv, target_ids, True)
    hat1, r1, first, low1 = close(sm, 3, target.astype(F32), 0)
    ck, cv, cq = project(memory, 4), project(memory, 5, 3), project(low1, 6, 2)
    cm, cross_logs = attend(cq, ck, cv, memory_ids, False)
    hat2, r2, _, low2 = close(cm, 7, first, 3)
    hidden = jnp.einsum("td,shd->sth", low2, full[:, head_rows : head_rows + hidden_rows], preferred_element_type=F32)
    act, slope = erf_pair(hidden + bias[:, 4, None, :])
    logs = jnp.concatenate((self_logs, cross_logs), axis=0).T
    logs = jnp.pad(logs, ((0, 0), (0, 128 - logs.shape[1])))
    spread = jnp.pad(jnp.concatenate((r1, r2), axis=1), ((0, 0), (0, 126)))
    heads = [padded(x) for x in (sq, sk, sv, sm, cq, ck, cv, cm)]
    kept = jnp.concatenate((full[:, : 3 * width], full[:, 4 * width : 6 * width]), axis=1)
    columns = padded(lax.dynamic_slice_in_dim(kept, lax.axis_index("tensor") * width, width, 2))
    return columns, full, *heads, logs, hat1, hat2, spread, low1, low2, act.astype(BF), slope.astype(BF)


def attend_back_kernel(
    heads, base, block, causal, q_ref, k_ref, v_ref, gm_ref, logs_ref, dots_ref, q_row_ref, k_row_ref, gq_ref, gk_ref,
    gv_ref, gq_sum, logs, dots, k_ids_ref, q_ids_ref, bounds
):
    length = q_ref.shape[1]
    lane = lax.broadcasted_iota(jnp.int32, (1, 128), 1)
    scale = HEAD_DIM**-0.5
    s = pl.program_id(0)

    @pl.when(s == 0)
    def _():
        logs[...] = jnp.transpose(logs_ref[...])
        dots[...] = jnp.transpose(dots_ref[...])
        k_ids_ref[...] = as_column(k_row_ref[...].astype(F32))
        q_ids_ref[...] = q_row_ref[...].astype(F32)
        if not causal:
            for b in range(length // block):
                ids = k_row_ref[:, b * block : (b + 1) * block]
                low = jnp.sum((q_row_ref[...] < jnp.min(ids)).astype(jnp.int32)) // block
                high = (jnp.sum((q_row_ref[...] <= jnp.max(ids)).astype(jnp.int32)) + block - 1) // block
                bounds[0, b] = low
                bounds[1, b] = high - low

    gq_sum[...] = jnp.zeros_like(gq_sum)

    def one_block(at, first, reach):
        k_span = pl.ds(at, block)
        q_span = pl.ds(first, reach)
        allowed = k_ids_ref[k_span, :] == q_ids_ref[:, q_span]
        if causal:
            allowed = allowed & (
                lax.broadcasted_iota(jnp.int32, (block, reach), 0) <= lax.broadcasted_iota(jnp.int32, (block, reach), 1)
            )
        grads = []
        for h in range(heads):
            mine = (lane // HEAD_DIM) == (h % 2)
            columns = slice(128 * (h // 2), 128 * (h // 2) + 128)
            keys = k_ref[0, k_span, columns]
            keys = jnp.where(mine, keys, jnp.zeros_like(keys))
            values = v_ref[0, k_span, columns]
            values = jnp.where(mine, values, jnp.zeros_like(values))
            queries = q_ref[0, q_span, columns]
            gm = gm_ref[0, q_span, columns]
            scores = dot_nt(keys * jnp.asarray(scale, BF), queries)
            probs = jnp.where(allowed, jnp.exp(scores - logs[pl.ds(base + heads * s + h, 1), q_span]), 0.0)
            grad_scores = (probs * (dot_nt(values, gm) - dots[pl.ds(heads * s + h, 1), q_span])).astype(BF)
            grads.append((dot_nn(grad_scores, queries) * scale, dot_nn(probs.astype(BF), gm)))
            gq_sum[q_span, columns] += dot_tn(grad_scores, keys)
        left = lane < HEAD_DIM
        for i, out_ref in enumerate((gk_ref, gv_ref)):
            out_ref[0, k_span, 0:128] = jnp.where(left, grads[0][i], grads[1][i]).astype(BF)
            out_ref[0, k_span, 128:256] = jnp.where(left, grads[2][i], 0.0).astype(BF)

    if causal:
        for b in range(length // block):
            one_block(b * block, b * block, length - b * block)
    else:

        @pl.loop(0, length // block)
        def _(b):
            start = pl.multiple_of(bounds[0, b] * block, block)
            for number in range(1, length // block + 1):

                @pl.when(bounds[1, b] == number)
                def _(number=number):
                    one_block(pl.multiple_of(b * block, block), start, number * block)

    gq_ref[0] = (gq_sum[...] * scale).astype(BF)


def attend_back(causal, base, queries, keys, values, grad_mixed, logs, dots, query_ids, key_ids):
    slices, length, wide = queries.shape
    part = pl.BlockSpec((1, length, wide), lambda i: (i, 0, 0))
    out = jax.ShapeDtypeStruct((slices, length, wide), BF)
    lanes = pl.BlockSpec((length, 128), lambda i: (0, 0))
    return pl.pallas_call(
        partial(attend_back_kernel, 3, base, 256, causal),
        grid=(slices,),
        in_specs=[part] * 4
        + [lanes, lanes, pl.BlockSpec((1, length), lambda i: (0, 0)), pl.BlockSpec((1, length), lambda i: (0, 0))],
        out_specs=[part] * 3,
        out_shape=[out] * 3,
        scratch_shapes=[
            pltpu.VMEM((length, wide), F32),
            pltpu.VMEM((128, length), F32),
            pltpu.VMEM((128, length), F32),
            pltpu.VMEM((length, 1), F32),
            pltpu.VMEM((1, length), F32),
            pltpu.SMEM((2, 8), jnp.int32),
        ],
        compiler_params=pltpu.CompilerParams(vmem_limit_bytes=60 * MIB),
    )(queries, keys, values, grad_mixed, logs, dots, query_ids, key_ids)


def norm_back(grad, hat, scale, gain):
    scaled = grad * gain
    return scale * (
        scaled - jnp.mean(scaled, axis=1, keepdims=True) - hat * jnp.mean(scaled * hat, axis=1, keepdims=True)
    )


def clear_first(sums_ref):
    @pl.when(pl.program_id(0) == 0)
    def _():
        sums_ref[...] = jnp.zeros_like(sums_ref)


def add_sums(sums_ref, rows):
    for row, value in rows:
        sums_ref[row : row + 1, :] += jnp.sum(value, axis=0, keepdims=True)


def head_products(grad_mixed, mixed, s, heads, dots):
    product = grad_mixed * mixed.astype(F32)
    lane = lax.broadcasted_iota(jnp.int32, (1, WIDE), 1)
    out_lane = lax.broadcasted_iota(jnp.int32, (1, 128), 1)
    for h in range(heads):
        total = jnp.sum(jnp.where(lane // HEAD_DIM == h, product, 0.0), axis=1, keepdims=True)
        dots = jnp.where(out_lane == heads * s + h, total, dots)
    return dots


def mixed_back(grad_low, out_weight, mixed_ref, gm_ref, dots_ref):
    slices = mixed_ref.shape[0]
    width = out_weight.shape[1]
    dots = jnp.zeros(dots_ref.shape, F32)
    for s in range(slices):
        grad_mixed = dot_nt(grad_low, out_weight[s]).astype(BF)
        grad_mixed = jnp.concatenate((grad_mixed, jnp.zeros((grad_mixed.shape[0], WIDE - width), BF)), axis=1)
        gm_ref[s] = grad_mixed
        dots = head_products(grad_mixed.astype(F32), mixed_ref[s], s, 3, dots)
    dots_ref[...] = dots


def feed_back_kernel(
    act_ref, slope_ref, hat2_ref, r_ref, grad_ref, mixed_ref, expand_ref, contract_ref, out_weight_ref,
    v0_ref, v1_ref, v2_ref, v3_ref, v4_ref, out_ref, grad_ffn_ref, grad_hidden_ref, grad_sum_ref, grad_cross_ref, gm_ref, dots_ref, sums_ref,
    vectors_ref
):
    slices = act_ref.shape[0]
    fill_rows(vectors_ref, (v0_ref, v1_ref, v2_ref, v3_ref, v4_ref))
    clear_first(sums_ref)
    vector = [vectors_ref[i : i + 1, :] for i in range(5)]
    hat2 = hat2_ref[...]
    value = hat2 * vector[0] + vector[1] + vector[2]
    for s in range(slices):
        value = value + dot_nn(act_ref[s], contract_ref[s])
    centered = value - jnp.mean(value, axis=1, keepdims=True)
    scale = lax.rsqrt(jnp.mean(centered * centered, axis=1, keepdims=True) + EPSILON)
    hat3 = centered * scale
    out_ref[...] = (hat3 * vector[3] + vector[4]).astype(BF)
    grad = grad_ref[...].astype(F32)
    grad_third = norm_back(grad, hat3, scale, vector[3])
    grad_ffn = grad_third.astype(BF)
    grad_ffn_ref[...] = grad_ffn
    grad_second = grad_third
    rows = [(0, grad * hat3), (1, grad), (2, grad_ffn.astype(F32))]
    for s in range(slices):
        grad_hidden = (dot_nt(grad_ffn, contract_ref[s]) * slope_ref[s].astype(F32)).astype(BF)
        grad_hidden_ref[s] = grad_hidden
        rows.append((8 + s, grad_hidden.astype(F32)))
        grad_second = grad_second + dot_nn(grad_hidden, expand_ref[s])
    grad_sum = norm_back(grad_second, hat2, r_ref[:, 1:2], vector[0])
    grad_sum_ref[...] = grad_sum
    grad_cross = grad_sum.astype(BF)
    grad_cross_ref[...] = grad_cross
    rows += [(3, grad_second * hat2), (4, grad_second), (5, grad_cross.astype(F32))]
    add_sums(sums_ref, rows)
    mixed_back(grad_cross, out_weight_ref, mixed_ref, gm_ref, dots_ref)


def feed_back(act, slope, hat2, spread, output_grad, mixed, full, vectors, head_rows):
    slices, length, units = act.shape
    model = hat2.shape[1]
    block = TOKEN_BLOCK
    width = head_rows // 8
    tokens = pl.BlockSpec((block, model), lambda i: (i, 0))
    lanes = pl.BlockSpec((block, 128), lambda i: (i, 0))
    wide = pl.BlockSpec((slices, block, units), lambda i: (0, i, 0))
    heads = pl.BlockSpec((slices, block, WIDE), lambda i: (0, i, 0))
    rows = pl.BlockSpec((16, model), lambda i: (0, 0))

    def weight(first, size):
        return pl.BlockSpec((slices, size, model), lambda i: (0, first // size, 0))

    low = jax.ShapeDtypeStruct((length, model), BF)
    return pl.pallas_call(
        feed_back_kernel,
        grid=(length // block,),
        in_specs=[wide, wide, tokens, lanes, tokens, heads]
        + [weight(head_rows, units), weight(head_rows + units, units), weight(7 * width, width)]
        + [pl.BlockSpec((model,), lambda i: (0,))] * 5,
        scratch_shapes=[pltpu.VMEM((8, model), F32)],
        out_specs=[tokens, tokens, wide, tokens, tokens, heads, lanes, rows],
        out_shape=[
            low,
            low,
            jax.ShapeDtypeStruct(act.shape, BF),
            jax.ShapeDtypeStruct((length, model), F32),
            low,
            jax.ShapeDtypeStruct((slices, length, WIDE), BF),
            jax.ShapeDtypeStruct((length, 128), F32),
            jax.ShapeDtypeStruct((16, model), F32),
        ],
        compiler_params=pltpu.CompilerParams(vmem_limit_bytes=62 * MIB),
    )(act, slope, hat2, spread, output_grad, mixed, full, full, full, *vectors)


def first_back_kernel(
    z_ref, gq_ref, grad_sum_ref, hat1_ref, r_ref, mixed_ref, query_ref, out_weight_ref, gain_ref,
    rest_ref, grad_self_ref, gm_ref, dots_ref, sums_ref, vectors_ref
):
    fill_rows(vectors_ref, (gain_ref,))
    clear_first(sums_ref)
    slices = gq_ref.shape[0]
    width = query_ref.shape[1]
    grad = grad_sum_ref[...]
    for s in range(slices):
        grad = grad + dot_nn(gq_ref[s][:, :width], query_ref[s])
    hat = hat1_ref[...]
    grad_first = norm_back(grad, hat, r_ref[:, 0:1], vectors_ref[0:1, :])
    rest_ref[...] = pltpu.roll(grad_first, grad_first.shape[1] - z_ref[0] * width, 1)[:, :width]
    grad_self = grad_first.astype(BF)
    grad_self_ref[...] = grad_self
    add_sums(sums_ref, [(0, grad * hat), (1, grad), (2, grad_self.astype(F32))])
    mixed_back(grad_self, out_weight_ref, mixed_ref, gm_ref, dots_ref)


def first_back(z, gq, grad_sum, hat1, spread, mixed, full, vectors, head_rows):
    slices, length, _ = gq.shape
    model = hat1.shape[1]
    block = TOKEN_BLOCK
    width = head_rows // 8
    tokens = pl.BlockSpec((block, model), lambda i, _: (i, 0))
    lanes = pl.BlockSpec((block, 128), lambda i, _: (i, 0))
    share = pl.BlockSpec((block, width), lambda i, _: (i, 0))
    heads = pl.BlockSpec((slices, block, WIDE), lambda i, _: (0, i, 0))
    rows = pl.BlockSpec((8, model), lambda i, _: (0, 0))
    return pl.pallas_call(
        first_back_kernel,
        grid_spec=pltpu.PrefetchScalarGridSpec(
            num_scalar_prefetch=1,
            grid=(length // block,),
            in_specs=[heads, tokens, tokens, lanes, heads]
            + [pl.BlockSpec((slices, width, model), lambda i, _, j=j: (0, j, 0)) for j in (6, 3)]
            + [pl.BlockSpec((model,), lambda i, _: (0,))],
            scratch_shapes=[pltpu.VMEM((8, model), F32)],
            out_specs=[share, tokens, heads, lanes, rows],
        ),
        out_shape=[
            jax.ShapeDtypeStruct((length, width), F32),
            jax.ShapeDtypeStruct((length, model), BF),
            jax.ShapeDtypeStruct((slices, length, WIDE), BF),
            jax.ShapeDtypeStruct((length, 128), F32),
            jax.ShapeDtypeStruct((8, model), F32),
        ],
        compiler_params=pltpu.CompilerParams(vmem_limit_bytes=62 * MIB),
    )(z.reshape(1), gq, grad_sum, hat1, spread, mixed, full, full, vectors)


def input_grad_kernel(count, *refs):
    out_ref = refs[-1]
    weight_ref = refs[count]
    slices = refs[0].shape[0]
    width = weight_ref.shape[1] // count
    total = refs[count + 1][...] if len(refs) == count + 3 else jnp.zeros(out_ref.shape, F32)
    for i in range(count):
        for s in range(slices):
            total = total + dot_nn(refs[i][s][:, :width], weight_ref[s, i * width : (i + 1) * width, :])
    out_ref[...] = total.astype(BF)


def input_grad(grads, weights, rest=None):
    slices, length, wide = grads[0].shape
    share = weights.shape[2]
    block = length // 2
    tokens = pl.BlockSpec((block, share), lambda i: (i, 0))
    specs = [pl.BlockSpec((slices, block, wide), lambda i: (0, i, 0))] * len(grads)
    specs.append(pl.BlockSpec(weights.shape, lambda i: (0, 0, 0)))
    operands = (*grads, weights)
    if rest is not None:
        operands += (rest,)
        specs.append(tokens)
    return pl.pallas_call(
        partial(input_grad_kernel, len(grads)),
        grid=(2,),
        in_specs=specs,
        out_specs=tokens,
        out_shape=jax.ShapeDtypeStruct((length, share), BF),
        compiler_params=pltpu.CompilerParams(vmem_limit_bytes=60 * MIB),
    )(*operands)


def weight_grad_kernel(plan, width, z_ref, *refs):
    del z_ref
    out_ref, sums_ref = refs[-2:]
    sums_ref[...] = jnp.zeros_like(sums_ref)
    products = []
    index = 0
    row = 0
    for count in plan:
        left = refs[index][...]
        rights = [refs[index + 1 + i][0][:, :width] for i in range(count)]
        index += 1 + count
        for right in rights:
            sums_ref[row : row + 1, 0:width] = jnp.sum(right.astype(F32), axis=0, keepdims=True)
            row += 1
        products.append(dot_tn(left, rights[0] if count == 1 else jnp.concatenate(rights, axis=1)))
    out_ref[...] = jnp.concatenate(products, axis=1)


def weight_grad(z, width, *pairs):
    operands, specs = [], []
    for left, rights in pairs:
        operands.append(left)
        specs.append(pl.BlockSpec(left.shape, lambda i, z_ref: (0, 0)))
        for right in rights:
            operands.append(right)
            specs.append(pl.BlockSpec((1,) + right.shape[1:], lambda i, z_ref: (z_ref[0], 0, 0)))
    model = pairs[0][0].shape[1]
    plan = [len(rights) for _, rights in pairs]
    return pl.pallas_call(
        partial(weight_grad_kernel, plan, width),
        grid_spec=pltpu.PrefetchScalarGridSpec(
            num_scalar_prefetch=1,
            grid=(1,),
            in_specs=specs,
            out_specs=[
                pl.BlockSpec((model, sum(plan) * width), lambda i, z_ref: (0, 0)),
                pl.BlockSpec((8, model), lambda i, z_ref: (0, 0)),
            ],
        ),
        out_shape=[jax.ShapeDtypeStruct((model, sum(plan) * width), F32), jax.ShapeDtypeStruct((8, model), F32)],
        compiler_params=pltpu.CompilerParams(vmem_limit_bytes=60 * MIB),
    )(z.reshape(1), *operands)


def scattered(products):
    return lax.psum_scatter(products, "dp", scatter_dimension=0, tiled=True)


def finish_kernel(
    width, prod_f_ref, prod_c_ref, q_ref, k_ref, v_ref, gm_ref, sm_ref, gck_ref, gcv_ref, target_ref, grad_self_ref,
    logs_ref, dots_ref, t_ids_ref, columns_ref, rest_ref, sums_ref, cross_sums_ref, first_sums_ref,
    total_f_ref, total_c_ref, total_s_ref, vector_total_ref, target_grad_ref, memory_grad_ref,
    q_all, k_all, v_all, gm_all, sm_own, gck_all, gcv_all, target, grad_self, gq_all, gk_all, gv_all, gq_sum, logs, dots,
    mine_f, mine_c, prod_s, land_f, land_c, land_s, one_f, one_c, one_s, two_f, two_c, two_s, vec, vec_land, t_col_ref, t_row_ref,
    send_sem, recv_sem, load_sem,
):
    d = lax.axis_index("dp")
    z = lax.axis_index("tensor")
    c = d % 2
    x = (d // 2) % 2
    y = d // 4
    dc = d + 1 - 2 * c
    dx = d + 2 - 4 * x
    dy = d + 4 - 8 * y
    slices, length, _ = q_all.shape
    heads = 3

    def to(slot, source, place, other):
        return pltpu.make_async_remote_copy(
            src_ref=source,
            dst_ref=place,
            send_sem=send_sem.at[slot],
            recv_sem=recv_sem.at[slot],
            device_id={"dp": other},
            device_id_type=MESH,
        )

    families = (
        (prod_f_ref, mine_f, land_f, one_f, two_f, total_f_ref),
        (prod_c_ref, mine_c, land_c, one_c, two_c, total_c_ref),
        (prod_s, None, land_s, one_s, two_s, total_s_ref),
    )

    def over_core(i):
        return to(5 * i, families[i][0].at[:, :, 1 - c], families[i][2], dc)

    def halves(i):
        half = families[i][2].shape[3] // 2
        return pl.ds(0, half), pl.ds(half, half)

    def first_a(i):
        return to(5 * i + 1, families[i][2].at[:, 1 - x, :, halves(i)[0]], families[i][3].at[0], dx)

    def first_b(i):
        return to(5 * i + 2, families[i][2].at[1 - y, :, :, halves(i)[1]], families[i][3].at[1], dy)

    def second_a(i):
        return to(5 * i + 3, families[i][3].at[0, 1 - y], families[i][4].at[0], dy)

    def second_b(i):
        return to(5 * i + 4, families[i][3].at[1, 1 - x], families[i][4].at[1], dx)

    def after_core(i):
        _, mine, land, _, _, _ = families[i]
        over_core(i).wait_recv()

        @pl.loop(0, 4)
        def _(j):
            part = prod_s[j // 2, j % 2, c] if mine is None else mine[j // 2, j % 2]
            land[j // 2, j % 2] = land[j // 2, j % 2] + part

        first_a(i).start()
        first_b(i).start()

    def after_first(i):
        _, _, land, one, _, _ = families[i]
        first_a(i).wait_recv()
        first_b(i).wait_recv()
        left, right = halves(i)
        for j in range(2):
            one[0, j] = one[0, j] + land[j, x, :, left]
            one[1, j] = one[1, j] + land[y, j, :, right]
        second_a(i).start()
        second_b(i).start()

    def after_second(i):
        _, _, _, one, two, total_ref = families[i]
        second_a(i).wait_recv()
        second_b(i).wait_recv()
        left, right = halves(i)
        total_ref[:, left] = one[0, y] + two[0]
        total_ref[:, right] = one[1, x] + two[1]

    def vector_copy(i):
        return to(15 + i, vec.at[i], vec_land.at[i], (dc, dx, dy)[i])

    def vector_step(i):
        vector_copy(i).wait_recv()
        vec[i + 1] = vec[i] + vec_land[i]
        if i < 2:
            vector_copy(i + 1).start()

    barrier = pltpu.get_barrier_semaphore()
    for other in (dc, dx, dy):
        pl.semaphore_signal(barrier, inc=1, device_id={"dp": other}, device_id_type=MESH)

    def slice_loads(s):
        pairs = ((q_ref, q_all), (k_ref, k_all), (v_ref, v_all), (gm_ref, gm_all))
        return [
            pltpu.make_async_copy(source.at[s], place.at[s], load_sem.at[4 * s + i])
            for i, (source, place) in enumerate(pairs)
        ]

    late = 4 * slices
    late_loads = [
        pltpu.make_async_copy(sm_ref.at[z], sm_own, load_sem.at[late]),
        pltpu.make_async_copy(target_ref, target, load_sem.at[late + 1]),
        pltpu.make_async_copy(grad_self_ref, grad_self, load_sem.at[late + 2]),
        pltpu.make_async_copy(gck_ref, gck_all, load_sem.at[late + 3]),
        pltpu.make_async_copy(gcv_ref, gcv_all, load_sem.at[late + 4]),
    ]
    mine_loads = [
        pltpu.make_async_copy(prod_f_ref.at[:, :, c], mine_f, load_sem.at[late + 5]),
        pltpu.make_async_copy(prod_c_ref.at[:, :, c], mine_c, load_sem.at[late + 6]),
    ]
    for s in range(slices):
        for load in slice_loads(s):
            load.start()
    for load in mine_loads + late_loads:
        load.start()
    t_row_ref[...] = t_ids_ref[...].astype(F32)
    t_col_ref[...] = as_column(t_row_ref[...])
    logs[...] = jnp.transpose(logs_ref[...])
    dots[...] = jnp.transpose(dots_ref[...])
    pl.semaphore_wait(barrier, 3)
    over_core(0).start()
    over_core(1).start()

    vec[0] = jnp.zeros(vec.shape[1:], F32)
    for row, source, at in (
        (2, first_sums_ref, 2), (3, first_sums_ref, 0), (4, first_sums_ref, 1), (5, cross_sums_ref, 0),
        (6, cross_sums_ref, 2), (7, sums_ref, 5), (8, sums_ref, 3), (9, sums_ref, 4), (11, sums_ref, 2),
        (12, sums_ref, 0), (13, sums_ref, 1),
    ):
        vec[0, row : row + 1, :] = source[at : at + 1, :]
    vec[0, 10:11, :] = sums_ref[pl.ds(8 + z, 1), :]

    lane = lax.broadcasted_iota(jnp.int32, (1, 128), 1)
    scale = HEAD_DIM**-0.5
    block = 256

    def one_block(s, at):
        reach = length - at
        span = slice(at, at + block)
        allowed = (t_col_ref[span, :] == t_row_ref[:, at:]) & (
            lax.broadcasted_iota(jnp.int32, (block, reach), 0) <= lax.broadcasted_iota(jnp.int32, (block, reach), 1)
        )
        grads = []
        for h in range(heads):
            mine = (lane // HEAD_DIM) == (h % 2)
            columns = slice(128 * (h // 2), 128 * (h // 2) + 128)
            keys = k_all[s, span, columns]
            keys = jnp.where(mine, keys, jnp.zeros_like(keys))
            values = v_all[s, span, columns]
            values = jnp.where(mine, values, jnp.zeros_like(values))
            queries = q_all[s, at:, columns]
            gm = gm_all[s, at:, columns]
            scores = dot_nt(keys * jnp.asarray(scale, BF), queries)
            row = pl.ds(heads * s + h, 1)
            probs = jnp.where(allowed, jnp.exp(scores - logs[row, at:]), 0.0)
            grad_scores = (probs * (dot_nt(values, gm) - dots[row, at:])).astype(BF)
            grads.append((dot_nn(grad_scores, queries) * scale, dot_nn(probs.astype(BF), gm)))
            gq_sum[at:, columns] += dot_tn(grad_scores, keys)
        left = lane < HEAD_DIM
        for i, out in enumerate((gk_all, gv_all)):
            out[s, span, 0:128] = jnp.where(left, grads[0][i], grads[1][i]).astype(BF)
            out[s, span, 128:256] = jnp.where(left, grads[2][i], 0.0).astype(BF)

    for s in range(slices):
        for load in slice_loads(s):
            load.wait()

    @pl.loop(0, slices)
    def _(s):
        gq_sum[...] = jnp.zeros_like(gq_sum)
        for at in range(0, length, block):
            one_block(s, at)
        gq_all[s] = (gq_sum[...] * scale).astype(BF)

        @pl.when(s == 0)
        def _():
            for load in mine_loads:
                load.wait()
            after_core(0)
            after_core(1)

        @pl.when(s == slices - 1)
        def _():
            after_first(0)
            after_first(1)

    for load in late_loads:
        load.wait()
    right = jnp.concatenate((gq_all[z][:, :width], gk_all[z][:, :width], gv_all[z][:, :width]), axis=1)
    products = jnp.concatenate((dot_tn(target[...], right), dot_tn(grad_self[...], sm_own[:, :width])), axis=1)
    prod_s[...] = products.reshape(prod_s.shape)
    vec[0, 0:1, 0:width] = jnp.sum(gq_all[z][:, :width].astype(F32), axis=0, keepdims=True)
    vec[0, 1:2, 0:width] = jnp.sum(gv_all[z][:, :width].astype(F32), axis=0, keepdims=True)
    over_core(2).start()
    vector_copy(0).start()

    def input_grad(grads, first, rest, out_ref):
        @pl.loop(0, 4)
        def _(i):
            span = pl.ds(pl.multiple_of(i * (length // 4), length // 4), length // 4)
            total = 0.0
            for j, grad in enumerate(grads):
                for s in range(slices):
                    weight = columns_ref[s, (first + j) * width : (first + j + 1) * width, :]
                    total = total + dot_nn(grad[s, span, :width], weight)
            total = total[:, :width]
            if rest is not None:
                total = total + rest[span, :]
            out_ref[span, :] = total.astype(BF)

    after_core(2)
    vector_step(0)
    input_grad((gq_all, gk_all, gv_all), 0, rest_ref, target_grad_ref)
    after_first(2)
    vector_step(1)
    input_grad((gck_all, gcv_all), 3, None, memory_grad_ref)
    after_second(0)
    after_second(1)
    after_second(2)
    vector_step(2)
    vector_total_ref[...] = vec[3]
    for i in range(3):
        over_core(i).wait_send()
        for copy in (first_a(i), first_b(i), second_a(i), second_b(i)):
            copy.wait_send()
        vector_copy(i).wait_send()


def finish(prod_f, prod_c, heads, cross_grads, target, grad_self, logs, dots, ids, columns, rest, sums, cross_sums, first_sums):
    slices, length, wide = heads[0].shape
    model = target.shape[1]
    width = model // slices
    n = model // 8
    anywhere = pl.BlockSpec(memory_space=pl.ANY)
    inside = pl.BlockSpec(memory_space=pltpu.VMEM)
    columns_f, columns_c = prod_f.shape[1], prod_c.shape[1]

    def half(size):
        return pltpu.VMEM((2, 2, n, size), F32)

    sizes = (columns_f, columns_c, model)
    group = pltpu.VMEM((slices, length, wide), BF)
    tokens = pltpu.VMEM((length, model), BF)
    share = jax.ShapeDtypeStruct((length, model // slices), BF)
    return pl.pallas_call(
        partial(finish_kernel, width),
        out_shape=[jax.ShapeDtypeStruct((n, size), F32) for size in sizes]
        + [jax.ShapeDtypeStruct((16, model), F32), share, share],
        in_specs=[anywhere] * 11 + [inside] * 8,
        out_specs=[inside] * 6,
        scratch_shapes=[group] * 4
        + [pltpu.VMEM((length, wide), BF), group, group, tokens, tokens, group, group, group]
        + [pltpu.VMEM((length, wide), F32), pltpu.VMEM((128, length), F32), pltpu.VMEM((128, length), F32)]
        + [half(columns_f), half(columns_c), pltpu.VMEM((2, 2, 2, n, model), F32)]
        + [half(size) for size in sizes]
        + [pltpu.VMEM((2, 2, n, size // 2), F32) for size in sizes]
        + [pltpu.VMEM((2, n, size // 2), F32) for size in sizes]
        + [pltpu.VMEM((4, 16, model), F32), pltpu.VMEM((3, 16, model), F32), pltpu.VMEM((length, 1), F32), pltpu.VMEM((1, length), F32)]
        + [pltpu.SemaphoreType.DMA((18,)), pltpu.SemaphoreType.DMA((18,)), pltpu.SemaphoreType.DMA((4 * slices + 7,))],
        compiler_params=pltpu.CompilerParams(collective_id=1, has_side_effects=True, vmem_limit_bytes=63 * MIB),
    )(
        prod_f.reshape(2, 2, 2, n, columns_f), prod_c.reshape(2, 2, 2, n, columns_c), *heads, *cross_grads, target,
        grad_self, logs, dots, ids, columns, rest, sums, cross_sums, first_sums,
    )


def part_kernel(width, units, total_f_ref, total_c_ref, total_s_ref, vectors_ref, target_ref, memory_ref, *outs):
    matrices, lines, inputs = outs[:10], outs[10:-2], outs[-2:]
    for out, ref in zip(inputs, (target_ref, memory_ref), strict=True):
        out[...] = jnp.transpose(ref[...].astype(F32)).astype(BF)
    for i, ref in enumerate((total_s_ref, total_c_ref)):
        for j in range(4):
            part = ref[:, j * width : (j + 1) * width]
            matrices[4 * i + j][...] = part.T if j == 3 else part
    matrices[8][...] = total_f_ref[:, :units]
    matrices[9][...] = total_f_ref[:, units:]
    for i, out in enumerate(lines):
        out[...] = vectors_ref[i, : out.shape[0]]


def parts_of(total_f, total_c, total_s, vectors, target_grad, memory_grad, width, units):
    n, model = total_s.shape
    matrices = [(n, width), (n, width), (n, width), (width, n)] * 2 + [(n, units)] * 2
    lines = [width, width, model, model, model, width, width] + [model] * 3 + [units] + [model] * 3
    out = pl.pallas_call(
        partial(part_kernel, width, units),
        out_shape=[jax.ShapeDtypeStruct(shape, F32) for shape in matrices]
        + [jax.ShapeDtypeStruct((size,), F32) for size in lines]
        + [jax.ShapeDtypeStruct(target_grad.shape[::-1], BF)] * 2,
    )(total_f, total_c, total_s, vectors, target_grad, memory_grad)
    return [*out[:9], out[9].T], out[10:-2], out[-2].T, out[-1].T


def per_device(
    n_dp, n_tensor, target, memory, target_segments, memory_segments, self_query, self_query_bias, self_key, self_value,
    self_value_bias, self_output, self_output_bias, first_gain, first_shift, cross_query, cross_query_bias, cross_key,
    cross_value, cross_value_bias, cross_output, cross_output_bias, second_gain, second_shift, expand_weight, expand_bias,
    contract_weight, contract_bias, third_gain, third_shift, output_grad,
):
    model, width = self_query.shape
    units = expand_weight.shape[1]
    head_rows = 8 * width
    z = lax.axis_index("tensor")
    target_ids = target_segments.reshape(1, -1)
    memory_ids = memory_segments.reshape(1, -1)

    own = (
        self_query, self_key, self_value, self_output, cross_key, cross_value, cross_query, cross_output, expand_weight,
        contract_weight,
    )

    def rows_of(count, vectors):
        return jnp.stack([jnp.pad(v, (0, model - v.shape[0])) for v in vectors] + [jnp.zeros(model, F32)] * (count - len(vectors)))

    biases = (self_query_bias, self_value_bias, cross_query_bias, cross_value_bias, expand_bias)
    vectors = (self_output_bias, first_gain, first_shift, cross_output_bias, second_gain, second_shift)
    run = forward if (n_dp, n_tensor) == (8, 4) else forward_plain
    columns, full, sq, sk, sv, sm, cq, ck, cv, cm, logs, hat1, hat2, spread, low1, low2, act, slope = run(
        own, biases, target, memory, target_ids, memory_ids, vectors, n_dp, n_tensor, head_rows, units
    )
    layer_output, grad_ffn, grad_hidden, grad_second_sum, grad_cross, gcm, cross_dots, sums = feed_back(
        act, slope, hat2, spread, output_grad, cm, full,
        (second_gain, second_shift, contract_bias, third_gain, third_shift), head_rows,
    )
    ffn_products = weight_grad(z, units, (low2, [grad_hidden]), (grad_ffn, [act]))[0]
    gcq, gck, gcv = attend_back(False, 3 * n_tensor, cq, ck, cv, gcm, logs, cross_dots, target_ids, memory_ids)
    cross_products, cross_sums = weight_grad(z, width, (low1, [gcq]), (memory, [gck, gcv]), (grad_cross, [cm]))
    rest, grad_self, gsm, self_dots, first_sums = first_back(
        z, gcq, grad_second_sum, hat1, spread, sm, full, first_gain, head_rows
    )
    if (n_dp, n_tensor) == (8, 4):
        total_f, total_c, total_s, vectors, target_grad, memory_grad = finish(
            ffn_products, cross_products, (sq, sk, sv, gsm, sm), (gck, gcv), target, grad_self, logs, self_dots, target_ids,
            columns, rest, sums, cross_sums, first_sums,
        )
    else:
        gsq, gsk, gsv = attend_back(True, 0, sq, sk, sv, gsm, logs, self_dots, target_ids, target_ids)
        self_products, self_sums = weight_grad(z, width, (target, [gsq, gsk, gsv]), (grad_self, [sm]))
        total_f, total_c, total_s = scattered(ffn_products), scattered(cross_products), scattered(self_products)
        memory_grad = input_grad((gck, gcv), columns[:, 3 * width :, :width])
        target_grad = input_grad((gsq, gsk, gsv), columns[:, : 3 * width, :width], rest)
        vectors = (
            self_sums[0], self_sums[2], first_sums[2], first_sums[0], first_sums[1], cross_sums[0], cross_sums[2], sums[5],
            sums[3], sums[4], lax.dynamic_index_in_dim(sums, 8 + z, 0, keepdims=False), sums[2], sums[0], sums[1],
        )
        vectors = lax.psum(rows_of(16, vectors), "dp")
    parts, totals, target_grad, memory_grad = parts_of(
        total_f, total_c, total_s, vectors, target_grad, memory_grad, width, units
    )
    return (
        layer_output, target_grad, memory_grad, parts[0], totals[0], parts[1], parts[2], totals[1], parts[3], totals[2],
        totals[3], totals[4], parts[4], totals[5], parts[5], parts[6], totals[6], parts[7], totals[7], totals[8], totals[9],
        parts[8], totals[10], parts[9], totals[11], totals[12], totals[13],
    )


def solution(mesh):
    rows = P("dp", None)
    split = P(None, "tensor")
    both = P("dp", "tensor")
    turned = P("tensor", "dp")
    own = P("tensor")
    in_specs = (
        rows, rows, rows, rows,
        split, own, split, split, own, P("tensor", None), P(), P(), P(),
        split, own, split, split, own, P("tensor", None), P(), P(), P(),
        split, own, P("tensor", None), P(), P(), P(),
        rows,
    )
    out_specs = (
        rows, both, both,
        both, own, both, both, own, turned, P(), P(), P(),
        both, own, both, both, own, turned, P(), P(), P(),
        both, own, turned, P(), P(), P(),
    )
    return jax.shard_map(
        partial(per_device, mesh.shape["dp"], mesh.shape["tensor"]),
        mesh=mesh,
        in_specs=in_specs,
        out_specs=out_specs,
        check_vma=False,
    )
```

```python
from functools import partial

import jax
import jax.numpy as jnp
from jax import lax
from jax.experimental import pallas as pl
from jax.experimental.pallas import tpu as pltpu
from jax.sharding import PartitionSpec as P

HEAD_DIM = 64
EPSILON = 1e-05
NEGATIVE = -1e30
BF = jnp.bfloat16
F32 = jnp.float32
MESH = pl.DeviceIdType.MESH
MIB = 2**20


def dot_nn(a, b):
    return lax.dot_general(a, b, (((1,), (0,)), ((), ())), preferred_element_type=F32)


def dot_nt(a, b):
    return lax.dot_general(a, b, (((1,), (1,)), ((), ())), preferred_element_type=F32)


def dot_tn(a, b):
    return lax.dot_general(a, b, (((0,), (0,)), ((), ())), preferred_element_type=F32)


WIDE = 256
TOKEN_BLOCK = 256


def as_column(row):
    return jnp.transpose(jnp.broadcast_to(row, (128, row.shape[1])))[:, 0:1]


def fill_rows(rows_ref, lines):
    rows_ref[...] = jnp.zeros_like(rows_ref)
    for i, line in enumerate(lines):
        rows_ref[i, 0 : line.shape[0]] = line[...]


def erf_pair(hidden):
    phi = 0.5 * (1.0 + lax.erf(hidden * 0.7071067811865476))
    slope = phi + hidden * (jnp.exp(-0.5 * hidden * hidden) * 0.3989422804014327)
    return hidden * phi, slope


def forward_kernel(
    n_dp, n_tensor, count, rows, head_rows, hidden_rows,
    sqw_ref, skw_ref, svw_ref, sow_ref, ckw_ref, cvw_ref, cqw_ref, cow_ref, exw_ref, ctw_ref, target_ref, memory_ref, t_ids_ref, m_ids_ref,
    b0_ref, b1_ref, b2_ref, b3_ref, b4_ref, v0_ref, v1_ref, v2_ref, v3_ref, v4_ref, v5_ref,
    chunk_ref, columns_ref, found_ref, full_ref, sq_ref, sk_ref, sv_ref, sm_ref, cq_ref, ck_ref, cv_ref, cm_ref, logs_ref, hat1_ref, hat2_ref,
    r_ref, low1_ref, low2_ref, act_ref, slope_ref,
    columns, vectors_ref, bias_ref, t_row_ref, m_row_ref, t_col_ref, stage, full, low, bias, q_all, k_all, v_all, mixed, logs, hat1, hat2, spread, low1, low2, act, slope,
    send_sem, recv_sem, bias_send, bias_recv, load_sem, store_sem, out_sem,
):
    d = lax.axis_index("dp")
    z = lax.axis_index("tensor")
    others = n_tensor - 1
    length, model = target_ref.shape
    size = n_dp * rows
    dc = d + 1 - 2 * (d % 2)
    dx = d + 2 - 4 * ((d // 2) % 2)
    dy = d + 4 - 8 * (d // 4)
    dxy = dx + 4 - 8 * (d // 4)

    def slice_of(k):
        return (z + others - k) % n_tensor

    def slice_at(j):
        return (z + n_tensor - j) % n_tensor

    def along_z(g, source, k, step, slot):
        return pltpu.make_async_remote_copy(
            src_ref=source,
            dst_ref=found_ref.at[d, k, pl.ds(g * rows, rows)],
            send_sem=send_sem.at[g, slot],
            recv_sem=recv_sem.at[g, k],
            device_id={"tensor": z + step},
            device_id_type=MESH,
        )

    near = ((1, 0, 0), (2, 1, 1), (-1, 2, 2), (-2, 1, 11))

    def own_along(g, step, k, slot):
        return along_z(g, chunk_ref.at[pl.ds(g * rows, rows)], k, step, slot)

    def reaches(step):
        return z + step <= others if step > 0 else z + step >= 0

    inner = jnp.logical_and(z > 0, z < others)

    def relay(g):
        step = 2 * z - 3
        return along_z(g, found_ref.at[d, 1, pl.ds(g * rows, rows)], 1 + step, step, 12)

    def from_z(g, k):
        own_along(g, 0, k, 0).wait_recv()

    lead = 2

    def own_z(g):
        for step_z, k, slot in near:

            @pl.when(reaches(step_z))
            def _(step_z=step_z, k=k, slot=slot):
                own_along(g, step_z, k, slot).start()

    def pass_z(g):
        @pl.when(inner)
        def _():
            from_z(g, 1)
            relay(g).start()

        if g + lead < count:
            own_z(g + lead)

    def in_plane(g, slot, chunk, half, other):
        span = pl.ds(g * rows, rows) if half is None else pl.ds(g * rows + half * (rows // 2), rows // 2)
        piece = found_ref.at[chunk, :, span]
        return pltpu.make_async_remote_copy(
            src_ref=piece,
            dst_ref=piece,
            send_sem=send_sem.at[g, slot],
            recv_sem=recv_sem.at[g, slot],
            device_id={"dp": other},
            device_id_type=MESH,
        )

    def bias_copy(k):
        return pltpu.make_async_remote_copy(
            src_ref=bias_ref,
            dst_ref=bias.at[z],
            send_sem=bias_send.at[k],
            recv_sem=bias_recv.at[k],
            device_id={"tensor": (z + k + 1) % n_tensor},
            device_id_type=MESH,
        )

    routes = {3: (d, None, dx), 4: (d, None, dy), 5: (d, None, dc), 6: (dx, 0, dy), 7: (dy, 1, dx)}
    routes.update({8 + i: (chunk, None, dc) for i, chunk in enumerate((dx, dy, dxy))})

    def send(g, slot):
        return in_plane(g, slot, *routes[slot])

    def arrive(g, slot, half=None):
        in_plane(g, slot, d, half, dc).wait_recv()

    def first_hop(g):
        from_z(g, 0)
        from_z(g, 2)

        @pl.when(jnp.logical_not(inner))
        def _():
            from_z(g, 1)

        for slot in (3, 4, 5):
            send(g, slot).start()

    def pass_on(g):
        arrive(g, 3)
        send(g, 6).start()
        send(g, 8).start()
        arrive(g, 4)
        send(g, 7).start()
        send(g, 9).start()

    def load_of(g, k):
        return pltpu.make_async_copy(found_ref.at[:, k, pl.ds(g * rows, rows)], stage.at[k], load_sem.at[k])

    def last_hop(g):
        arrive(g, 6, 0)
        arrive(g, 7, 1)
        send(g, 10).start()

    def landed(g):
        arrive(g, 5)
        for slot in (8, 9, 10):
            arrive(g, slot)
        for k in range(others):
            load_of(g, k).start()

    def home(g):
        kept = hidden_rows // size + head_rows // size
        return (full, pl.ds(g * size, size)) if g < kept else (low, pl.ds((g % 2) * size, size))

    def store_of(g, s):
        place, span = home(g)
        return pltpu.make_async_copy(place.at[s, span], full_ref.at[s, pl.ds(g * size, size)], store_sem.at[g, s])

    def rounded(g):
        place, span = home(g)
        @pl.loop(0, others)
        def _(k):
            load_of(g, k).wait()
            place[slice_of(k), span] = stage[k].reshape(size, model).astype(BF)

        for s in range(n_tensor):
            store_of(g, s).start()

    def pause(step, between):
        for at, *moves in between:

            @pl.when(step == at)
            def _(moves=moves):
                for move, g in moves:
                    move(g)

    def project(x_ref, s, first, bias_row, out_ref):
        @pl.loop(0, 2)
        def _(i):
            span = pl.ds(pl.multiple_of(i * (length // 2), length // 2), length // 2)
            value = dot_nt(x_ref[span, :], full[s, pl.ds(first, WIDE), :])
            if bias_row is not None:
                value = value + bias[s, bias_row : bias_row + 1, :WIDE]
            filled = lax.broadcasted_iota(jnp.int32, (1, WIDE), 1) < head_rows // 8
            out_ref[s, span, :] = jnp.where(filled, value, 0.0).astype(BF)

    def attend(first, number, causal, k_ids_ref, base, *between):
        half = length // 2
        lane = lax.broadcasted_iota(jnp.int32, (1, 128), 1)

        @pl.loop(3 * first, 3 * (first + number))
        def _(step):
            s = (z + n_tensor - step // 3) % n_tensor
            h = step % 3
            columns = pl.ds(pl.multiple_of((h // 2) * 128, 128), 128)
            mine = (lane // HEAD_DIM) == (h % 2)
            log_lane = lane == base + 3 * s + h
            for b in range(2):
                reach = (b + 1) * half if causal else length
                span = slice(b * half, (b + 1) * half)
                queries = q_all[s, span, columns] * jnp.asarray(HEAD_DIM**-0.5, BF)
                scores = dot_nt(jnp.where(mine, queries, jnp.zeros_like(queries)), k_all[s, :reach, columns])
                allowed = t_col_ref[span, :] == k_ids_ref[:, :reach]
                if causal:
                    allowed = allowed & (
                        lax.broadcasted_iota(jnp.int32, (half, reach), 0) + b * half
                        >= lax.broadcasted_iota(jnp.int32, (half, reach), 1)
                    )
                scores = jnp.where(allowed, scores, NEGATIVE)
                top = jnp.max(scores, axis=1, keepdims=True)
                weights = jnp.exp(scores - top)
                total = jnp.sum(weights, axis=1, keepdims=True)
                out = (dot_nn(weights.astype(BF), v_all[s, :reach, columns]) * (1.0 / total)).astype(BF)
                before = mixed[s, span, columns]
                before = jnp.where(h % 2 == 1, before, jnp.zeros_like(before))
                mixed[s, span, columns] = jnp.where(mine, out, before)
                logs[span, :] = jnp.where(log_lane, top + jnp.log(total), logs[span, :])
            pause(step, between)

    def close(first, bias_row, residual, hat, low_out, column):
        block = length // 4

        @pl.loop(0, 4)
        def _(i):
            span = pl.ds(pl.multiple_of(i * block, block), block)
            value = residual(span) + vectors_ref[bias_row : bias_row + 1, :]
            for s in range(n_tensor):
                value = value + dot_nn(mixed[s, span, :], full[s, pl.ds(first, WIDE), :])
            centered = value - jnp.mean(value, axis=1, keepdims=True)
            scale = lax.rsqrt(jnp.mean(centered * centered, axis=1, keepdims=True) + EPSILON)
            normed = centered * scale
            hat[span, :] = normed
            here = lax.broadcasted_iota(jnp.int32, (1, 128), 1) == column
            spread[span, :] = jnp.where(here, scale, spread[span, :])
            low_out[span, :] = (
                normed * vectors_ref[bias_row + 1 : bias_row + 2, :] + vectors_ref[bias_row + 2 : bias_row + 3, :]
            ).astype(BF)

    def expand(s, slot):
        @pl.loop(0, 4)
        def _(i):
            span = pl.ds(pl.multiple_of(i * (length // 4), length // 4), length // 4)
            hidden = dot_nt(low2[span, :], full[s, pl.ds(head_rows, hidden_rows), :]) + bias[s, 4:5, :]
            value, change = erf_pair(hidden)
            act[slot, span, :] = value.astype(BF)
            slope[slot, span, :] = change.astype(BF)

    def own_columns(s):
        for i, first in enumerate((q0, k0, v0, ck0, cv0)):
            value = full[s, pl.ds(first, step), :].astype(F32)
            columns[s, pl.ds(i * step, step), :] = pltpu.roll(value, model - z * step, 1)[:, :WIDE].astype(BF)

    def out_copy(i, source, target):
        return pltpu.make_async_copy(source, target, out_sem.at[i])

    def expand_out(s, slot):
        return (
            out_copy(13 + 2 * slot, act.at[slot], act_ref.at[s]),
            out_copy(14 + 2 * slot, slope.at[slot], slope_ref.at[s]),
        )

    barrier = pltpu.get_barrier_semaphore()
    for k in range(1, n_tensor):
        pl.semaphore_signal(barrier, inc=1, device_id={"tensor": (z + k) % n_tensor}, device_id_type=MESH)
    for other in (dc, dx, dy):
        pl.semaphore_signal(barrier, inc=1, device_id={"dp": other}, device_id_type=MESH)
    step = head_rows // 8
    q0, k0, v0, o0, ck0, cv0, cq0, co0 = (i * step for i in range(8))
    own_loads = [
        pltpu.make_async_copy(source, place, load_sem.at[3 + i])
        for i, (source, place) in enumerate(
            (
                (sqw_ref, full.at[z, pl.ds(q0, step)]),
                (skw_ref, full.at[z, pl.ds(k0, step)]),
                (svw_ref, full.at[z, pl.ds(v0, step)]),
                (ckw_ref, full.at[z, pl.ds(ck0, step)]),
                (cvw_ref, full.at[z, pl.ds(cv0, step)]),
                (cqw_ref, full.at[z, pl.ds(cq0, step)]),
                (sow_ref, full.at[z, pl.ds(o0, step)]),
                (cow_ref, full.at[z, pl.ds(co0, step)]),
                (exw_ref, act.at[0, pl.ds(0, model)]),
                (ctw_ref, low.at[z]),
            )
        )
    ]
    for load in own_loads:
        load.start()
    t_row_ref[...] = t_ids_ref[...].astype(F32)
    m_row_ref[...] = m_ids_ref[...].astype(F32)
    t_col_ref[...] = as_column(t_row_ref[...])
    fill_rows(bias_ref, (b0_ref, b1_ref, b2_ref, b3_ref, b4_ref))
    fill_rows(vectors_ref, (v0_ref, v1_ref, v2_ref, v3_ref, v4_ref, v5_ref))
    bias[z] = bias_ref[...]
    pl.semaphore_wait(barrier, others + 3)
    for k in range(others):
        bias_copy(k).start()
    def chunk_copy(g):
        return pltpu.make_async_copy(stage.at[0, g], chunk_ref.at[pl.ds(g * rows, rows)], load_sem.at[g % 3])

    def offer(g):
        place, span = home(g)
        first = span.start + d * rows
        stage[0, g] = place[z, pl.ds(pl.multiple_of(first, 16), rows), :].astype(F32)
        chunk_copy(g).start()

    def give(g):
        chunk_copy(g).wait()
        if g < lead:
            own_z(g)

    own_loads[0].wait()
    own_loads[1].wait()
    offer(0)
    own_loads[2].wait()
    own_loads[6].wait()
    give(0)
    offer(1)
    own_loads[3].wait()
    own_loads[4].wait()
    give(1)
    offer(2)
    own_loads[5].wait()
    own_loads[7].wait()
    give(2)
    offer(3)
    own_loads[8].wait()
    full[z, pl.ds(head_rows, hidden_rows), :] = jnp.transpose(act[0, :model, :].astype(F32)).astype(BF)
    offer(4)
    give(3)
    offer(5)
    own_loads[9].wait()
    give(4)
    offer(6)
    give(5)
    offer(7)
    give(6)
    give(7)

    logs[...] = jnp.zeros_like(logs)
    spread[...] = jnp.zeros_like(spread)
    project(target_ref, z, q0, 0, q_all)
    project(target_ref, z, k0, None, k_all)
    project(target_ref, z, v0, 1, v_all)
    attend(0, 1, True, t_row_ref, 0)
    for k in range(others):
        bias_copy(k).wait_recv()
    pass_z(0)
    first_hop(0)
    pass_z(1)
    first_hop(1)
    pass_on(0)
    pass_z(2)
    first_hop(2)
    pass_on(1)
    pass_z(3)
    last_hop(0)
    landed(0)
    first_hop(3)
    rounded(0)
    @pl.loop(0, others)
    def _(k):
        project(target_ref, slice_of(k), q0, 0, q_all)
        project(target_ref, slice_of(k), k0, None, k_all)

    pass_z(4)
    pass_on(2)
    last_hop(1)
    first_hop(4)
    landed(1)
    pass_z(5)
    rounded(1)
    @pl.loop(0, others)
    def _(k):
        project(target_ref, slice_of(k), v0, 1, v_all)

    attend(
        1, 3, True, t_row_ref, 0, (3, (last_hop, 2)), (4, (pass_on, 3), (first_hop, 5)), (6, (landed, 2)), (7, (pass_z, 6)),
        (8, (rounded, 2)), (9, (last_hop, 3), (pass_on, 4)), (10, (first_hop, 6)),
    )
    pass_z(7)
    self_out = [
        out_copy(0, q_all, sq_ref), out_copy(1, k_all, sk_ref), out_copy(2, v_all, sv_ref), out_copy(3, mixed, sm_ref)
    ]
    for copy in self_out:
        copy.start()
    close(o0, 0, lambda span: target_ref[span, :].astype(F32), hat1, low1, 0)
    landed(3)
    out_copy(4, hat1, hat1_ref).start()
    out_copy(5, low1, low1_ref).start()
    for copy in self_out:
        copy.wait()

    @pl.loop(0, n_tensor)
    def _(s):
        project(memory_ref, s, ck0, None, k_all)
        project(memory_ref, s, cv0, 3, v_all)

    pass_on(5)
    first_hop(7)
    project(low1, z, cq0, 2, q_all)

    def rest_of_queries(g):
        rounded(g)

        @pl.loop(0, others)
        def _(k):
            project(low1, slice_of(k), cq0, 2, q_all)

    def shares(g):
        @pl.loop(0, n_tensor)
        def _(s):
            own_columns(s)

        out_copy(10, columns, columns_ref).start()
        rounded(g)

    attend(
        0, 4, False, m_row_ref, 3 * n_tensor, (1, (last_hop, 4)), (2, (rest_of_queries, 3), (landed, 4)), (3, (pass_on, 6)),
        (4, (last_hop, 5)), (5, (rounded, 4)), (6, (landed, 5)), (7, (pass_on, 7)), (8, (shares, 5)), (9, (last_hop, 6)),
        (11, (last_hop, 7)),
    )
    cross_out = [
        out_copy(0, q_all, cq_ref), out_copy(1, k_all, ck_ref), out_copy(2, v_all, cv_ref), out_copy(3, mixed, cm_ref),
        out_copy(6, logs, logs_ref),
    ]
    for copy in cross_out:
        copy.start()
    close(co0, 3, lambda span: hat1[span, :] * vectors_ref[1:2, :] + vectors_ref[2:3, :], hat2, low2, 1)
    out_copy(7, hat2, hat2_ref).start()
    out_copy(8, low2, low2_ref).start()
    out_copy(9, spread, r_ref).start()
    landed(6)

    @pl.loop(0, n_tensor)
    def _(j):
        @pl.when(j >= 2)
        def _():
            for copy in expand_out(slice_at(j - 2), j % 2):
                copy.wait()

        @pl.when(j == 1)
        def _():
            rounded(6)
            landed(7)

        @pl.when(j == 2)
        def _():
            rounded(7)

        expand(slice_at(j), j % 2)
        for copy in expand_out(slice_at(j), j % 2):
            copy.start()

    for copy in expand_out(slice_at(2), 0) + expand_out(slice_at(3), 1) + tuple(cross_out):
        copy.wait()
    for i, source, target in ((4, hat1, hat1_ref), (5, low1, low1_ref), (7, hat2, hat2_ref), (8, low2, low2_ref)):
        out_copy(i, source, target).wait()
    out_copy(9, spread, r_ref).wait()
    out_copy(10, columns, columns_ref).wait()
    for g in range(count):
        for s in range(n_tensor):
            store_of(g, s).wait()
    for k in range(others):
        bias_copy(k).wait_send()
    for g in range(count):
        for step_z, k, slot in near:

            @pl.when(reaches(step_z))
            def _(g=g, step_z=step_z, k=k, slot=slot):
                own_along(g, step_z, k, slot).wait_send()

        @pl.when(inner)
        def _(g=g):
            relay(g).wait_send()

        for slot in routes:
            send(g, slot).wait_send()


def forward(own, biases, target, memory, target_ids, memory_ids, vectors, n_dp, n_tensor, head_rows, hidden_rows):
    length, model = target.shape
    count = 8
    total = head_rows + 2 * hidden_rows
    size = total // count
    rows = size // n_dp
    step = head_rows // 8
    anywhere = pl.BlockSpec(memory_space=pl.ANY)
    inside = pl.BlockSpec(memory_space=pltpu.VMEM)
    heads = jax.ShapeDtypeStruct((n_tensor, length, WIDE), BF)
    tokens = jax.ShapeDtypeStruct((length, model), F32)
    tokens_low = jax.ShapeDtypeStruct((length, model), BF)
    lanes = jax.ShapeDtypeStruct((length, 128), F32)
    units = jax.ShapeDtypeStruct((n_tensor, length, hidden_rows), BF)
    out_shape = (
        jax.ShapeDtypeStruct((count * rows, model), F32),
        jax.ShapeDtypeStruct((n_tensor, 5 * step, WIDE), BF),
        jax.ShapeDtypeStruct((n_dp, n_tensor - 1, count * rows, model), F32),
        jax.ShapeDtypeStruct((n_tensor, total, model), BF),
        heads, heads, heads, heads, heads, heads, heads, heads,
        lanes, tokens, tokens, lanes, tokens_low, tokens_low, units, units,
    )
    flops = 2 * length * model * (2 * n_tensor * head_rows) + 4 * length * model * n_tensor * hidden_rows
    outs = pl.pallas_call(
        partial(forward_kernel, n_dp, n_tensor, count, rows, head_rows, hidden_rows),
        out_shape=out_shape,
        in_specs=[anywhere] * 10 + [inside] * 15,
        out_specs=[anywhere] * len(out_shape),
        scratch_shapes=[
            pltpu.VMEM((n_tensor, 5 * step, WIDE), BF),
            pltpu.VMEM((8, model), F32),
            pltpu.VMEM((8, model), F32),
            pltpu.VMEM((1, length), F32),
            pltpu.VMEM((1, length), F32),
            pltpu.VMEM((length, 1), F32),
            pltpu.VMEM((n_tensor - 1, n_dp, rows, model), F32),
            pltpu.VMEM((n_tensor, head_rows + hidden_rows, model), BF),
            pltpu.VMEM((n_tensor, hidden_rows, model), BF),
            pltpu.VMEM((n_tensor, 8, model), F32),
            pltpu.VMEM(heads.shape, BF),
            pltpu.VMEM(heads.shape, BF),
            pltpu.VMEM(heads.shape, BF),
            pltpu.VMEM(heads.shape, BF),
            pltpu.VMEM(lanes.shape, F32),
            pltpu.VMEM(tokens.shape, F32),
            pltpu.VMEM(tokens.shape, F32),
            pltpu.VMEM(lanes.shape, F32),
            pltpu.VMEM(tokens.shape, BF),
            pltpu.VMEM(tokens.shape, BF),
            pltpu.VMEM((2, length, hidden_rows), BF),
            pltpu.VMEM((2, length, hidden_rows), BF),
            pltpu.SemaphoreType.DMA((count, 13)),
            pltpu.SemaphoreType.DMA((count, 11)),
            pltpu.SemaphoreType.DMA((n_tensor - 1,)),
            pltpu.SemaphoreType.DMA((n_tensor - 1,)),
            pltpu.SemaphoreType.DMA((13,)),
            pltpu.SemaphoreType.DMA((count, n_tensor)),
            pltpu.SemaphoreType.DMA((17,)),
        ],
        cost_estimate=pl.CostEstimate(flops=flops, bytes_accessed=60 * MIB, transcendentals=0),
        compiler_params=pltpu.CompilerParams(collective_id=0, has_side_effects=True, vmem_limit_bytes=63 * MIB),
    )(
        *(x.T if x.shape[0] > x.shape[1] else x for x in own), target, memory, target_ids, memory_ids, *biases, *vectors
    )
    return outs[1], *outs[3:]


def round_kernel(wide_ref, low_ref):
    low_ref[...] = wide_ref[...].astype(BF)


def rounded_copy(array):
    slices, rows, width = array.shape
    block = pl.BlockSpec((1, rows // 4, width), lambda i, j: (i, j, 0))
    return pl.pallas_call(
        round_kernel,
        grid=(slices, 4),
        in_specs=[block],
        out_specs=block,
        out_shape=jax.ShapeDtypeStruct(array.shape, BF),
    )(array)


def forward_plain(own, biases, target, memory, target_ids, memory_ids, vectors, n_dp, n_tensor, head_rows, hidden_rows):
    length, model = target.shape
    width = head_rows // 8
    sq, sk, sv, so, ck, cv, cq, co, expand, contract = own
    own = jnp.concatenate((sq.T, sk.T, sv.T, so, ck.T, cv.T, cq.T, co, expand.T, contract), axis=0)
    full = rounded_copy(lax.all_gather(own.astype(F32), "tensor", axis=0))
    bias = lax.all_gather(jnp.stack([jnp.pad(b, (0, model - b.shape[0])) for b in biases]), "tensor", axis=0)
    target_ids, memory_ids = target_ids.reshape(-1), memory_ids.reshape(-1)

    def weight(i):
        return full[:, i * width : (i + 1) * width]

    def padded(x):
        return jnp.pad(x, ((0, 0), (0, 0), (0, WIDE - width)))

    def project(x, i, row=None):
        value = jnp.einsum("td,swd->stw", x, weight(i), preferred_element_type=F32)
        if row is not None:
            value = value + bias[:, row, None, :width]
        return value.astype(BF)

    def attend(queries, keys, values, key_ids, causal):
        def split(x):
            return x.reshape(n_tensor, length, -1, HEAD_DIM)

        def one(items):
            q, k, v = items
            scores = jnp.einsum("qhd,khd->hqk", q, k, preferred_element_type=F32) * HEAD_DIM**-0.5
            allowed = target_ids[:, None] == key_ids[None, :]
            if causal:
                at = jnp.arange(length, dtype=jnp.int32)
                allowed = allowed & (at[:, None] >= at[None, :])
            scores = jnp.where(allowed[None], scores, NEGATIVE)
            probs = jax.nn.softmax(scores, axis=-1).astype(BF)
            out = jnp.einsum("hqk,khd->qhd", probs, v, preferred_element_type=F32)
            return out.astype(BF), jax.nn.logsumexp(scores, axis=-1)

        mixed, logs = lax.map(one, (split(queries), split(keys), split(values)))
        return mixed.reshape(n_tensor, length, width), logs.reshape(-1, length)

    def close(mixed, i, residual, row):
        value = residual + vectors[row] + jnp.einsum("stw,swd->td", mixed, weight(i), preferred_element_type=F32)
        centered = value - jnp.mean(value, axis=1, keepdims=True)
        scale = lax.rsqrt(jnp.mean(centered * centered, axis=1, keepdims=True) + EPSILON)
        hat = centered * scale
        normed = hat * vectors[row + 1] + vectors[row + 2]
        return hat, scale, normed, normed.astype(BF)

    sq, sk, sv = project(target, 0, 0), project(target, 1), project(target, 2, 1)
    sm, self_logs = attend(sq, sk, sv, target_ids, True)
    hat1, r1, first, low1 = close(sm, 3, target.astype(F32), 0)
    ck, cv, cq = project(memory, 4), project(memory, 5, 3), project(low1, 6, 2)
    cm, cross_logs = attend(cq, ck, cv, memory_ids, False)
    hat2, r2, _, low2 = close(cm, 7, first, 3)
    hidden = jnp.einsum("td,shd->sth", low2, full[:, head_rows : head_rows + hidden_rows], preferred_element_type=F32)
    act, slope = erf_pair(hidden + bias[:, 4, None, :])
    logs = jnp.concatenate((self_logs, cross_logs), axis=0).T
    logs = jnp.pad(logs, ((0, 0), (0, 128 - logs.shape[1])))
    spread = jnp.pad(jnp.concatenate((r1, r2), axis=1), ((0, 0), (0, 126)))
    heads = [padded(x) for x in (sq, sk, sv, sm, cq, ck, cv, cm)]
    kept = jnp.concatenate((full[:, : 3 * width], full[:, 4 * width : 6 * width]), axis=1)
    columns = padded(lax.dynamic_slice_in_dim(kept, lax.axis_index("tensor") * width, width, 2))
    return columns, full, *heads, logs, hat1, hat2, spread, low1, low2, act.astype(BF), slope.astype(BF)


def attend_back_kernel(
    heads, base, block, causal, q_ref, k_ref, v_ref, gm_ref, logs_ref, dots_ref, q_row_ref, k_row_ref, gq_ref, gk_ref,
    gv_ref, gq_sum, logs, dots, k_ids_ref, q_ids_ref, bounds
):
    length = q_ref.shape[1]
    lane = lax.broadcasted_iota(jnp.int32, (1, 128), 1)
    scale = HEAD_DIM**-0.5
    s = pl.program_id(0)

    @pl.when(s == 0)
    def _():
        logs[...] = jnp.transpose(logs_ref[...])
        dots[...] = jnp.transpose(dots_ref[...])
        k_ids_ref[...] = as_column(k_row_ref[...].astype(F32))
        q_ids_ref[...] = q_row_ref[...].astype(F32)
        if not causal:
            for b in range(length // block):
                ids = k_row_ref[:, b * block : (b + 1) * block]
                low = jnp.sum((q_row_ref[...] < jnp.min(ids)).astype(jnp.int32)) // block
                high = (jnp.sum((q_row_ref[...] <= jnp.max(ids)).astype(jnp.int32)) + block - 1) // block
                bounds[0, b] = low
                bounds[1, b] = high - low

    gq_sum[...] = jnp.zeros_like(gq_sum)

    def one_block(at, first, reach):
        k_span = pl.ds(at, block)
        q_span = pl.ds(first, reach)
        allowed = k_ids_ref[k_span, :] == q_ids_ref[:, q_span]
        if causal:
            allowed = allowed & (
                lax.broadcasted_iota(jnp.int32, (block, reach), 0) <= lax.broadcasted_iota(jnp.int32, (block, reach), 1)
            )
        grads = []
        for h in range(heads):
            mine = (lane // HEAD_DIM) == (h % 2)
            columns = slice(128 * (h // 2), 128 * (h // 2) + 128)
            keys = k_ref[0, k_span, columns]
            keys = jnp.where(mine, keys, jnp.zeros_like(keys))
            values = v_ref[0, k_span, columns]
            values = jnp.where(mine, values, jnp.zeros_like(values))
            queries = q_ref[0, q_span, columns]
            gm = gm_ref[0, q_span, columns]
            scores = dot_nt(keys * jnp.asarray(scale, BF), queries)
            probs = jnp.where(allowed, jnp.exp(scores - logs[pl.ds(base + heads * s + h, 1), q_span]), 0.0)
            grad_scores = (probs * (dot_nt(values, gm) - dots[pl.ds(heads * s + h, 1), q_span])).astype(BF)
            grads.append((dot_nn(grad_scores, queries) * scale, dot_nn(probs.astype(BF), gm)))
            gq_sum[q_span, columns] += dot_tn(grad_scores, keys)
        left = lane < HEAD_DIM
        for i, out_ref in enumerate((gk_ref, gv_ref)):
            out_ref[0, k_span, 0:128] = jnp.where(left, grads[0][i], grads[1][i]).astype(BF)
            out_ref[0, k_span, 128:256] = jnp.where(left, grads[2][i], 0.0).astype(BF)

    if causal:
        for b in range(length // block):
            one_block(b * block, b * block, length - b * block)
    else:

        @pl.loop(0, length // block)
        def _(b):
            start = pl.multiple_of(bounds[0, b] * block, block)
            for number in range(1, length // block + 1):

                @pl.when(bounds[1, b] == number)
                def _(number=number):
                    one_block(pl.multiple_of(b * block, block), start, number * block)

    gq_ref[0] = (gq_sum[...] * scale).astype(BF)


def attend_back(causal, base, queries, keys, values, grad_mixed, logs, dots, query_ids, key_ids):
    slices, length, wide = queries.shape
    part = pl.BlockSpec((1, length, wide), lambda i: (i, 0, 0))
    out = jax.ShapeDtypeStruct((slices, length, wide), BF)
    lanes = pl.BlockSpec((length, 128), lambda i: (0, 0))
    return pl.pallas_call(
        partial(attend_back_kernel, 3, base, 256, causal),
        grid=(slices,),
        in_specs=[part] * 4
        + [lanes, lanes, pl.BlockSpec((1, length), lambda i: (0, 0)), pl.BlockSpec((1, length), lambda i: (0, 0))],
        out_specs=[part] * 3,
        out_shape=[out] * 3,
        scratch_shapes=[
            pltpu.VMEM((length, wide), F32),
            pltpu.VMEM((128, length), F32),
            pltpu.VMEM((128, length), F32),
            pltpu.VMEM((length, 1), F32),
            pltpu.VMEM((1, length), F32),
            pltpu.SMEM((2, 8), jnp.int32),
        ],
        compiler_params=pltpu.CompilerParams(vmem_limit_bytes=60 * MIB),
    )(queries, keys, values, grad_mixed, logs, dots, query_ids, key_ids)


def norm_back(grad, hat, scale, gain):
    scaled = grad * gain
    return scale * (
        scaled - jnp.mean(scaled, axis=1, keepdims=True) - hat * jnp.mean(scaled * hat, axis=1, keepdims=True)
    )


def clear_first(sums_ref):
    @pl.when(pl.program_id(0) == 0)
    def _():
        sums_ref[...] = jnp.zeros_like(sums_ref)


def add_sums(sums_ref, rows):
    for row, value in rows:
        sums_ref[row : row + 1, :] += jnp.sum(value, axis=0, keepdims=True)


def head_products(grad_mixed, mixed, s, heads, dots):
    product = grad_mixed * mixed.astype(F32)
    lane = lax.broadcasted_iota(jnp.int32, (1, WIDE), 1)
    out_lane = lax.broadcasted_iota(jnp.int32, (1, 128), 1)
    for h in range(heads):
        total = jnp.sum(jnp.where(lane // HEAD_DIM == h, product, 0.0), axis=1, keepdims=True)
        dots = jnp.where(out_lane == heads * s + h, total, dots)
    return dots


def mixed_back(grad_low, out_weight, mixed_ref, gm_ref, dots_ref):
    slices = mixed_ref.shape[0]
    width = out_weight.shape[1]
    dots = jnp.zeros(dots_ref.shape, F32)
    for s in range(slices):
        grad_mixed = dot_nt(grad_low, out_weight[s]).astype(BF)
        grad_mixed = jnp.concatenate((grad_mixed, jnp.zeros((grad_mixed.shape[0], WIDE - width), BF)), axis=1)
        gm_ref[s] = grad_mixed
        dots = head_products(grad_mixed.astype(F32), mixed_ref[s], s, 3, dots)
    dots_ref[...] = dots


def feed_back_kernel(
    act_ref, slope_ref, hat2_ref, r_ref, grad_ref, mixed_ref, expand_ref, contract_ref, out_weight_ref,
    v0_ref, v1_ref, v2_ref, v3_ref, v4_ref, out_ref, grad_ffn_ref, grad_hidden_ref, grad_sum_ref, grad_cross_ref, gm_ref, dots_ref, sums_ref,
    vectors_ref
):
    slices = act_ref.shape[0]
    fill_rows(vectors_ref, (v0_ref, v1_ref, v2_ref, v3_ref, v4_ref))
    clear_first(sums_ref)
    vector = [vectors_ref[i : i + 1, :] for i in range(5)]
    hat2 = hat2_ref[...]
    value = hat2 * vector[0] + vector[1] + vector[2]
    for s in range(slices):
        value = value + dot_nn(act_ref[s], contract_ref[s])
    centered = value - jnp.mean(value, axis=1, keepdims=True)
    scale = lax.rsqrt(jnp.mean(centered * centered, axis=1, keepdims=True) + EPSILON)
    hat3 = centered * scale
    out_ref[...] = (hat3 * vector[3] + vector[4]).astype(BF)
    grad = grad_ref[...].astype(F32)
    grad_third = norm_back(grad, hat3, scale, vector[3])
    grad_ffn = grad_third.astype(BF)
    grad_ffn_ref[...] = grad_ffn
    grad_second = grad_third
    rows = [(0, grad * hat3), (1, grad), (2, grad_ffn.astype(F32))]
    for s in range(slices):
        grad_hidden = (dot_nt(grad_ffn, contract_ref[s]) * slope_ref[s].astype(F32)).astype(BF)
        grad_hidden_ref[s] = grad_hidden
        rows.append((8 + s, grad_hidden.astype(F32)))
        grad_second = grad_second + dot_nn(grad_hidden, expand_ref[s])
    grad_sum = norm_back(grad_second, hat2, r_ref[:, 1:2], vector[0])
    grad_sum_ref[...] = grad_sum
    grad_cross = grad_sum.astype(BF)
    grad_cross_ref[...] = grad_cross
    rows += [(3, grad_second * hat2), (4, grad_second), (5, grad_cross.astype(F32))]
    add_sums(sums_ref, rows)
    mixed_back(grad_cross, out_weight_ref, mixed_ref, gm_ref, dots_ref)


def feed_back(act, slope, hat2, spread, output_grad, mixed, full, vectors, head_rows):
    slices, length, units = act.shape
    model = hat2.shape[1]
    block = TOKEN_BLOCK
    width = head_rows // 8
    tokens = pl.BlockSpec((block, model), lambda i: (i, 0))
    lanes = pl.BlockSpec((block, 128), lambda i: (i, 0))
    wide = pl.BlockSpec((slices, block, units), lambda i: (0, i, 0))
    heads = pl.BlockSpec((slices, block, WIDE), lambda i: (0, i, 0))
    rows = pl.BlockSpec((16, model), lambda i: (0, 0))

    def weight(first, size):
        return pl.BlockSpec((slices, size, model), lambda i: (0, first // size, 0))

    low = jax.ShapeDtypeStruct((length, model), BF)
    return pl.pallas_call(
        feed_back_kernel,
        grid=(length // block,),
        in_specs=[wide, wide, tokens, lanes, tokens, heads]
        + [weight(head_rows, units), weight(head_rows + units, units), weight(7 * width, width)]
        + [pl.BlockSpec((model,), lambda i: (0,))] * 5,
        scratch_shapes=[pltpu.VMEM((8, model), F32)],
        out_specs=[tokens, tokens, wide, tokens, tokens, heads, lanes, rows],
        out_shape=[
            low,
            low,
            jax.ShapeDtypeStruct(act.shape, BF),
            jax.ShapeDtypeStruct((length, model), F32),
            low,
            jax.ShapeDtypeStruct((slices, length, WIDE), BF),
            jax.ShapeDtypeStruct((length, 128), F32),
            jax.ShapeDtypeStruct((16, model), F32),
        ],
        compiler_params=pltpu.CompilerParams(vmem_limit_bytes=62 * MIB),
    )(act, slope, hat2, spread, output_grad, mixed, full, full, full, *vectors)


def first_back_kernel(
    z_ref, gq_ref, grad_sum_ref, hat1_ref, r_ref, mixed_ref, query_ref, out_weight_ref, gain_ref,
    rest_ref, grad_self_ref, gm_ref, dots_ref, sums_ref, vectors_ref
):
    fill_rows(vectors_ref, (gain_ref,))
    clear_first(sums_ref)
    slices = gq_ref.shape[0]
    width = query_ref.shape[1]
    grad = grad_sum_ref[...]
    for s in range(slices):
        grad = grad + dot_nn(gq_ref[s][:, :width], query_ref[s])
    hat = hat1_ref[...]
    grad_first = norm_back(grad, hat, r_ref[:, 0:1], vectors_ref[0:1, :])
    rest_ref[...] = pltpu.roll(grad_first, grad_first.shape[1] - z_ref[0] * width, 1)[:, :width]
    grad_self = grad_first.astype(BF)
    grad_self_ref[...] = grad_self
    add_sums(sums_ref, [(0, grad * hat), (1, grad), (2, grad_self.astype(F32))])
    mixed_back(grad_self, out_weight_ref, mixed_ref, gm_ref, dots_ref)


def first_back(z, gq, grad_sum, hat1, spread, mixed, full, vectors, head_rows):
    slices, length, _ = gq.shape
    model = hat1.shape[1]
    block = TOKEN_BLOCK
    width = head_rows // 8
    tokens = pl.BlockSpec((block, model), lambda i, _: (i, 0))
    lanes = pl.BlockSpec((block, 128), lambda i, _: (i, 0))
    share = pl.BlockSpec((block, width), lambda i, _: (i, 0))
    heads = pl.BlockSpec((slices, block, WIDE), lambda i, _: (0, i, 0))
    rows = pl.BlockSpec((8, model), lambda i, _: (0, 0))
    return pl.pallas_call(
        first_back_kernel,
        grid_spec=pltpu.PrefetchScalarGridSpec(
            num_scalar_prefetch=1,
            grid=(length // block,),
            in_specs=[heads, tokens, tokens, lanes, heads]
            + [pl.BlockSpec((slices, width, model), lambda i, _, j=j: (0, j, 0)) for j in (6, 3)]
            + [pl.BlockSpec((model,), lambda i, _: (0,))],
            scratch_shapes=[pltpu.VMEM((8, model), F32)],
            out_specs=[share, tokens, heads, lanes, rows],
        ),
        out_shape=[
            jax.ShapeDtypeStruct((length, width), F32),
            jax.ShapeDtypeStruct((length, model), BF),
            jax.ShapeDtypeStruct((slices, length, WIDE), BF),
            jax.ShapeDtypeStruct((length, 128), F32),
            jax.ShapeDtypeStruct((8, model), F32),
        ],
        compiler_params=pltpu.CompilerParams(vmem_limit_bytes=62 * MIB),
    )(z.reshape(1), gq, grad_sum, hat1, spread, mixed, full, full, vectors)


def input_grad_kernel(count, *refs):
    out_ref = refs[-1]
    weight_ref = refs[count]
    slices = refs[0].shape[0]
    width = weight_ref.shape[1] // count
    total = refs[count + 1][...] if len(refs) == count + 3 else jnp.zeros(out_ref.shape, F32)
    for i in range(count):
        for s in range(slices):
            total = total + dot_nn(refs[i][s][:, :width], weight_ref[s, i * width : (i + 1) * width, :])
    out_ref[...] = total.astype(BF)


def input_grad(grads, weights, rest=None):
    slices, length, wide = grads[0].shape
    share = weights.shape[2]
    block = length // 2
    tokens = pl.BlockSpec((block, share), lambda i: (i, 0))
    specs = [pl.BlockSpec((slices, block, wide), lambda i: (0, i, 0))] * len(grads)
    specs.append(pl.BlockSpec(weights.shape, lambda i: (0, 0, 0)))
    operands = (*grads, weights)
    if rest is not None:
        operands += (rest,)
        specs.append(tokens)
    return pl.pallas_call(
        partial(input_grad_kernel, len(grads)),
        grid=(2,),
        in_specs=specs,
        out_specs=tokens,
        out_shape=jax.ShapeDtypeStruct((length, share), BF),
        compiler_params=pltpu.CompilerParams(vmem_limit_bytes=60 * MIB),
    )(*operands)


def weight_grad_kernel(plan, width, z_ref, *refs):
    del z_ref
    out_ref, sums_ref = refs[-2:]
    sums_ref[...] = jnp.zeros_like(sums_ref)
    products = []
    index = 0
    row = 0
    for count in plan:
        left = refs[index][...]
        rights = [refs[index + 1 + i][0][:, :width] for i in range(count)]
        index += 1 + count
        for right in rights:
            sums_ref[row : row + 1, 0:width] = jnp.sum(right.astype(F32), axis=0, keepdims=True)
            row += 1
        products.append(dot_tn(left, rights[0] if count == 1 else jnp.concatenate(rights, axis=1)))
    out_ref[...] = jnp.concatenate(products, axis=1)


def weight_grad(z, width, *pairs):
    operands, specs = [], []
    for left, rights in pairs:
        operands.append(left)
        specs.append(pl.BlockSpec(left.shape, lambda i, z_ref: (0, 0)))
        for right in rights:
            operands.append(right)
            specs.append(pl.BlockSpec((1,) + right.shape[1:], lambda i, z_ref: (z_ref[0], 0, 0)))
    model = pairs[0][0].shape[1]
    plan = [len(rights) for _, rights in pairs]
    return pl.pallas_call(
        partial(weight_grad_kernel, plan, width),
        grid_spec=pltpu.PrefetchScalarGridSpec(
            num_scalar_prefetch=1,
            grid=(1,),
            in_specs=specs,
            out_specs=[
                pl.BlockSpec((model, sum(plan) * width), lambda i, z_ref: (0, 0)),
                pl.BlockSpec((8, model), lambda i, z_ref: (0, 0)),
            ],
        ),
        out_shape=[jax.ShapeDtypeStruct((model, sum(plan) * width), F32), jax.ShapeDtypeStruct((8, model), F32)],
        compiler_params=pltpu.CompilerParams(vmem_limit_bytes=60 * MIB),
    )(z.reshape(1), *operands)


def products_kernel(
    width, z_ref, low2_ref, gh_ref, gf_ref, act_ref, low1_ref, gcq_ref, memory_ref, gck_ref, gcv_ref, gc_ref, cm_ref,
    out_f_ref, out_c_ref, sums_ref, low2, gh, gf, act, low1, gcq, memory, gck, gcv, gc, cm, prod_f, prod_c, load_sem, out_sem
):
    z = z_ref[0]
    whole = ((low2_ref, low2), (gf_ref, gf), (low1_ref, low1), (memory_ref, memory), (gc_ref, gc))
    sliced = ((gh_ref, gh), (act_ref, act), (gcq_ref, gcq), (gck_ref, gck), (gcv_ref, gcv), (cm_ref, cm))
    loads = [pltpu.make_async_copy(source, place, load_sem.at[i]) for i, (source, place) in enumerate(whole)]
    parts = [pltpu.make_async_copy(source.at[z], place, load_sem.at[5 + i]) for i, (source, place) in enumerate(sliced)]
    order = [loads[0], parts[0], loads[1], parts[1], loads[2], parts[2], loads[3], parts[3], parts[4], loads[4], parts[5]]
    for load in order:
        load.start()
    units = gh.shape[1]
    outs = []
    for i, (left, right) in enumerate(((low2, gh), (gf, act))):
        for load in order[2 * i : 2 * i + 2]:
            load.wait()
        columns = pl.ds(i * units, units)
        prod_f[:, columns] = dot_tn(left[...], right[...])
        outs.append(pltpu.make_async_copy(prod_f.at[:, columns], out_f_ref.at[:, columns], out_sem.at[i]))
        outs[-1].start()
    for load in order[4:]:
        load.wait()
    queries, keys, values = (x[:, :width] for x in (gcq, gck, gcv))
    prod_c[...] = jnp.concatenate(
        (
            dot_tn(low1[...], queries),
            dot_tn(memory[...], jnp.concatenate((keys, values), axis=1)),
            dot_tn(gc[...], cm[:, :width]),
        ),
        axis=1,
    )
    outs.append(pltpu.make_async_copy(prod_c, out_c_ref, out_sem.at[2]))
    outs[-1].start()
    sums_ref[...] = jnp.zeros_like(sums_ref)
    sums_ref[0:1, 0:width] = jnp.sum(queries.astype(F32), axis=0, keepdims=True)
    sums_ref[2:3, 0:width] = jnp.sum(values.astype(F32), axis=0, keepdims=True)
    for out in outs:
        out.wait()


def products(z, width, low2, grad_hidden, grad_ffn, act, low1, gcq, memory, gck, gcv, grad_cross, cm):
    length, model = low2.shape
    units = act.shape[2]
    anywhere = pl.BlockSpec(memory_space=pl.ANY)
    tokens = pltpu.VMEM((length, model), BF)
    hidden = pltpu.VMEM((length, units), BF)
    heads = pltpu.VMEM((length, gcq.shape[2]), BF)
    shapes = [(model, 2 * units), (model, 4 * width)]
    return pl.pallas_call(
        partial(products_kernel, width),
        grid_spec=pltpu.PrefetchScalarGridSpec(
            num_scalar_prefetch=1,
            grid=(1,),
            in_specs=[anywhere] * 11,
            out_specs=[anywhere, anywhere, pl.BlockSpec((8, model), lambda i, _: (0, 0))],
            scratch_shapes=[tokens, hidden, tokens, hidden, tokens, heads, tokens, heads, heads, tokens, heads]
            + [pltpu.VMEM(shape, F32) for shape in shapes]
            + [pltpu.SemaphoreType.DMA((11,)), pltpu.SemaphoreType.DMA((3,))],
        ),
        out_shape=[jax.ShapeDtypeStruct(shape, F32) for shape in shapes] + [jax.ShapeDtypeStruct((8, model), F32)],
        compiler_params=pltpu.CompilerParams(vmem_limit_bytes=60 * MIB),
    )(z.reshape(1), low2, grad_hidden, grad_ffn, act, low1, gcq, memory, gck, gcv, grad_cross, cm)


def scattered(partial_sums):
    return lax.psum_scatter(partial_sums, "dp", scatter_dimension=0, tiled=True)


def finish_kernel(
    width, prod_f_ref, prod_c_ref, q_ref, k_ref, v_ref, gm_ref, sm_ref, gck_ref, gcv_ref, target_ref, grad_self_ref,
    logs_ref, dots_ref, t_ids_ref, columns_ref, rest_ref, sums_ref, cross_sums_ref, first_sums_ref,
    total_f_ref, total_c_ref, total_s_ref, vector_total_ref, target_grad_ref, memory_grad_ref,
    q_all, k_all, v_all, gm_all, sm_own, gck_all, gcv_all, target, grad_self, gq_all, gk_all, gv_all, gq_sum, logs, dots,
    mine_f, mine_c, prod_s, land_f, land_c, land_s, one_f, one_c, one_s, two_f, two_c, two_s, vec, vec_land, t_col_ref, t_row_ref,
    send_sem, recv_sem, load_sem,
):
    d = lax.axis_index("dp")
    z = lax.axis_index("tensor")
    c = d % 2
    x = (d // 2) % 2
    y = d // 4
    dc = d + 1 - 2 * c
    dx = d + 2 - 4 * x
    dy = d + 4 - 8 * y
    slices, length, _ = q_all.shape
    heads = 3

    def to(slot, source, place, other):
        return pltpu.make_async_remote_copy(
            src_ref=source,
            dst_ref=place,
            send_sem=send_sem.at[slot],
            recv_sem=recv_sem.at[slot],
            device_id={"dp": other},
            device_id_type=MESH,
        )

    families = (
        (prod_f_ref, mine_f, land_f, one_f, two_f, total_f_ref),
        (prod_c_ref, mine_c, land_c, one_c, two_c, total_c_ref),
        (prod_s, None, land_s, one_s, two_s, total_s_ref),
    )

    def over_core(i):
        return to(5 * i, families[i][0].at[:, :, 1 - c], families[i][2], dc)

    def halves(i):
        half = families[i][2].shape[3] // 2
        return pl.ds(0, half), pl.ds(half, half)

    def first_a(i):
        return to(5 * i + 1, families[i][2].at[:, 1 - x, :, halves(i)[0]], families[i][3].at[0], dx)

    def first_b(i):
        return to(5 * i + 2, families[i][2].at[1 - y, :, :, halves(i)[1]], families[i][3].at[1], dy)

    def second_a(i):
        return to(5 * i + 3, families[i][3].at[0, 1 - y], families[i][4].at[0], dy)

    def second_b(i):
        return to(5 * i + 4, families[i][3].at[1, 1 - x], families[i][4].at[1], dx)

    def after_core(i):
        _, mine, land, _, _, _ = families[i]
        over_core(i).wait_recv()

        @pl.loop(0, 4)
        def _(j):
            part = prod_s[j // 2, j % 2, c] if mine is None else mine[j // 2, j % 2]
            land[j // 2, j % 2] = land[j // 2, j % 2] + part

        first_a(i).start()
        first_b(i).start()

    def after_first(i):
        _, _, land, one, _, _ = families[i]
        first_a(i).wait_recv()
        first_b(i).wait_recv()
        left, right = halves(i)
        for j in range(2):
            one[0, j] = one[0, j] + land[j, x, :, left]
            one[1, j] = one[1, j] + land[y, j, :, right]
        second_a(i).start()
        second_b(i).start()

    def after_second(i):
        _, _, _, one, two, total_ref = families[i]
        second_a(i).wait_recv()
        second_b(i).wait_recv()
        left, right = halves(i)
        total_ref[:, left] = one[0, y] + two[0]
        total_ref[:, right] = one[1, x] + two[1]

    def vector_copy(i):
        return to(15 + i, vec.at[i], vec_land.at[i], (dc, dx, dy)[i])

    def vector_step(i):
        vector_copy(i).wait_recv()
        vec[i + 1] = vec[i] + vec_land[i]
        if i < 2:
            vector_copy(i + 1).start()

    barrier = pltpu.get_barrier_semaphore()
    for other in (dc, dx, dy):
        pl.semaphore_signal(barrier, inc=1, device_id={"dp": other}, device_id_type=MESH)

    def slice_loads(s):
        pairs = ((q_ref, q_all), (k_ref, k_all), (v_ref, v_all), (gm_ref, gm_all))
        return [
            pltpu.make_async_copy(source.at[s], place.at[s], load_sem.at[4 * s + i])
            for i, (source, place) in enumerate(pairs)
        ]

    late = 4 * slices
    late_loads = [
        pltpu.make_async_copy(sm_ref.at[z], sm_own, load_sem.at[late]),
        pltpu.make_async_copy(target_ref, target, load_sem.at[late + 1]),
        pltpu.make_async_copy(grad_self_ref, grad_self, load_sem.at[late + 2]),
        pltpu.make_async_copy(gck_ref, gck_all, load_sem.at[late + 3]),
        pltpu.make_async_copy(gcv_ref, gcv_all, load_sem.at[late + 4]),
    ]
    mine_loads = [
        pltpu.make_async_copy(prod_f_ref.at[:, :, c], mine_f, load_sem.at[late + 5]),
        pltpu.make_async_copy(prod_c_ref.at[:, :, c], mine_c, load_sem.at[late + 6]),
    ]
    for s in range(slices):
        for load in slice_loads(s):
            load.start()
    for load in mine_loads + late_loads:
        load.start()
    pl.semaphore_wait(barrier, 3)
    over_core(0).start()
    over_core(1).start()
    t_row_ref[...] = t_ids_ref[...].astype(F32)
    t_col_ref[...] = as_column(t_row_ref[...])
    logs[...] = jnp.transpose(logs_ref[...])
    dots[...] = jnp.transpose(dots_ref[...])

    vec[0] = jnp.zeros(vec.shape[1:], F32)
    for row, source, at in (
        (2, first_sums_ref, 2), (3, first_sums_ref, 0), (4, first_sums_ref, 1), (5, cross_sums_ref, 0),
        (6, cross_sums_ref, 2), (7, sums_ref, 5), (8, sums_ref, 3), (9, sums_ref, 4), (11, sums_ref, 2),
        (12, sums_ref, 0), (13, sums_ref, 1),
    ):
        vec[0, row : row + 1, :] = source[at : at + 1, :]
    vec[0, 10:11, :] = sums_ref[pl.ds(8 + z, 1), :]

    lane = lax.broadcasted_iota(jnp.int32, (1, 128), 1)
    scale = HEAD_DIM**-0.5
    block = 256

    def one_block(s, at):
        reach = length - at
        span = slice(at, at + block)
        allowed = (t_col_ref[span, :] == t_row_ref[:, at:]) & (
            lax.broadcasted_iota(jnp.int32, (block, reach), 0) <= lax.broadcasted_iota(jnp.int32, (block, reach), 1)
        )
        grads = []
        for h in range(heads):
            mine = (lane // HEAD_DIM) == (h % 2)
            columns = slice(128 * (h // 2), 128 * (h // 2) + 128)
            keys = k_all[s, span, columns]
            keys = jnp.where(mine, keys, jnp.zeros_like(keys))
            values = v_all[s, span, columns]
            values = jnp.where(mine, values, jnp.zeros_like(values))
            queries = q_all[s, at:, columns]
            gm = gm_all[s, at:, columns]
            scores = dot_nt(keys * jnp.asarray(scale, BF), queries)
            row = pl.ds(heads * s + h, 1)
            probs = jnp.where(allowed, jnp.exp(scores - logs[row, at:]), 0.0)
            grad_scores = (probs * (dot_nt(values, gm) - dots[row, at:])).astype(BF)
            grads.append((dot_nn(grad_scores, queries) * scale, dot_nn(probs.astype(BF), gm)))
            gq_sum[at:, columns] += dot_tn(grad_scores, keys)
        left = lane < HEAD_DIM
        for i, out in enumerate((gk_all, gv_all)):
            out[s, span, 0:128] = jnp.where(left, grads[0][i], grads[1][i]).astype(BF)
            out[s, span, 128:256] = jnp.where(left, grads[2][i], 0.0).astype(BF)

    for s in range(slices):
        for load in slice_loads(s):
            load.wait()

    def own_products():
        for load in late_loads[:3]:
            load.wait()
        right = jnp.concatenate((gq_all[z][:, :width], gk_all[z][:, :width], gv_all[z][:, :width]), axis=1)
        products = jnp.concatenate((dot_tn(target[...], right), dot_tn(grad_self[...], sm_own[:, :width])), axis=1)
        prod_s[...] = products.reshape(prod_s.shape)
        vec[0, 0:1, 0:width] = jnp.sum(gq_all[z][:, :width].astype(F32), axis=0, keepdims=True)
        vec[0, 1:2, 0:width] = jnp.sum(gv_all[z][:, :width].astype(F32), axis=0, keepdims=True)
        over_core(2).start()
        vector_copy(0).start()

    @pl.loop(0, slices)
    def _(j):
        s = (z + j) % slices
        gq_sum[...] = jnp.zeros_like(gq_sum)
        for at in range(0, length, block):
            one_block(s, at)
        gq_all[s] = (gq_sum[...] * scale).astype(BF)

        @pl.when(j == 0)
        def _():
            for load in mine_loads:
                load.wait()
            after_core(0)
            after_core(1)
            own_products()

        @pl.when(j == 1)
        def _():
            after_core(2)
            vector_step(0)

        @pl.when(j == 2)
        def _():
            after_first(0)
            after_first(1)
            vector_step(1)

    for load in late_loads[3:]:
        load.wait()

    def input_grad(grads, first, rest, out_ref):
        @pl.loop(0, 4)
        def _(i):
            span = pl.ds(pl.multiple_of(i * (length // 4), length // 4), length // 4)
            total = 0.0
            for j, grad in enumerate(grads):
                for s in range(slices):
                    weight = columns_ref[s, (first + j) * width : (first + j + 1) * width, :]
                    total = total + dot_nn(grad[s, span, :width], weight)
            total = total[:, :width]
            if rest is not None:
                total = total + rest[span, :]
            out_ref[span, :] = total.astype(BF)

    after_first(2)
    input_grad((gq_all, gk_all, gv_all), 0, rest_ref, target_grad_ref)
    after_second(0)
    input_grad((gck_all, gcv_all), 3, None, memory_grad_ref)
    after_second(1)
    vector_step(2)
    after_second(2)
    vector_total_ref[...] = vec[3]
    for i in range(3):
        over_core(i).wait_send()
        for copy in (first_a(i), first_b(i), second_a(i), second_b(i)):
            copy.wait_send()
        vector_copy(i).wait_send()


def finish(prod_f, prod_c, heads, cross_grads, target, grad_self, logs, dots, ids, columns, rest, sums, cross_sums, first_sums):
    slices, length, wide = heads[0].shape
    model = target.shape[1]
    width = model // slices
    n = model // 8
    anywhere = pl.BlockSpec(memory_space=pl.ANY)
    inside = pl.BlockSpec(memory_space=pltpu.VMEM)
    columns_f, columns_c = prod_f.shape[1], prod_c.shape[1]

    def half(size):
        return pltpu.VMEM((2, 2, n, size), F32)

    sizes = (columns_f, columns_c, model)
    group = pltpu.VMEM((slices, length, wide), BF)
    tokens = pltpu.VMEM((length, model), BF)
    share = jax.ShapeDtypeStruct((length, model // slices), BF)
    return pl.pallas_call(
        partial(finish_kernel, width),
        out_shape=[jax.ShapeDtypeStruct((n, size), F32) for size in sizes]
        + [jax.ShapeDtypeStruct((16, model), F32), share, share],
        in_specs=[anywhere] * 11 + [inside] * 8,
        out_specs=[inside] * 6,
        scratch_shapes=[group] * 4
        + [pltpu.VMEM((length, wide), BF), group, group, tokens, tokens, group, group, group]
        + [pltpu.VMEM((length, wide), F32), pltpu.VMEM((128, length), F32), pltpu.VMEM((128, length), F32)]
        + [half(columns_f), half(columns_c), pltpu.VMEM((2, 2, 2, n, model), F32)]
        + [half(size) for size in sizes]
        + [pltpu.VMEM((2, 2, n, size // 2), F32) for size in sizes]
        + [pltpu.VMEM((2, n, size // 2), F32) for size in sizes]
        + [pltpu.VMEM((4, 16, model), F32), pltpu.VMEM((3, 16, model), F32), pltpu.VMEM((length, 1), F32), pltpu.VMEM((1, length), F32)]
        + [pltpu.SemaphoreType.DMA((18,)), pltpu.SemaphoreType.DMA((18,)), pltpu.SemaphoreType.DMA((4 * slices + 7,))],
        compiler_params=pltpu.CompilerParams(collective_id=1, has_side_effects=True, vmem_limit_bytes=63 * MIB),
    )(
        prod_f.reshape(2, 2, 2, n, columns_f), prod_c.reshape(2, 2, 2, n, columns_c), *heads, *cross_grads, target,
        grad_self, logs, dots, ids, columns, rest, sums, cross_sums, first_sums,
    )


def part_kernel(width, units, total_f_ref, total_c_ref, total_s_ref, vectors_ref, target_ref, memory_ref, *outs):
    matrices, lines, inputs = outs[:10], outs[10:-2], outs[-2:]
    for out, ref in zip(inputs, (target_ref, memory_ref), strict=True):
        out[...] = jnp.transpose(ref[...].astype(F32)).astype(BF)
    for i, ref in enumerate((total_s_ref, total_c_ref)):
        for j in range(4):
            part = ref[:, j * width : (j + 1) * width]
            matrices[4 * i + j][...] = part.T if j == 3 else part
    matrices[8][...] = total_f_ref[:, :units]
    matrices[9][...] = total_f_ref[:, units:]
    for i, out in enumerate(lines):
        out[...] = vectors_ref[i, : out.shape[0]]


def parts_of(total_f, total_c, total_s, vectors, target_grad, memory_grad, width, units):
    n, model = total_s.shape
    matrices = [(n, width), (n, width), (n, width), (width, n)] * 2 + [(n, units)] * 2
    lines = [width, width, model, model, model, width, width] + [model] * 3 + [units] + [model] * 3
    out = pl.pallas_call(
        partial(part_kernel, width, units),
        out_shape=[jax.ShapeDtypeStruct(shape, F32) for shape in matrices]
        + [jax.ShapeDtypeStruct((size,), F32) for size in lines]
        + [jax.ShapeDtypeStruct(target_grad.shape[::-1], BF)] * 2,
    )(total_f, total_c, total_s, vectors, target_grad, memory_grad)
    return [*out[:9], out[9].T], out[10:-2], out[-2].T, out[-1].T


def per_device(
    n_dp, n_tensor, target, memory, target_segments, memory_segments, self_query, self_query_bias, self_key, self_value,
    self_value_bias, self_output, self_output_bias, first_gain, first_shift, cross_query, cross_query_bias, cross_key,
    cross_value, cross_value_bias, cross_output, cross_output_bias, second_gain, second_shift, expand_weight, expand_bias,
    contract_weight, contract_bias, third_gain, third_shift, output_grad,
):
    model, width = self_query.shape
    units = expand_weight.shape[1]
    head_rows = 8 * width
    z = lax.axis_index("tensor")
    target_ids = target_segments.reshape(1, -1)
    memory_ids = memory_segments.reshape(1, -1)

    own = (
        self_query, self_key, self_value, self_output, cross_key, cross_value, cross_query, cross_output, expand_weight,
        contract_weight,
    )

    def rows_of(count, vectors):
        return jnp.stack([jnp.pad(v, (0, model - v.shape[0])) for v in vectors] + [jnp.zeros(model, F32)] * (count - len(vectors)))

    biases = (self_query_bias, self_value_bias, cross_query_bias, cross_value_bias, expand_bias)
    vectors = (self_output_bias, first_gain, first_shift, cross_output_bias, second_gain, second_shift)
    run = forward if (n_dp, n_tensor) == (8, 4) else forward_plain
    columns, full, sq, sk, sv, sm, cq, ck, cv, cm, logs, hat1, hat2, spread, low1, low2, act, slope = run(
        own, biases, target, memory, target_ids, memory_ids, vectors, n_dp, n_tensor, head_rows, units
    )
    layer_output, grad_ffn, grad_hidden, grad_second_sum, grad_cross, gcm, cross_dots, sums = feed_back(
        act, slope, hat2, spread, output_grad, cm, full,
        (second_gain, second_shift, contract_bias, third_gain, third_shift), head_rows,
    )
    gcq, gck, gcv = attend_back(False, 3 * n_tensor, cq, ck, cv, gcm, logs, cross_dots, target_ids, memory_ids)
    ffn_products, cross_products, cross_sums = products(
        z, width, low2, grad_hidden, grad_ffn, act, low1, gcq, memory, gck, gcv, grad_cross, cm
    )
    rest, grad_self, gsm, self_dots, first_sums = first_back(
        z, gcq, grad_second_sum, hat1, spread, sm, full, first_gain, head_rows
    )
    if (n_dp, n_tensor) == (8, 4):
        total_f, total_c, total_s, vectors, target_grad, memory_grad = finish(
            ffn_products, cross_products, (sq, sk, sv, gsm, sm), (gck, gcv), target, grad_self, logs, self_dots, target_ids,
            columns, rest, sums, cross_sums, first_sums,
        )
    else:
        gsq, gsk, gsv = attend_back(True, 0, sq, sk, sv, gsm, logs, self_dots, target_ids, target_ids)
        self_products, self_sums = weight_grad(z, width, (target, [gsq, gsk, gsv]), (grad_self, [sm]))
        total_f, total_c, total_s = scattered(ffn_products), scattered(cross_products), scattered(self_products)
        memory_grad = input_grad((gck, gcv), columns[:, 3 * width :, :width])
        target_grad = input_grad((gsq, gsk, gsv), columns[:, : 3 * width, :width], rest)
        vectors = (
            self_sums[0], self_sums[2], first_sums[2], first_sums[0], first_sums[1], cross_sums[0], cross_sums[2], sums[5],
            sums[3], sums[4], lax.dynamic_index_in_dim(sums, 8 + z, 0, keepdims=False), sums[2], sums[0], sums[1],
        )
        vectors = lax.psum(rows_of(16, vectors), "dp")
    parts, totals, target_grad, memory_grad = parts_of(
        total_f, total_c, total_s, vectors, target_grad, memory_grad, width, units
    )
    return (
        layer_output, target_grad, memory_grad, parts[0], totals[0], parts[1], parts[2], totals[1], parts[3], totals[2],
        totals[3], totals[4], parts[4], totals[5], parts[5], parts[6], totals[6], parts[7], totals[7], totals[8], totals[9],
        parts[8], totals[10], parts[9], totals[11], totals[12], totals[13],
    )


def solution(mesh):
    rows = P("dp", None)
    split = P(None, "tensor")
    both = P("dp", "tensor")
    turned = P("tensor", "dp")
    own = P("tensor")
    in_specs = (
        rows, rows, rows, rows,
        split, own, split, split, own, P("tensor", None), P(), P(), P(),
        split, own, split, split, own, P("tensor", None), P(), P(), P(),
        split, own, P("tensor", None), P(), P(), P(),
        rows,
    )
    out_specs = (
        rows, both, both,
        both, own, both, both, own, turned, P(), P(), P(),
        both, own, both, both, own, turned, P(), P(), P(),
        both, own, turned, P(), P(), P(),
    )
    return jax.shard_map(
        partial(per_device, mesh.shape["dp"], mesh.shape["tensor"]),
        mesh=mesh,
        in_specs=in_specs,
        out_specs=out_specs,
        check_vma=False,
    )
```

```python
from functools import partial

import jax
import jax.numpy as jnp
from jax import lax
from jax.experimental import pallas as pl
from jax.experimental.pallas import tpu as pltpu
from jax.sharding import PartitionSpec as P

HEAD_DIM = 64
EPSILON = 1e-05
NEGATIVE = -1e30
BF = jnp.bfloat16
F32 = jnp.float32
MESH = pl.DeviceIdType.MESH
MIB = 2**20


def dot_nn(a, b):
    return lax.dot_general(a, b, (((1,), (0,)), ((), ())), preferred_element_type=F32)


def dot_nt(a, b):
    return lax.dot_general(a, b, (((1,), (1,)), ((), ())), preferred_element_type=F32)


def dot_tn(a, b):
    return lax.dot_general(a, b, (((0,), (0,)), ((), ())), preferred_element_type=F32)


WIDE = 256
TOKEN_BLOCK = 256


def as_column(row):
    return jnp.transpose(jnp.broadcast_to(row, (128, row.shape[1])))[:, 0:1]


def fill_rows(rows_ref, lines):
    rows_ref[...] = jnp.zeros_like(rows_ref)
    for i, line in enumerate(lines):
        rows_ref[i, 0 : line.shape[0]] = line[...]


def erf_pair(hidden):
    phi = 0.5 * (1.0 + lax.erf(hidden * 0.7071067811865476))
    slope = phi + hidden * (jnp.exp(-0.5 * hidden * hidden) * 0.3989422804014327)
    return hidden * phi, slope


def forward_kernel(
    n_dp, n_tensor, count, rows, head_rows, hidden_rows,
    sqw_ref, skw_ref, svw_ref, sow_ref, ckw_ref, cvw_ref, cqw_ref, cow_ref, exw_ref, ctw_ref, target_ref, memory_ref, t_ids_ref, m_ids_ref,
    b0_ref, b1_ref, b2_ref, b3_ref, b4_ref, v0_ref, v1_ref, v2_ref, v3_ref, v4_ref, v5_ref,
    chunk_ref, found_ref, full_ref, sq_ref, sk_ref, sv_ref, sm_ref, cq_ref, ck_ref, cv_ref, cm_ref, logs_ref, hat1_ref, hat2_ref,
    r_ref, low1_ref, low2_ref, act_ref, slope_ref,
    vectors_ref, bias_ref, t_row_ref, m_row_ref, t_col_ref, stage, full, low, bias, q_all, k_all, v_all, mixed, logs, hat1, hat2, spread, low1, low2, act, slope,
    send_sem, recv_sem, bias_send, bias_recv, load_sem, store_sem, out_sem,
):
    d = lax.axis_index("dp")
    z = lax.axis_index("tensor")
    others = n_tensor - 1
    length, model = target_ref.shape
    size = n_dp * rows
    dc = d + 1 - 2 * (d % 2)
    dx = d + 2 - 4 * ((d // 2) % 2)
    dy = d + 4 - 8 * (d // 4)
    dxy = dx + 4 - 8 * (d // 4)

    def slice_of(k):
        return (z + others - k) % n_tensor

    def along_z(g, source, k, step, slot):
        return pltpu.make_async_remote_copy(
            src_ref=source,
            dst_ref=found_ref.at[d, k, pl.ds(g * rows, rows)],
            send_sem=send_sem.at[g, slot],
            recv_sem=recv_sem.at[g, k],
            device_id={"tensor": z + step},
            device_id_type=MESH,
        )

    near = ((1, 0, 0), (2, 1, 1), (-1, 2, 2), (-2, 1, 11))

    def own_along(g, step, k, slot):
        return along_z(g, chunk_ref.at[pl.ds(g * rows, rows)], k, step, slot)

    def reaches(step):
        return z + step <= others if step > 0 else z + step >= 0

    inner = jnp.logical_and(z > 0, z < others)

    def relay(g):
        step = 2 * z - 3
        return along_z(g, found_ref.at[d, 1, pl.ds(g * rows, rows)], 1 + step, step, 12)

    def from_z(g, k):
        own_along(g, 0, k, 0).wait_recv()

    lead = 2

    def own_z(g):
        for step_z, k, slot in near:

            @pl.when(reaches(step_z))
            def _(step_z=step_z, k=k, slot=slot):
                own_along(g, step_z, k, slot).start()

    def pass_z(g):
        @pl.when(inner)
        def _():
            from_z(g, 1)
            relay(g).start()

        if g + lead < count:
            own_z(g + lead)

    def in_plane(g, slot, chunk, half, other):
        span = pl.ds(g * rows, rows) if half is None else pl.ds(g * rows + half * (rows // 2), rows // 2)
        piece = found_ref.at[chunk, :, span]
        return pltpu.make_async_remote_copy(
            src_ref=piece,
            dst_ref=piece,
            send_sem=send_sem.at[g, slot],
            recv_sem=recv_sem.at[g, slot],
            device_id={"dp": other},
            device_id_type=MESH,
        )

    def bias_copy(k):
        return pltpu.make_async_remote_copy(
            src_ref=bias_ref,
            dst_ref=bias.at[z],
            send_sem=bias_send.at[k],
            recv_sem=bias_recv.at[k],
            device_id={"tensor": (z + k + 1) % n_tensor},
            device_id_type=MESH,
        )

    routes = {3: (d, None, dx), 4: (d, None, dy), 5: (d, None, dc), 6: (dx, 0, dy), 7: (dy, 1, dx)}
    routes.update({8 + i: (chunk, None, dc) for i, chunk in enumerate((dx, dy, dxy))})

    def send(g, slot):
        return in_plane(g, slot, *routes[slot])

    def arrive(g, slot, half=None):
        in_plane(g, slot, d, half, dc).wait_recv()

    def first_hop(g):
        from_z(g, 0)
        from_z(g, 2)

        @pl.when(jnp.logical_not(inner))
        def _():
            from_z(g, 1)

        for slot in (3, 4, 5):
            send(g, slot).start()

    def pass_on(g):
        arrive(g, 3)
        send(g, 6).start()
        send(g, 8).start()
        arrive(g, 4)
        send(g, 7).start()
        send(g, 9).start()

    def load_of(g, k):
        return pltpu.make_async_copy(found_ref.at[:, k, pl.ds(g * rows, rows)], stage.at[k], load_sem.at[k])

    def last_hop(g):
        arrive(g, 6, 0)
        arrive(g, 7, 1)
        send(g, 10).start()

    def landed(g):
        arrive(g, 5)
        for slot in (8, 9, 10):
            arrive(g, slot)
        for k in range(others):
            load_of(g, k).start()

    def home(g):
        kept = hidden_rows // size + head_rows // size
        return (full, pl.ds(g * size, size)) if g < kept else (low, pl.ds((g % 2) * size, size))

    def store_of(g, s):
        place, span = home(g)
        return pltpu.make_async_copy(place.at[s, span], full_ref.at[s, pl.ds(g * size, size)], store_sem.at[g, s])

    def rounded(g):
        place, span = home(g)
        for k in range(others):
            load_of(g, k).wait()
            place[slice_of(k), span] = stage[k].reshape(size, model).astype(BF)
        for s in range(n_tensor):
            store_of(g, s).start()

    def pause(step, between):
        for at, *moves in between:

            @pl.when(step == at)
            def _(moves=moves):
                for move, g in moves:
                    move(g)

    def project(x_ref, s, first, bias_row, out_ref):
        @pl.loop(0, 2)
        def _(i):
            span = pl.ds(pl.multiple_of(i * (length // 2), length // 2), length // 2)
            value = dot_nt(x_ref[span, :], full[s, pl.ds(first, WIDE), :])
            if bias_row is not None:
                value = value + bias[s, bias_row : bias_row + 1, :WIDE]
            filled = lax.broadcasted_iota(jnp.int32, (1, WIDE), 1) < head_rows // 8
            out_ref[s, span, :] = jnp.where(filled, value, 0.0).astype(BF)

    def attend(s, causal, k_ids_ref, base, *between):
        half = length // 2
        lane = lax.broadcasted_iota(jnp.int32, (1, 128), 1)

        @pl.loop(0, 3)
        def _(h):
            columns = pl.ds(pl.multiple_of((h // 2) * 128, 128), 128)
            mine = (lane // HEAD_DIM) == (h % 2)
            log_lane = lane == base + 3 * s + h
            for b in range(2):
                reach = (b + 1) * half if causal else length
                span = slice(b * half, (b + 1) * half)
                queries = q_all[s, span, columns] * jnp.asarray(HEAD_DIM**-0.5, BF)
                scores = dot_nt(jnp.where(mine, queries, jnp.zeros_like(queries)), k_all[s, :reach, columns])
                allowed = t_col_ref[span, :] == k_ids_ref[:, :reach]
                if causal:
                    allowed = allowed & (
                        lax.broadcasted_iota(jnp.int32, (half, reach), 0) + b * half
                        >= lax.broadcasted_iota(jnp.int32, (half, reach), 1)
                    )
                scores = jnp.where(allowed, scores, NEGATIVE)
                top = jnp.max(scores, axis=1, keepdims=True)
                weights = jnp.exp(scores - top)
                total = jnp.sum(weights, axis=1, keepdims=True)
                out = (dot_nn(weights.astype(BF), v_all[s, :reach, columns]) * (1.0 / total)).astype(BF)
                before = mixed[s, span, columns]
                before = jnp.where(h % 2 == 1, before, jnp.zeros_like(before))
                mixed[s, span, columns] = jnp.where(mine, out, before)
                logs[span, :] = jnp.where(log_lane, top + jnp.log(total), logs[span, :])
            pause(h, between)

    def close(first, bias_row, residual, hat, low_out, column):
        block = length // 4

        @pl.loop(0, 4)
        def _(i):
            span = pl.ds(pl.multiple_of(i * block, block), block)
            value = residual(span) + vectors_ref[bias_row : bias_row + 1, :]
            for s in range(n_tensor):
                value = value + dot_nn(mixed[s, span, :], full[s, pl.ds(first, WIDE), :])
            centered = value - jnp.mean(value, axis=1, keepdims=True)
            scale = lax.rsqrt(jnp.mean(centered * centered, axis=1, keepdims=True) + EPSILON)
            normed = centered * scale
            hat[span, :] = normed
            here = lax.broadcasted_iota(jnp.int32, (1, 128), 1) == column
            spread[span, :] = jnp.where(here, scale, spread[span, :])
            low_out[span, :] = (
                normed * vectors_ref[bias_row + 1 : bias_row + 2, :] + vectors_ref[bias_row + 2 : bias_row + 3, :]
            ).astype(BF)

    def expand(s, slot):
        @pl.loop(0, 4)
        def _(i):
            span = pl.ds(pl.multiple_of(i * (length // 4), length // 4), length // 4)
            hidden = dot_nt(low2[span, :], full[s, pl.ds(head_rows, hidden_rows), :]) + bias[s, 4:5, :]
            value, change = erf_pair(hidden)
            act[slot, span, :] = value.astype(BF)
            slope[slot, span, :] = change.astype(BF)

    def out_copy(i, source, target):
        return pltpu.make_async_copy(source, target, out_sem.at[i])

    def expand_out(s, slot):
        return (
            out_copy(13 + 2 * slot, act.at[slot], act_ref.at[s]),
            out_copy(14 + 2 * slot, slope.at[slot], slope_ref.at[s]),
        )

    barrier = pltpu.get_barrier_semaphore()
    for k in range(1, n_tensor):
        pl.semaphore_signal(barrier, inc=1, device_id={"tensor": (z + k) % n_tensor}, device_id_type=MESH)
    for other in (dc, dx, dy):
        pl.semaphore_signal(barrier, inc=1, device_id={"dp": other}, device_id_type=MESH)
    step = head_rows // 8
    q0, k0, v0, o0, ck0, cv0, cq0, co0 = (i * step for i in range(8))
    own_loads = [
        pltpu.make_async_copy(source, place, load_sem.at[3 + i])
        for i, (source, place) in enumerate(
            (
                (sqw_ref, full.at[z, pl.ds(q0, step)]),
                (skw_ref, full.at[z, pl.ds(k0, step)]),
                (svw_ref, full.at[z, pl.ds(v0, step)]),
                (ckw_ref, full.at[z, pl.ds(ck0, step)]),
                (cvw_ref, full.at[z, pl.ds(cv0, step)]),
                (cqw_ref, full.at[z, pl.ds(cq0, step)]),
                (sow_ref, full.at[z, pl.ds(o0, step)]),
                (cow_ref, full.at[z, pl.ds(co0, step)]),
                (exw_ref, act.at[0, pl.ds(0, model)]),
                (ctw_ref, low.at[z]),
            )
        )
    ]
    for load in own_loads:
        load.start()
    t_row_ref[...] = t_ids_ref[...].astype(F32)
    m_row_ref[...] = m_ids_ref[...].astype(F32)
    t_col_ref[...] = as_column(t_row_ref[...])
    fill_rows(bias_ref, (b0_ref, b1_ref, b2_ref, b3_ref, b4_ref))
    fill_rows(vectors_ref, (v0_ref, v1_ref, v2_ref, v3_ref, v4_ref, v5_ref))
    bias[z] = bias_ref[...]
    pl.semaphore_wait(barrier, others + 3)
    for k in range(others):
        bias_copy(k).start()
    def chunk_copy(g):
        return pltpu.make_async_copy(stage.at[0, g], chunk_ref.at[pl.ds(g * rows, rows)], load_sem.at[g % 3])

    def offer(g):
        place, span = home(g)
        first = span.start + d * rows
        stage[0, g] = place[z, pl.ds(pl.multiple_of(first, 16), rows), :].astype(F32)
        chunk_copy(g).start()

    def give(g):
        chunk_copy(g).wait()
        if g < lead:
            own_z(g)

    own_loads[0].wait()
    own_loads[1].wait()
    offer(0)
    own_loads[2].wait()
    own_loads[6].wait()
    give(0)
    offer(1)
    own_loads[3].wait()
    own_loads[4].wait()
    give(1)
    offer(2)
    own_loads[5].wait()
    own_loads[7].wait()
    give(2)
    offer(3)
    own_loads[8].wait()
    full[z, pl.ds(head_rows, hidden_rows), :] = jnp.transpose(act[0, :model, :].astype(F32)).astype(BF)
    offer(4)
    give(3)
    offer(5)
    own_loads[9].wait()
    give(4)
    offer(6)
    give(5)
    offer(7)
    give(6)
    give(7)

    logs[...] = jnp.zeros_like(logs)
    spread[...] = jnp.zeros_like(spread)
    project(target_ref, z, q0, 0, q_all)
    project(target_ref, z, k0, None, k_all)
    project(target_ref, z, v0, 1, v_all)
    attend(z, True, t_row_ref, 0)
    for k in range(others):
        bias_copy(k).wait_recv()
    pass_z(0)
    first_hop(0)
    pass_z(1)
    first_hop(1)
    pass_on(0)
    pass_z(2)
    first_hop(2)
    pass_on(1)
    pass_z(3)
    last_hop(0)
    landed(0)
    first_hop(3)
    rounded(0)
    for k in range(others):
        project(target_ref, slice_of(k), q0, 0, q_all)
        project(target_ref, slice_of(k), k0, None, k_all)
    pass_z(4)
    pass_on(2)
    last_hop(1)
    first_hop(4)
    landed(1)
    pass_z(5)
    rounded(1)
    for k in range(others):
        project(target_ref, slice_of(k), v0, 1, v_all)
    attend(slice_of(0), True, t_row_ref, 0, (0, (last_hop, 2)), (1, (pass_on, 3), (first_hop, 5)))
    attend(slice_of(1), True, t_row_ref, 0, (0, (landed, 2)), (1, (pass_z, 6)))
    rounded(2)
    attend(slice_of(2), True, t_row_ref, 0, (0, (last_hop, 3), (pass_on, 4)), (1, (first_hop, 6)))
    pass_z(7)
    self_out = [
        out_copy(0, q_all, sq_ref), out_copy(1, k_all, sk_ref), out_copy(2, v_all, sv_ref), out_copy(3, mixed, sm_ref)
    ]
    for copy in self_out:
        copy.start()
    close(o0, 0, lambda span: target_ref[span, :].astype(F32), hat1, low1, 0)
    landed(3)
    out_copy(4, hat1, hat1_ref).start()
    out_copy(5, low1, low1_ref).start()
    for copy in self_out:
        copy.wait()

    @pl.loop(0, n_tensor)
    def _(s):
        project(memory_ref, s, ck0, None, k_all)
        project(memory_ref, s, cv0, 3, v_all)

    pass_on(5)
    first_hop(7)
    project(low1, z, cq0, 2, q_all)
    attend(z, False, m_row_ref, 3 * n_tensor, (1, (last_hop, 4)))
    rounded(3)
    for k in range(others):
        project(low1, slice_of(k), cq0, 2, q_all)
    landed(4)
    attend(slice_of(0), False, m_row_ref, 3 * n_tensor, (0, (pass_on, 6)), (1, (last_hop, 5)))
    rounded(4)
    attend(slice_of(1), False, m_row_ref, 3 * n_tensor, (0, (landed, 5)), (1, (pass_on, 7)))
    rounded(5)
    attend(slice_of(2), False, m_row_ref, 3 * n_tensor, (0, (last_hop, 6)), (2, (last_hop, 7)))
    cross_out = [
        out_copy(0, q_all, cq_ref), out_copy(1, k_all, ck_ref), out_copy(2, v_all, cv_ref), out_copy(3, mixed, cm_ref),
        out_copy(6, logs, logs_ref),
    ]
    for copy in cross_out:
        copy.start()
    close(co0, 3, lambda span: hat1[span, :] * vectors_ref[1:2, :] + vectors_ref[2:3, :], hat2, low2, 1)
    out_copy(7, hat2, hat2_ref).start()
    out_copy(8, low2, low2_ref).start()
    out_copy(9, spread, r_ref).start()
    landed(6)
    expand(z, 0)
    for copy in expand_out(z, 0):
        copy.start()
    rounded(6)
    landed(7)
    expand(slice_of(0), 1)
    for copy in expand_out(slice_of(0), 1):
        copy.start()
    rounded(7)
    for copy in expand_out(z, 0):
        copy.wait()
    expand(slice_of(1), 0)
    for copy in expand_out(slice_of(1), 0):
        copy.start()
    for copy in expand_out(slice_of(0), 1):
        copy.wait()
    expand(slice_of(2), 1)
    for copy in expand_out(slice_of(2), 1):
        copy.start()

    for copy in expand_out(slice_of(1), 0) + expand_out(slice_of(2), 1) + tuple(cross_out):
        copy.wait()
    for i, source, target in ((4, hat1, hat1_ref), (5, low1, low1_ref), (7, hat2, hat2_ref), (8, low2, low2_ref)):
        out_copy(i, source, target).wait()
    out_copy(9, spread, r_ref).wait()
    for g in range(count):
        for s in range(n_tensor):
            store_of(g, s).wait()
    for k in range(others):
        bias_copy(k).wait_send()
    for g in range(count):
        for step_z, k, slot in near:

            @pl.when(reaches(step_z))
            def _(g=g, step_z=step_z, k=k, slot=slot):
                own_along(g, step_z, k, slot).wait_send()

        @pl.when(inner)
        def _(g=g):
            relay(g).wait_send()

        for slot in routes:
            send(g, slot).wait_send()


def forward(own, biases, target, memory, target_ids, memory_ids, vectors, n_dp, n_tensor, head_rows, hidden_rows):
    length, model = target.shape
    count = 8
    total = head_rows + 2 * hidden_rows
    size = total // count
    rows = size // n_dp
    step = head_rows // 8
    anywhere = pl.BlockSpec(memory_space=pl.ANY)
    inside = pl.BlockSpec(memory_space=pltpu.VMEM)
    heads = jax.ShapeDtypeStruct((n_tensor, length, WIDE), BF)
    tokens = jax.ShapeDtypeStruct((length, model), F32)
    tokens_low = jax.ShapeDtypeStruct((length, model), BF)
    lanes = jax.ShapeDtypeStruct((length, 128), F32)
    units = jax.ShapeDtypeStruct((n_tensor, length, hidden_rows), BF)
    out_shape = (
        jax.ShapeDtypeStruct((count * rows, model), F32),
        jax.ShapeDtypeStruct((n_dp, n_tensor - 1, count * rows, model), F32),
        jax.ShapeDtypeStruct((n_tensor, total, model), BF),
        heads, heads, heads, heads, heads, heads, heads, heads,
        lanes, tokens, tokens, lanes, tokens_low, tokens_low, units, units,
    )
    flops = 2 * length * model * (2 * n_tensor * head_rows) + 4 * length * model * n_tensor * hidden_rows
    outs = pl.pallas_call(
        partial(forward_kernel, n_dp, n_tensor, count, rows, head_rows, hidden_rows),
        out_shape=out_shape,
        in_specs=[anywhere] * 10 + [inside] * 15,
        out_specs=[anywhere] * len(out_shape),
        scratch_shapes=[
            pltpu.VMEM((8, model), F32),
            pltpu.VMEM((8, model), F32),
            pltpu.VMEM((1, length), F32),
            pltpu.VMEM((1, length), F32),
            pltpu.VMEM((length, 1), F32),
            pltpu.VMEM((n_tensor - 1, n_dp, rows, model), F32),
            pltpu.VMEM((n_tensor, head_rows + hidden_rows, model), BF),
            pltpu.VMEM((n_tensor, hidden_rows, model), BF),
            pltpu.VMEM((n_tensor, 8, model), F32),
            pltpu.VMEM(heads.shape, BF),
            pltpu.VMEM(heads.shape, BF),
            pltpu.VMEM(heads.shape, BF),
            pltpu.VMEM(heads.shape, BF),
            pltpu.VMEM(lanes.shape, F32),
            pltpu.VMEM(tokens.shape, F32),
            pltpu.VMEM(tokens.shape, F32),
            pltpu.VMEM(lanes.shape, F32),
            pltpu.VMEM(tokens.shape, BF),
            pltpu.VMEM(tokens.shape, BF),
            pltpu.VMEM((2, length, hidden_rows), BF),
            pltpu.VMEM((2, length, hidden_rows), BF),
            pltpu.SemaphoreType.DMA((count, 13)),
            pltpu.SemaphoreType.DMA((count, 11)),
            pltpu.SemaphoreType.DMA((n_tensor - 1,)),
            pltpu.SemaphoreType.DMA((n_tensor - 1,)),
            pltpu.SemaphoreType.DMA((13,)),
            pltpu.SemaphoreType.DMA((count, n_tensor)),
            pltpu.SemaphoreType.DMA((17,)),
        ],
        cost_estimate=pl.CostEstimate(flops=flops, bytes_accessed=60 * MIB, transcendentals=0),
        compiler_params=pltpu.CompilerParams(collective_id=0, has_side_effects=True, vmem_limit_bytes=63 * MIB),
    )(
        *(x.T if x.shape[0] > x.shape[1] else x for x in own), target, memory, target_ids, memory_ids, *biases, *vectors
    )
    return None, *outs[2:]


def round_kernel(wide_ref, low_ref):
    low_ref[...] = wide_ref[...].astype(BF)


def rounded_copy(array):
    slices, rows, width = array.shape
    block = pl.BlockSpec((1, rows // 4, width), lambda i, j: (i, j, 0))
    return pl.pallas_call(
        round_kernel,
        grid=(slices, 4),
        in_specs=[block],
        out_specs=block,
        out_shape=jax.ShapeDtypeStruct(array.shape, BF),
    )(array)


def forward_plain(own, biases, target, memory, target_ids, memory_ids, vectors, n_dp, n_tensor, head_rows, hidden_rows):
    length, model = target.shape
    width = head_rows // 8
    sq, sk, sv, so, ck, cv, cq, co, expand, contract = own
    own = jnp.concatenate((sq.T, sk.T, sv.T, so, ck.T, cv.T, cq.T, co, expand.T, contract), axis=0)
    full = rounded_copy(lax.all_gather(own.astype(F32), "tensor", axis=0))
    bias = lax.all_gather(jnp.stack([jnp.pad(b, (0, model - b.shape[0])) for b in biases]), "tensor", axis=0)
    target_ids, memory_ids = target_ids.reshape(-1), memory_ids.reshape(-1)

    def weight(i):
        return full[:, i * width : (i + 1) * width]

    def padded(x):
        return jnp.pad(x, ((0, 0), (0, 0), (0, WIDE - width)))

    def project(x, i, row=None):
        value = jnp.einsum("td,swd->stw", x, weight(i), preferred_element_type=F32)
        if row is not None:
            value = value + bias[:, row, None, :width]
        return value.astype(BF)

    def attend(queries, keys, values, key_ids, causal):
        def split(x):
            return x.reshape(n_tensor, length, -1, HEAD_DIM)

        def one(items):
            q, k, v = items
            scores = jnp.einsum("qhd,khd->hqk", q, k, preferred_element_type=F32) * HEAD_DIM**-0.5
            allowed = target_ids[:, None] == key_ids[None, :]
            if causal:
                at = jnp.arange(length, dtype=jnp.int32)
                allowed = allowed & (at[:, None] >= at[None, :])
            scores = jnp.where(allowed[None], scores, NEGATIVE)
            probs = jax.nn.softmax(scores, axis=-1).astype(BF)
            out = jnp.einsum("hqk,khd->qhd", probs, v, preferred_element_type=F32)
            return out.astype(BF), jax.nn.logsumexp(scores, axis=-1)

        mixed, logs = lax.map(one, (split(queries), split(keys), split(values)))
        return mixed.reshape(n_tensor, length, width), logs.reshape(-1, length)

    def close(mixed, i, residual, row):
        value = residual + vectors[row] + jnp.einsum("stw,swd->td", mixed, weight(i), preferred_element_type=F32)
        centered = value - jnp.mean(value, axis=1, keepdims=True)
        scale = lax.rsqrt(jnp.mean(centered * centered, axis=1, keepdims=True) + EPSILON)
        hat = centered * scale
        normed = hat * vectors[row + 1] + vectors[row + 2]
        return hat, scale, normed, normed.astype(BF)

    sq, sk, sv = project(target, 0, 0), project(target, 1), project(target, 2, 1)
    sm, self_logs = attend(sq, sk, sv, target_ids, True)
    hat1, r1, first, low1 = close(sm, 3, target.astype(F32), 0)
    ck, cv, cq = project(memory, 4), project(memory, 5, 3), project(low1, 6, 2)
    cm, cross_logs = attend(cq, ck, cv, memory_ids, False)
    hat2, r2, _, low2 = close(cm, 7, first, 3)
    hidden = jnp.einsum("td,shd->sth", low2, full[:, head_rows : head_rows + hidden_rows], preferred_element_type=F32)
    act, slope = erf_pair(hidden + bias[:, 4, None, :])
    logs = jnp.concatenate((self_logs, cross_logs), axis=0).T
    logs = jnp.pad(logs, ((0, 0), (0, 128 - logs.shape[1])))
    spread = jnp.pad(jnp.concatenate((r1, r2), axis=1), ((0, 0), (0, 126)))
    heads = [padded(x) for x in (sq, sk, sv, sm, cq, ck, cv, cm)]
    kept = jnp.concatenate((full[:, : 3 * width], full[:, 4 * width : 6 * width]), axis=1)
    columns = padded(lax.dynamic_slice_in_dim(kept, lax.axis_index("tensor") * width, width, 2))
    return columns, full, *heads, logs, hat1, hat2, spread, low1, low2, act.astype(BF), slope.astype(BF)


def attend_back_kernel(
    heads, base, block, causal, q_ref, k_ref, v_ref, gm_ref, logs_ref, dots_ref, q_row_ref, k_row_ref, gq_ref, gk_ref,
    gv_ref, gq_sum, logs, dots, k_ids_ref, q_ids_ref, bounds
):
    length = q_ref.shape[1]
    lane = lax.broadcasted_iota(jnp.int32, (1, 128), 1)
    scale = HEAD_DIM**-0.5
    s = pl.program_id(0)

    @pl.when(s == 0)
    def _():
        logs[...] = jnp.transpose(logs_ref[...])
        dots[...] = jnp.transpose(dots_ref[...])
        k_ids_ref[...] = as_column(k_row_ref[...].astype(F32))
        q_ids_ref[...] = q_row_ref[...].astype(F32)
        if not causal:
            for b in range(length // block):
                ids = k_row_ref[:, b * block : (b + 1) * block]
                low = jnp.sum((q_row_ref[...] < jnp.min(ids)).astype(jnp.int32)) // block
                high = (jnp.sum((q_row_ref[...] <= jnp.max(ids)).astype(jnp.int32)) + block - 1) // block
                bounds[0, b] = low
                bounds[1, b] = high - low

    gq_sum[...] = jnp.zeros_like(gq_sum)

    def one_block(at, first, reach):
        k_span = pl.ds(at, block)
        q_span = pl.ds(first, reach)
        allowed = k_ids_ref[k_span, :] == q_ids_ref[:, q_span]
        if causal:
            allowed = allowed & (
                lax.broadcasted_iota(jnp.int32, (block, reach), 0) <= lax.broadcasted_iota(jnp.int32, (block, reach), 1)
            )
        grads = []
        for h in range(heads):
            mine = (lane // HEAD_DIM) == (h % 2)
            columns = slice(128 * (h // 2), 128 * (h // 2) + 128)
            keys = k_ref[0, k_span, columns]
            keys = jnp.where(mine, keys, jnp.zeros_like(keys))
            values = v_ref[0, k_span, columns]
            values = jnp.where(mine, values, jnp.zeros_like(values))
            queries = q_ref[0, q_span, columns]
            gm = gm_ref[0, q_span, columns]
            scores = dot_nt(keys * jnp.asarray(scale, BF), queries)
            probs = jnp.where(allowed, jnp.exp(scores - logs[pl.ds(base + heads * s + h, 1), q_span]), 0.0)
            grad_scores = (probs * (dot_nt(values, gm) - dots[pl.ds(heads * s + h, 1), q_span])).astype(BF)
            grads.append((dot_nn(grad_scores, queries) * scale, dot_nn(probs.astype(BF), gm)))
            gq_sum[q_span, columns] += dot_tn(grad_scores, keys)
        left = lane < HEAD_DIM
        for i, out_ref in enumerate((gk_ref, gv_ref)):
            out_ref[0, k_span, 0:128] = jnp.where(left, grads[0][i], grads[1][i]).astype(BF)
            out_ref[0, k_span, 128:256] = jnp.where(left, grads[2][i], 0.0).astype(BF)

    if causal:
        for b in range(length // block):
            one_block(b * block, b * block, length - b * block)
    else:

        @pl.loop(0, length // block)
        def _(b):
            start = pl.multiple_of(bounds[0, b] * block, block)
            for number in range(1, length // block + 1):

                @pl.when(bounds[1, b] == number)
                def _(number=number):
                    one_block(pl.multiple_of(b * block, block), start, number * block)

    gq_ref[0] = (gq_sum[...] * scale).astype(BF)


def attend_back(causal, base, queries, keys, values, grad_mixed, logs, dots, query_ids, key_ids):
    slices, length, wide = queries.shape
    part = pl.BlockSpec((1, length, wide), lambda i: (i, 0, 0))
    out = jax.ShapeDtypeStruct((slices, length, wide), BF)
    lanes = pl.BlockSpec((length, 128), lambda i: (0, 0))
    return pl.pallas_call(
        partial(attend_back_kernel, 3, base, 256, causal),
        grid=(slices,),
        in_specs=[part] * 4
        + [lanes, lanes, pl.BlockSpec((1, length), lambda i: (0, 0)), pl.BlockSpec((1, length), lambda i: (0, 0))],
        out_specs=[part] * 3,
        out_shape=[out] * 3,
        scratch_shapes=[
            pltpu.VMEM((length, wide), F32),
            pltpu.VMEM((128, length), F32),
            pltpu.VMEM((128, length), F32),
            pltpu.VMEM((length, 1), F32),
            pltpu.VMEM((1, length), F32),
            pltpu.SMEM((2, 8), jnp.int32),
        ],
        compiler_params=pltpu.CompilerParams(vmem_limit_bytes=60 * MIB),
    )(queries, keys, values, grad_mixed, logs, dots, query_ids, key_ids)


def norm_back(grad, hat, scale, gain):
    scaled = grad * gain
    return scale * (
        scaled - jnp.mean(scaled, axis=1, keepdims=True) - hat * jnp.mean(scaled * hat, axis=1, keepdims=True)
    )


def clear_first(sums_ref):
    @pl.when(pl.program_id(0) == 0)
    def _():
        sums_ref[...] = jnp.zeros_like(sums_ref)


def add_sums(sums_ref, rows):
    for row, value in rows:
        sums_ref[row : row + 1, :] += jnp.sum(value, axis=0, keepdims=True)


def head_products(grad_mixed, mixed, s, heads, dots):
    product = grad_mixed * mixed.astype(F32)
    lane = lax.broadcasted_iota(jnp.int32, (1, WIDE), 1)
    out_lane = lax.broadcasted_iota(jnp.int32, (1, 128), 1)
    for h in range(heads):
        total = jnp.sum(jnp.where(lane // HEAD_DIM == h, product, 0.0), axis=1, keepdims=True)
        dots = jnp.where(out_lane == heads * s + h, total, dots)
    return dots


def mixed_back(grad_low, out_weight, mixed_ref, gm_ref, dots_ref):
    slices = mixed_ref.shape[0]
    width = out_weight.shape[1]
    dots = jnp.zeros(dots_ref.shape, F32)
    for s in range(slices):
        grad_mixed = dot_nt(grad_low, out_weight[s]).astype(BF)
        grad_mixed = jnp.concatenate((grad_mixed, jnp.zeros((grad_mixed.shape[0], WIDE - width), BF)), axis=1)
        gm_ref[s] = grad_mixed
        dots = head_products(grad_mixed.astype(F32), mixed_ref[s], s, 3, dots)
    dots_ref[...] = dots


def feed_back_kernel(
    act_ref, slope_ref, hat2_ref, r_ref, grad_ref, mixed_ref, expand_ref, contract_ref, out_weight_ref,
    v0_ref, v1_ref, v2_ref, v3_ref, v4_ref, out_ref, grad_ffn_ref, grad_hidden_ref, grad_sum_ref, grad_cross_ref, gm_ref, dots_ref, sums_ref,
    vectors_ref
):
    slices = act_ref.shape[0]
    fill_rows(vectors_ref, (v0_ref, v1_ref, v2_ref, v3_ref, v4_ref))
    clear_first(sums_ref)
    vector = [vectors_ref[i : i + 1, :] for i in range(5)]
    hat2 = hat2_ref[...]
    value = hat2 * vector[0] + vector[1] + vector[2]
    for s in range(slices):
        value = value + dot_nn(act_ref[s], contract_ref[s])
    centered = value - jnp.mean(value, axis=1, keepdims=True)
    scale = lax.rsqrt(jnp.mean(centered * centered, axis=1, keepdims=True) + EPSILON)
    hat3 = centered * scale
    out_ref[...] = (hat3 * vector[3] + vector[4]).astype(BF)
    grad = grad_ref[...].astype(F32)
    grad_third = norm_back(grad, hat3, scale, vector[3])
    grad_ffn = grad_third.astype(BF)
    grad_ffn_ref[...] = grad_ffn
    grad_second = grad_third
    rows = [(0, grad * hat3), (1, grad), (2, grad_ffn.astype(F32))]
    for s in range(slices):
        grad_hidden = (dot_nt(grad_ffn, contract_ref[s]) * slope_ref[s].astype(F32)).astype(BF)
        grad_hidden_ref[s] = grad_hidden
        rows.append((8 + s, grad_hidden.astype(F32)))
        grad_second = grad_second + dot_nn(grad_hidden, expand_ref[s])
    grad_sum = norm_back(grad_second, hat2, r_ref[:, 1:2], vector[0])
    grad_sum_ref[...] = grad_sum
    grad_cross = grad_sum.astype(BF)
    grad_cross_ref[...] = grad_cross
    rows += [(3, grad_second * hat2), (4, grad_second), (5, grad_cross.astype(F32))]
    add_sums(sums_ref, rows)
    mixed_back(grad_cross, out_weight_ref, mixed_ref, gm_ref, dots_ref)


def feed_back(act, slope, hat2, spread, output_grad, mixed, full, vectors, head_rows):
    slices, length, units = act.shape
    model = hat2.shape[1]
    block = TOKEN_BLOCK
    width = head_rows // 8
    tokens = pl.BlockSpec((block, model), lambda i: (i, 0))
    lanes = pl.BlockSpec((block, 128), lambda i: (i, 0))
    wide = pl.BlockSpec((slices, block, units), lambda i: (0, i, 0))
    heads = pl.BlockSpec((slices, block, WIDE), lambda i: (0, i, 0))
    rows = pl.BlockSpec((16, model), lambda i: (0, 0))

    def weight(first, size):
        return pl.BlockSpec((slices, size, model), lambda i: (0, first // size, 0))

    low = jax.ShapeDtypeStruct((length, model), BF)
    return pl.pallas_call(
        feed_back_kernel,
        grid=(length // block,),
        in_specs=[wide, wide, tokens, lanes, tokens, heads]
        + [weight(head_rows, units), weight(head_rows + units, units), weight(7 * width, width)]
        + [pl.BlockSpec((model,), lambda i: (0,))] * 5,
        scratch_shapes=[pltpu.VMEM((8, model), F32)],
        out_specs=[tokens, tokens, wide, tokens, tokens, heads, lanes, rows],
        out_shape=[
            low,
            low,
            jax.ShapeDtypeStruct(act.shape, BF),
            jax.ShapeDtypeStruct((length, model), F32),
            low,
            jax.ShapeDtypeStruct((slices, length, WIDE), BF),
            jax.ShapeDtypeStruct((length, 128), F32),
            jax.ShapeDtypeStruct((16, model), F32),
        ],
        compiler_params=pltpu.CompilerParams(vmem_limit_bytes=62 * MIB),
    )(act, slope, hat2, spread, output_grad, mixed, full, full, full, *vectors)


def first_back_kernel(
    z_ref, gq_ref, grad_sum_ref, hat1_ref, r_ref, mixed_ref, query_ref, out_weight_ref, gain_ref,
    rest_ref, grad_self_ref, gm_ref, dots_ref, sums_ref, vectors_ref
):
    fill_rows(vectors_ref, (gain_ref,))
    clear_first(sums_ref)
    slices = gq_ref.shape[0]
    width = query_ref.shape[1]
    grad = grad_sum_ref[...]
    for s in range(slices):
        grad = grad + dot_nn(gq_ref[s][:, :width], query_ref[s])
    hat = hat1_ref[...]
    grad_first = norm_back(grad, hat, r_ref[:, 0:1], vectors_ref[0:1, :])
    rest_ref[...] = pltpu.roll(grad_first, grad_first.shape[1] - z_ref[0] * width, 1)[:, :width]
    grad_self = grad_first.astype(BF)
    grad_self_ref[...] = grad_self
    add_sums(sums_ref, [(0, grad * hat), (1, grad), (2, grad_self.astype(F32))])
    mixed_back(grad_self, out_weight_ref, mixed_ref, gm_ref, dots_ref)


def first_back(z, gq, grad_sum, hat1, spread, mixed, full, vectors, head_rows):
    slices, length, _ = gq.shape
    model = hat1.shape[1]
    block = TOKEN_BLOCK
    width = head_rows // 8
    tokens = pl.BlockSpec((block, model), lambda i, _: (i, 0))
    lanes = pl.BlockSpec((block, 128), lambda i, _: (i, 0))
    share = pl.BlockSpec((block, width), lambda i, _: (i, 0))
    heads = pl.BlockSpec((slices, block, WIDE), lambda i, _: (0, i, 0))
    rows = pl.BlockSpec((8, model), lambda i, _: (0, 0))
    return pl.pallas_call(
        first_back_kernel,
        grid_spec=pltpu.PrefetchScalarGridSpec(
            num_scalar_prefetch=1,
            grid=(length // block,),
            in_specs=[heads, tokens, tokens, lanes, heads]
            + [pl.BlockSpec((slices, width, model), lambda i, _, j=j: (0, j, 0)) for j in (6, 3)]
            + [pl.BlockSpec((model,), lambda i, _: (0,))],
            scratch_shapes=[pltpu.VMEM((8, model), F32)],
            out_specs=[share, tokens, heads, lanes, rows],
        ),
        out_shape=[
            jax.ShapeDtypeStruct((length, width), F32),
            jax.ShapeDtypeStruct((length, model), BF),
            jax.ShapeDtypeStruct((slices, length, WIDE), BF),
            jax.ShapeDtypeStruct((length, 128), F32),
            jax.ShapeDtypeStruct((8, model), F32),
        ],
        compiler_params=pltpu.CompilerParams(vmem_limit_bytes=62 * MIB),
    )(z.reshape(1), gq, grad_sum, hat1, spread, mixed, full, full, vectors)


def input_grad_kernel(count, *refs):
    out_ref = refs[-1]
    weight_ref = refs[count]
    slices = refs[0].shape[0]
    width = weight_ref.shape[1] // count
    total = refs[count + 1][...] if len(refs) == count + 3 else jnp.zeros(out_ref.shape, F32)
    for i in range(count):
        for s in range(slices):
            total = total + dot_nn(refs[i][s][:, :width], weight_ref[s, i * width : (i + 1) * width, :])
    out_ref[...] = total.astype(BF)


def input_grad(grads, weights, rest=None):
    slices, length, wide = grads[0].shape
    share = weights.shape[2]
    block = length // 2
    tokens = pl.BlockSpec((block, share), lambda i: (i, 0))
    specs = [pl.BlockSpec((slices, block, wide), lambda i: (0, i, 0))] * len(grads)
    specs.append(pl.BlockSpec(weights.shape, lambda i: (0, 0, 0)))
    operands = (*grads, weights)
    if rest is not None:
        operands += (rest,)
        specs.append(tokens)
    return pl.pallas_call(
        partial(input_grad_kernel, len(grads)),
        grid=(2,),
        in_specs=specs,
        out_specs=tokens,
        out_shape=jax.ShapeDtypeStruct((length, share), BF),
        compiler_params=pltpu.CompilerParams(vmem_limit_bytes=60 * MIB),
    )(*operands)


def weight_grad_kernel(plan, width, z_ref, *refs):
    del z_ref
    out_ref, sums_ref = refs[-2:]
    sums_ref[...] = jnp.zeros_like(sums_ref)
    products = []
    index = 0
    row = 0
    for count in plan:
        left = refs[index][...]
        rights = [refs[index + 1 + i][0][:, :width] for i in range(count)]
        index += 1 + count
        for right in rights:
            sums_ref[row : row + 1, 0:width] = jnp.sum(right.astype(F32), axis=0, keepdims=True)
            row += 1
        products.append(dot_tn(left, rights[0] if count == 1 else jnp.concatenate(rights, axis=1)))
    out_ref[...] = jnp.concatenate(products, axis=1)


def weight_grad(z, width, *pairs):
    operands, specs = [], []
    for left, rights in pairs:
        operands.append(left)
        specs.append(pl.BlockSpec(left.shape, lambda i, z_ref: (0, 0)))
        for right in rights:
            operands.append(right)
            specs.append(pl.BlockSpec((1,) + right.shape[1:], lambda i, z_ref: (z_ref[0], 0, 0)))
    model = pairs[0][0].shape[1]
    plan = [len(rights) for _, rights in pairs]
    return pl.pallas_call(
        partial(weight_grad_kernel, plan, width),
        grid_spec=pltpu.PrefetchScalarGridSpec(
            num_scalar_prefetch=1,
            grid=(1,),
            in_specs=specs,
            out_specs=[
                pl.BlockSpec((model, sum(plan) * width), lambda i, z_ref: (0, 0)),
                pl.BlockSpec((8, model), lambda i, z_ref: (0, 0)),
            ],
        ),
        out_shape=[jax.ShapeDtypeStruct((model, sum(plan) * width), F32), jax.ShapeDtypeStruct((8, model), F32)],
        compiler_params=pltpu.CompilerParams(vmem_limit_bytes=60 * MIB),
    )(z.reshape(1), *operands)


def products_kernel(
    width, z_ref, low2_ref, gh_ref, gf_ref, act_ref, low1_ref, gcq_ref, memory_ref, gck_ref, gcv_ref, gc_ref, cm_ref,
    out_f_ref, out_c_ref, sums_ref, low2, gh, gf, act, low1, gcq, memory, gck, gcv, gc, cm, prod_f, prod_c, load_sem, out_sem
):
    z = z_ref[0]
    whole = ((low2_ref, low2), (gf_ref, gf), (low1_ref, low1), (memory_ref, memory), (gc_ref, gc))
    sliced = ((gh_ref, gh), (act_ref, act), (gcq_ref, gcq), (gck_ref, gck), (gcv_ref, gcv), (cm_ref, cm))
    loads = [pltpu.make_async_copy(source, place, load_sem.at[i]) for i, (source, place) in enumerate(whole)]
    parts = [pltpu.make_async_copy(source.at[z], place, load_sem.at[5 + i]) for i, (source, place) in enumerate(sliced)]
    order = [loads[0], parts[0], loads[1], parts[1], loads[2], parts[2], loads[3], parts[3], parts[4], loads[4], parts[5]]
    for load in order:
        load.start()
    units = gh.shape[1]
    outs = []
    for i, (left, right) in enumerate(((low2, gh), (gf, act))):
        for load in order[2 * i : 2 * i + 2]:
            load.wait()
        columns = pl.ds(i * units, units)
        prod_f[:, columns] = dot_tn(left[...], right[...])
        outs.append(pltpu.make_async_copy(prod_f.at[:, columns], out_f_ref.at[:, columns], out_sem.at[i]))
        outs[-1].start()
    for load in order[4:]:
        load.wait()
    queries, keys, values = (x[:, :width] for x in (gcq, gck, gcv))
    prod_c[...] = jnp.concatenate(
        (
            dot_tn(low1[...], queries),
            dot_tn(memory[...], jnp.concatenate((keys, values), axis=1)),
            dot_tn(gc[...], cm[:, :width]),
        ),
        axis=1,
    )
    outs.append(pltpu.make_async_copy(prod_c, out_c_ref, out_sem.at[2]))
    outs[-1].start()
    sums_ref[...] = jnp.zeros_like(sums_ref)
    sums_ref[0:1, 0:width] = jnp.sum(queries.astype(F32), axis=0, keepdims=True)
    sums_ref[2:3, 0:width] = jnp.sum(values.astype(F32), axis=0, keepdims=True)
    for out in outs:
        out.wait()


def products(z, width, low2, grad_hidden, grad_ffn, act, low1, gcq, memory, gck, gcv, grad_cross, cm):
    length, model = low2.shape
    units = act.shape[2]
    anywhere = pl.BlockSpec(memory_space=pl.ANY)
    tokens = pltpu.VMEM((length, model), BF)
    hidden = pltpu.VMEM((length, units), BF)
    heads = pltpu.VMEM((length, gcq.shape[2]), BF)
    shapes = [(model, 2 * units), (model, 4 * width)]
    return pl.pallas_call(
        partial(products_kernel, width),
        grid_spec=pltpu.PrefetchScalarGridSpec(
            num_scalar_prefetch=1,
            grid=(1,),
            in_specs=[anywhere] * 11,
            out_specs=[anywhere, anywhere, pl.BlockSpec((8, model), lambda i, _: (0, 0))],
            scratch_shapes=[tokens, hidden, tokens, hidden, tokens, heads, tokens, heads, heads, tokens, heads]
            + [pltpu.VMEM(shape, F32) for shape in shapes]
            + [pltpu.SemaphoreType.DMA((11,)), pltpu.SemaphoreType.DMA((3,))],
        ),
        out_shape=[jax.ShapeDtypeStruct(shape, F32) for shape in shapes] + [jax.ShapeDtypeStruct((8, model), F32)],
        compiler_params=pltpu.CompilerParams(vmem_limit_bytes=60 * MIB),
    )(z.reshape(1), low2, grad_hidden, grad_ffn, act, low1, gcq, memory, gck, gcv, grad_cross, cm)


def scattered(partial_sums):
    return lax.psum_scatter(partial_sums, "dp", scatter_dimension=0, tiled=True)


def finish_kernel(
    width, prod_f_ref, prod_c_ref, q_ref, k_ref, v_ref, gm_ref, sm_ref, gck_ref, gcv_ref, target_ref, grad_self_ref,
    full_ref, logs_ref, dots_ref, t_ids_ref, rest_ref, sums_ref, cross_sums_ref, first_sums_ref,
    total_f_ref, total_c_ref, total_s_ref, vector_total_ref, target_grad_ref, memory_grad_ref,
    q_all, k_all, v_all, gm_all, sm_own, gck_all, gcv_all, target, grad_self, gq_all, gk_all, gv_all, gq_sum, logs, dots,
    mine_f, mine_c, prod_s, land_f, land_c, land_s, one_f, one_c, one_s, two_f, two_c, two_s, vec, vec_land, t_col_ref, t_row_ref, weights, columns_ref,
    send_sem, recv_sem, load_sem,
):
    d = lax.axis_index("dp")
    z = lax.axis_index("tensor")
    c = d % 2
    x = (d // 2) % 2
    y = d // 4
    dc = d + 1 - 2 * c
    dx = d + 2 - 4 * x
    dy = d + 4 - 8 * y
    slices, length, _ = q_all.shape
    heads = 3

    def to(slot, source, place, other):
        return pltpu.make_async_remote_copy(
            src_ref=source,
            dst_ref=place,
            send_sem=send_sem.at[slot],
            recv_sem=recv_sem.at[slot],
            device_id={"dp": other},
            device_id_type=MESH,
        )

    families = (
        (prod_f_ref, mine_f, land_f, one_f, two_f, total_f_ref),
        (prod_c_ref, mine_c, land_c, one_c, two_c, total_c_ref),
        (prod_s, None, land_s, one_s, two_s, total_s_ref),
    )

    def over_core(i):
        return to(5 * i, families[i][0].at[:, :, 1 - c], families[i][2], dc)

    def halves(i):
        half = families[i][2].shape[3] // 2
        return pl.ds(0, half), pl.ds(half, half)

    def first_a(i):
        return to(5 * i + 1, families[i][2].at[:, 1 - x, :, halves(i)[0]], families[i][3].at[0], dx)

    def first_b(i):
        return to(5 * i + 2, families[i][2].at[1 - y, :, :, halves(i)[1]], families[i][3].at[1], dy)

    def second_a(i):
        return to(5 * i + 3, families[i][3].at[0, 1 - y], families[i][4].at[0], dy)

    def second_b(i):
        return to(5 * i + 4, families[i][3].at[1, 1 - x], families[i][4].at[1], dx)

    def after_core(i):
        _, mine, land, _, _, _ = families[i]
        over_core(i).wait_recv()

        @pl.loop(0, 4)
        def _(j):
            part = prod_s[j // 2, j % 2, c] if mine is None else mine[j // 2, j % 2]
            land[j // 2, j % 2] = land[j // 2, j % 2] + part

        first_a(i).start()
        first_b(i).start()

    def after_first(i):
        _, _, land, one, _, _ = families[i]
        first_a(i).wait_recv()
        first_b(i).wait_recv()
        left, right = halves(i)
        for j in range(2):
            one[0, j] = one[0, j] + land[j, x, :, left]
            one[1, j] = one[1, j] + land[y, j, :, right]
        second_a(i).start()
        second_b(i).start()

    def after_second(i):
        _, _, _, one, two, total_ref = families[i]
        second_a(i).wait_recv()
        second_b(i).wait_recv()
        left, right = halves(i)
        total_ref[:, left] = one[0, y] + two[0]
        total_ref[:, right] = one[1, x] + two[1]

    def vector_copy(i):
        return to(15 + i, vec.at[i], vec_land.at[i], (dc, dx, dy)[i])

    def vector_step(i):
        vector_copy(i).wait_recv()
        vec[i + 1] = vec[i] + vec_land[i]
        if i < 2:
            vector_copy(i + 1).start()

    barrier = pltpu.get_barrier_semaphore()
    for other in (dc, dx, dy):
        pl.semaphore_signal(barrier, inc=1, device_id={"dp": other}, device_id_type=MESH)

    def slice_loads(s):
        pairs = ((q_ref, q_all), (k_ref, k_all), (v_ref, v_all), (gm_ref, gm_all))
        return [
            pltpu.make_async_copy(source.at[s], place.at[s], load_sem.at[4 * s + i])
            for i, (source, place) in enumerate(pairs)
        ]

    late = 4 * slices
    late_loads = [
        pltpu.make_async_copy(sm_ref.at[z], sm_own, load_sem.at[late]),
        pltpu.make_async_copy(target_ref, target, load_sem.at[late + 1]),
        pltpu.make_async_copy(grad_self_ref, grad_self, load_sem.at[late + 2]),
        pltpu.make_async_copy(gck_ref, gck_all, load_sem.at[late + 3]),
        pltpu.make_async_copy(gcv_ref, gcv_all, load_sem.at[late + 4]),
        pltpu.make_async_copy(full_ref.at[:, pl.ds(0, 3 * width)], weights.at[:, pl.ds(0, 3 * width)], load_sem.at[late + 7]),
        pltpu.make_async_copy(
            full_ref.at[:, pl.ds(4 * width, 2 * width)], weights.at[:, pl.ds(3 * width, 2 * width)], load_sem.at[late + 8]
        ),
    ]
    mine_loads = [
        pltpu.make_async_copy(prod_f_ref.at[:, :, c], mine_f, load_sem.at[late + 5]),
        pltpu.make_async_copy(prod_c_ref.at[:, :, c], mine_c, load_sem.at[late + 6]),
    ]
    for s in range(slices):
        for load in slice_loads(s):
            load.start()
    for load in mine_loads + late_loads:
        load.start()
    pl.semaphore_wait(barrier, 3)
    over_core(0).start()
    over_core(1).start()
    t_row_ref[...] = t_ids_ref[...].astype(F32)
    t_col_ref[...] = as_column(t_row_ref[...])
    logs[...] = jnp.transpose(logs_ref[...])
    dots[...] = jnp.transpose(dots_ref[...])

    vec[0] = jnp.zeros(vec.shape[1:], F32)
    for row, source, at in (
        (2, first_sums_ref, 2), (3, first_sums_ref, 0), (4, first_sums_ref, 1), (5, cross_sums_ref, 0),
        (6, cross_sums_ref, 2), (7, sums_ref, 5), (8, sums_ref, 3), (9, sums_ref, 4), (11, sums_ref, 2),
        (12, sums_ref, 0), (13, sums_ref, 1),
    ):
        vec[0, row : row + 1, :] = source[at : at + 1, :]
    vec[0, 10:11, :] = sums_ref[pl.ds(8 + z, 1), :]

    lane = lax.broadcasted_iota(jnp.int32, (1, 128), 1)
    scale = HEAD_DIM**-0.5
    block = 256

    def one_block(s, at):
        reach = length - at
        span = slice(at, at + block)
        allowed = (t_col_ref[span, :] == t_row_ref[:, at:]) & (
            lax.broadcasted_iota(jnp.int32, (block, reach), 0) <= lax.broadcasted_iota(jnp.int32, (block, reach), 1)
        )
        grads = []
        for h in range(heads):
            mine = (lane // HEAD_DIM) == (h % 2)
            columns = slice(128 * (h // 2), 128 * (h // 2) + 128)
            keys = k_all[s, span, columns]
            keys = jnp.where(mine, keys, jnp.zeros_like(keys))
            values = v_all[s, span, columns]
            values = jnp.where(mine, values, jnp.zeros_like(values))
            queries = q_all[s, at:, columns]
            gm = gm_all[s, at:, columns]
            scores = dot_nt(keys * jnp.asarray(scale, BF), queries)
            row = pl.ds(heads * s + h, 1)
            probs = jnp.where(allowed, jnp.exp(scores - logs[row, at:]), 0.0)
            grad_scores = (probs * (dot_nt(values, gm) - dots[row, at:])).astype(BF)
            grads.append((dot_nn(grad_scores, queries) * scale, dot_nn(probs.astype(BF), gm)))
            gq_sum[at:, columns] += dot_tn(grad_scores, keys)
        left = lane < HEAD_DIM
        for i, out in enumerate((gk_all, gv_all)):
            out[s, span, 0:128] = jnp.where(left, grads[0][i], grads[1][i]).astype(BF)
            out[s, span, 128:256] = jnp.where(left, grads[2][i], 0.0).astype(BF)

    for s in range(slices):
        for load in slice_loads(s):
            load.wait()

    def own_products():
        for load in late_loads[:3]:
            load.wait()
        right = jnp.concatenate((gq_all[z][:, :width], gk_all[z][:, :width], gv_all[z][:, :width]), axis=1)
        products = jnp.concatenate((dot_tn(target[...], right), dot_tn(grad_self[...], sm_own[:, :width])), axis=1)
        prod_s[...] = products.reshape(prod_s.shape)
        vec[0, 0:1, 0:width] = jnp.sum(gq_all[z][:, :width].astype(F32), axis=0, keepdims=True)
        vec[0, 1:2, 0:width] = jnp.sum(gv_all[z][:, :width].astype(F32), axis=0, keepdims=True)
        over_core(2).start()
        vector_copy(0).start()

    @pl.loop(0, slices)
    def _(j):
        s = (z + j) % slices
        gq_sum[...] = jnp.zeros_like(gq_sum)
        for at in range(0, length, block):
            one_block(s, at)
        gq_all[s] = (gq_sum[...] * scale).astype(BF)

        @pl.when(j == 0)
        def _():
            for load in mine_loads:
                load.wait()
            after_core(0)
            after_core(1)
            own_products()

        @pl.when(j == 1)
        def _():
            after_core(2)
            vector_step(0)

        @pl.when(j == 2)
        def _():
            after_first(0)
            after_first(1)
            vector_step(1)

    for load in late_loads[3:]:
        load.wait()

    @pl.loop(0, slices)
    def _(s):
        model = weights.shape[2]
        for i in range(5):
            rows = pl.ds(i * width, width)
            turned = pltpu.roll(weights[s, rows, :].astype(F32), model - z * width, 1)
            columns_ref[s, rows, :] = turned[:, :WIDE].astype(BF)

    def input_grad(grads, first, rest, out_ref):
        @pl.loop(0, 4)
        def _(i):
            span = pl.ds(pl.multiple_of(i * (length // 4), length // 4), length // 4)
            total = 0.0
            for j, grad in enumerate(grads):
                for s in range(slices):
                    weight = columns_ref[s, (first + j) * width : (first + j + 1) * width, :]
                    total = total + dot_nn(grad[s, span, :width], weight)
            total = total[:, :width]
            if rest is not None:
                total = total + rest[span, :]
            out_ref[span, :] = total.astype(BF)

    after_first(2)
    input_grad((gq_all, gk_all, gv_all), 0, rest_ref, target_grad_ref)
    after_second(0)
    input_grad((gck_all, gcv_all), 3, None, memory_grad_ref)
    after_second(1)
    vector_step(2)
    after_second(2)
    vector_total_ref[...] = vec[3]
    for i in range(3):
        over_core(i).wait_send()
        for copy in (first_a(i), first_b(i), second_a(i), second_b(i)):
            copy.wait_send()
        vector_copy(i).wait_send()


def finish(prod_f, prod_c, heads, cross_grads, target, grad_self, full, logs, dots, ids, rest, sums, cross_sums, first_sums):
    slices, length, wide = heads[0].shape
    model = target.shape[1]
    width = model // slices
    n = model // 8
    anywhere = pl.BlockSpec(memory_space=pl.ANY)
    inside = pl.BlockSpec(memory_space=pltpu.VMEM)
    columns_f, columns_c = prod_f.shape[1], prod_c.shape[1]

    def half(size):
        return pltpu.VMEM((2, 2, n, size), F32)

    sizes = (columns_f, columns_c, model)
    group = pltpu.VMEM((slices, length, wide), BF)
    tokens = pltpu.VMEM((length, model), BF)
    share = jax.ShapeDtypeStruct((length, model // slices), BF)
    return pl.pallas_call(
        partial(finish_kernel, width),
        out_shape=[jax.ShapeDtypeStruct((n, size), F32) for size in sizes]
        + [jax.ShapeDtypeStruct((16, model), F32), share, share],
        in_specs=[anywhere] * 12 + [inside] * 7,
        out_specs=[inside] * 6,
        scratch_shapes=[group] * 4
        + [pltpu.VMEM((length, wide), BF), group, group, tokens, tokens, group, group, group]
        + [pltpu.VMEM((length, wide), F32), pltpu.VMEM((128, length), F32), pltpu.VMEM((128, length), F32)]
        + [half(columns_f), half(columns_c), pltpu.VMEM((2, 2, 2, n, model), F32)]
        + [half(size) for size in sizes]
        + [pltpu.VMEM((2, 2, n, size // 2), F32) for size in sizes]
        + [pltpu.VMEM((2, n, size // 2), F32) for size in sizes]
        + [pltpu.VMEM((4, 16, model), F32), pltpu.VMEM((3, 16, model), F32), pltpu.VMEM((length, 1), F32), pltpu.VMEM((1, length), F32)]
        + [pltpu.VMEM((slices, 5 * width, model), BF), pltpu.VMEM((slices, 5 * width, WIDE), BF)]
        + [pltpu.SemaphoreType.DMA((18,)), pltpu.SemaphoreType.DMA((18,)), pltpu.SemaphoreType.DMA((4 * slices + 9,))],
        compiler_params=pltpu.CompilerParams(collective_id=1, has_side_effects=True, vmem_limit_bytes=63 * MIB),
    )(
        prod_f.reshape(2, 2, 2, n, columns_f), prod_c.reshape(2, 2, 2, n, columns_c), *heads, *cross_grads, target,
        grad_self, full, logs, dots, ids, rest, sums, cross_sums, first_sums,
    )


def part_kernel(width, units, total_f_ref, total_c_ref, total_s_ref, vectors_ref, target_ref, memory_ref, *outs):
    matrices, lines, inputs = outs[:10], outs[10:-2], outs[-2:]
    for out, ref in zip(inputs, (target_ref, memory_ref), strict=True):
        out[...] = jnp.transpose(ref[...].astype(F32)).astype(BF)
    for i, ref in enumerate((total_s_ref, total_c_ref)):
        for j in range(4):
            part = ref[:, j * width : (j + 1) * width]
            matrices[4 * i + j][...] = part.T if j == 3 else part
    matrices[8][...] = total_f_ref[:, :units]
    matrices[9][...] = total_f_ref[:, units:]
    for i, out in enumerate(lines):
        out[...] = vectors_ref[i, : out.shape[0]]


def parts_of(total_f, total_c, total_s, vectors, target_grad, memory_grad, width, units):
    n, model = total_s.shape
    matrices = [(n, width), (n, width), (n, width), (width, n)] * 2 + [(n, units)] * 2
    lines = [width, width, model, model, model, width, width] + [model] * 3 + [units] + [model] * 3
    out = pl.pallas_call(
        partial(part_kernel, width, units),
        out_shape=[jax.ShapeDtypeStruct(shape, F32) for shape in matrices]
        + [jax.ShapeDtypeStruct((size,), F32) for size in lines]
        + [jax.ShapeDtypeStruct(target_grad.shape[::-1], BF)] * 2,
    )(total_f, total_c, total_s, vectors, target_grad, memory_grad)
    return [*out[:9], out[9].T], out[10:-2], out[-2].T, out[-1].T


def per_device(
    n_dp, n_tensor, target, memory, target_segments, memory_segments, self_query, self_query_bias, self_key, self_value,
    self_value_bias, self_output, self_output_bias, first_gain, first_shift, cross_query, cross_query_bias, cross_key,
    cross_value, cross_value_bias, cross_output, cross_output_bias, second_gain, second_shift, expand_weight, expand_bias,
    contract_weight, contract_bias, third_gain, third_shift, output_grad,
):
    model, width = self_query.shape
    units = expand_weight.shape[1]
    head_rows = 8 * width
    z = lax.axis_index("tensor")
    target_ids = target_segments.reshape(1, -1)
    memory_ids = memory_segments.reshape(1, -1)

    own = (
        self_query, self_key, self_value, self_output, cross_key, cross_value, cross_query, cross_output, expand_weight,
        contract_weight,
    )

    def rows_of(count, vectors):
        return jnp.stack([jnp.pad(v, (0, model - v.shape[0])) for v in vectors] + [jnp.zeros(model, F32)] * (count - len(vectors)))

    biases = (self_query_bias, self_value_bias, cross_query_bias, cross_value_bias, expand_bias)
    vectors = (self_output_bias, first_gain, first_shift, cross_output_bias, second_gain, second_shift)
    run = forward if (n_dp, n_tensor) == (8, 4) else forward_plain
    columns, full, sq, sk, sv, sm, cq, ck, cv, cm, logs, hat1, hat2, spread, low1, low2, act, slope = run(
        own, biases, target, memory, target_ids, memory_ids, vectors, n_dp, n_tensor, head_rows, units
    )
    layer_output, grad_ffn, grad_hidden, grad_second_sum, grad_cross, gcm, cross_dots, sums = feed_back(
        act, slope, hat2, spread, output_grad, cm, full,
        (second_gain, second_shift, contract_bias, third_gain, third_shift), head_rows,
    )
    gcq, gck, gcv = attend_back(False, 3 * n_tensor, cq, ck, cv, gcm, logs, cross_dots, target_ids, memory_ids)
    ffn_products, cross_products, cross_sums = products(
        z, width, low2, grad_hidden, grad_ffn, act, low1, gcq, memory, gck, gcv, grad_cross, cm
    )
    rest, grad_self, gsm, self_dots, first_sums = first_back(
        z, gcq, grad_second_sum, hat1, spread, sm, full, first_gain, head_rows
    )
    if (n_dp, n_tensor) == (8, 4):
        total_f, total_c, total_s, vectors, target_grad, memory_grad = finish(
            ffn_products, cross_products, (sq, sk, sv, gsm, sm), (gck, gcv), target, grad_self, full, logs, self_dots,
            target_ids, rest, sums, cross_sums, first_sums,
        )
    else:
        gsq, gsk, gsv = attend_back(True, 0, sq, sk, sv, gsm, logs, self_dots, target_ids, target_ids)
        self_products, self_sums = weight_grad(z, width, (target, [gsq, gsk, gsv]), (grad_self, [sm]))
        total_f, total_c, total_s = scattered(ffn_products), scattered(cross_products), scattered(self_products)
        memory_grad = input_grad((gck, gcv), columns[:, 3 * width :, :width])
        target_grad = input_grad((gsq, gsk, gsv), columns[:, : 3 * width, :width], rest)
        vectors = (
            self_sums[0], self_sums[2], first_sums[2], first_sums[0], first_sums[1], cross_sums[0], cross_sums[2], sums[5],
            sums[3], sums[4], lax.dynamic_index_in_dim(sums, 8 + z, 0, keepdims=False), sums[2], sums[0], sums[1],
        )
        vectors = lax.psum(rows_of(16, vectors), "dp")
    parts, totals, target_grad, memory_grad = parts_of(
        total_f, total_c, total_s, vectors, target_grad, memory_grad, width, units
    )
    return (
        layer_output, target_grad, memory_grad, parts[0], totals[0], parts[1], parts[2], totals[1], parts[3], totals[2],
        totals[3], totals[4], parts[4], totals[5], parts[5], parts[6], totals[6], parts[7], totals[7], totals[8], totals[9],
        parts[8], totals[10], parts[9], totals[11], totals[12], totals[13],
    )


def solution(mesh):
    rows = P("dp", None)
    split = P(None, "tensor")
    both = P("dp", "tensor")
    turned = P("tensor", "dp")
    own = P("tensor")
    in_specs = (
        rows, rows, rows, rows,
        split, own, split, split, own, P("tensor", None), P(), P(), P(),
        split, own, split, split, own, P("tensor", None), P(), P(), P(),
        split, own, P("tensor", None), P(), P(), P(),
        rows,
    )
    out_specs = (
        rows, both, both,
        both, own, both, both, own, turned, P(), P(), P(),
        both, own, both, both, own, turned, P(), P(), P(),
        both, own, turned, P(), P(), P(),
    )
    return jax.shard_map(
        partial(per_device, mesh.shape["dp"], mesh.shape["tensor"]),
        mesh=mesh,
        in_specs=in_specs,
        out_specs=out_specs,
        check_vma=False,
    )
```
